32 devices in a mesh: dp: 16 (over z, y, core), fsdp: 2 (over x).
Axes of the slice: x: 2, y: 2, z: 4, core: 2. Of those that a mesh axis runs over, the one named last changes fastest.
Arguments:
- text_states: bfloat16 [256, 128, 768], P(('dp', 'fsdp')), may hold values from -6 to 6
- image_states: bfloat16 [64, 36, 1024], P(('dp', 'fsdp')), may hold values from -6 to 6
- text_lengths: int32 [256], P(('dp', 'fsdp')), may hold values from 8 to 128, as said below
- region_mask: int32 [64, 36], P(('dp', 'fsdp')), may hold values from 0 to 1, as said below
- group_ids: int32 [256], P(('dp', 'fsdp')), may hold values from 0 to 63, as said below
- image_query: bfloat16 [1024, 1024], P('dp', 'fsdp'), may hold values from -0.1875 to 0.1875
- image_key: bfloat16 [1024, 1024], P('dp', 'fsdp'), may hold values from -0.1875 to 0.1875
- image_value: bfloat16 [1024, 1024], P('dp', 'fsdp'), may hold values from -0.1875 to 0.1875
- text_query: bfloat16 [768, 1024], P('dp', 'fsdp'), may hold values from -0.21875 to 0.21875
- text_key: bfloat16 [768, 1024], P('dp', 'fsdp'), may hold values from -0.21875 to 0.21875
- text_value: bfloat16 [768, 1024], P('dp', 'fsdp'), may hold values from -0.21875 to 0.21875
- image_output: bfloat16 [1024, 1024], P('dp', 'fsdp'), may hold values from -1.5 to 1.5
- text_output: bfloat16 [1024, 768], P('dp', 'fsdp'), may hold values from -0.75 to 0.75
- image_inner: bfloat16 [1024, 1024], P('dp', 'fsdp'), may hold values from -0.1875 to 0.1875
- image_outer: bfloat16 [1024, 1024], P('dp', 'fsdp'), may hold values from -0.1875 to 0.1875
- text_inner: bfloat16 [768, 3072], P('dp', 'fsdp'), may hold values from -0.21875 to 0.21875
- text_outer: bfloat16 [3072, 768], P('dp', 'fsdp'), may hold values from -0.109375 to 0.109375
- norm_params: float32 [4, 1792], P(None, ('dp', 'fsdp')), may hold values from -1.2 to 2, as said below
- cot_text: bfloat16 [256, 128, 768], P(('dp', 'fsdp')), may hold values from -6 to 6
- cot_image: bfloat16 [256, 36, 1024], P(('dp', 'fsdp')), may hold values from -6 to 6
Outputs:
- text_out: bfloat16 [256, 128, 768], P(('dp', 'fsdp'))
- image_out: bfloat16 [256, 36, 1024], P(('dp', 'fsdp'))
- text_grad: float32 [256, 128, 768], P(('dp', 'fsdp'))
- image_grad: float32 [64, 36, 1024], P(('dp', 'fsdp'))
- image_query_grad: float32 [1024, 1024], P('dp', 'fsdp')
- image_key_grad: float32 [1024, 1024], P('dp', 'fsdp')
- image_value_grad: float32 [1024, 1024], P('dp', 'fsdp')
- text_query_grad: float32 [768, 1024], P('dp', 'fsdp')
- text_key_grad: float32 [768, 1024], P('dp', 'fsdp')
- text_value_grad: float32 [768, 1024], P('dp', 'fsdp')
- image_output_grad: float32 [1024, 1024], P('dp', 'fsdp')
- text_output_grad: float32 [1024, 768], P('dp', 'fsdp')
- image_inner_grad: float32 [1024, 1024], P('dp', 'fsdp')
- image_outer_grad: float32 [1024, 1024], P('dp', 'fsdp')
- text_inner_grad: float32 [768, 3072], P('dp', 'fsdp')
- text_outer_grad: float32 [3072, 768], P('dp', 'fsdp')
- norm_grad: float32 [4, 1792], P(None, ('dp', 'fsdp'))
The draws below stay inside these ranges and needn't reach their ends.
Inputs may be any that keep to these rules, and one draw needn't show every extreme that they name: `text_lengths`: one pair has exactly 128 tokens and one has 8. `region_mask`: each image's regions fill a leading run of its slots, of 9 to 36 regions; one image has 36, one has 9. `group_ids`: the pairs of each aligned block of 8 pairs name the 2 images of the same block index, each of them exactly four times. `norm_params`: rows 0 and 2 are gains between 0.5 and 2, rows 1 and 3 shifts.
All inputs are finite; a program needn't handle non-finite values.
Results may differ from the reference program's by a relative error of at most 0.019.
Values may be sent and summed in bfloat16 or wider, within the bound.
A program may use at most 192 MiB of HBM per device.

```python
import jax
import jax.numpy as jnp
from jax import lax

D_T = 768
D_V = 1024
HEADS = 8
HDIM = 128
FF_T = 3072
FF_V = 1024
L_T = 128
R = 36
PAIR_DEV = 8
BI = 1024
PAIRS = 256
IMAGES = 64


def draw_text_lengths(key, part):
    shortest = max(L_T // 16, 1)
    values = jax.random.randint(key, (PAIRS,), shortest, L_T + 1, dtype=jnp.int32)
    values = values.at[0].set(L_T).at[1].set(shortest)
    return values.astype(jnp.int32)


def draw_region_mask(key, part):
    fewest = max(R // 4, 1)
    counts = jax.random.randint(key, (IMAGES,), fewest, R + 1, dtype=jnp.int32)
    counts = counts.at[0].set(R).at[1].set(fewest)
    slots = jnp.arange(R, dtype=jnp.int32)
    return (slots[None, :] < counts[:, None]).astype(jnp.int32)


def draw_group_ids(key, part):
    blocks = PAIRS // PAIR_DEV
    base = jnp.arange(PAIR_DEV, dtype=jnp.int32) // 4
    keys = jax.random.split(key, blocks)

    def shuffled(block_key):
        return jax.random.permutation(block_key, base)
    local = jax.vmap(shuffled)(keys)
    offsets = jnp.arange(blocks, dtype=jnp.int32)[:, None] * (PAIR_DEV // 4)
    return (local + offsets).reshape(PAIRS).astype(jnp.int32)


def draw_norm_params(key, part):
    first, second = jax.random.split(key)
    width = D_T + D_V
    gains = jnp.exp(jax.random.uniform(first, (2, width), jnp.float32, -0.6, 0.6))
    shifts = jnp.clip(0.4 * jax.random.normal(second, (2, width), jnp.float32), -1.2, 1.2)
    return jnp.stack([gains[0], shifts[0], gains[1], shifts[1]]).astype(jnp.float32)


def block_levels(own_key, dims, pieces, least, largest):
    level = 1.0
    for axis_at, shards_of in pieces:
        draws = jax.random.uniform(jax.random.fold_in(jax.random.fold_in(own_key, 6), axis_at), (shards_of,), jnp.float32, least / len(pieces), largest / len(pieces))
        level = level * jnp.repeat(jnp.exp(draws), dims[axis_at] // shards_of).reshape((-1,) + (1,) * (len(dims) - 1 - axis_at))
    return level


def normal_values(own_key, dims, deviation, most, shards=(), kind=jnp.bfloat16):
    drawn = deviation * jax.random.normal(own_key, dims, jnp.float32)
    if shards:
        drawn = drawn * block_levels(own_key, dims, shards, -0.22, 0.18)
    return jnp.clip(drawn, -most, most).astype(kind)


def setup_inputs(seed: int = 0) -> dict:
    key_of = jax.random.split(jax.random.key(seed), 21)
    text_states = normal_values(key_of[0], (PAIRS, L_T, D_T), 1.0, 6.0, ((0, 32),))
    image_states = normal_values(key_of[1], (IMAGES, R, D_V), 1.0, 6.0, ((0, 32),))
    text_lengths = draw_text_lengths(jax.random.fold_in(key_of[20], 71), 0)
    region_mask = draw_region_mask(jax.random.fold_in(key_of[20], 71), 0)
    group_ids = draw_group_ids(jax.random.fold_in(key_of[20], 71), 0)
    image_query = normal_values(key_of[5], (D_V, BI), D_V ** -0.5, 0.1875, ((0, 16), (1, 2)))
    image_key = normal_values(key_of[6], (D_V, BI), D_V ** -0.5, 0.1875, ((0, 16), (1, 2)))
    image_value = normal_values(key_of[7], (D_V, BI), D_V ** -0.5, 0.1875, ((0, 16), (1, 2)))
    text_query = normal_values(key_of[8], (D_T, BI), D_T ** -0.5, 0.21875, ((0, 16), (1, 2)))
    text_key = normal_values(key_of[9], (D_T, BI), D_T ** -0.5, 0.21875, ((0, 16), (1, 2)))
    text_value = normal_values(key_of[10], (D_T, BI), D_T ** -0.5, 0.21875, ((0, 16), (1, 2)))
    image_output = normal_values(key_of[11], (BI, D_V), (max(BI // 64, 1)) ** -0.5, 1.5, ((0, 16), (1, 2)))
    text_output = normal_values(key_of[12], (BI, D_T), (max(BI // 16, 1)) ** -0.5, 0.75, ((0, 16), (1, 2)))
    image_inner = normal_values(key_of[13], (D_V, FF_V), D_V ** -0.5, 0.1875, ((0, 16), (1, 2)))
    image_outer = normal_values(key_of[14], (FF_V, D_V), FF_V ** -0.5, 0.1875, ((0, 16), (1, 2)))
    text_inner = normal_values(key_of[15], (D_T, FF_T), D_T ** -0.5, 0.21875, ((0, 16), (1, 2)))
    text_outer = normal_values(key_of[16], (FF_T, D_T), FF_T ** -0.5, 0.109375, ((0, 16), (1, 2)))
    norm_params = draw_norm_params(jax.random.fold_in(key_of[20], 71), 0)
    cot_text = normal_values(key_of[18], (PAIRS, L_T, D_T), 1.0, 6.0, ((0, 32),))
    cot_image = normal_values(key_of[19], (PAIRS, R, D_V), 1.0, 6.0, ((0, 32),))
    return dict(text_states=text_states, image_states=image_states, text_lengths=text_lengths, region_mask=region_mask, group_ids=group_ids, image_query=image_query, image_key=image_key, image_value=image_value, text_query=text_query, text_key=text_key, text_value=text_value, image_output=image_output, text_output=text_output, image_inner=image_inner, image_outer=image_outer, text_inner=text_inner, text_outer=text_outer, norm_params=norm_params, cot_text=cot_text, cot_image=cot_image)


@jax.custom_vjp
def low(v):
    return lax.optimization_barrier(v.astype(jnp.bfloat16)).astype(jnp.float32)

@jax.custom_vjp
def low_back(v):
    return v

def low_keep(v):
    return (low(v), None)

def low_pass(kept, grad):
    return (grad,)

def back_keep(v):
    return (v, None)

def back_low(kept, grad):
    return (low(grad),)
low.defvjp(low_keep, low_pass)
low_back.defvjp(back_keep, back_low)
highest = lax.Precision.HIGHEST
norm_eps = 1e-12
masked_score = -1e+30

def rounded(v):
    return low_back(low(v))

def product(x, w):
    return jnp.einsum('bti,io->bto', x, w, precision=highest)

def layer_norm(z, gain, shift):
    centre = lax.optimization_barrier(jnp.mean(z, axis=-1, keepdims=True))
    offset = z - centre
    spread = lax.optimization_barrier(jnp.mean(offset * offset, axis=-1, keepdims=True))
    return offset * lax.rsqrt(spread + norm_eps) * gain + shift

def stream(resid, context, w_out, w_inner, w_outer, norms, keep):
    branch = low_back(product(context, w_out))
    mid = layer_norm(resid + branch, norms[0], norms[1])
    hidden = low_back(product(low(mid), w_inner))
    act = low(jax.nn.gelu(hidden, approximate=False))
    ffn = low_back(product(act, w_outer))
    return layer_norm(mid + ffn, norms[2], norms[3]) * keep[..., None]

def heads_of(x):
    return x.reshape(x.shape[0], x.shape[1], HEADS, HDIM)

def block_forward(weights, norms, text, visual, text_keep, region_keep):
    query_image, key_image, value_image, query_text, key_text, value_text, out_image, out_text, inner_image, outer_image, inner_text, outer_text = weights
    scale = 1.0 / HDIM ** 0.5
    image_queries = heads_of(rounded(product(visual, query_image)))
    image_keys = heads_of(rounded(product(visual, key_image)))
    image_values = heads_of(rounded(product(visual, value_image)))
    text_queries = heads_of(rounded(product(text, query_text)))
    text_keys = heads_of(rounded(product(text, key_text)))
    text_values = heads_of(rounded(product(text, value_text)))
    image_scores = low_back(scale * jnp.einsum('brhe,blhe->bhrl', image_queries, text_keys, precision=highest))
    image_scores = jnp.where(text_keep[:, None, None, :] > 0, image_scores, masked_score)
    image_probs = low(jax.nn.softmax(image_scores, axis=3))
    image_context = rounded(jnp.einsum('bhrl,blhe->brhe', image_probs, text_values, precision=highest))
    image_context = image_context.reshape(visual.shape[0], visual.shape[1], HEADS * HDIM)
    text_scores = low_back(scale * jnp.einsum('brhe,blhe->bhrl', image_keys, text_queries, precision=highest))
    text_scores = jnp.where(region_keep[:, None, :, None] > 0, text_scores, masked_score)
    text_probs = low(jax.nn.softmax(text_scores, axis=2))
    text_context = rounded(jnp.einsum('bhrl,brhe->blhe', text_probs, image_values, precision=highest))
    text_context = text_context.reshape(text.shape[0], text.shape[1], HEADS * HDIM)
    text_out = stream(text, text_context, out_text, inner_text, outer_text, norms[:, :D_T], text_keep)
    image_out = stream(visual, image_context, out_image, inner_image, outer_image, norms[:, D_T:], region_keep)
    return (text_out, image_out)

def reference(text_states, image_states, text_lengths, region_mask, group_ids, image_query, image_key, image_value, text_query, text_key, text_value, image_output, text_output, image_inner, image_outer, text_inner, text_outer, norm_params, cot_text, cot_image):
    positions = jnp.arange(L_T, dtype=jnp.int32)
    text_keep = (positions[None, :] < text_lengths[:, None]).astype(jnp.float32)
    region_keep = jnp.take(region_mask, group_ids, axis=0).astype(jnp.float32)
    weights = (image_query.astype(jnp.float32), image_key.astype(jnp.float32), image_value.astype(jnp.float32), text_query.astype(jnp.float32), text_key.astype(jnp.float32), text_value.astype(jnp.float32), image_output.astype(jnp.float32), text_output.astype(jnp.float32), image_inner.astype(jnp.float32), image_outer.astype(jnp.float32), text_inner.astype(jnp.float32), text_outer.astype(jnp.float32))
    text_float = text_states.astype(jnp.float32)
    image_float = image_states.astype(jnp.float32)
    block_pairs = 16
    blocks = PAIRS // block_pairs

    def forward(weights, norms, text_float, image_float):
        visual = jnp.take(image_float, group_ids, axis=0)

        def run(items):
            return block_forward(weights, norms, items[0], items[1], items[2], items[3])
        text_out, image_out = lax.map(jax.checkpoint(run), (text_float.reshape(blocks, block_pairs, L_T, D_T), visual.reshape(blocks, block_pairs, R, D_V), text_keep.reshape(blocks, block_pairs, L_T), region_keep.reshape(blocks, block_pairs, R)))
        return (text_out.reshape(PAIRS, L_T, D_T), image_out.reshape(PAIRS, R, D_V))
    outputs, pullback = jax.vjp(forward, weights, norm_params, text_float, image_float)
    grads, norm_grad, text_grad, image_grad = pullback((cot_text.astype(jnp.float32), cot_image.astype(jnp.float32)))
    return (outputs[0].astype(jnp.bfloat16), outputs[1].astype(jnp.bfloat16), text_grad, image_grad, grads[0], grads[1], grads[2], grads[3], grads[4], grads[5], grads[6], grads[7], grads[8], grads[9], grads[10], grads[11], norm_grad)
```

```python
import functools
import math

import jax
import jax.numpy as jnp
from jax import lax
from jax.experimental import pallas as pl
from jax.experimental.pallas import tpu as pltpu
from jax.sharding import PartitionSpec as P

HDIM = 128


norm_eps = 1e-12
masked_score = -1e30

MESH_IDS = pl.DeviceIdType.MESH


def bits_of(size):
    count = size.bit_length() - 1
    assert 1 << count == size
    return count


def hop_orders(nd, nf):
    high = [("d", b) for b in range(nd - 1, 2, -1)]
    low = [("d", 2)]
    near = [("d", 1)]
    wide = [("f", b) for b in range(nf)]
    return (
        high + near + low + wide,
        low + high + wide + near,
        high + wide + near + low,
    )


CORE = ("d", 0)


class Place:
    def __init__(self, nd, nf):
        self.d = lax.axis_index("dp")
        self.f = lax.axis_index("fsdp")
        self.axes = [("f", b) for b in range(nf - 1, -1, -1)] + [
            ("d", b) for b in range(nd - 1, -1, -1)
        ]

    def bit(self, axis):
        value = self.f if axis[0] == "f" else self.d
        return lax.rem(value // (1 << axis[1]), 2)

    def partner(self, axis):
        step = (1 << axis[1]) * (1 - 2 * self.bit(axis))
        if axis[0] == "f":
            return (self.d, self.f + step)
        return (self.d + step, self.f)

    def index(self, whole, flip=None):
        picked = []
        for axis in self.axes:
            if axis in whole:
                picked.append(slice(None))
            elif axis == flip:
                picked.append(1 - self.bit(axis))
            else:
                picked.append(self.bit(axis))
        return tuple(picked)

    def barrier(self):
        sem = pltpu.get_barrier_semaphore()
        for axis in self.axes:
            pl.semaphore_signal(
                sem, inc=1, device_id=self.partner(axis), device_id_type=MESH_IDS
            )
        pl.semaphore_wait(sem, len(self.axes))


def gather_kernel(nd, nf, routes, *refs):
    count = len(routes)
    ins, outs = refs[:count], refs[count : 2 * count]
    local_sem, send_sem, recv_sem = refs[2 * count :]
    place = Place(nd, nf)
    local = []
    for m in range(count):
        copy = pltpu.make_async_copy(ins[m], outs[m].at[place.index(())], local_sem.at[m])
        copy.start()
        local.append(copy)
    place.barrier()
    hops = len(routes[0])
    sent = [[] for _ in range(count)]
    for h in range(hops):
        for m in range(count):
            if h == 0:
                local[m].wait()
            else:
                sent[m][h - 1].wait_recv()
            region = outs[m].at[place.index(routes[m][:h])]
            copy = pltpu.make_async_remote_copy(
                src_ref=region,
                dst_ref=region,
                send_sem=send_sem.at[m, h],
                recv_sem=recv_sem.at[m, h],
                device_id=place.partner(routes[m][h]),
                device_id_type=MESH_IDS,
            )
            copy.start()
            sent[m].append(copy)
    for m in range(count):
        sent[m][hops - 1].wait_recv()
        for h in range(hops):
            sent[m][h].wait_send()


def gather_blocks(shards, parts, nd, nf, collective_id):
    orders = hop_orders(nd, nf)
    routes = [tuple(orders[part]) + (CORE,) for part in parts]
    count, hops = len(shards), len(routes[0])
    lead = (2,) * (nd + nf)
    return pl.pallas_call(
        functools.partial(gather_kernel, nd, nf, routes),
        out_shape=[jax.ShapeDtypeStruct(lead + s.shape, s.dtype) for s in shards],
        in_specs=[pl.BlockSpec(memory_space=pl.ANY)] * count,
        out_specs=[pl.BlockSpec(memory_space=pl.ANY)] * count,
        scratch_shapes=[
            pltpu.SemaphoreType.DMA((count,)),
            pltpu.SemaphoreType.DMA((count, hops)),
            pltpu.SemaphoreType.DMA((count, hops)),
        ],
        compiler_params=pltpu.CompilerParams(
            collective_id=collective_id, has_side_effects=True
        ),
    )(*shards)


def add_blocks(place, acc, index, incoming, out=None):
    lead = incoming.shape[:-2]
    total = math.prod(lead)

    def spot(i):
        inner = []
        for size in reversed(lead):
            inner.append(lax.rem(i, size))
            i = i // size
        return tuple(reversed(inner))

    def full(at):
        at = list(at)
        return tuple(at.pop(0) if isinstance(p, slice) else p for p in index)

    if out is not None:
        out[...] = acc[index].astype(jnp.float32) + incoming[...].astype(jnp.float32)
        return

    def one(i, carry):
        at = spot(i)
        where = full(at)
        acc[where] = acc[where] + incoming[at]
        return carry

    lax.fori_loop(0, total, one, 0)


def reduce_kernel(nd, nf, routes, *refs):
    count = len(routes)
    hops = len(routes[0])
    ins, outs = refs[:count], refs[count : 2 * count]
    accs = refs[2 * count : 3 * count]
    temps = [refs[3 * count + m * hops : 3 * count + (m + 1) * hops] for m in range(count)]
    local_sem, send_sem, recv_sem = refs[3 * count + count * hops :]
    place = Place(nd, nf)
    rest = [axis for axis in place.axes if axis != CORE]
    local = []
    for m in range(count):
        copy = pltpu.make_async_copy(ins[m].at[place.index(rest)], accs[m], local_sem.at[m])
        copy.start()
        local.append(copy)
    place.barrier()
    sent = [[] for _ in range(count)]

    def send(m, h, region):
        copy = pltpu.make_async_remote_copy(
            src_ref=region,
            dst_ref=temps[m][h],
            send_sem=send_sem.at[m, h],
            recv_sem=recv_sem.at[m, h],
            device_id=place.partner(routes[m][h]),
            device_id_type=MESH_IDS,
        )
        copy.start()
        sent[m].append(copy)

    def within(m, h, flip=None):
        whole = routes[m][h + 1 :]
        full = place.index(whole, flip)
        return tuple(p for p, axis in zip(full, place.axes) if axis != CORE)

    for m in range(count):
        send(m, 0, ins[m].at[place.index(routes[m][1:], CORE)])
    for m in range(count):
        local[m].wait()
    for h in range(1, hops + 1):
        for m in range(count):
            sent[m][h - 1].wait_recv()
            here = within(m, h - 1)
            if h == hops:
                add_blocks(place, accs[m], here, temps[m][h - 1], outs[m])
            else:
                add_blocks(place, accs[m], here, temps[m][h - 1])
                send(m, h, accs[m].at[within(m, h, routes[m][h])])
    for m in range(count):
        for h in range(hops):
            sent[m][h].wait_send()


def reduce_blocks(blocks, parts, nd, nf, collective_id):
    orders = hop_orders(nd, nf)
    routes = [(CORE,) + tuple(reversed(orders[part])) for part in parts]
    count, hops = len(blocks), len(routes[0])
    shapes = [b.shape[-2:] for b in blocks]
    scratch = [
        pltpu.VMEM((2,) * (nd + nf - 1) + s, b.dtype) for s, b in zip(shapes, blocks)
    ]
    for s, b in zip(shapes, blocks):
        for h in range(hops):
            scratch.append(pltpu.VMEM((2,) * (hops - 1 - h) + s, b.dtype))
    return pl.pallas_call(
        functools.partial(reduce_kernel, nd, nf, routes),
        out_shape=[jax.ShapeDtypeStruct(s, jnp.float32) for s in shapes],
        in_specs=[pl.BlockSpec(memory_space=pl.ANY)] * count,
        out_specs=[pl.BlockSpec(memory_space=pltpu.VMEM)] * count,
        scratch_shapes=scratch
        + [
            pltpu.SemaphoreType.DMA((count,)),
            pltpu.SemaphoreType.DMA((count, hops)),
            pltpu.SemaphoreType.DMA((count, hops)),
        ],
        compiler_params=pltpu.CompilerParams(
            collective_id=collective_id,
            has_side_effects=True,
            vmem_limit_bytes=60 * 1024 * 1024,
        ),
    )(*blocks)


def layer_norm(z, gain, shift):
    centre = jnp.mean(z, axis=-1, keepdims=True)
    offset = z - centre
    spread = jnp.mean(offset * offset, axis=-1, keepdims=True)
    return offset * lax.rsqrt(spread + norm_eps) * gain + shift


def gelu_exact(value):
    return jax.nn.gelu(value, approximate=False)


def project(inputs, matrix):
    return jnp.einsum("bti,io->bto", inputs, matrix, preferred_element_type=jnp.float32)


def project_back(grads, matrix):
    return jnp.einsum("bto,io->bti", grads, matrix, preferred_element_type=jnp.float32)


def weight_grad(inputs, grads):
    return jnp.einsum("bti,bto->io", inputs, grads, preferred_element_type=jnp.float32)


def split_heads(value):
    return value.reshape(value.shape[0], value.shape[1], value.shape[2] // HDIM, HDIM)


def merge_low(value):
    return value.reshape(value.shape[0], value.shape[1], -1).astype(jnp.bfloat16)


PARTS = (0, 1, 2, 0, 1, 2, 2, 0, 2, 1, 0, 1)


def mesh_bits():
    return bits_of(lax.axis_size("dp")), bits_of(lax.axis_size("fsdp"))


def gather_weights(shards, norm_params):
    nd, nf = mesh_bits()
    devices = 1 << (nd + nf)
    wide = norm_params.shape[1]
    padded = jnp.pad(norm_params, ((0, 8 - norm_params.shape[0]), (0, 128 - wide)))
    blocks = gather_blocks(list(shards) + [padded], PARTS + (0,), nd, nf, 0)
    weights = []
    for shard, block in zip(shards, blocks):
        rows, cols = shard.shape
        block = block.reshape(1 << nf, rows << nd, cols)
        weights.append(jnp.swapaxes(block, 0, 1).reshape(rows << nd, cols << nf))
    norms = blocks[-1].reshape(1 << nf, 1 << nd, 8, 128)[:, :, :4, :wide]
    norms = norms.transpose(2, 1, 0, 3).reshape(4, devices * wide)
    return tuple(weights), norms


def reduce_grads(grads, norm_rows):
    nd, nf = mesh_bits()
    lead = (2,) * (nd + nf)
    blocks = []
    for grad in grads:
        rows, cols = grad.shape[0] >> nd, grad.shape[1] >> nf
        low = grad.astype(jnp.bfloat16).reshape(grad.shape[0], 1 << nf, cols)
        blocks.append(jnp.swapaxes(low, 0, 1).reshape(lead + (rows, cols)))
    wide = norm_rows.shape[1] >> (nd + nf)
    split = norm_rows.reshape(4, 1 << nd, 1 << nf, wide).transpose(2, 1, 0, 3)
    split = jnp.pad(split, ((0, 0), (0, 0), (0, 4), (0, 128 - wide)))
    blocks.append(split.reshape(lead + (8, 128)))
    owned = reduce_blocks(blocks, PARTS + (0,), nd, nf, 1)
    return tuple(owned[:-1]), owned[-1][:4, :wide]


def stream_forward(resid, context, w_out, w_inner, w_outer, norms, keep):
    branch = project(context, w_out)
    mid, first_back = jax.vjp(layer_norm, resid + branch, norms[0], norms[1])
    mid_low = mid.astype(jnp.bfloat16)
    hidden = project(mid_low, w_inner)
    act = gelu_exact(hidden).astype(jnp.bfloat16)
    ffn = project(act, w_outer)

    def closing(total, gain, shift):
        return layer_norm(total, gain, shift) * keep[..., None]

    result, second_back = jax.vjp(closing, mid + ffn, norms[2], norms[3])
    return (result, (first_back, second_back, mid_low, hidden, act))


def stream_backward(cotangent, kept, context, w_out, w_inner, w_outer):
    first_back, second_back, mid_low, hidden, act = kept
    second_dz, second_gain, second_shift = second_back(cotangent)
    ffn_low = second_dz.astype(jnp.bfloat16)
    outer_grad = weight_grad(act, ffn_low)
    act_grad = project_back(ffn_low, w_outer)
    hidden_grad = jax.vjp(gelu_exact, hidden)[1](act_grad)[0]
    hidden_low = hidden_grad.astype(jnp.bfloat16)
    inner_grad = weight_grad(mid_low, hidden_low)
    mid_grad = second_dz + project_back(hidden_low, w_inner)
    first_dz, first_gain, first_shift = first_back(mid_grad)
    branch_low = first_dz.astype(jnp.bfloat16)
    out_grad = weight_grad(context, branch_low)
    context_grad = project_back(branch_low, w_out).astype(jnp.bfloat16)
    return (
        first_dz,
        context_grad,
        (out_grad, inner_grad, outer_grad),
        (first_gain, first_shift, second_gain, second_shift),
    )


def body(
    text_states,
    image_states,
    text_lengths,
    region_mask,
    group_ids,
    image_query,
    image_key,
    image_value,
    text_query,
    text_key,
    text_value,
    image_output,
    text_output,
    image_inner,
    image_outer,
    text_inner,
    text_outer,
    norm_params,
    cot_text,
    cot_image,
):
    shards = (
        image_query,
        image_key,
        image_value,
        text_query,
        text_key,
        text_value,
        image_output,
        text_output,
        image_inner,
        image_outer,
        text_inner,
        text_outer,
    )
    weights, norms = gather_weights(shards, norm_params)
    width_text = text_states.shape[2]
    images = image_states.shape[0]
    length = text_states.shape[1]
    device = lax.axis_index("dp") * lax.axis_size("fsdp") + lax.axis_index("fsdp")
    local = group_ids - device * images
    visual = jnp.take(image_states, local, axis=0)
    text_keep = (jnp.arange(length, dtype=jnp.int32)[None, :] < text_lengths[:, None]).astype(
        jnp.float32
    )
    region_keep = jnp.take(region_mask, local, axis=0).astype(jnp.float32)
    scale = 1.0 / math.sqrt(HDIM)
    (
        query_image,
        key_image,
        value_image,
        query_text,
        key_text,
        value_text,
        out_image,
        out_text,
        inner_image,
        outer_image,
        inner_text,
        outer_text,
    ) = weights
    image_queries = split_heads(project(visual, query_image).astype(jnp.bfloat16))
    image_keys = split_heads(project(visual, key_image).astype(jnp.bfloat16))
    image_values = split_heads(project(visual, value_image).astype(jnp.bfloat16))
    text_queries = split_heads(project(text_states, query_text).astype(jnp.bfloat16))
    text_keys = split_heads(project(text_states, key_text).astype(jnp.bfloat16))
    text_values = split_heads(project(text_states, value_text).astype(jnp.bfloat16))
    image_scores = scale * jnp.einsum(
        "brhe,blhe->bhrl", image_queries, text_keys, preferred_element_type=jnp.float32
    )
    image_scores = jnp.where(text_keep[:, None, None, :] > 0, image_scores, masked_score)
    image_probs = jax.nn.softmax(image_scores, axis=3)
    image_low = image_probs.astype(jnp.bfloat16)
    image_context = merge_low(
        jnp.einsum("bhrl,blhe->brhe", image_low, text_values, preferred_element_type=jnp.float32)
    )
    text_scores = scale * jnp.einsum(
        "brhe,blhe->bhrl", image_keys, text_queries, preferred_element_type=jnp.float32
    )
    text_scores = jnp.where(region_keep[:, None, :, None] > 0, text_scores, masked_score)
    text_probs = jax.nn.softmax(text_scores, axis=2)
    text_low = text_probs.astype(jnp.bfloat16)
    text_context = merge_low(
        jnp.einsum("bhrl,brhe->blhe", text_low, image_values, preferred_element_type=jnp.float32)
    )
    text_result, text_kept = stream_forward(
        text_states.astype(jnp.float32),
        text_context,
        out_text,
        inner_text,
        outer_text,
        norms[:, :width_text],
        text_keep,
    )
    image_result, image_kept = stream_forward(
        visual.astype(jnp.float32),
        image_context,
        out_image,
        inner_image,
        outer_image,
        norms[:, width_text:],
        region_keep,
    )
    text_dz, text_dcontext, text_wgrads, text_ngrads = stream_backward(
        cot_text.astype(jnp.float32), text_kept, text_context, out_text, inner_text, outer_text
    )
    image_dz, image_dcontext, image_wgrads, image_ngrads = stream_backward(
        cot_image.astype(jnp.float32),
        image_kept,
        image_context,
        out_image,
        inner_image,
        outer_image,
    )
    image_ctx_grad = split_heads(image_dcontext)
    text_ctx_grad = split_heads(text_dcontext)
    image_dprobs = jnp.einsum(
        "brhe,blhe->bhrl", image_ctx_grad, text_values, preferred_element_type=jnp.float32
    )
    text_values_grad = jnp.einsum(
        "bhrl,brhe->blhe", image_low, image_ctx_grad, preferred_element_type=jnp.float32
    )
    image_dscores = (
        image_probs * (image_dprobs - jnp.sum(image_probs * image_dprobs, axis=3, keepdims=True))
    ).astype(jnp.bfloat16)
    image_queries_grad = scale * jnp.einsum(
        "bhrl,blhe->brhe", image_dscores, text_keys, preferred_element_type=jnp.float32
    )
    text_keys_grad = scale * jnp.einsum(
        "bhrl,brhe->blhe", image_dscores, image_queries, preferred_element_type=jnp.float32
    )
    text_dprobs = jnp.einsum(
        "blhe,brhe->bhrl", text_ctx_grad, image_values, preferred_element_type=jnp.float32
    )
    image_values_grad = jnp.einsum(
        "bhrl,blhe->brhe", text_low, text_ctx_grad, preferred_element_type=jnp.float32
    )
    text_dscores = (
        text_probs * (text_dprobs - jnp.sum(text_probs * text_dprobs, axis=2, keepdims=True))
    ).astype(jnp.bfloat16)
    text_queries_grad = scale * jnp.einsum(
        "bhrl,brhe->blhe", text_dscores, image_keys, preferred_element_type=jnp.float32
    )
    image_keys_grad = scale * jnp.einsum(
        "bhrl,blhe->brhe", text_dscores, text_queries, preferred_element_type=jnp.float32
    )
    image_query_low = merge_low(image_queries_grad)
    image_key_low = merge_low(image_keys_grad)
    image_value_low = merge_low(image_values_grad)
    text_query_low = merge_low(text_queries_grad)
    text_key_low = merge_low(text_keys_grad)
    text_value_low = merge_low(text_values_grad)
    visual_grad = (
        image_dz
        + project_back(image_query_low, query_image)
        + project_back(image_key_low, key_image)
    )
    visual_grad = visual_grad + project_back(image_value_low, value_image)
    selector = (local[:, None] == jnp.arange(images, dtype=jnp.int32)[None, :]).astype(jnp.float32)
    image_grad = jnp.einsum("pi,prd->ird", selector, visual_grad, precision=lax.Precision.HIGHEST)
    text_grad = (
        text_dz + project_back(text_query_low, query_text) + project_back(text_key_low, key_text)
    )
    text_grad = text_grad + project_back(text_value_low, value_text)
    local_grads = (
        weight_grad(visual, image_query_low),
        weight_grad(visual, image_key_low),
        weight_grad(visual, image_value_low),
        weight_grad(text_states, text_query_low),
        weight_grad(text_states, text_key_low),
        weight_grad(text_states, text_value_low),
        image_wgrads[0],
        text_wgrads[0],
        image_wgrads[1],
        image_wgrads[2],
        text_wgrads[1],
        text_wgrads[2],
    )
    norm_rows = jnp.stack(
        [
            jnp.concatenate([text_ngrads[0], image_ngrads[0]]),
            jnp.concatenate([text_ngrads[1], image_ngrads[1]]),
            jnp.concatenate([text_ngrads[2], image_ngrads[2]]),
            jnp.concatenate([text_ngrads[3], image_ngrads[3]]),
        ]
    )
    owned, norm_grad = reduce_grads(local_grads, norm_rows)
    return (
        text_result.astype(jnp.bfloat16),
        image_result.astype(jnp.bfloat16),
        text_grad,
        image_grad,
        owned[0],
        owned[1],
        owned[2],
        owned[3],
        owned[4],
        owned[5],
        owned[6],
        owned[7],
        owned[8],
        owned[9],
        owned[10],
        owned[11],
        norm_grad,
    )


def solution(mesh):
    placed = (
        P(("dp", "fsdp"), None, None),
        P(("dp", "fsdp"), None, None),
        P(("dp", "fsdp")),
        P(("dp", "fsdp"), None),
        P(("dp", "fsdp")),
        P("dp", "fsdp"),
        P("dp", "fsdp"),
        P("dp", "fsdp"),
        P("dp", "fsdp"),
        P("dp", "fsdp"),
        P("dp", "fsdp"),
        P("dp", "fsdp"),
        P("dp", "fsdp"),
        P("dp", "fsdp"),
        P("dp", "fsdp"),
        P("dp", "fsdp"),
        P("dp", "fsdp"),
        P(None, ("dp", "fsdp")),
        P(("dp", "fsdp"), None, None),
        P(("dp", "fsdp"), None, None),
    )
    return jax.shard_map(
        body,
        mesh=mesh,
        in_specs=placed,
        out_specs=(
            P(("dp", "fsdp"), None, None),
            P(("dp", "fsdp"), None, None),
            P(("dp", "fsdp"), None, None),
            P(("dp", "fsdp"), None, None),
            P("dp", "fsdp"),
            P("dp", "fsdp"),
            P("dp", "fsdp"),
            P("dp", "fsdp"),
            P("dp", "fsdp"),
            P("dp", "fsdp"),
            P("dp", "fsdp"),
            P("dp", "fsdp"),
            P("dp", "fsdp"),
            P("dp", "fsdp"),
            P("dp", "fsdp"),
            P("dp", "fsdp"),
            P(None, ("dp", "fsdp")),
        ),
        check_vma=False,
    )
```

```python
import functools
import math

import jax
import jax.numpy as jnp
from jax import lax
from jax.experimental import pallas as pl
from jax.experimental.pallas import tpu as pltpu
from jax.sharding import PartitionSpec as P

HDIM = 128

norm_eps = 1e-12
masked_score = -1e30

MESH_IDS = pl.DeviceIdType.MESH


def bits_of(size):
    count = size.bit_length() - 1
    assert 1 << count == size
    return count


def hop_orders(nd, nf):
    high = [("d", b) for b in range(nd - 1, 2, -1)]
    low = [("d", 2)]
    near = [("d", 1)]
    wide = [("f", b) for b in range(nf)]
    return (
        high + near + low + wide,
        low + high + wide + near,
        high + wide + near + low,
    )


CORE = ("d", 0)


class Place:
    def __init__(self, nd, nf):
        self.d = lax.axis_index("dp")
        self.f = lax.axis_index("fsdp")
        self.axes = [("f", b) for b in range(nf - 1, -1, -1)] + [
            ("d", b) for b in range(nd - 1, -1, -1)
        ]

    def bit(self, axis):
        value = self.f if axis[0] == "f" else self.d
        return lax.rem(value // (1 << axis[1]), 2)

    def partner(self, axis):
        step = (1 << axis[1]) * (1 - 2 * self.bit(axis))
        if axis[0] == "f":
            return (self.d, self.f + step)
        return (self.d + step, self.f)

    def index(self, whole, flip=None):
        picked = []
        for axis in self.axes:
            if axis in whole:
                picked.append(slice(None))
            elif axis == flip:
                picked.append(1 - self.bit(axis))
            else:
                picked.append(self.bit(axis))
        return tuple(picked)

    def barrier(self):
        sem = pltpu.get_barrier_semaphore()
        for axis in self.axes:
            pl.semaphore_signal(
                sem, inc=1, device_id=self.partner(axis), device_id_type=MESH_IDS
            )
        pl.semaphore_wait(sem, len(self.axes))


def gather_kernel(nd, nf, routes, *refs):
    count = len(routes)
    ins, outs = refs[:count], refs[count : 2 * count]
    local_sem, send_sem, recv_sem = refs[2 * count :]
    place = Place(nd, nf)
    local = []
    for m in range(count):
        copy = pltpu.make_async_copy(ins[m], outs[m].at[place.index(())], local_sem.at[m])
        copy.start()
        local.append(copy)
    place.barrier()
    hops = len(routes[0])
    sent = [[] for _ in range(count)]
    for h in range(hops):
        for m in range(count):
            if h == 0:
                local[m].wait()
            else:
                sent[m][h - 1].wait_recv()
            region = outs[m].at[place.index(routes[m][:h])]
            copy = pltpu.make_async_remote_copy(
                src_ref=region,
                dst_ref=region,
                send_sem=send_sem.at[m, h],
                recv_sem=recv_sem.at[m, h],
                device_id=place.partner(routes[m][h]),
                device_id_type=MESH_IDS,
            )
            copy.start()
            sent[m].append(copy)
    for m in range(count):
        sent[m][hops - 1].wait_recv()
        for h in range(hops):
            sent[m][h].wait_send()


def gather_blocks(shards, parts, nd, nf, collective_id):
    orders = hop_orders(nd, nf)
    routes = [tuple(orders[part]) + (CORE,) for part in parts]
    count, hops = len(shards), len(routes[0])
    lead = (2,) * (nd + nf)
    return pl.pallas_call(
        functools.partial(gather_kernel, nd, nf, routes),
        out_shape=[jax.ShapeDtypeStruct(lead + s.shape, s.dtype) for s in shards],
        in_specs=[pl.BlockSpec(memory_space=pl.ANY)] * count,
        out_specs=[pl.BlockSpec(memory_space=pl.ANY)] * count,
        scratch_shapes=[
            pltpu.SemaphoreType.DMA((count,)),
            pltpu.SemaphoreType.DMA((count, hops)),
            pltpu.SemaphoreType.DMA((count, hops)),
        ],
        compiler_params=pltpu.CompilerParams(
            collective_id=collective_id, has_side_effects=True
        ),
    )(*shards)


def add_blocks(place, acc, index, incoming, out=None):
    lead = incoming.shape[:-2]
    total = math.prod(lead)

    def spot(i):
        inner = []
        for size in reversed(lead):
            inner.append(lax.rem(i, size))
            i = i // size
        return tuple(reversed(inner))

    def full(at):
        at = list(at)
        return tuple(at.pop(0) if isinstance(p, slice) else p for p in index)

    if out is not None:
        out[...] = acc[index].astype(jnp.float32) + incoming[...].astype(jnp.float32)
        return

    def one(i, carry):
        at = spot(i)
        where = full(at)
        acc[where] = acc[where] + incoming[at]
        return carry

    lax.fori_loop(0, total, one, 0)


def reduce_kernel(nd, nf, routes, *refs):
    count = len(routes)
    hops = len(routes[0])
    ins, outs = refs[:count], refs[count : 2 * count]
    accs = refs[2 * count : 3 * count]
    temps = [refs[3 * count + m * hops : 3 * count + (m + 1) * hops] for m in range(count)]
    local_sem, send_sem, recv_sem = refs[3 * count + count * hops :]
    place = Place(nd, nf)
    rest = [axis for axis in place.axes if axis != CORE]
    local = []
    for m in range(count):
        copy = pltpu.make_async_copy(ins[m].at[place.index(rest)], accs[m], local_sem.at[m])
        copy.start()
        local.append(copy)
    place.barrier()
    sent = [[] for _ in range(count)]

    def send(m, h, region):
        copy = pltpu.make_async_remote_copy(
            src_ref=region,
            dst_ref=temps[m][h],
            send_sem=send_sem.at[m, h],
            recv_sem=recv_sem.at[m, h],
            device_id=place.partner(routes[m][h]),
            device_id_type=MESH_IDS,
        )
        copy.start()
        sent[m].append(copy)

    def within(m, h, flip=None):
        whole = routes[m][h + 1 :]
        full = place.index(whole, flip)
        return tuple(p for p, axis in zip(full, place.axes) if axis != CORE)

    for m in range(count):
        send(m, 0, ins[m].at[place.index(routes[m][1:], CORE)])
    for m in range(count):
        local[m].wait()
    for h in range(1, hops + 1):
        for m in range(count):
            sent[m][h - 1].wait_recv()
            here = within(m, h - 1)
            if h == hops:
                add_blocks(place, accs[m], here, temps[m][h - 1], outs[m])
            else:
                add_blocks(place, accs[m], here, temps[m][h - 1])
                send(m, h, accs[m].at[within(m, h, routes[m][h])])
    for m in range(count):
        for h in range(hops):
            sent[m][h].wait_send()


def reduce_blocks(blocks, parts, nd, nf, collective_id):
    orders = hop_orders(nd, nf)
    routes = [(CORE,) + tuple(reversed(orders[part])) for part in parts]
    count, hops = len(blocks), len(routes[0])
    shapes = [b.shape[-2:] for b in blocks]
    scratch = [
        pltpu.VMEM((2,) * (nd + nf - 1) + s, b.dtype) for s, b in zip(shapes, blocks)
    ]
    for s, b in zip(shapes, blocks):
        for h in range(hops):
            scratch.append(pltpu.VMEM((2,) * (hops - 1 - h) + s, b.dtype))
    return pl.pallas_call(
        functools.partial(reduce_kernel, nd, nf, routes),
        out_shape=[jax.ShapeDtypeStruct(s, jnp.float32) for s in shapes],
        in_specs=[pl.BlockSpec(memory_space=pl.ANY)] * count,
        out_specs=[pl.BlockSpec(memory_space=pltpu.VMEM)] * count,
        scratch_shapes=scratch
        + [
            pltpu.SemaphoreType.DMA((count,)),
            pltpu.SemaphoreType.DMA((count, hops)),
            pltpu.SemaphoreType.DMA((count, hops)),
        ],
        compiler_params=pltpu.CompilerParams(
            collective_id=collective_id,
            has_side_effects=True,
            vmem_limit_bytes=60 * 1024 * 1024,
        ),
    )(*blocks)


def dot_nn(a, b):
    return lax.dot_general(a, b, (((1,), (0,)), ((), ())), preferred_element_type=jnp.float32)


def dot_nt(a, b):
    return lax.dot_general(a, b, (((1,), (1,)), ((), ())), preferred_element_type=jnp.float32)


def dot_tn(a, b):
    return lax.dot_general(a, b, (((0,), (0,)), ((), ())), preferred_element_type=jnp.float32)


def low(value):
    return value.astype(jnp.bfloat16)


def times(value, matrix):
    parts = [dot_nn(value, matrix[f]) for f in range(matrix.shape[0])]
    return parts[0] if len(parts) == 1 else jnp.concatenate(parts, axis=1)


def times_back(value, matrix):
    cols = matrix.shape[2]
    total = None
    for f in range(matrix.shape[0]):
        term = dot_nt(value[:, f * cols : (f + 1) * cols], matrix[f])
        total = term if total is None else total + term
    return total


VMEM_LIMIT = 60 * 1024 * 1024
WHOLE = pl.BlockSpec(memory_space=pltpu.VMEM)
SCALARS = pl.BlockSpec(memory_space=pltpu.SMEM)


def project_rows(x_ref, w_ref, out_ref, block):
    cols = w_ref.shape[2]

    def one(i, carry):
        at = pl.ds(pl.multiple_of(i * block, block), block)
        rows = x_ref[at, :]
        for f in range(w_ref.shape[0]):
            out_ref[at, f * cols : (f + 1) * cols] = low(dot_nn(rows, w_ref[f]))
        return carry

    lax.fori_loop(0, x_ref.shape[0] // block, one, 0)


def softmax(scores, axis):
    top = jnp.max(scores, axis=axis, keepdims=True)
    weight = jnp.exp(scores - top)
    return weight / jnp.sum(weight, axis=axis, keepdims=True)


def attention_pair(p, refs):
    (lens, owner, counts, iq, ik, iv, tq, tk, tv, iprob, tprob, ictx, tctx) = refs
    regions = iprob.shape[1]
    length = tq.shape[0] // lens.shape[0]
    heads = tq.shape[1] // HDIM
    scale = 1.0 / math.sqrt(HDIM)
    image = owner[p]
    kept_text = lax.broadcasted_iota(jnp.int32, (regions, length), 1) < lens[p]
    kept_region = lax.broadcasted_iota(jnp.int32, (regions, length), 0) < counts[p]
    rows_t = pl.ds(pl.multiple_of(p * length, length), length)
    rows_i = pl.ds(pl.multiple_of(p * regions, regions), regions)
    for h in range(heads):
        at = slice(h * HDIM, (h + 1) * HDIM)
        scores = scale * dot_nt(iq[image, :, at], tk[rows_t, at])
        probs = softmax(jnp.where(kept_text, scores, masked_score), 1)
        iprob[p * heads + h] = probs
        ictx[rows_i, at] = low(dot_nn(low(probs), tv[rows_t, at]))
        scores = scale * dot_nt(ik[image, :, at], tq[rows_t, at])
        probs = softmax(jnp.where(kept_region, scores, masked_score), 0)
        tprob[p * heads + h] = probs
        tctx[rows_t, at] = low(dot_tn(low(probs), iv[image, :, at]))


def forward_kernel(lens, owner, counts, text, image, *refs):
    weights, (iq, ik, iv, tq, tk, tv, iprob, tprob, ictx, tctx) = refs[:6], refs[6:]
    for w_ref, out_ref in zip(weights[:3], (iq, ik, iv)):
        wide = times(image[...], w_ref)
        out_ref[...] = low(wide).reshape(out_ref.shape)
    for w_ref, out_ref in zip(weights[3:], (tq, tk, tv)):
        project_rows(text, w_ref, out_ref, 256)
    shared = (lens, owner, counts, iq, ik, iv, tq, tk, tv, iprob, tprob, ictx, tctx)

    def one(p, carry):
        attention_pair(p, shared)
        return carry

    lax.fori_loop(0, lens.shape[0], one, 0)


def forward_attention(lens, owner, counts, text, image, weights, images):
    pairs = lens.shape[0]
    regions = image.shape[0] // images
    wide = weights[0].shape[0] * weights[0].shape[2]
    heads = wide // HDIM
    length = text.shape[0] // pairs
    bf = jnp.bfloat16
    shapes = (
        [jax.ShapeDtypeStruct((images, regions, wide), bf)] * 3
        + [jax.ShapeDtypeStruct((text.shape[0], wide), bf)] * 3
        + [jax.ShapeDtypeStruct((pairs * heads, regions, length), jnp.float32)] * 2
        + [
            jax.ShapeDtypeStruct((pairs * regions, wide), bf),
            jax.ShapeDtypeStruct((text.shape[0], wide), bf),
        ]
    )
    return pl.pallas_call(
        forward_kernel,
        out_shape=shapes,
        in_specs=[SCALARS] * 3 + [WHOLE] * 8,
        out_specs=[WHOLE] * len(shapes),
        compiler_params=pltpu.CompilerParams(vmem_limit_bytes=VMEM_LIMIT),
    )(lens, owner, counts, text, image, *weights)


def gelu_pair(x):
    scaled = jnp.abs(x) * (1.0 / math.sqrt(2.0))
    bell = jnp.exp(-0.5 * x * x)
    t = 1.0 / (1.0 + 0.3275911 * scaled)
    poly = t * (
        0.254829592
        + t * (-0.284496736 + t * (1.421413741 + t * (-1.453152027 + t * 1.061405429)))
    )
    tail = 0.5 * poly * bell
    below = jnp.where(x < 0, tail, 1.0 - tail)
    return x * below, below + x * bell * (1.0 / math.sqrt(2.0 * math.pi))


def row_mean(value):
    return jnp.mean(value, axis=-1, keepdims=True)


def col_sum(value):
    return jnp.sum(value, axis=0, keepdims=True)


def stream_kernel(x, ctx, cot, keep, norms, w_out, w_inner, w_outer, *refs):
    (out, dz_out, mid_out, act_out, hid_out, ffn_out, branch_out, dctx_out, ngrad, slope) = refs

    def normalize(z):
        offset = z - row_mean(z)
        inv = lax.rsqrt(row_mean(offset * offset) + norm_eps)
        return offset * inv, inv

    def normalize_back(dy, xhat, inv, gain):
        dx = dy * gain
        return inv * (dx - row_mean(dx) - xhat * row_mean(dx * xhat))

    kept = keep[...]
    first_hat, first_inv = normalize(x[...].astype(jnp.float32) + times(ctx[...], w_out))
    mid = first_hat * norms[0:1, :] + norms[1:2, :]
    mid_low = low(mid)
    mid_out[...] = mid_low
    cols = w_inner.shape[2]
    for f in range(w_inner.shape[0]):
        at = slice(f * cols, (f + 1) * cols)
        act, grad = gelu_pair(dot_nn(mid_low, w_inner[f]))
        act_out[:, at] = low(act)
        slope[:, at] = grad
    second_hat, second_inv = normalize(mid + times(act_out[...], w_outer))
    out[...] = low((second_hat * norms[2:3, :] + norms[3:4, :]) * kept)
    dy = cot[...].astype(jnp.float32) * kept
    second_dz = normalize_back(dy, second_hat, second_inv, norms[2:3, :])
    ffn_low = low(second_dz)
    ffn_out[...] = ffn_low
    rows = [col_sum(dy * second_hat), col_sum(dy)]
    hid_out[...] = low(times_back(ffn_low, w_outer) * slope[...])
    mid_grad = second_dz + times_back(hid_out[...], w_inner)
    first_dz = normalize_back(mid_grad, first_hat, first_inv, norms[0:1, :])
    dz_out[...] = first_dz
    branch_low = low(first_dz)
    branch_out[...] = branch_low
    dctx_out[...] = low(times_back(branch_low, w_out))
    rows = [col_sum(mid_grad * first_hat), col_sum(mid_grad)] + rows

    @pl.when(pl.program_id(0) == 0)
    def _():
        ngrad[...] = jnp.zeros_like(ngrad)

    for r in range(4):
        ngrad[r : r + 1, :] += rows[r]


def stream(x, ctx, cot, keep, norms, w_out, w_inner, w_outer, block):
    rows, wide = x.shape
    inner = w_inner.shape[0] * w_inner.shape[2]
    bi = ctx.shape[1]
    bf, f32 = jnp.bfloat16, jnp.float32

    def by_row(cols):
        return pl.BlockSpec((block, cols), lambda i: (i, 0))

    def resident(shape):
        return pl.BlockSpec(
            shape, lambda i: (0,) * len(shape), pipeline_mode=pl.Buffered(1)
        )

    outs = [
        (wide, bf),
        (wide, f32),
        (wide, bf),
        (inner, bf),
        (inner, bf),
        (wide, bf),
        (wide, bf),
        (bi, bf),
    ]
    return pl.pallas_call(
        stream_kernel,
        grid=(rows // block,),
        in_specs=[by_row(wide), by_row(bi), by_row(wide), by_row(1)]
        + [resident(v.shape) for v in (norms, w_out, w_inner, w_outer)],
        out_specs=[by_row(cols) for cols, _ in outs]
        + [pl.BlockSpec((4, wide), lambda i: (0, 0))],
        out_shape=[jax.ShapeDtypeStruct((rows, cols), dt) for cols, dt in outs]
        + [jax.ShapeDtypeStruct((4, wide), f32)],
        scratch_shapes=[pltpu.VMEM((block, inner), f32)],
        compiler_params=pltpu.CompilerParams(vmem_limit_bytes=VMEM_LIMIT),
    )(x, ctx, cot, keep, norms, w_out, w_inner, w_outer)


def weight_grad_kernel(x, d, out):
    out[0] = low(dot_tn(x[...], d[...]))


def weight_grad(x, d, splits):
    rows, inner = x.shape
    cols = d.shape[1] // splits
    block = 512 if inner % 512 == 0 else 256
    return pl.pallas_call(
        weight_grad_kernel,
        grid=(splits, inner // block),
        in_specs=[
            pl.BlockSpec((rows, block), lambda f, i: (0, i)),
            pl.BlockSpec((rows, cols), lambda f, i: (0, f)),
        ],
        out_specs=pl.BlockSpec((1, block, cols), lambda f, i: (f, i, 0)),
        out_shape=jax.ShapeDtypeStruct((splits, inner, cols), jnp.bfloat16),
        compiler_params=pltpu.CompilerParams(vmem_limit_bytes=VMEM_LIMIT),
    )(x, d)


def attention_back_pair(p, refs):
    (owner, iq, ik, iv, tq, tk, tv, iprob, tprob, dic, dtc, diq, dik, div, dtq, dtk, dtv) = refs
    regions = iprob.shape[1]
    length = tq.shape[0] // owner.shape[0]
    heads = tq.shape[1] // HDIM
    scale = 1.0 / math.sqrt(HDIM)
    image = owner[p]
    rows_t = pl.ds(pl.multiple_of(p * length, length), length)
    rows_i = pl.ds(pl.multiple_of(p * regions, regions), regions)

    def add_to(ref, at, value):
        value = low(value).astype(jnp.float32)
        for i in range(ref.shape[0]):
            ref[i, :, at] += jnp.where(image == i, value, 0.0)

    for h in range(heads):
        at = slice(h * HDIM, (h + 1) * HDIM)
        grad = dic[rows_i, at]
        probs = iprob[p * heads + h]
        keys = tk[rows_t, at]
        dprobs = dot_nt(grad, tv[rows_t, at])
        dtv[rows_t, at] = low(dot_tn(low(probs), grad))
        inner = jnp.sum(probs * dprobs, axis=1, keepdims=True)
        dscores = low(probs * (dprobs - inner))
        add_to(diq, at, scale * dot_nn(dscores, keys))
        dtk[rows_t, at] = low(scale * dot_tn(dscores, iq[image, :, at]))
        grad = dtc[rows_t, at]
        probs = tprob[p * heads + h]
        dprobs = dot_nt(iv[image, :, at], grad)
        add_to(div, at, dot_nn(low(probs), grad))
        inner = jnp.sum(probs * dprobs, axis=0, keepdims=True)
        dscores = low(probs * (dprobs - inner))
        add_to(dik, at, scale * dot_nn(dscores, tq[rows_t, at]))
        dtq[rows_t, at] = low(scale * dot_tn(dscores, ik[image, :, at]))


def backward_kernel(owner, *refs):
    shared = (owner,) + refs
    for ref in refs[10:13]:
        ref[...] = jnp.zeros_like(ref)

    def one(p, carry):
        attention_back_pair(p, shared)
        return carry

    lax.fori_loop(0, owner.shape[0], one, 0)


def backward_attention(owner, kept, dic, dtc):
    iq, ik, iv, tq, tk, tv, iprob, tprob = kept
    bf, f32 = jnp.bfloat16, jnp.float32
    shapes = [jax.ShapeDtypeStruct(iq.shape, f32)] * 3 + [jax.ShapeDtypeStruct(tq.shape, bf)] * 3
    return pl.pallas_call(
        backward_kernel,
        out_shape=shapes,
        in_specs=[SCALARS] + [WHOLE] * 10,
        out_specs=[WHOLE] * 6,
        compiler_params=pltpu.CompilerParams(vmem_limit_bytes=VMEM_LIMIT),
    )(owner, iq, ik, iv, tq, tk, tv, iprob, tprob, dic, dtc)


def data_grad_kernel(base, dq, dk, dv, wq, wk, wv, out):
    total = base[...]
    for d, w in ((dq, wq), (dk, wk), (dv, wv)):
        total = total + times_back(d[...], w)
    out[...] = total


def data_grad(base, grads, weights, block):
    rows, wide = base.shape
    bi = grads[0].shape[1]
    return pl.pallas_call(
        data_grad_kernel,
        grid=(rows // block,),
        in_specs=[pl.BlockSpec((block, wide), lambda i: (i, 0))]
        + [pl.BlockSpec((block, bi), lambda i: (i, 0))] * 3
        + [
            pl.BlockSpec(w.shape, lambda i: (0, 0, 0), pipeline_mode=pl.Buffered(1))
            for w in weights
        ],
        out_specs=pl.BlockSpec((block, wide), lambda i: (i, 0)),
        out_shape=jax.ShapeDtypeStruct((rows, wide), jnp.float32),
        compiler_params=pltpu.CompilerParams(vmem_limit_bytes=VMEM_LIMIT),
    )(base, *grads, *weights)


PARTS = (0, 1, 2, 0, 1, 2, 2, 0, 2, 1, 0, 1)


def mesh_bits():
    return bits_of(lax.axis_size("dp")), bits_of(lax.axis_size("fsdp"))


def gather_weights(shards, norm_params):
    nd, nf = mesh_bits()
    wide = norm_params.shape[1]
    padded = jnp.pad(norm_params, ((0, 8 - norm_params.shape[0]), (0, 128 - wide)))
    blocks = gather_blocks(list(shards) + [padded], PARTS + (0,), nd, nf, 0)
    weights = []
    for shard, block in zip(shards, blocks):
        rows, cols = shard.shape
        block = block.reshape(1 << nf, rows << nd, cols)
        if cols % 128:
            block = jnp.swapaxes(block, 0, 1).reshape(1, rows << nd, cols << nf)
        weights.append(block)
    norms = blocks[-1].reshape(1 << nf, 1 << nd, 8, 128)[:, :, :4, :wide]
    norms = norms.transpose(2, 1, 0, 3).reshape(4, wide << (nd + nf))
    return tuple(weights), norms


def reduce_grads(grads, shards, norm_rows):
    nd, nf = mesh_bits()
    lead = (2,) * (nd + nf)
    blocks = []
    for grad, shard in zip(grads, shards):
        rows, cols = shard.shape
        if cols % 128:
            grad = jnp.swapaxes(grad.reshape(rows << nd, 1 << nf, cols), 0, 1)
        blocks.append(grad.reshape(lead + (rows, cols)))
    wide = norm_rows.shape[1] >> (nd + nf)
    split = norm_rows.reshape(4, 1 << nd, 1 << nf, wide).transpose(2, 1, 0, 3)
    split = jnp.pad(split, ((0, 0), (0, 0), (0, 4), (0, 128 - wide)))
    blocks.append(split.reshape(lead + (8, 128)))
    owned = reduce_blocks(blocks, PARTS + (0,), nd, nf, 1)
    return tuple(owned[:-1]), owned[-1][:4, :wide]


def body(
    text_states,
    image_states,
    text_lengths,
    region_mask,
    group_ids,
    image_query,
    image_key,
    image_value,
    text_query,
    text_key,
    text_value,
    image_output,
    text_output,
    image_inner,
    image_outer,
    text_inner,
    text_outer,
    norm_params,
    cot_text,
    cot_image,
):
    shards = (
        image_query,
        image_key,
        image_value,
        text_query,
        text_key,
        text_value,
        image_output,
        text_output,
        image_inner,
        image_outer,
        text_inner,
        text_outer,
    )
    weights, norms = gather_weights(shards, norm_params)
    device = lax.axis_index("dp") * lax.axis_size("fsdp") + lax.axis_index("fsdp")
    results, grads, norm_rows = layer(
        text_states,
        image_states,
        text_lengths,
        region_mask,
        group_ids - device * image_states.shape[0],
        weights,
        norms,
        cot_text,
        cot_image,
    )
    owned, norm_grad = reduce_grads(grads, shards, norm_rows)
    return results + owned + (norm_grad,)


def layer(
    text_states, image_states, text_lengths, region_mask, owner, weights, norms, cot_text, cot_image
):
    pairs, length, width_text = text_states.shape
    images, regions, width_image = image_states.shape
    padded = -(-regions // 16) * 16
    extra = ((0, 0), (0, padded - regions), (0, 0))
    (
        query_image,
        key_image,
        value_image,
        query_text,
        key_text,
        value_text,
        out_image,
        out_text,
        inner_image,
        outer_image,
        inner_text,
        outer_text,
    ) = weights
    region_counts = jnp.sum(region_mask, axis=1)
    mine = owner[:, None] == jnp.arange(images, dtype=jnp.int32)[None, :]
    counts = jnp.sum(jnp.where(mine, region_counts[None, :], 0), axis=1)
    text = text_states.reshape(pairs * length, width_text)
    image = jnp.pad(image_states, extra)
    visual = image[0]
    for i in range(1, images):
        visual = jnp.where(mine[:, i, None, None], image[i], visual)
    visual = visual.reshape(pairs * padded, width_image)
    image = image.reshape(images * padded, width_image)
    cot_rows = jnp.pad(cot_image, extra).reshape(pairs * padded, width_image)

    def keep_rows(limits, slots):
        kept = jnp.arange(slots, dtype=jnp.int32)[None, :] < limits[:, None]
        return kept.astype(jnp.float32).reshape(-1, 1)

    *kept, image_context, text_context = forward_attention(
        text_lengths, owner, counts, text, image, weights[:6], images
    )
    (
        text_out,
        text_dz,
        text_mid,
        text_act,
        text_hid,
        text_ffn,
        text_branch,
        text_dctx,
        text_ngrad,
    ) = stream(
        text,
        text_context,
        cot_text.reshape(text.shape),
        keep_rows(text_lengths, length),
        norms[:, :width_text],
        out_text,
        inner_text,
        outer_text,
        256,
    )
    (
        image_out,
        image_dz,
        image_mid,
        image_act,
        image_hid,
        image_ffn,
        image_branch,
        image_dctx,
        image_ngrad,
    ) = stream(
        visual,
        image_context,
        cot_rows,
        keep_rows(counts, padded),
        norms[:, width_text:],
        out_image,
        inner_image,
        outer_image,
        pairs * padded // 2,
    )
    diq, dik, div, dtq, dtk, dtv = backward_attention(owner, kept, image_dctx, text_dctx)
    diq, dik, div = (low(d).reshape(image.shape[0], -1) for d in (diq, dik, div))
    text_grad = data_grad(text_dz, (dtq, dtk, dtv), weights[3:6], 256)
    by_pair = image_dz.reshape(pairs, padded, width_image)
    base = jnp.stack(
        [jnp.sum(jnp.where(mine[:, i, None, None], by_pair, 0.0), axis=0) for i in range(images)]
    )
    image_grad = data_grad(
        base.reshape(image.shape), (diq, dik, div), weights[:3], image.shape[0]
    )
    grads = []
    for x, d, w in (
        (image, diq, query_image),
        (image, dik, key_image),
        (image, div, value_image),
        (text, dtq, query_text),
        (text, dtk, key_text),
        (text, dtv, value_text),
        (image_context, image_branch, out_image),
        (text_context, text_branch, out_text),
        (image_mid, image_hid, inner_image),
        (image_act, image_ffn, outer_image),
        (text_mid, text_hid, inner_text),
        (text_act, text_ffn, outer_text),
    ):
        grads.append(weight_grad(x, d, w.shape[0]))
    norm_rows = jnp.concatenate([text_ngrad, image_ngrad], axis=1)
    results = (
        text_out.reshape(text_states.shape),
        image_out.reshape(pairs, padded, width_image)[:, :regions],
        text_grad.reshape(text_states.shape),
        image_grad.reshape(images, padded, width_image)[:, :regions],
    )
    return results, tuple(grads), norm_rows


def solution(mesh):
    placed = (
        P(("dp", "fsdp"), None, None),
        P(("dp", "fsdp"), None, None),
        P(("dp", "fsdp")),
        P(("dp", "fsdp"), None),
        P(("dp", "fsdp")),
        P("dp", "fsdp"),
        P("dp", "fsdp"),
        P("dp", "fsdp"),
        P("dp", "fsdp"),
        P("dp", "fsdp"),
        P("dp", "fsdp"),
        P("dp", "fsdp"),
        P("dp", "fsdp"),
        P("dp", "fsdp"),
        P("dp", "fsdp"),
        P("dp", "fsdp"),
        P("dp", "fsdp"),
        P(None, ("dp", "fsdp")),
        P(("dp", "fsdp"), None, None),
        P(("dp", "fsdp"), None, None),
    )
    return jax.shard_map(
        body,
        mesh=mesh,
        in_specs=placed,
        out_specs=(
            P(("dp", "fsdp"), None, None),
            P(("dp", "fsdp"), None, None),
            P(("dp", "fsdp"), None, None),
            P(("dp", "fsdp"), None, None),
            P("dp", "fsdp"),
            P("dp", "fsdp"),
            P("dp", "fsdp"),
            P("dp", "fsdp"),
            P("dp", "fsdp"),
            P("dp", "fsdp"),
            P("dp", "fsdp"),
            P("dp", "fsdp"),
            P("dp", "fsdp"),
            P("dp", "fsdp"),
            P("dp", "fsdp"),
            P("dp", "fsdp"),
            P(None, ("dp", "fsdp")),
        ),
        check_vma=False,
    )
```

```python
import functools
import math

import jax
import jax.numpy as jnp
from jax import lax
from jax.experimental import pallas as pl
from jax.experimental.pallas import tpu as pltpu
from jax.sharding import PartitionSpec as P

HDIM = 128

norm_eps = 1e-12
masked_score = -1e30

MESH_IDS = pl.DeviceIdType.MESH
VMEM_LIMIT = 60 * 1024 * 1024
WHOLE = pl.BlockSpec(memory_space=pltpu.VMEM)
SCALARS = pl.BlockSpec(memory_space=pltpu.SMEM)
ANYWHERE = pl.BlockSpec(memory_space=pl.ANY)
CORE = ("d", 0)


def bits_of(size):
    count = size.bit_length() - 1
    assert 1 << count == size
    return count


def mesh_bits():
    return bits_of(lax.axis_size("dp")), bits_of(lax.axis_size("fsdp"))


def hop_orders(nd, nf):
    high = [("d", b) for b in range(nd - 1, 2, -1)]
    low = [("d", 2)]
    near = [("d", 1)]
    wide = [("f", b) for b in range(nf)]
    return (
        high + near + low + wide,
        low + high + wide + near,
        high + wide + near + low,
    )


class Place:
    def __init__(self, nd, nf):
        self.d = lax.axis_index("dp")
        self.f = lax.axis_index("fsdp")
        self.axes = [("f", b) for b in range(nf - 1, -1, -1)] + [
            ("d", b) for b in range(nd - 1, -1, -1)
        ]

    def bit(self, axis):
        value = self.f if axis[0] == "f" else self.d
        return lax.rem(value // (1 << axis[1]), 2)

    def partner(self, axis):
        step = (1 << axis[1]) * (1 - 2 * self.bit(axis))
        if axis[0] == "f":
            return (self.d, self.f + step)
        return (self.d + step, self.f)

    def index(self, whole, flip=None):
        picked = []
        for axis in self.axes:
            if axis in whole:
                picked.append(slice(None))
            elif axis == flip:
                picked.append(1 - self.bit(axis))
            else:
                picked.append(self.bit(axis))
        return tuple(picked)

    def barrier(self):
        sem = pltpu.get_barrier_semaphore()
        for axis in self.axes:
            pl.semaphore_signal(
                sem, inc=1, device_id=self.partner(axis), device_id_type=MESH_IDS
            )
        pl.semaphore_wait(sem, len(self.axes))


class Gather:
    def __init__(self, arrays, parts, waves, thirds=False):
        self.arrays = arrays
        self.nd, self.nf = mesh_bits()
        orders = hop_orders(self.nd, self.nf)
        self.pieces = []
        for m, array in enumerate(arrays):
            rows = array.shape[0]
            cuts = [(0, rows, parts[m])]
            if thirds and rows % 48 == 0:
                third = rows // 3
                cuts = [(k * third, third, k) for k in range(3)]
            for first, size, part in cuts:
                self.pieces.append((m, first, size, tuple(orders[part]) + (CORE,), waves[m]))
        self.hops = self.nd + self.nf
        lead = (2,) * self.hops
        self.out_shape = [jax.ShapeDtypeStruct(lead + a.shape, a.dtype) for a in arrays]
        self.out_specs = [ANYWHERE] * len(arrays)
        count = len(self.pieces)
        self.scratch = [
            pltpu.SemaphoreType.DMA((count,)),
            pltpu.SemaphoreType.DMA((count, self.hops)),
            pltpu.SemaphoreType.DMA((count, self.hops)),
        ]

    def sizes(self, k):
        m, first, size, route, wave = self.pieces[k]
        block = size * self.arrays[m].shape[1] * self.arrays[m].dtype.itemsize
        return [block << h for h in range(self.hops)]

    def bind(self, place, ins, outs, scratch):
        self.place, self.ins, self.outs = place, ins, outs
        self.local_sem, self.send_sem, self.recv_sem = scratch

    def local(self, k):
        m, first, size, route, wave = self.pieces[k]
        rows = pl.ds(first, size)
        return pltpu.make_async_copy(
            self.ins[m].at[rows],
            self.outs[m].at[self.place.index(()) + (rows,)],
            self.local_sem.at[k],
        )

    def hop(self, k, h):
        m, first, size, route, wave = self.pieces[k]
        region = self.outs[m].at[self.place.index(route[:h]) + (pl.ds(first, size),)]
        return pltpu.make_async_remote_copy(
            src_ref=region,
            dst_ref=region,
            send_sem=self.send_sem.at[k, h],
            recv_sem=self.recv_sem.at[k, h],
            device_id=self.place.partner(route[h]),
            device_id_type=MESH_IDS,
        )

    def start(self):
        for k in range(len(self.pieces)):
            self.local(k).start()

    def step(self, k, h):
        if h == 0:
            self.local(k).wait()
        else:
            self.hop(k, h - 1).wait_recv()
        if h < self.hops:
            self.hop(k, h).start()
        else:
            for g in range(self.hops):
                self.hop(k, g).wait_send()


def add_blocks(acc, index, incoming):
    lead = incoming.shape[:-2]

    def one(i, carry):
        inner = []
        for size in reversed(lead):
            inner.append(lax.rem(i, size))
            i = i // size
        at = tuple(reversed(inner))
        inner = list(at)
        where = tuple(inner.pop(0) if isinstance(p, slice) else p for p in index)
        acc[where] = acc[where] + incoming[at]
        return carry

    lax.fori_loop(0, math.prod(lead), one, 0)


class Reduce:
    def __init__(self, arrays, parts, waves, thirds=False):
        self.arrays = arrays
        self.nd, self.nf = mesh_bits()
        orders = hop_orders(self.nd, self.nf)
        self.hops = self.nd + self.nf
        self.pieces = []
        self.scratch = []
        for m, array in enumerate(arrays):
            rows, cols = array.shape[-2:]
            cuts = [(0, rows, parts[m])]
            if thirds and rows % 48 == 0:
                third = rows // 3
                cuts = [(k * third, third, k) for k in range(3)]
            for first, size, part in cuts:
                route = (CORE,) + tuple(reversed(orders[part]))
                self.pieces.append((m, first, size, route, waves[m]))
                for h in range(-1, self.hops):
                    free = self.hops - 1 - max(h, 0)
                    self.scratch.append(pltpu.VMEM((2,) * free + (size, cols), array.dtype))
        count = len(self.pieces)
        self.scratch += [
            pltpu.SemaphoreType.DMA((count,)),
            pltpu.SemaphoreType.DMA((count, self.hops)),
            pltpu.SemaphoreType.DMA((count, self.hops)),
        ]
        shapes = [a.shape[-2:] for a in arrays]
        self.out_shape = [jax.ShapeDtypeStruct(s, jnp.float32) for s in shapes]
        self.out_specs = [pl.BlockSpec(s, lambda *_: (0, 0)) for s in shapes]

    def sizes(self, k):
        m, first, size, route, wave = self.pieces[k]
        block = size * self.arrays[m].shape[-1] * self.arrays[m].dtype.itemsize
        return [block << (self.hops - 1 - h) for h in range(self.hops)]

    def bind(self, place, ins, outs, scratch):
        self.place, self.ins, self.outs = place, ins, outs
        self.local_sem, self.send_sem, self.recv_sem = scratch[-3:]
        each = self.hops + 1
        self.accs = [scratch[k * each] for k in range(len(self.pieces))]
        self.temps = [scratch[k * each + 1 : (k + 1) * each] for k in range(len(self.pieces))]
        self.rest = [axis for axis in place.axes if axis != CORE]

    def local(self, k):
        m, first, size, route, wave = self.pieces[k]
        source = self.ins[m].at[self.place.index(self.rest) + (pl.ds(first, size),)]
        return pltpu.make_async_copy(source, self.accs[k], self.local_sem.at[k])

    def within(self, k, h, flip=None):
        route = self.pieces[k][3]
        full = self.place.index(route[h + 1 :], flip)
        return tuple(p for p, axis in zip(full, self.place.axes) if axis != CORE)

    def hop(self, k, h):
        m, first, size, route, wave = self.pieces[k]
        if h == 0:
            region = self.ins[m].at[self.place.index(route[1:], CORE) + (pl.ds(first, size),)]
        else:
            region = self.accs[k].at[self.within(k, h, route[h])]
        return pltpu.make_async_remote_copy(
            src_ref=region,
            dst_ref=self.temps[k][h],
            send_sem=self.send_sem.at[k, h],
            recv_sem=self.recv_sem.at[k, h],
            device_id=self.place.partner(route[h]),
            device_id_type=MESH_IDS,
        )

    def start(self):
        for k in range(len(self.pieces)):
            self.local(k).start()

    def step(self, k, h):
        if h > 0:
            self.hop(k, h - 1).wait_recv()
            if h == 1:
                self.local(k).wait()
            here = self.within(k, h - 1)
            if h < self.hops:
                add_blocks(self.accs[k], here, self.temps[k][h - 1])
            else:
                m, first, size, route, wave = self.pieces[k]
                last = self.accs[k][here].astype(jnp.float32)
                self.outs[m][first : first + size, :] = last + self.temps[k][h - 1][
                    ...
                ].astype(jnp.float32)
        if h < self.hops:
            self.hop(k, h).start()
        else:
            for g in range(self.hops):
                self.hop(k, g).wait_send()


LINK_RATE = 100e3
CORE_RATE = 350e3
LATENCY = 1.5


def plan_steps(jobs, steps, ticks, spacing):
    todo = []
    for j, job in enumerate(jobs):
        for k, (m, first, size, route, wave) in enumerate(job.pieces):
            for h in range(job.hops + 1):
                todo.append((wave + h, wave, j, k, h))
    todo.sort()
    total = steps * ticks
    slots = [[] for _ in range(total)]
    tail = []
    done = {}
    free = {"link": 0.0, "core": 0.0}
    at = 0
    for slot, wave, j, k, h in todo:
        job = jobs[j]
        ready = 0.0 if h == 0 else done[j, k, h - 1]
        while at < total and at * spacing < ready:
            at += 1
        now = max(at * spacing, ready)
        if h < job.hops:
            core = job.pieces[k][3][h] == CORE
            lane, rate = ("core", CORE_RATE) if core else ("link", LINK_RATE)
            free[lane] = max(free[lane], now) + job.sizes(k)[h] / rate
            done[j, k, h] = free[lane] + LATENCY
        (slots[at] if at < total else tail).append((j, k, h))
    return slots, tail


def carrying_kernel(kernel, jobs, steps, ticks, plan, counts, *refs):
    spans = []
    start = 0
    for count in counts:
        spans.append(refs[start : start + count])
        start += count
    njobs = len(jobs)
    own_in, job_in = spans[0], spans[1 : 1 + njobs]
    own_out, job_out = spans[1 + njobs], spans[2 + njobs : 2 + 2 * njobs]
    own_scratch, job_scratch = spans[2 + 2 * njobs], spans[3 + 2 * njobs :]
    nd, nf = jobs[0].nd, jobs[0].nf
    place = Place(nd, nf)
    for job, ins, outs, scratch in zip(jobs, job_in, job_out, job_scratch):
        job.bind(place, ins, outs, scratch)
    slots, tail = plan
    now = pl.program_id(0)

    def run(items, opening):
        if opening:
            for job in jobs:
                job.start()
            place.barrier()
        for j, k, h in items:
            jobs[j].step(k, h)

    passed = [0]

    def tick():
        t = passed[0]
        passed[0] += 1
        if t >= ticks:
            return
        for s in range(steps):
            items = slots[s * ticks + t]
            if items or (s == 0 and t == 0):
                pl.when(now == s)(functools.partial(run, items, s == 0 and t == 0))

    kernel(tick, *own_in, *own_out, *own_scratch)
    assert passed[0] == ticks
    if tail:
        pl.when(now == steps - 1)(functools.partial(run, tail, False))


def carry(
    kernel, steps, ticks, spacing, args, in_specs, out_shape, out_specs, scratch, jobs, ident
):
    if not jobs:
        def plain(*refs):
            kernel(lambda: None, *refs)

        outs = pl.pallas_call(
            plain,
            grid=(steps,),
            in_specs=in_specs,
            out_specs=out_specs,
            out_shape=out_shape,
            scratch_shapes=scratch,
            compiler_params=pltpu.CompilerParams(vmem_limit_bytes=VMEM_LIMIT),
        )(*args)
        return [outs]
    plan = plan_steps(jobs, steps, ticks, spacing)
    counts = [len(args)] + [len(job.arrays) for job in jobs]
    counts += [len(out_shape)] + [len(job.out_shape) for job in jobs]
    counts += [len(scratch)] + [len(job.scratch) for job in jobs]
    outs = pl.pallas_call(
        functools.partial(carrying_kernel, kernel, jobs, steps, ticks, plan, counts),
        grid=(steps,),
        in_specs=in_specs + [ANYWHERE for job in jobs for _ in job.arrays],
        out_specs=out_specs + [spec for job in jobs for spec in job.out_specs],
        out_shape=out_shape + [shape for job in jobs for shape in job.out_shape],
        scratch_shapes=scratch + [item for job in jobs for item in job.scratch],
        compiler_params=pltpu.CompilerParams(
            collective_id=ident, has_side_effects=True, vmem_limit_bytes=VMEM_LIMIT
        ),
    )(*args, *(array for job in jobs for array in job.arrays))
    result = [outs[: len(out_shape)]]
    start = len(out_shape)
    for job in jobs:
        result.append(outs[start : start + len(job.out_shape)])
        start += len(job.out_shape)
    return result


def dot_nn(a, b):
    return lax.dot_general(a, b, (((1,), (0,)), ((), ())), preferred_element_type=jnp.float32)


def dot_nt(a, b):
    return lax.dot_general(a, b, (((1,), (1,)), ((), ())), preferred_element_type=jnp.float32)


def dot_tn(a, b):
    return lax.dot_general(a, b, (((0,), (0,)), ((), ())), preferred_element_type=jnp.float32)


def low(value):
    return value.astype(jnp.bfloat16)


def times(value, matrix):
    parts = [dot_nn(value, matrix[f]) for f in range(matrix.shape[0])]
    return parts[0] if len(parts) == 1 else jnp.concatenate(parts, axis=1)


def times_back(value, matrix):
    cols = matrix.shape[2]
    total = None
    for f in range(matrix.shape[0]):
        term = dot_nt(value[:, f * cols : (f + 1) * cols], matrix[f])
        total = term if total is None else total + term
    return total


def by_row(block, cols):
    return pl.BlockSpec((block, cols), lambda i: (i, 0))


def fixed(shape):
    return pl.BlockSpec(shape, lambda i: (0,) * len(shape))


def resident(shape):
    return pl.BlockSpec(shape, lambda i: (0,) * len(shape), pipeline_mode=pl.Buffered(1))


def struct(shape, dtype):
    return jax.ShapeDtypeStruct(shape, dtype)


PAIRS_STEP = 2


def softmax(scores, axis):
    top = jnp.max(scores, axis=axis, keepdims=True)
    weight = jnp.exp(scores - top)
    return weight * (1.0 / jnp.sum(weight, axis=axis, keepdims=True))


def forward_kernel(tick, lens, owner, counts, text, image, *refs):
    weights, (iq, ik, iv, tq, tk, tv, iprob, tprob, ictx, tctx) = refs[:6], refs[6:]
    regions, length = iprob.shape[1:]
    heads = tq.shape[1] // HDIM
    scale = 1.0 / math.sqrt(HDIM)
    tick()

    @pl.when(pl.program_id(0) == 0)
    def _():
        for w_ref, out_ref in zip(weights[:3], (iq, ik, iv)):
            out_ref[...] = low(times(image[...], w_ref)).reshape(out_ref.shape)

    for w_ref, out_ref in zip(weights[3:], (tq, tk, tv)):
        out_ref[...] = low(times(text[...], w_ref))
    tick()
    for q in range(PAIRS_STEP):
        p = pl.program_id(0) * PAIRS_STEP + q
        mine = owner[p]
        kept_text = lax.broadcasted_iota(jnp.int32, (regions, length), 1) < lens[p]
        kept_region = lax.broadcasted_iota(jnp.int32, (regions, length), 0) < counts[p]
        rows_t = slice(q * length, (q + 1) * length)
        rows_i = slice(q * regions, (q + 1) * regions)
        for h in range(heads):
            at = slice(h * HDIM, (h + 1) * HDIM)
            scores = scale * dot_nt(iq[mine, :, at], tk[rows_t, at])
            probs = softmax(jnp.where(kept_text, scores, masked_score), 1)
            iprob[q * heads + h] = probs
            ictx[rows_i, at] = low(dot_nn(low(probs), tv[rows_t, at]))
            scores = scale * dot_nt(ik[mine, :, at], tq[rows_t, at])
            probs = softmax(jnp.where(kept_region, scores, masked_score), 0)
            tprob[q * heads + h] = probs
            tctx[rows_t, at] = low(dot_tn(low(probs), iv[mine, :, at]))
        tick()


def forward_attention(lens, owner, counts, text, image, weights, images, jobs, ident):
    pairs = lens.shape[0]
    regions = image.shape[0] // images
    wide = weights[0].shape[0] * weights[0].shape[2]
    heads = wide // HDIM
    length = text.shape[0] // pairs
    n = PAIRS_STEP
    bf, f32 = jnp.bfloat16, jnp.float32
    probs = pl.BlockSpec((n * heads, regions, length), lambda i: (i, 0, 0))
    return carry(
        forward_kernel,
        pairs // n,
        2 + n,
        3.0,
        (lens, owner, counts, text, image, *weights),
        [SCALARS] * 3
        + [by_row(n * length, text.shape[1]), resident(image.shape)]
        + [resident(w.shape) for w in weights],
        [struct((images, regions, wide), bf)] * 3
        + [struct((text.shape[0], wide), bf)] * 3
        + [struct((pairs * heads, regions, length), f32)] * 2
        + [struct((pairs * regions, wide), bf), struct((text.shape[0], wide), bf)],
        [fixed((images, regions, wide))] * 3
        + [by_row(n * length, wide)] * 3
        + [probs] * 2
        + [by_row(n * regions, wide), by_row(n * length, wide)],
        [],
        jobs,
        ident,
    )


def gelu_pair(x):
    scaled = jnp.abs(x) * (1.0 / math.sqrt(2.0))
    bell = jnp.exp(-0.5 * x * x)
    t = 1.0 / (1.0 + 0.3275911 * scaled)
    poly = t * (
        0.254829592
        + t * (-0.284496736 + t * (1.421413741 + t * (-1.453152027 + t * 1.061405429)))
    )
    tail = 0.5 * poly * bell
    below = jnp.where(x < 0, tail, 1.0 - tail)
    return x * below, below + x * bell * (1.0 / math.sqrt(2.0 * math.pi))


def row_mean(value):
    return jnp.mean(value, axis=-1, keepdims=True)


def col_sum(value):
    return jnp.sum(value, axis=0, keepdims=True)


def stream_kernel(first_col, tick, limits, x, ctx, cot, norms_ref, w_out, w_inner, w_outer, *refs):
    (out, dz_out, mid_out, act_out, hid_out, ffn_out, branch_out, dctx_out, ngrad) = refs[:9]
    slope, cot_wide = refs[9:]
    rows, wide = x.shape
    group, real = cot.shape[:2]
    slots = rows // group
    norms = [norms_ref[r : r + 1, first_col : first_col + wide] for r in range(4)]
    now = pl.program_id(0)

    def normalize(z):
        offset = z - row_mean(z)
        inv = lax.rsqrt(row_mean(offset * offset) + norm_eps)
        return offset * inv, inv

    def normalize_back(dy, xhat, inv, gain):
        dx = dy * gain
        return inv * (dx - row_mean(dx) - xhat * row_mean(dx * xhat))

    tick()

    @pl.when(now == 0)
    def _():
        ngrad[...] = jnp.zeros_like(ngrad)
        if real < slots:
            cot_wide[...] = jnp.zeros_like(cot_wide)

    row = lax.broadcasted_iota(jnp.int32, (rows, 1), 0)
    kept = row < 0
    for q in range(group):
        inside = (row >= q * slots) & (row < q * slots + limits[now * group + q])
        kept = kept | inside
        cot_wide[q * slots : q * slots + real, :] = cot[q].astype(jnp.float32)
    kept = kept.astype(jnp.float32)
    first_hat, first_inv = normalize(x[...].astype(jnp.float32) + times(ctx[...], w_out))
    mid = first_hat * norms[0] + norms[1]
    mid_low = low(mid)
    mid_out[...] = mid_low
    tick()
    cols = w_inner.shape[2]
    for f in range(w_inner.shape[0]):
        at = slice(f * cols, (f + 1) * cols)
        act, grad = gelu_pair(dot_nn(mid_low, w_inner[f]))
        act_out[:, at] = low(act)
        slope[:, at] = grad
        tick()
    second_hat, second_inv = normalize(mid + times(act_out[...], w_outer))
    result = low((second_hat * norms[2] + norms[3]) * kept)
    for q in range(group):
        out[q] = result[q * slots : q * slots + real]
    dy = cot_wide[...] * kept
    second_dz = normalize_back(dy, second_hat, second_inv, norms[2])
    ffn_low = low(second_dz)
    ffn_out[...] = ffn_low
    sums = [col_sum(dy * second_hat), col_sum(dy)]
    tick()
    hid_out[...] = low(times_back(ffn_low, w_outer) * slope[...])
    tick()
    mid_grad = second_dz + times_back(hid_out[...], w_inner)
    first_dz = normalize_back(mid_grad, first_hat, first_inv, norms[0])
    dz_out[...] = first_dz
    branch_low = low(first_dz)
    branch_out[...] = branch_low
    tick()
    dctx_out[...] = low(times_back(branch_low, w_out))
    sums = [col_sum(mid_grad * first_hat), col_sum(mid_grad)] + sums
    for r in range(4):
        ngrad[r : r + 1, :] += sums[r]
    tick()


def stream(limits, x, ctx, cot, norms, first_col, weights, group, spacing, jobs, ident):
    rows, wide = x.shape
    pairs, real = cot.shape[:2]
    block = rows // pairs * group
    w_inner = weights[1]
    inner = w_inner.shape[0] * w_inner.shape[2]
    bi = ctx.shape[1]
    bf, f32 = jnp.bfloat16, jnp.float32
    outs = [
        (wide, f32),
        (wide, bf),
        (inner, bf),
        (inner, bf),
        (wide, bf),
        (wide, bf),
        (bi, bf),
    ]
    by_pair = pl.BlockSpec((group, real, wide), lambda i: (i, 0, 0))
    return carry(
        functools.partial(stream_kernel, first_col),
        pairs // group,
        7 + w_inner.shape[0] - 1,
        spacing,
        (limits, x, ctx, cot, norms, *weights),
        [SCALARS, by_row(block, wide), by_row(block, bi), by_pair]
        + [resident(v.shape) for v in (norms, *weights)],
        [struct(cot.shape, bf)]
        + [struct((rows, cols), dt) for cols, dt in outs]
        + [struct((4, wide), f32)],
        [by_pair] + [by_row(block, cols) for cols, _ in outs] + [fixed((4, wide))],
        [pltpu.VMEM((block, inner), f32), pltpu.VMEM((block, wide), f32)],
        jobs,
        ident,
    )


def weight_grad_kernel(count, tick, x, *refs):
    tick()
    for d, out in zip(refs[:count], refs[count:]):
        cols = out.shape[2]
        whole = low(dot_tn(x[...], d[...]))
        for f in range(out.shape[0]):
            out[f] = whole[:, f * cols : (f + 1) * cols]
    tick()


def weight_grads(x, grads, splits, block, spacing, jobs, ident):
    rows, inner = x.shape
    shapes = [(n, inner, d.shape[1] // n) for d, n in zip(grads, splits)]
    return carry(
        functools.partial(weight_grad_kernel, len(grads)),
        inner // block,
        2,
        spacing,
        (x, *grads),
        [pl.BlockSpec((rows, block), lambda i: (0, i))] + [resident(d.shape) for d in grads],
        [struct(s, jnp.bfloat16) for s in shapes],
        [pl.BlockSpec((s[0], block, s[2]), lambda i: (0, i, 0)) for s in shapes],
        [],
        jobs,
        ident,
    )


def add_to(ref, mine, at, value):
    value = low(value).astype(jnp.float32)
    for i in range(ref.shape[0]):
        ref[i, :, at] += jnp.where(mine == i, value, 0.0)


def back_image_kernel(tick, owner, iq, tk, tv, iprob, dic, diq, dtk, dtv):
    regions, length = iprob.shape[1:]
    heads = tk.shape[1] // HDIM
    scale = 1.0 / math.sqrt(HDIM)
    tick()

    @pl.when(pl.program_id(0) == 0)
    def _():
        diq[...] = jnp.zeros_like(diq)

    for q in range(PAIRS_STEP):
        mine = owner[pl.program_id(0) * PAIRS_STEP + q]
        rows_t = slice(q * length, (q + 1) * length)
        rows_i = slice(q * regions, (q + 1) * regions)
        for h in range(heads):
            at = slice(h * HDIM, (h + 1) * HDIM)
            grad = dic[rows_i, at]
            probs = iprob[q * heads + h]
            dprobs = dot_nt(grad, tv[rows_t, at])
            dtv[rows_t, at] = low(dot_tn(low(probs), grad))
            inner = jnp.sum(probs * dprobs, axis=1, keepdims=True)
            dscores = low(probs * (dprobs - inner))
            add_to(diq, mine, at, scale * dot_nn(dscores, tk[rows_t, at]))
            dtk[rows_t, at] = low(scale * dot_tn(dscores, iq[mine, :, at]))
        tick()


def back_image(owner, iq, tk, tv, iprob, dic, jobs, ident):
    pairs = owner.shape[0]
    n = PAIRS_STEP
    wide = tk.shape[1]
    length, regions = tk.shape[0] // pairs, iprob.shape[1]
    heads = wide // HDIM
    rows = by_row(n * length, wide)
    probs = pl.BlockSpec((n * heads, regions, length), lambda i: (i, 0, 0))
    return carry(
        back_image_kernel,
        pairs // n,
        1 + n,
        2.0,
        (owner, iq, tk, tv, iprob, dic),
        [SCALARS, resident(iq.shape), rows, rows, probs, by_row(n * regions, wide)],
        [struct(iq.shape, jnp.float32)] + [struct(tk.shape, jnp.bfloat16)] * 2,
        [fixed(iq.shape), rows, rows],
        [],
        jobs,
        ident,
    )


def back_text_kernel(tick, owner, ik, iv, tq, tprob, dtc, dik, div, dtq):
    regions, length = tprob.shape[1:]
    heads = tq.shape[1] // HDIM
    scale = 1.0 / math.sqrt(HDIM)
    tick()

    @pl.when(pl.program_id(0) == 0)
    def _():
        dik[...] = jnp.zeros_like(dik)
        div[...] = jnp.zeros_like(div)

    for q in range(PAIRS_STEP):
        mine = owner[pl.program_id(0) * PAIRS_STEP + q]
        rows_t = slice(q * length, (q + 1) * length)
        for h in range(heads):
            at = slice(h * HDIM, (h + 1) * HDIM)
            grad = dtc[rows_t, at]
            probs = tprob[q * heads + h]
            dprobs = dot_nt(iv[mine, :, at], grad)
            add_to(div, mine, at, dot_nn(low(probs), grad))
            inner = jnp.sum(probs * dprobs, axis=0, keepdims=True)
            dscores = low(probs * (dprobs - inner))
            add_to(dik, mine, at, scale * dot_nn(dscores, tq[rows_t, at]))
            dtq[rows_t, at] = low(scale * dot_tn(dscores, ik[mine, :, at]))
        tick()


def back_text(owner, ik, iv, tq, tprob, dtc, jobs, ident):
    pairs = owner.shape[0]
    n = PAIRS_STEP
    wide = tq.shape[1]
    length, regions = tq.shape[0] // pairs, tprob.shape[1]
    heads = wide // HDIM
    rows = by_row(n * length, wide)
    probs = pl.BlockSpec((n * heads, regions, length), lambda i: (i, 0, 0))
    return carry(
        back_text_kernel,
        pairs // n,
        1 + n,
        2.0,
        (owner, ik, iv, tq, tprob, dtc),
        [SCALARS, resident(ik.shape), resident(iv.shape), rows, probs, rows],
        [struct(ik.shape, jnp.float32)] * 2 + [struct(tq.shape, jnp.bfloat16)],
        [fixed(ik.shape), fixed(ik.shape), rows],
        [],
        jobs,
        ident,
    )


def data_grad_kernel(tick, owner, text_dz, dtq, dtk, dtv, image_dz, diq, dik, div, *refs):
    weights, (text_grad, image_grad) = refs[:6], refs[6:]
    images, real = image_grad.shape[:2]
    pairs = owner.shape[0]
    slots = image_dz.shape[0] // pairs
    tick()

    @pl.when(pl.program_id(0) == 0)
    def _():
        for i in range(images):
            total = jnp.zeros((slots, image_dz.shape[1]), jnp.float32)
            for p in range(pairs):
                total += jnp.where(owner[p] == i, image_dz[p * slots : (p + 1) * slots, :], 0.0)
            for d, w in zip((diq, dik, div), weights[:3]):
                total = total + times_back(d[i], w)
            image_grad[i] = total[:real]

    total = text_dz[...]
    for d, w in zip((dtq, dtk, dtv), weights[3:]):
        total = total + times_back(d[...], w)
        tick()
    text_grad[...] = total


def data_grads(owner, text_dz, text_grads, image_dz, image_grads, weights, image_shape, jobs, ident):
    rows, wide = text_dz.shape
    bi = text_grads[0].shape[1]
    block = 256
    f32 = jnp.float32
    return carry(
        data_grad_kernel,
        rows // block,
        4,
        0.9,
        (owner, text_dz, *text_grads, image_dz, *image_grads, *weights),
        [SCALARS, by_row(block, wide)]
        + [by_row(block, bi)] * 3
        + [resident(image_dz.shape)]
        + [resident(d.shape) for d in image_grads]
        + [resident(w.shape) for w in weights],
        [struct((rows, wide), f32), struct(image_shape, f32)],
        [by_row(block, wide), fixed(image_shape)],
        [],
        jobs,
        ident,
    )


def pass_kernel(count, *refs):
    for source, target in zip(refs[:count], refs[count:]):
        target[...] = source[...]


def pass_on(arrays):
    return pl.pallas_call(
        functools.partial(pass_kernel, len(arrays)),
        out_shape=[struct(a.shape, a.dtype) for a in arrays],
        in_specs=[WHOLE] * len(arrays),
        out_specs=[WHOLE] * len(arrays),
        compiler_params=pltpu.CompilerParams(vmem_limit_bytes=VMEM_LIMIT),
    )(*arrays)


def only_transfers(jobs, ident):
    return carry(lambda tick: tick(), 1, 1, 1.0, (), [], [], [], [], jobs, ident)[1:]


def whole_weights(shards, gathered):
    nd, nf = mesh_bits()
    weights = []
    for shard, block in zip(shards, gathered):
        rows, cols = shard.shape
        block = block.reshape(1 << nf, rows << nd, cols)
        if cols % 128:
            block = jnp.swapaxes(block, 0, 1).reshape(1, rows << nd, cols << nf)
        weights.append(block)
    return weights


def device_blocks(grads, shards):
    nd, nf = mesh_bits()
    blocks = []
    for grad, shard in zip(grads, shards):
        rows, cols = shard.shape
        if cols % 128:
            grad = jnp.swapaxes(grad.reshape(rows << nd, 1 << nf, cols), 0, 1)
        blocks.append(grad.reshape((2,) * (nd + nf) + (rows, cols)))
    return blocks


def pad_norms(norm_params):
    return jnp.pad(norm_params, ((0, 4), (0, 128 - norm_params.shape[1])))


def whole_norms(gathered, wide):
    nd, nf = mesh_bits()
    norms = gathered.reshape(1 << nf, 1 << nd, 8, 128)[:, :, :4, :wide]
    return norms.transpose(2, 1, 0, 3).reshape(4, wide << (nd + nf))


def norm_blocks(rows):
    nd, nf = mesh_bits()
    wide = rows.shape[1] >> (nd + nf)
    split = rows.reshape(4, 1 << nd, 1 << nf, wide).transpose(2, 1, 0, 3)
    split = jnp.pad(split, ((0, 0), (0, 0), (0, 4), (0, 128 - wide)))
    return split.reshape((2,) * (nd + nf) + (8, 128))


def body(
    text_states,
    image_states,
    text_lengths,
    region_mask,
    group_ids,
    image_query,
    image_key,
    image_value,
    text_query,
    text_key,
    text_value,
    image_output,
    text_output,
    image_inner,
    image_outer,
    text_inner,
    text_outer,
    norm_params,
    cot_text,
    cot_image,
):
    pairs, length, width_text = text_states.shape
    images, regions, width_image = image_states.shape
    padded = -(-regions // 16) * 16
    device = lax.axis_index("dp") * lax.axis_size("fsdp") + lax.axis_index("fsdp")
    owner = group_ids - device * images
    mine = owner[:, None] == jnp.arange(images, dtype=jnp.int32)[None, :]
    region_counts = jnp.sum(region_mask, axis=1)
    counts = jnp.sum(jnp.where(mine, region_counts[None, :], 0), axis=1)
    text = text_states.reshape(pairs * length, width_text)
    image = jnp.pad(image_states, ((0, 0), (0, padded - regions), (0, 0)))
    visual = image[0]
    for i in range(1, images):
        visual = jnp.where(mine[:, i, None, None], image[i], visual)
    visual = visual.reshape(pairs * padded, width_image)
    image = image.reshape(images * padded, width_image)

    entry = [text_query, text_key, text_value, image_query, image_key, image_value]
    job = Gather(entry + [pad_norms(norm_params)], (0, 1, 2, 0, 1, 2, 0), (0, 0, 0, 1, 1, 1, 1))
    (gathered,) = only_transfers([job], 0)
    w_tq, w_tk, w_tv, w_iq, w_ik, w_iv = whole_weights(entry, gathered)
    norms = whole_norms(gathered[-1], norm_params.shape[1])

    rest = [image_output, image_inner, image_outer, text_output, text_inner]
    job = Gather(rest, (0, 1, 2, 0, 1), (0, 0, 0, 1, 1))
    kept, gathered = forward_attention(
        text_lengths,
        owner,
        counts,
        text,
        image,
        (w_iq, w_ik, w_iv, w_tq, w_tk, w_tv),
        images,
        [job],
        1,
    )
    iq, ik, iv, tq, tk, tv, iprob, tprob, image_context, text_context = kept
    w_io, w_ii, w_iu, w_to, w_ti = whole_weights(rest, gathered)

    job = Gather([text_outer], (0,), (0,), thirds=True)
    streamed, gathered = stream(
        counts,
        visual,
        image_context,
        cot_image,
        norms,
        width_text,
        (w_io, w_ii, w_iu),
        pairs // 2,
        1.0,
        [job],
        2,
    )
    (
        image_out,
        image_dz,
        image_mid,
        image_act,
        image_hid,
        image_ffn,
        image_branch,
        image_dctx,
        image_ngrad,
    ) = streamed
    (w_tu,) = whole_weights([text_outer], gathered)

    def wgrads(x, grads, weights, block):
        return weight_grads(x, grads, [w.shape[0] for w in weights], block, 1.0, [], 0)[0]

    (g_io,) = wgrads(image_context, [image_branch], [w_io], 512)
    (g_ii,) = wgrads(image_mid, [image_hid], [w_ii], 512)
    (g_iu,) = wgrads(image_act, [image_ffn], [w_iu], 512)
    diq, dtk, dtv = back_image(owner, iq, tk, tv, iprob, image_dctx, [], 0)[0]
    diq = low(diq)
    (g_iq,) = wgrads(image, [diq.reshape(image.shape[0], -1)], [w_iq], 512)
    g_tk, g_tv = wgrads(text, [dtk, dtv], [w_tk, w_tv], 256)

    shards = [image_output, image_inner, image_outer, image_query, text_key, text_value]
    blocks = device_blocks([g_io, g_ii, g_iu, g_iq, g_tk, g_tv], shards)
    job = Reduce(blocks, (0, 1, 2, 0, 1, 2), (0, 0, 0, 1, 1, 1))
    streamed, owned = stream(
        text_lengths,
        text,
        text_context,
        cot_text,
        norms,
        0,
        (w_to, w_ti, w_tu),
        2,
        1.6,
        [job],
        3,
    )
    o_io, o_ii, o_iu, o_iq, o_tk, o_tv = owned
    (
        text_out,
        text_dz,
        text_mid,
        text_act,
        text_hid,
        text_ffn,
        text_branch,
        text_dctx,
        text_ngrad,
    ) = streamed

    (g_tu,) = wgrads(text_act, [text_ffn], [w_tu], 512)
    blocks = device_blocks([g_tu], [text_outer])
    job = Reduce(blocks, (0,), (0,), thirds=True)
    (dik, div, dtq), (o_tu,) = back_text(owner, ik, iv, tq, tprob, text_dctx, [job], 4)
    dik, div = low(dik), low(div)
    (g_ti,) = wgrads(text_mid, [text_hid], [w_ti], 256)
    (g_to,) = wgrads(text_context, [text_branch], [w_to], 512)
    (g_tq,) = wgrads(text, [dtq], [w_tq], 256)
    flat = [d.reshape(image.shape[0], -1) for d in (dik, div)]
    g_ik, g_iv = wgrads(image, flat, [w_ik, w_iv], 512)
    shards = [text_inner, text_output, text_query, image_key, image_value]
    blocks = device_blocks([g_ti, g_to, g_tq, g_ik, g_iv], shards)
    norm_rows = norm_blocks(jnp.concatenate([text_ngrad, image_ngrad], axis=1))
    job = Reduce(blocks + [norm_rows], (0, 1, 2, 1, 2, 1), (0, 0, 0, 1, 1, 1))
    (text_grad, image_grad), owned = data_grads(
        owner,
        text_dz,
        (dtq, dtk, dtv),
        image_dz,
        (diq, dik, div),
        (w_iq, w_ik, w_iv, w_tq, w_tk, w_tv),
        image_states.shape,
        [job],
        5,
    )
    o_ti, o_to, o_tq, o_ik, o_iv, o_norm = owned
    owned = pass_on(
        [o_iq, o_ik, o_iv, o_tq, o_tk, o_tv, o_io, o_to, o_ii, o_iu, o_ti, o_tu]
    )
    norm_grad = o_norm[:4, : norm_params.shape[1]]
    return (
        text_out,
        image_out,
        text_grad.reshape(text_states.shape),
        image_grad,
        *owned,
        norm_grad,
    )


def solution(mesh):
    placed = (
        P(("dp", "fsdp"), None, None),
        P(("dp", "fsdp"), None, None),
        P(("dp", "fsdp")),
        P(("dp", "fsdp"), None),
        P(("dp", "fsdp")),
        P("dp", "fsdp"),
        P("dp", "fsdp"),
        P("dp", "fsdp"),
        P("dp", "fsdp"),
        P("dp", "fsdp"),
        P("dp", "fsdp"),
        P("dp", "fsdp"),
        P("dp", "fsdp"),
        P("dp", "fsdp"),
        P("dp", "fsdp"),
        P("dp", "fsdp"),
        P("dp", "fsdp"),
        P(None, ("dp", "fsdp")),
        P(("dp", "fsdp"), None, None),
        P(("dp", "fsdp"), None, None),
    )
    return jax.shard_map(
        body,
        mesh=mesh,
        in_specs=placed,
        out_specs=(
            P(("dp", "fsdp"), None, None),
            P(("dp", "fsdp"), None, None),
            P(("dp", "fsdp"), None, None),
            P(("dp", "fsdp"), None, None),
            P("dp", "fsdp"),
            P("dp", "fsdp"),
            P("dp", "fsdp"),
            P("dp", "fsdp"),
            P("dp", "fsdp"),
            P("dp", "fsdp"),
            P("dp", "fsdp"),
            P("dp", "fsdp"),
            P("dp", "fsdp"),
            P("dp", "fsdp"),
            P("dp", "fsdp"),
            P("dp", "fsdp"),
            P(None, ("dp", "fsdp")),
        ),
        check_vma=False,
    )
```

```python
import functools
import math

import jax
import jax.numpy as jnp
from jax import lax
from jax.experimental import pallas as pl
from jax.experimental.pallas import tpu as pltpu
from jax.sharding import PartitionSpec as P

HDIM = 128

norm_eps = 1e-12
masked_score = -1e30

MESH_IDS = pl.DeviceIdType.MESH
VMEM_LIMIT = 63 * 1024 * 1024
WHOLE = pl.BlockSpec(memory_space=pltpu.VMEM)
SCALARS = pl.BlockSpec(memory_space=pltpu.SMEM)
ANYWHERE = pl.BlockSpec(memory_space=pl.ANY)
CORE = ("d", 0)


def bits_of(size):
    count = size.bit_length() - 1
    assert 1 << count == size
    return count


def mesh_bits():
    return bits_of(lax.axis_size("dp")), bits_of(lax.axis_size("fsdp"))


def hop_orders(nd, nf):
    high = [("d", b) for b in range(nd - 1, 2, -1)]
    low = [("d", 2)]
    near = [("d", 1)]
    wide = [("f", b) for b in range(nf)]
    return (low + near + high + wide, high + wide + low + near)


def cut_pieces(shapes):
    pieces = []
    for m, (rows, cols) in enumerate(shapes):
        count = 4 if rows * cols > 40000 else 2
        if rows % (16 * count) == 0:
            each = rows // count
            cuts = [(k * each, each, 0, cols) for k in range(count)]
        elif cols % (128 * count) == 0 and rows % 8 == 0:
            each = cols // count
            cuts = [(0, rows, k * each, each) for k in range(count)]
        else:
            cuts = [(0, rows, 0, cols)]
        for cut in cuts:
            pieces.append((m, *cut, len(pieces) % 2))
    return pieces


class Place:
    def __init__(self, nd, nf):
        self.d = lax.axis_index("dp")
        self.f = lax.axis_index("fsdp")
        self.axes = [("f", b) for b in range(nf - 1, -1, -1)] + [
            ("d", b) for b in range(nd - 1, -1, -1)
        ]

    def bit(self, axis):
        value = self.f if axis[0] == "f" else self.d
        return lax.rem(value // (1 << axis[1]), 2)

    def partner(self, axis):
        step = (1 << axis[1]) * (1 - 2 * self.bit(axis))
        if axis[0] == "f":
            return (self.d, self.f + step)
        return (self.d + step, self.f)

    def index(self, whole, flip=None):
        picked = []
        for axis in self.axes:
            if axis in whole:
                picked.append(slice(None))
            elif axis == flip:
                picked.append(1 - self.bit(axis))
            else:
                picked.append(self.bit(axis))
        return tuple(picked)

    def barrier(self):
        sem = pltpu.get_barrier_semaphore()
        for axis in self.axes:
            pl.semaphore_signal(
                sem, inc=1, device_id=self.partner(axis), device_id_type=MESH_IDS
            )
        pl.semaphore_wait(sem, len(self.axes))


class Gather:
    def __init__(self, arrays):
        self.arrays = arrays
        self.given = arrays
        self.made = []
        self.nd, self.nf = mesh_bits()
        orders = hop_orders(self.nd, self.nf)
        self.cuts = cut_pieces([a.shape for a in arrays])
        self.routes = [tuple(orders[cut[-1]]) + (CORE,) for cut in self.cuts]
        self.hops = self.nd + self.nf
        lead = (2,) * self.hops
        self.out_shape = [jax.ShapeDtypeStruct(lead + a.shape, a.dtype) for a in arrays]
        self.out_specs = [ANYWHERE] * len(arrays)
        count = len(self.cuts)
        self.scratch = [
            pltpu.SemaphoreType.DMA((count,)),
            pltpu.SemaphoreType.DMA((count, self.hops)),
            pltpu.SemaphoreType.DMA((count, self.hops)),
        ]

    def sizes(self, k):
        m, row, rows, col, cols, _ = self.cuts[k]
        block = rows * cols * self.arrays[m].dtype.itemsize
        return [block << h for h in range(self.hops)]

    def window(self, k):
        m, row, rows, col, cols, _ = self.cuts[k]
        return (pl.ds(row, rows), pl.ds(col, cols))

    def bind(self, place, ins, outs, scratch):
        self.place, self.ins, self.outs = place, ins, outs
        self.local_sem, self.send_sem, self.recv_sem = scratch

    def local(self, k):
        m = self.cuts[k][0]
        return pltpu.make_async_copy(
            self.ins[m].at[self.window(k)],
            self.outs[m].at[self.place.index(()) + self.window(k)],
            self.local_sem.at[k],
        )

    def hop(self, k, h):
        m, route = self.cuts[k][0], self.routes[k]
        region = self.outs[m].at[self.place.index(route[:h]) + self.window(k)]
        return pltpu.make_async_remote_copy(
            src_ref=region,
            dst_ref=region,
            send_sem=self.send_sem.at[k, h],
            recv_sem=self.recv_sem.at[k, h],
            device_id=self.place.partner(route[h]),
            device_id_type=MESH_IDS,
        )

    def start(self):
        for k in range(len(self.cuts)):
            self.local(k).start()

    def step(self, k, h):
        if h == 0:
            self.local(k).wait()
        else:
            self.hop(k, h - 1).wait_recv()
        if h < self.hops:
            self.hop(k, h).start()
        else:
            for g in range(self.hops):
                self.hop(k, g).wait_send()


def add_blocks(acc, index, incoming):
    lead = incoming.shape[:-2]

    def one(i, carry):
        inner = []
        for size in reversed(lead):
            inner.append(lax.rem(i, size))
            i = i // size
        at = tuple(reversed(inner))
        inner = list(at)
        where = tuple(inner.pop(0) if isinstance(p, slice) else p for p in index)
        acc[where] = acc[where] + incoming[at]
        return carry

    lax.fori_loop(0, math.prod(lead), one, 0)


class Reduce:
    def __init__(self, given, made=None):
        made = made or {}
        self.given = given
        self.made = list(made)
        arrays = list(given) + list(made.values())
        self.arrays = arrays
        self.nd, self.nf = mesh_bits()
        orders = hop_orders(self.nd, self.nf)
        self.hops = self.nd + self.nf
        self.cuts = cut_pieces([a.shape[-2:] for a in arrays])
        self.routes = [(CORE,) + tuple(reversed(orders[cut[-1]])) for cut in self.cuts]
        self.scratch = []
        for m, row, rows, col, cols, _ in self.cuts:
            for h in range(-1, self.hops):
                free = self.hops - 1 - max(h, 0)
                self.scratch.append(pltpu.VMEM((2,) * free + (rows, cols), arrays[m].dtype))
        count = len(self.cuts)
        self.scratch += [
            pltpu.SemaphoreType.DMA((count,)),
            pltpu.SemaphoreType.DMA((count, self.hops)),
            pltpu.SemaphoreType.DMA((count, self.hops)),
        ]
        shapes = [a.shape[-2:] for a in arrays]
        self.out_shape = [jax.ShapeDtypeStruct(s, jnp.float32) for s in shapes]
        self.out_specs = [pl.BlockSpec(s, lambda *_: (0, 0)) for s in shapes]

    def sizes(self, k):
        m, row, rows, col, cols, _ = self.cuts[k]
        block = rows * cols * self.arrays[m].dtype.itemsize
        return [block << (self.hops - 1 - h) for h in range(self.hops)]

    def window(self, k):
        m, row, rows, col, cols, _ = self.cuts[k]
        return (pl.ds(row, rows), pl.ds(col, cols))

    def bind(self, place, ins, outs, scratch):
        self.place, self.ins, self.outs = place, ins, outs
        self.local_sem, self.send_sem, self.recv_sem = scratch[-3:]
        each = self.hops + 1
        self.accs = [scratch[k * each] for k in range(len(self.cuts))]
        self.temps = [scratch[k * each + 1 : (k + 1) * each] for k in range(len(self.cuts))]
        self.rest = [axis for axis in place.axes if axis != CORE]

    def local(self, k):
        source = self.ins[self.cuts[k][0]].at[self.place.index(self.rest) + self.window(k)]
        return pltpu.make_async_copy(source, self.accs[k], self.local_sem.at[k])

    def within(self, k, h, flip=None):
        full = self.place.index(self.routes[k][h + 1 :], flip)
        return tuple(p for p, axis in zip(full, self.place.axes) if axis != CORE)

    def hop(self, k, h):
        m, route = self.cuts[k][0], self.routes[k]
        if h == 0:
            region = self.ins[m].at[self.place.index(route[1:], CORE) + self.window(k)]
        else:
            region = self.accs[k].at[self.within(k, h, route[h])]
        return pltpu.make_async_remote_copy(
            src_ref=region,
            dst_ref=self.temps[k][h],
            send_sem=self.send_sem.at[k, h],
            recv_sem=self.recv_sem.at[k, h],
            device_id=self.place.partner(route[h]),
            device_id_type=MESH_IDS,
        )

    def start(self):
        pass

    def step(self, k, h):
        if h == 0:
            self.local(k).start()
        if h > 0:
            self.hop(k, h - 1).wait_recv()
            if h == 1:
                self.local(k).wait()
            here = self.within(k, h - 1)
            if h < self.hops:
                add_blocks(self.accs[k], here, self.temps[k][h - 1])
            else:
                m, row, rows, col, cols, _ = self.cuts[k]
                last = self.accs[k][here].astype(jnp.float32)
                last = last + self.temps[k][h - 1][...].astype(jnp.float32)
                self.outs[m][row : row + rows, col : col + cols] = last
        if h < self.hops:
            self.hop(k, h).start()
        else:
            for g in range(self.hops):
                self.hop(k, g).wait_send()


LINK_RATE = 46e3
CORE_RATE = 380e3
LATENCY = 2.5


class Phase:
    def __init__(self, run, steps, marks, needs=(), makes=()):
        self.run, self.steps, self.marks = run, steps, marks
        self.needs, self.makes = set(needs), set(makes)


def plan_steps(job, phases):
    pieces = range(len(job.cuts))
    order = sorted((n // 4 + h, n // 4, n, h) for n in pieces for h in range(job.hops + 1))
    times, first, after = [], [], {}
    clock = 0.0
    for phase in phases:
        first.append(len(times))
        for _ in range(phase.steps):
            times += [clock + mark for mark in phase.marks]
            clock += phase.marks[-1]
        for m in phase.makes:
            after[m] = len(times)
    total = len(times)
    limit = [total] * len(order)
    for phase, begin in zip(phases, first):
        last = -1
        for i, (_, _, n, h) in enumerate(order):
            if h == job.hops and job.cuts[n][0] in phase.needs:
                last = i
        for i in range(last + 1):
            limit[i] = min(limit[i], begin)
    waiting, active, done = {}, {}, {}
    now = 0.0

    def advance(key, until):
        nonlocal now
        while key not in done and now < until:
            for axis, queue in waiting.items():
                if queue and axis not in active:
                    active[axis] = queue.pop(0)
            far = any(axis[0] == "d" and axis[1] > 2 for axis in active)
            rates, span = {}, until - now
            for axis, (_, left) in active.items():
                halved = far and axis[0] == "d" and axis[1] > 1
                rates[axis] = CORE_RATE if axis == CORE else LINK_RATE / (2 if halved else 1)
                span = min(span, left / rates[axis])
            now += span
            for axis in list(active):
                active[axis][1] -= span * rates[axis]
                if active[axis][1] <= 1e-3:
                    done[active.pop(axis)[0]] = now + LATENCY

    slots = [[] for _ in range(total)]
    tail = []
    at, late = 0, 0.0
    for i, (_, _, n, h) in enumerate(order):
        ready = now
        if h:
            advance((n, h - 1), math.inf)
            ready = max(ready, done[n, h - 1])
        else:
            at = max(at, after.get(job.cuts[n][0], 0))
        while at < min(limit[i], total) and times[at] + late < ready - 0.3:
            at += 1
        if at < total:
            slots[at].append((n, h))
            late += max(ready - times[at] - late, 0.0)
            ready = max(ready, times[at] + late)
        else:
            tail.append((n, h))
        advance(None, ready)
        if h < job.hops:
            waiting.setdefault(job.routes[n][h], []).append([(n, h), float(job.sizes(n)[h])])
    return slots, tail


class Names:
    def __init__(self, names, refs):
        for name, ref in zip(names, refs):
            setattr(self, name, ref)


def carrying_kernel(phases, job, plan, names, *refs):
    spans, start = [], 0
    for group in names:
        spans.append(refs[start : start + len(group)])
        start += len(group)
    own_in, job_in, own_out, job_out, own_scratch, job_scratch = spans
    r = Names(names[0] + names[2] + names[4], own_in + own_out + own_scratch)
    now = pl.program_id(0)
    slots, tail = plan
    if job:
        place = Place(job.nd, job.nf)
        r.gathered = job_out
        made = [getattr(r, name) for name in job.made]
        job.bind(place, list(job_in) + made, job_out, job_scratch)

    def run(items, opening=False):
        if opening:
            job.start()
            place.barrier()
        for k, h in items:
            job.step(k, h)

    base, begin = 0, 0
    for phase in phases:
        ticks = len(phase.marks)

        def one(phase=phase, base=base, begin=begin, ticks=ticks):
            passed = [0]

            def tick():
                t = passed[0]
                passed[0] += 1
                for s in range(phase.steps if job else 0):
                    items = slots[base + s * ticks + t]
                    opening = base + s * ticks + t == 0
                    if items or opening:
                        pl.when(now == begin + s)(functools.partial(run, items, opening))

            phase.run(r, now - begin, tick)
            assert passed[0] == ticks

        if len(phases) == 1:
            one()
        else:
            pl.when((now >= begin) & (now < begin + phase.steps))(one)
        base += ticks * phase.steps
        begin += phase.steps
    if tail:
        pl.when(now == begin - 1)(functools.partial(run, tail))


def carry(phases, ins, outs, scratch, job=None, ident=None):
    plan = plan_steps(job, phases) if job else (None, None)
    given = list(job.given) if job else []
    landed = list(job.out_shape) if job else []
    names = (
        list(ins),
        [None] * len(given),
        list(outs),
        [None] * len(landed),
        list(scratch),
        [None] * (len(job.scratch) if job else 0),
    )
    params = {"vmem_limit_bytes": VMEM_LIMIT}
    if job:
        params.update(collective_id=ident, has_side_effects=True)
    results = pl.pallas_call(
        functools.partial(carrying_kernel, phases, job, plan, names),
        grid=(sum(phase.steps for phase in phases),),
        in_specs=[spec for _, spec in ins.values()] + [ANYWHERE] * len(given),
        out_specs=[spec for _, spec in outs.values()] + (list(job.out_specs) if job else []),
        out_shape=[shape for shape, _ in outs.values()] + landed,
        scratch_shapes=list(scratch.values()) + (list(job.scratch) if job else []),
        compiler_params=pltpu.CompilerParams(**params),
    )(*[array for array, _ in ins.values()], *given)
    r = Names(list(outs), results)
    r.gathered = results[len(outs) :]
    return r


def dot_nn(a, b):
    return lax.dot_general(a, b, (((1,), (0,)), ((), ())), preferred_element_type=jnp.float32)


def dot_nt(a, b):
    return lax.dot_general(a, b, (((1,), (1,)), ((), ())), preferred_element_type=jnp.float32)


def dot_tn(a, b):
    return lax.dot_general(a, b, (((0,), (0,)), ((), ())), preferred_element_type=jnp.float32)


def low(value):
    return value.astype(jnp.bfloat16)


def times(value, matrix):
    parts = [dot_nn(value, matrix[f]) for f in range(matrix.shape[0])]
    return parts[0] if len(parts) == 1 else jnp.concatenate(parts, axis=1)


def times_back(value, matrix):
    cols = matrix.shape[2]
    total = None
    for f in range(matrix.shape[0]):
        term = dot_nt(value[:, f * cols : (f + 1) * cols], matrix[f])
        total = term if total is None else total + term
    return total


def fixed(shape):
    return pl.BlockSpec(shape, lambda i: (0,) * len(shape))


def resident(array):
    zeros = (0,) * array.ndim
    return (array, pl.BlockSpec(array.shape, lambda i: zeros, pipeline_mode=pl.Buffered(1)))


def during(begin, steps, block, axis=0):
    def index(i):
        at = jnp.minimum(jnp.maximum(i - begin, 0), steps - 1)
        return tuple(at if d == axis else 0 for d in range(len(block)))

    return pl.BlockSpec(block, index)


def struct(shape, dtype):
    return jax.ShapeDtypeStruct(shape, dtype)


def rows_at(step, size):
    return pl.ds(pl.multiple_of(step * size, size), size)


def fetch(pairs, sems):
    copies = [
        pltpu.make_async_copy(source, target, sems.at[n])
        for n, (source, target) in enumerate(pairs)
    ]
    for copy in copies:
        copy.start()
    for copy in copies:
        copy.wait()


PAIRS_STEP = 2


def softmax(scores, axis):
    top = jnp.max(scores, axis=axis, keepdims=True)
    weight = jnp.exp(scores - top)
    return weight * (1.0 / jnp.sum(weight, axis=axis, keepdims=True))


def gelu_pair(x):
    scaled = jnp.abs(x) * (1.0 / math.sqrt(2.0))
    bell = jnp.exp(-0.5 * x * x)
    t = 1.0 / (1.0 + 0.3275911 * scaled)
    poly = t * (
        0.254829592
        + t * (-0.284496736 + t * (1.421413741 + t * (-1.453152027 + t * 1.061405429)))
    )
    tail = 0.5 * poly * bell
    below = jnp.where(x < 0, tail, 1.0 - tail)
    return x * below, below + x * bell * (1.0 / math.sqrt(2.0 * math.pi))


def row_mean(value):
    return jnp.mean(value, axis=-1, keepdims=True)


def col_sum(value):
    return jnp.sum(value, axis=0, keepdims=True)


def attend(r, q, p, rows_t, rows_i, iq, ik, iv, tq, tk, tv, iprob, tprob, ictx, tctx):
    regions, length = tprob.shape[1:]
    heads = tq.shape[1] // HDIM
    scale = 1.0 / math.sqrt(HDIM)
    mine = r.owner[p]
    kept_text = lax.broadcasted_iota(jnp.int32, (regions, length), 1) < r.lens[p]
    kept_region = lax.broadcasted_iota(jnp.int32, (regions, length), 0) < r.counts[p]
    for h in range(heads):
        at = slice(h * HDIM, (h + 1) * HDIM)
        values = tv[:, at]
        scores = scale * dot_nt(iq[mine, :, at], tk[:, at])
        probs = softmax(jnp.where(kept_text, scores, masked_score), 1)
        iprob[p * heads + h] = probs
        ictx[rows_i, at] = low(dot_nn(low(probs), values))
        scores = scale * dot_nt(ik[mine, :, at], tq[:, at])
        probs = softmax(jnp.where(kept_region, scores, masked_score), 0)
        tprob[q * heads + h] = probs
        tctx[rows_t, at] = low(dot_tn(low(probs), iv[mine, :, at]))


def forward_phase(norm_wide, r, step, tick):
    tick()
    pairs = r.lens.shape[0]
    length = r.text.shape[0] // pairs
    regions = r.tprob.shape[1]
    block = PAIRS_STEP * length

    @pl.when(step == 0)
    def _():
        targets = (r.w_tq, r.w_tk, r.w_tv, r.w_iq, r.w_ik, r.w_iv)
        fetch(
            [(g.reshape(w.shape), w) for g, w in zip(r.gathered, targets)]
            + [(r.gathered[6], r.norm_parts)],
            r.sems,
        )
        parts = r.norm_parts.shape[0:-2]
        nf = bits_of(lax.axis_size("fsdp"))
        for i in range(math.prod(parts)):
            at, rest = [], i
            for _ in parts:
                at.append(rest % 2)
                rest //= 2
            at = at[::-1]
            f = int("".join(map(str, at[:nf])) or "0", 2)
            d = int("".join(map(str, at[nf:])), 2)
            first = (d * (1 << nf) + f) * norm_wide
            r.norms[:, first : first + norm_wide] = r.norm_parts[tuple(at)][:4, :norm_wide]
        for w, out in ((r.w_iq, r.iq), (r.w_ik, r.ik), (r.w_iv, r.iv)):
            out[...] = low(times(r.image[...], w)).reshape(out.shape)

    here = rows_at(step, block)
    rows = r.text[here, :]
    r.tq[...] = low(times(rows, r.w_tq))
    r.tk[here, :] = low(times(rows, r.w_tk))
    r.tv[here, :] = low(times(rows, r.w_tv))
    tick()
    for q in range(PAIRS_STEP):
        p = step * PAIRS_STEP + q
        local = slice(q * length, (q + 1) * length)
        attend(
            r,
            q,
            p,
            local,
            rows_at(p, regions),
            r.iq,
            r.ik,
            r.iv,
            r.tq.at[local],
            r.tk.at[rows_at(p, length)],
            r.tv.at[rows_at(p, length)],
            r.iprob,
            r.tprob,
            r.ictx,
            r.tctx,
        )
        tick()


def stream_rows(r, step, tick, limits, x, ctx, cot, norms, weights, keeps, outs):
    w_out, w_inner, w_outer = weights
    mid_ref, act_ref, hid_ref, ffn_ref, branch_ref = keeps
    out, dz_out, dctx_out, ngrad = outs
    rows = x.shape[0]
    group, real = cot.shape[:2]
    slots = rows // group

    def normalize(z):
        offset = z - row_mean(z)
        inv = lax.rsqrt(row_mean(offset * offset) + norm_eps)
        return offset * inv, inv

    def normalize_back(dy, xhat, inv, gain):
        dx = dy * gain
        return inv * (dx - row_mean(dx) - xhat * row_mean(dx * xhat))

    @pl.when(step == 0)
    def _():
        ngrad[...] = jnp.zeros_like(ngrad)
        if real < slots:
            r.cot_wide[...] = jnp.zeros_like(r.cot_wide)

    row = lax.broadcasted_iota(jnp.int32, (rows, 1), 0)
    kept = row < 0
    for q in range(group):
        inside = (row >= q * slots) & (row < q * slots + limits[step * group + q])
        kept = kept | inside
        if real < slots:
            r.cot_wide[q * slots : q * slots + real, :] = cot[q].astype(jnp.float32)
    kept = kept.astype(jnp.float32)
    first_hat, first_inv = normalize(x[...].astype(jnp.float32) + times(ctx[...], w_out))
    mid = first_hat * norms[0] + norms[1]
    mid_low = low(mid)
    mid_ref[...] = mid_low
    tick()
    cols = w_inner.shape[2]
    for f in range(w_inner.shape[0]):
        at = slice(f * cols, (f + 1) * cols)
        act, grad = gelu_pair(dot_nn(mid_low, w_inner[f]))
        act_ref[:, at] = low(act)
        hid_ref[:, at] = low(grad)
        tick()
    second_hat, second_inv = normalize(mid + times(act_ref[...], w_outer))
    result = low((second_hat * norms[2] + norms[3]) * kept)
    for q in range(group):
        out[q] = result[q * slots : q * slots + real]
    if real < slots:
        dy = r.cot_wide[...] * kept
    else:
        dy = cot[...].reshape(rows, -1).astype(jnp.float32) * kept
    second_dz = normalize_back(dy, second_hat, second_inv, norms[2])
    ffn_low = low(second_dz)
    ffn_ref[...] = ffn_low
    sums = [col_sum(dy * second_hat), col_sum(dy)]
    tick()
    hid_ref[...] = low(times_back(ffn_low, w_outer) * hid_ref[...].astype(jnp.float32))
    tick()
    mid_grad = second_dz + times_back(hid_ref[...], w_inner)
    first_dz = normalize_back(mid_grad, first_hat, first_inv, norms[0])
    dz_out[...] = first_dz
    branch_low = low(first_dz)
    branch_ref[...] = branch_low
    tick()
    dctx_out[...] = low(times_back(branch_low, w_out))
    sums = [col_sum(mid_grad * first_hat), col_sum(mid_grad)] + sums
    for n in range(4):
        ngrad[n : n + 1, :] += sums[n]
    tick()


def store_grad(out, x, d):
    cols = out.shape[2]
    whole = low(dot_tn(x, d))
    for f in range(out.shape[0]):
        out[f] = whole[:, f * cols : (f + 1) * cols]


def add_to(ref, mine, at, value):
    value = low(value).astype(jnp.float32)
    for i in range(ref.shape[0]):
        ref[i, :, at] += jnp.where(mine == i, value, 0.0)


def image_phase(first_col, r, step, tick):
    tick()

    @pl.when(step == 0)
    def _():
        targets = (r.w_io, r.w_ii, r.w_iu)
        fetch([(g.reshape(w.shape), w) for g, w in zip(r.gathered[7:10], targets)], r.sems)
        r.norms_out[...] = r.norms[...]

    rows = r.visual.shape[0]
    here = rows_at(step, rows)
    wide = r.visual.shape[1]
    norms = [r.norms[n : n + 1, first_col : first_col + wide] for n in range(4)]
    stream_rows(
        r,
        step,
        tick,
        r.counts,
        r.visual,
        r.ictx.at[here],
        r.cot,
        norms,
        (r.w_io, r.w_ii, r.w_iu),
        [ref.at[here] for ref in (r.mid, r.act, r.hid, r.ffn, r.branch)],
        (r.image_out, r.image_dz, r.dctx.at[here], r.image_ngrad),
    )


def back_image_phase(r, step, tick):
    tick()
    heads = r.tk.shape[1] // HDIM
    pairs = r.owner.shape[0]
    length, regions = r.tk.shape[0] // pairs, r.iprob.shape[1]
    scale = 1.0 / math.sqrt(HDIM)

    @pl.when(step == 0)
    def _():
        r.diq_sum[...] = jnp.zeros_like(r.diq_sum)

    for q in range(PAIRS_STEP):
        p = step * PAIRS_STEP + q
        mine = r.owner[p]
        rows_t = rows_at(p, length)
        rows_i = rows_at(p, regions)
        local = slice(q * length, (q + 1) * length)
        for h in range(heads):
            at = slice(h * HDIM, (h + 1) * HDIM)
            grad = r.dctx[rows_i, at]
            probs = r.iprob[p * heads + h]
            dprobs = dot_nt(grad, r.tv[rows_t, at])
            dvalues = low(dot_tn(low(probs), grad))
            r.dtv_all[rows_t, at] = dvalues
            r.dtv[local, at] = dvalues
            inner = jnp.sum(probs * dprobs, axis=1, keepdims=True)
            dscores = low(probs * (dprobs - inner))
            add_to(r.diq_sum, mine, at, scale * dot_nn(dscores, r.tk[rows_t, at]))
            dkeys = low(scale * dot_tn(dscores, r.iq[mine, :, at]))
            r.dtk_all[rows_t, at] = dkeys
            r.dtk[local, at] = dkeys
        tick()


def image_grads_phase(r, step, tick):
    tick()
    block = r.g_io.shape[1]
    here = rows_at(step, block)
    store_grad(r.g_io, r.ictx[:, here], r.branch[...])
    store_grad(r.g_ii, r.mid[:, here], r.hid[...])
    store_grad(r.g_iu, r.act[:, here], r.ffn[...])
    diq = low(r.diq_sum[...])
    r.diq[...] = diq
    store_grad(r.g_iq, r.image[:, here], diq.reshape(r.image.shape[0], diq.shape[2]))
    tick()


def text_grads_phase(r, step, tick):
    tick()
    here = rows_at(step, r.g_tk.shape[1])
    store_grad(r.g_tk, r.text[:, here], r.dtk_all[...])
    store_grad(r.g_tv, r.text[:, here], r.dtv_all[...])
    tick()


def text_phase(r, step, tick):
    tick()
    rows = r.x.shape[0]
    here = rows_at(step, rows)
    norms = [r.norms[n : n + 1, : r.x.shape[1]] for n in range(4)]
    stream_rows(
        r,
        step,
        tick,
        r.lens,
        r.x,
        r.tctx.at[here],
        r.cot,
        norms,
        (r.w_to, r.w_ti, r.w_tu),
        [ref.at[here] for ref in (r.mid, r.act, r.hid, r.ffn, r.branch)],
        (r.text_out, r.text_dz, r.dctx, r.text_ngrad),
    )


def grad_phase(out, x, d, r, step, tick):
    tick()
    out = getattr(r, out)
    here = rows_at(step, out.shape[1])
    store_grad(out, getattr(r, x)[:, here], getattr(r, d)[...])
    tick()


def back_text_phase(r, step, tick):
    tick()
    heads = r.tq.shape[1] // HDIM
    pairs = r.owner.shape[0]
    length = r.dtq.shape[0] // pairs
    scale = 1.0 / math.sqrt(HDIM)

    @pl.when(step == 0)
    def _():
        r.dik_sum[...] = jnp.zeros_like(r.dik_sum)
        r.div_sum[...] = jnp.zeros_like(r.div_sum)

    for q in range(PAIRS_STEP):
        p = step * PAIRS_STEP + q
        mine = r.owner[p]
        rows_t = rows_at(p, length)
        local = slice(q * length, (q + 1) * length)
        for h in range(heads):
            at = slice(h * HDIM, (h + 1) * HDIM)
            grad = r.dtc[local, at]
            probs = r.tprob[q * heads + h]
            dprobs = dot_nt(r.iv[mine, :, at], grad)
            add_to(r.div_sum, mine, at, dot_nn(low(probs), grad))
            inner = jnp.sum(probs * dprobs, axis=0, keepdims=True)
            dscores = low(probs * (dprobs - inner))
            add_to(r.dik_sum, mine, at, scale * dot_nn(dscores, r.tq[local, at]))
            r.dtq[rows_t, at] = low(scale * dot_tn(dscores, r.ik[mine, :, at]))
        tick()


def query_grads_phase(r, step, tick):
    tick()

    def put(out, x, d):
        cols = out.shape[-1]
        nf = bits_of(lax.axis_size("fsdp"))
        whole = low(dot_tn(x[...], d))
        for f in range(1 << nf):
            at = tuple((f >> b) % 2 for b in range(nf - 1, -1, -1))
            part = whole[:, f * cols : (f + 1) * cols]
            out[at] = part.reshape(out.shape[nf:])

    put(r.g_tq, r.text, r.dtq[...])
    dik, div = low(r.dik_sum[...]), low(r.div_sum[...])
    r.dik[...] = dik
    r.div[...] = div
    flat = (r.image.shape[0], dik.shape[2])
    put(r.g_ik, r.image, dik.reshape(flat))
    put(r.g_iv, r.image, div.reshape(flat))
    tick()


def data_grads_phase(r, step, tick):
    images, real = r.image_grad.shape[:2]
    pairs = r.owner.shape[0]
    slots = r.image_dz.shape[0] // pairs
    tick()

    @pl.when(step == 0)
    def _():
        for i in range(images):
            total = jnp.zeros((slots, r.image_dz.shape[1]), jnp.float32)
            for p in range(pairs):
                rows = r.image_dz[p * slots : (p + 1) * slots, :]
                total += jnp.where(r.owner[p] == i, rows, 0.0)
            for d, w in ((r.diq, r.w_iq), (r.dik, r.w_ik), (r.div, r.w_iv)):
                total = total + times_back(d[i], w)
            r.image_grad[i] = total[:real]

    total = r.text_dz[...]
    here = rows_at(step, total.shape[0])
    for d, w in ((r.dtq.at[here], r.w_tq), (r.dtk, r.w_tk), (r.dtv, r.w_tv)):
        total = total + times_back(d[...], w)
        tick()
    r.text_grad[...] = total


def pass_kernel(count, *refs):
    for source, target in zip(refs[:count], refs[count:]):
        target[...] = source[...]


def pass_on(arrays):
    return pl.pallas_call(
        functools.partial(pass_kernel, len(arrays)),
        out_shape=[struct(a.shape, a.dtype) for a in arrays],
        in_specs=[WHOLE] * len(arrays),
        out_specs=[WHOLE] * len(arrays),
        compiler_params=pltpu.CompilerParams(vmem_limit_bytes=VMEM_LIMIT),
    )(*arrays)


def whole_weight(shard, block):
    nd, nf = mesh_bits()
    rows, cols = shard.shape
    block = block.reshape(1 << nf, rows << nd, cols)
    if cols % 128:
        block = jnp.swapaxes(block, 0, 1).reshape(1, rows << nd, cols << nf)
    return block


def device_blocks(grad, shard):
    nd, nf = mesh_bits()
    rows, cols = shard.shape
    if cols % 128:
        grad = jnp.swapaxes(grad.reshape(rows << nd, 1 << nf, cols), 0, 1)
    return grad.reshape((2,) * (nd + nf) + (rows, cols))


def norm_blocks(rows):
    nd, nf = mesh_bits()
    wide = rows.shape[1] >> (nd + nf)
    split = rows.reshape(4, 1 << nd, 1 << nf, wide).transpose(2, 1, 0, 3)
    split = jnp.pad(split, ((0, 0), (0, 0), (0, 4), (0, 128 - wide)))
    return split.reshape((2,) * (nd + nf) + (8, 128))


def body(
    text_states,
    image_states,
    text_lengths,
    region_mask,
    group_ids,
    image_query,
    image_key,
    image_value,
    text_query,
    text_key,
    text_value,
    image_output,
    text_output,
    image_inner,
    image_outer,
    text_inner,
    text_outer,
    norm_params,
    cot_text,
    cot_image,
):
    nd, nf = mesh_bits()
    lead = (2,) * (nd + nf)
    bf, f32 = jnp.bfloat16, jnp.float32
    pairs, length, width_text = text_states.shape
    images, regions, width_image = image_states.shape
    padded = -(-regions // 16) * 16
    wide = image_query.shape[1] << nf
    heads = wide // HDIM
    rows_text, rows_image = pairs * length, pairs * padded
    norm_wide = norm_params.shape[1]
    device = lax.axis_index("dp") * lax.axis_size("fsdp") + lax.axis_index("fsdp")
    owner = group_ids - device * images
    mine = owner[:, None] == jnp.arange(images, dtype=jnp.int32)[None, :]
    region_counts = jnp.sum(region_mask, axis=1)
    counts = jnp.sum(jnp.where(mine, region_counts[None, :], 0), axis=1)
    text = text_states.reshape(rows_text, width_text)
    image = jnp.pad(image_states, ((0, 0), (0, padded - regions), (0, 0)))
    visual = image[0]
    for i in range(1, images):
        visual = jnp.where(mine[:, i, None, None], image[i], visual)
    visual = visual.reshape(rows_image, width_image)
    image = image.reshape(images * padded, width_image)

    def full(shard):
        rows, cols = shard.shape
        return pltpu.VMEM((1 << nf, rows << nd, cols), bf)

    def vmem(rows, cols, dtype=bf):
        return pltpu.VMEM((rows, cols), dtype)

    n = PAIRS_STEP
    steps = pairs // n
    group = pairs // 2
    block_i = group * padded
    padded_norms = jnp.pad(norm_params, ((0, 4), (0, 128 - norm_wide)))
    job = Gather(
        [text_query, text_key, text_value, image_query, image_key, image_value, padded_norms]
        + [image_output, image_inner, image_outer, text_output, text_inner, text_outer]
    )
    phases, begin = [], [0]

    def phase(run, count, marks, **kw):
        phases.append(Phase(run, count, marks, **kw))
        begin.append(begin[-1] + count)
        return begin[-2]

    forward_marks = (0.0, 2.0, 5.2, 8.5)
    at_forward = phase(
        functools.partial(forward_phase, norm_wide), steps, forward_marks, needs=range(7)
    )
    stages = 1 << nf
    marks = [0.0, 1.2] + [1.2 + 1.2 * (k + 1) / stages for k in range(stages)]
    marks += [4.0, 5.3, 6.8, 7.6]
    at_image = phase(
        functools.partial(image_phase, width_text), 2, marks, needs=range(7, 10)
    )
    at_back = phase(back_image_phase, steps, (0.0, 2.3, 4.6))
    at_grads = phase(image_grads_phase, 2, (0.0, 5.0))
    third = width_text // 3
    at_text_grads = phase(text_grads_phase, 3, (0.0, 2.5))

    def grad_out(weight_shard, inner, first, count, size):
        shape = (1 << nf, inner, weight_shard.shape[1])
        if weight_shard.shape[1] % 128:
            shape = (1, inner, weight_shard.shape[1] << nf)
        block = (shape[0], size, shape[2])
        return (struct(shape, bf), during(first, count, block, 1))

    by_pair = during(at_image, 2, (group, regions, width_image))
    probs = during(at_forward, steps, (n * heads, padded, length))
    a = carry(
        phases,
        dict(
            lens=(text_lengths, SCALARS),
            owner=(owner, SCALARS),
            counts=(counts, SCALARS),
            text=resident(text),
            image=resident(image),
            visual=(visual, during(at_image, 2, (block_i, width_image))),
            cot=(cot_image, by_pair),
        ),
        dict(
            ik=(struct((images, padded, wide), bf), fixed((images, padded, wide))),
            iv=(struct((images, padded, wide), bf), fixed((images, padded, wide))),
            tq=(struct((rows_text, wide), bf), during(at_forward, steps, (n * length, wide))),
            tprob=(struct((pairs * heads, padded, length), f32), probs),
            tctx=(struct((rows_text, wide), bf), during(at_forward, steps, (n * length, wide))),
            norms_out=(struct((4, norm_wide << (nd + nf)), f32), fixed((4, norm_wide << (nd + nf)))),
            image_out=(struct(cot_image.shape, bf), by_pair),
            image_dz=(
                struct((rows_image, width_image), f32),
                during(at_image, 2, (block_i, width_image)),
            ),
            image_ngrad=(struct((4, width_image), f32), fixed((4, width_image))),
            dtk=(struct((rows_text, wide), bf), during(at_back, steps, (n * length, wide))),
            dtv=(struct((rows_text, wide), bf), during(at_back, steps, (n * length, wide))),
            diq=(struct((images, padded, wide), bf), fixed((images, padded, wide))),
            g_io=grad_out(image_output, wide, at_grads, 2, wide // 2),
            g_ii=grad_out(image_inner, width_image, at_grads, 2, width_image // 2),
            g_iu=grad_out(image_outer, width_image, at_grads, 2, width_image // 2),
            g_iq=grad_out(image_query, width_image, at_grads, 2, width_image // 2),
            g_tk=grad_out(text_key, width_text, at_text_grads, 3, third),
            g_tv=grad_out(text_value, width_text, at_text_grads, 3, third),
        ),
        dict(
            w_tq=full(text_query),
            w_tk=full(text_key),
            w_tv=full(text_value),
            w_iq=full(image_query),
            w_ik=full(image_key),
            w_iv=full(image_value),
            w_io=full(image_output),
            w_ii=full(image_inner),
            w_iu=full(image_outer),
            norm_parts=pltpu.VMEM(lead + (8, 128), f32),
            norms=pltpu.VMEM((4, norm_wide << (nd + nf)), f32),
            sems=pltpu.SemaphoreType.DMA((7,)),
            iq=pltpu.VMEM((images, padded, wide), bf),
            tk=vmem(rows_text, wide),
            tv=vmem(rows_text, wide),
            iprob=pltpu.VMEM((pairs * heads, padded, length), f32),
            ictx=vmem(rows_image, wide),
            mid=vmem(rows_image, width_image),
            act=vmem(rows_image, width_image),
            hid=vmem(rows_image, width_image),
            ffn=vmem(rows_image, width_image),
            branch=vmem(rows_image, width_image),
            dctx=vmem(rows_image, wide),
            diq_sum=pltpu.VMEM((images, padded, wide), f32),
            dtk_all=vmem(rows_text, wide),
            dtv_all=vmem(rows_text, wide),
            cot_wide=vmem(block_i, width_image, f32),
        ),
        job,
        0,
    )
    w_tq, w_tk, w_tv, w_iq, w_ik, w_iv = (
        whole_weight(s, g) for s, g in zip(job.given[:6], a.gathered[:6])
    )
    w_to, w_ti, w_tu = (whole_weight(s, g) for s, g in zip(job.given[10:], a.gathered[10:]))

    job = Reduce(
        [
            device_blocks(grad, shard)
            for grad, shard in (
                (a.g_io, image_output),
                (a.g_ii, image_inner),
                (a.g_iu, image_outer),
                (a.g_iq, image_query),
                (a.g_tk, text_key),
                (a.g_tv, text_value),
            )
        ]
    )
    phases, begin = [], [0]
    inner = w_ti.shape[0] * w_ti.shape[2]
    block_t = n * length
    stages = w_ti.shape[0]
    marks = [0.0, 1.8] + [1.8 + 4.8 * (k + 1) / stages for k in range(stages)]
    marks += [9.2, 11.2, 13.4, 14.2]
    at_text = phase(text_phase, steps, marks)
    at_tu = phase(functools.partial(grad_phase, "g_tu", "act", "ffn"), 6, (0.0, 1.4))
    at_ti = phase(functools.partial(grad_phase, "g_ti", "mid", "hid"), 6, (0.0, 1.4))
    at_to = phase(functools.partial(grad_phase, "g_to", "tctx", "branch"), 2, (0.0, 1.6))
    by_pair = during(at_text, steps, (n, length, width_text))

    def text_rows(cols):
        return during(at_text, steps, (block_t, cols))

    b = carry(
        phases,
        dict(
            lens=(text_lengths, SCALARS),
            x=(text, text_rows(width_text)),
            tctx=resident(a.tctx),
            cot=(cot_text, by_pair),
            norms=resident(a.norms_out),
            w_to=resident(w_to),
            w_ti=resident(w_ti),
            w_tu=resident(w_tu),
        ),
        dict(
            text_out=(struct(cot_text.shape, bf), by_pair),
            text_dz=(struct((rows_text, width_text), f32), text_rows(width_text)),
            dctx=(struct((rows_text, wide), bf), text_rows(wide)),
            text_ngrad=(struct((4, width_text), f32), fixed((4, width_text))),
            g_tu=grad_out(text_outer, inner, at_tu, 6, inner // 6),
            g_ti=grad_out(text_inner, width_text, at_ti, 6, width_text // 6),
            g_to=grad_out(text_output, wide, at_to, 2, wide // 2),
        ),
        dict(
            mid=vmem(rows_text, width_text),
            act=vmem(rows_text, inner),
            hid=vmem(rows_text, inner),
            ffn=vmem(rows_text, width_text),
            branch=vmem(rows_text, width_text),
        ),
        job,
        1,
    )
    o_io, o_ii, o_iu, o_iq, o_tk, o_tv = b.gathered

    norm_rows = norm_blocks(jnp.concatenate([b.text_ngrad, a.image_ngrad], axis=1))
    job = Reduce(
        [
            device_blocks(b.g_tu, text_outer),
            device_blocks(b.g_ti, text_inner),
            device_blocks(b.g_to, text_output),
            norm_rows,
        ],
        dict(
            g_tq=struct(lead + text_query.shape, bf),
            g_ik=struct(lead + image_key.shape, bf),
            g_iv=struct(lead + image_value.shape, bf),
        ),
    )
    phases, begin = [], [0]
    at_back = phase(back_text_phase, steps, (0.0, 2.3, 4.6))
    phase(query_grads_phase, 1, (0.0, 7.0), makes=range(4, 7))
    at_data = phase(data_grads_phase, steps, (0.0, 1.0, 2.2, 3.6))
    probs = during(at_back, steps, (n * heads, padded, length))
    back_rows = during(at_back, steps, (block_t, wide))
    data_rows = during(at_data, steps, (block_t, wide))
    data_out = during(at_data, steps, (block_t, width_text))
    c = carry(
        phases,
        dict(
            owner=(owner, SCALARS),
            ik=resident(a.ik),
            iv=resident(a.iv),
            tq=(a.tq, back_rows),
            tprob=(a.tprob, probs),
            dtc=(b.dctx, back_rows),
            text=resident(text),
            image=resident(image),
            text_dz=(b.text_dz, data_out),
            dtk=(a.dtk, data_rows),
            dtv=(a.dtv, data_rows),
            image_dz=resident(a.image_dz),
            diq=resident(a.diq),
            w_tq=resident(w_tq),
            w_tk=resident(w_tk),
            w_tv=resident(w_tv),
            w_iq=resident(w_iq),
            w_ik=resident(w_ik),
            w_iv=resident(w_iv),
        ),
        dict(
            text_grad=(struct((rows_text, width_text), f32), data_out),
            image_grad=(struct(image_states.shape, f32), fixed(image_states.shape)),
        ),
        dict(
            dtq=vmem(rows_text, wide),
            dik=pltpu.VMEM((images, padded, wide), bf),
            div=pltpu.VMEM((images, padded, wide), bf),
            dik_sum=pltpu.VMEM((images, padded, wide), f32),
            div_sum=pltpu.VMEM((images, padded, wide), f32),
            g_tq=pltpu.VMEM(lead + text_query.shape, bf),
            g_ik=pltpu.VMEM(lead + image_key.shape, bf),
            g_iv=pltpu.VMEM(lead + image_value.shape, bf),
        ),
        job,
        2,
    )
    o_tu, o_ti, o_to, o_norm, o_tq, o_ik, o_iv = c.gathered
    owned = pass_on([o_iq, o_ik, o_iv, o_tq, o_tk, o_tv, o_io, o_to, o_ii, o_iu, o_ti, o_tu])
    return (
        b.text_out,
        a.image_out,
        c.text_grad.reshape(text_states.shape),
        c.image_grad,
        *owned,
        o_norm[:4, :norm_wide],
    )


def solution(mesh):
    placed = (
        P(("dp", "fsdp"), None, None),
        P(("dp", "fsdp"), None, None),
        P(("dp", "fsdp")),
        P(("dp", "fsdp"), None),
        P(("dp", "fsdp")),
        P("dp", "fsdp"),
        P("dp", "fsdp"),
        P("dp", "fsdp"),
        P("dp", "fsdp"),
        P("dp", "fsdp"),
        P("dp", "fsdp"),
        P("dp", "fsdp"),
        P("dp", "fsdp"),
        P("dp", "fsdp"),
        P("dp", "fsdp"),
        P("dp", "fsdp"),
        P("dp", "fsdp"),
        P(None, ("dp", "fsdp")),
        P(("dp", "fsdp"), None, None),
        P(("dp", "fsdp"), None, None),
    )
    return jax.shard_map(
        body,
        mesh=mesh,
        in_specs=placed,
        out_specs=(
            P(("dp", "fsdp"), None, None),
            P(("dp", "fsdp"), None, None),
            P(("dp", "fsdp"), None, None),
            P(("dp", "fsdp"), None, None),
            P("dp", "fsdp"),
            P("dp", "fsdp"),
            P("dp", "fsdp"),
            P("dp", "fsdp"),
            P("dp", "fsdp"),
            P("dp", "fsdp"),
            P("dp", "fsdp"),
            P("dp", "fsdp"),
            P("dp", "fsdp"),
            P("dp", "fsdp"),
            P("dp", "fsdp"),
            P("dp", "fsdp"),
            P(None, ("dp", "fsdp")),
        ),
        check_vma=False,
    )
```

```python
import functools
import math

import jax
import jax.numpy as jnp
from jax import lax
from jax.experimental import pallas as pl
from jax.experimental.pallas import tpu as pltpu
from jax.sharding import PartitionSpec as P

HDIM = 128

norm_eps = 1e-12
masked_score = -1e30

MESH_IDS = pl.DeviceIdType.MESH
VMEM_LIMIT = 63 * 1024 * 1024
WHOLE = pl.BlockSpec(memory_space=pltpu.VMEM)
SCALARS = pl.BlockSpec(memory_space=pltpu.SMEM)
ANYWHERE = pl.BlockSpec(memory_space=pl.ANY)
CORE = ("d", 0)


def bits_of(size):
    count = size.bit_length() - 1
    assert 1 << count == size
    return count


def mesh_bits():
    return bits_of(lax.axis_size("dp")), bits_of(lax.axis_size("fsdp"))


def hop_orders(nd, nf):
    high = [("d", b) for b in range(nd - 1, 2, -1)]
    low = [("d", 2)]
    near = [("d", 1)]
    wide = [("f", b) for b in range(nf)]
    return (low + near + high + wide, high + wide + low + near)


def cut_pieces(shapes):
    pieces, waves, large = [], [], 0
    for m, (rows, cols) in enumerate(shapes):
        count = 4 if rows * cols > 40000 else 2
        if rows % (16 * count) == 0:
            each = rows // count
            cuts = [(k * each, each, 0, cols) for k in range(count)]
        elif cols % (128 * count) == 0 and rows % 8 == 0:
            each = cols // count
            cuts = [(0, rows, k * each, each) for k in range(count)]
        else:
            cuts = [(0, rows, 0, cols)]
        for cut in cuts:
            pieces.append((m, *cut, large % 2))
            small = rows * cols < 2048
            waves.append(0 if small else large // 4)
            large += 0 if small else 1
    return pieces, waves


class Place:
    def __init__(self, nd, nf):
        self.d = lax.axis_index("dp")
        self.f = lax.axis_index("fsdp")
        self.axes = [("f", b) for b in range(nf - 1, -1, -1)] + [
            ("d", b) for b in range(nd - 1, -1, -1)
        ]

    def bit(self, axis):
        value = self.f if axis[0] == "f" else self.d
        return lax.rem(value // (1 << axis[1]), 2)

    def partner(self, axis):
        step = (1 << axis[1]) * (1 - 2 * self.bit(axis))
        if axis[0] == "f":
            return (self.d, self.f + step)
        return (self.d + step, self.f)

    def index(self, whole, flip=None):
        picked = []
        for axis in self.axes:
            if axis in whole:
                picked.append(slice(None))
            elif axis == flip:
                picked.append(1 - self.bit(axis))
            else:
                picked.append(self.bit(axis))
        return tuple(picked)

    def barrier(self):
        sem = pltpu.get_barrier_semaphore()
        for axis in self.axes:
            pl.semaphore_signal(
                sem, inc=1, device_id=self.partner(axis), device_id_type=MESH_IDS
            )
        pl.semaphore_wait(sem, len(self.axes))


class Gather:
    def __init__(self, arrays):
        self.arrays = arrays
        self.given = arrays
        self.made = []
        self.nd, self.nf = mesh_bits()
        orders = hop_orders(self.nd, self.nf)
        self.cuts, self.waves = cut_pieces([a.shape for a in arrays])
        self.routes = [tuple(orders[cut[-1]]) + (CORE,) for cut in self.cuts]
        self.hops = self.nd + self.nf
        lead = (2,) * self.hops
        self.out_shape = [jax.ShapeDtypeStruct(lead + a.shape, a.dtype) for a in arrays]
        self.out_specs = [ANYWHERE] * len(arrays)
        count = len(self.cuts)
        self.scratch = [
            pltpu.SemaphoreType.DMA((count,)),
            pltpu.SemaphoreType.DMA((count, self.hops)),
            pltpu.SemaphoreType.DMA((count, self.hops)),
        ]

    def sizes(self, k):
        m, row, rows, col, cols, _ = self.cuts[k]
        block = rows * cols * self.arrays[m].dtype.itemsize
        return [block << h for h in range(self.hops)]

    def window(self, k):
        m, row, rows, col, cols, _ = self.cuts[k]
        return (pl.ds(row, rows), pl.ds(col, cols))

    def bind(self, place, ins, outs, scratch):
        self.place, self.ins, self.outs = place, ins, outs
        self.local_sem, self.send_sem, self.recv_sem = scratch

    def local(self, k):
        m = self.cuts[k][0]
        return pltpu.make_async_copy(
            self.ins[m].at[self.window(k)],
            self.outs[m].at[self.place.index(()) + self.window(k)],
            self.local_sem.at[k],
        )

    def hop(self, k, h):
        m, route = self.cuts[k][0], self.routes[k]
        region = self.outs[m].at[self.place.index(route[:h]) + self.window(k)]
        return pltpu.make_async_remote_copy(
            src_ref=region,
            dst_ref=region,
            send_sem=self.send_sem.at[k, h],
            recv_sem=self.recv_sem.at[k, h],
            device_id=self.place.partner(route[h]),
            device_id_type=MESH_IDS,
        )

    def start(self):
        for k in range(len(self.cuts)):
            self.local(k).start()

    def step(self, k, h):
        if h == 0:
            self.local(k).wait()
        else:
            self.hop(k, h - 1).wait_recv()
        if h < self.hops:
            self.hop(k, h).start()
        else:
            for g in range(self.hops):
                self.hop(k, g).wait_send()


def add_blocks(acc, index, window, incoming):
    lead = incoming.shape[:-2]
    outer, inner = lead[:-2], lead[-2:]

    def one(i, carry):
        first = []
        for size in reversed(outer):
            first.append(lax.rem(i, size))
            i = i // size
        first = first[::-1]
        for j in range(math.prod(inner)):
            at, rest = [], j
            for size in reversed(inner):
                at.append(rest % size)
                rest //= size
            at = tuple(first + at[::-1])
            left = list(at)
            where = tuple(left.pop(0) if isinstance(p, slice) else p for p in index) + window
            acc[where] = acc[where] + incoming[at]
        return carry

    lax.fori_loop(0, math.prod(outer), one, 0)


class Reduce:
    def __init__(self, given, made=None):
        made = made or {}
        self.given = given
        self.made = list(made)
        arrays = list(given) + list(made.values())
        self.arrays = arrays
        self.nd, self.nf = mesh_bits()
        orders = hop_orders(self.nd, self.nf)
        self.hops = self.nd + self.nf
        self.cuts, self.waves = cut_pieces([a.shape[-2:] for a in arrays])
        self.routes = [(CORE,) + tuple(reversed(orders[cut[-1]])) for cut in self.cuts]
        self.scratch = []
        for m, row, rows, col, cols, _ in self.cuts:
            for h in range(-1 if m < len(self.given) else 0, self.hops):
                free = self.hops - 1 - max(h, 0)
                self.scratch.append(pltpu.VMEM((2,) * free + (rows, cols), arrays[m].dtype))
        count = len(self.cuts)
        self.scratch += [
            pltpu.SemaphoreType.DMA((count,)),
            pltpu.SemaphoreType.DMA((count, self.hops)),
            pltpu.SemaphoreType.DMA((count, self.hops)),
        ]
        shapes = [a.shape[-2:] for a in arrays]
        self.out_shape = [jax.ShapeDtypeStruct(s, jnp.float32) for s in shapes]
        self.out_specs = [pl.BlockSpec(s, lambda *_: (0, 0)) for s in shapes]

    def sizes(self, k):
        m, row, rows, col, cols, _ = self.cuts[k]
        block = rows * cols * self.arrays[m].dtype.itemsize
        return [block << (self.hops - 1 - h) for h in range(self.hops)]

    def window(self, k):
        m, row, rows, col, cols, _ = self.cuts[k]
        return (pl.ds(row, rows), pl.ds(col, cols))

    def bind(self, place, ins, outs, scratch):
        self.place, self.ins, self.outs = place, ins, outs
        self.local_sem, self.send_sem, self.recv_sem = scratch[-3:]
        rest = list(scratch[:-3])
        self.accs, self.temps = [], []
        for m, *_ in self.cuts:
            self.accs.append(rest.pop(0) if m < len(self.given) else None)
            self.temps.append([rest.pop(0) for _ in range(self.hops)])
        self.rest = [axis for axis in place.axes if axis != CORE]

    def local(self, k):
        source = self.ins[self.cuts[k][0]].at[self.place.index(self.rest) + self.window(k)]
        return pltpu.make_async_copy(source, self.accs[k], self.local_sem.at[k])

    def within(self, k, h, flip=None):
        full = self.place.index(self.routes[k][h + 1 :], flip)
        if self.accs[k] is None:
            m, row, rows, col, cols, _ = self.cuts[k]
            return self.ins[m], full, (slice(row, row + rows), slice(col, col + cols))
        return self.accs[k], tuple(p for p, a in zip(full, self.place.axes) if a != CORE), ()

    def hop(self, k, h):
        m, route = self.cuts[k][0], self.routes[k]
        if h == 0:
            region = self.ins[m].at[self.place.index(route[1:], CORE) + self.window(k)]
        else:
            acc, index, window = self.within(k, h, route[h])
            region = acc.at[index + window]
        return pltpu.make_async_remote_copy(
            src_ref=region,
            dst_ref=self.temps[k][h],
            send_sem=self.send_sem.at[k, h],
            recv_sem=self.recv_sem.at[k, h],
            device_id=self.place.partner(route[h]),
            device_id_type=MESH_IDS,
        )

    def start(self):
        pass

    def step(self, k, h):
        own = self.accs[k] is not None
        if h == 0 and own:
            self.local(k).start()
        if h > 0:
            self.hop(k, h - 1).wait_recv()
            if h == 1 and own:
                self.local(k).wait()
            acc, index, window = self.within(k, h - 1)
            if h < self.hops:
                add_blocks(acc, index, window, self.temps[k][h - 1])
            else:
                m, row, rows, col, cols, _ = self.cuts[k]
                last = acc[index + window].astype(jnp.float32)
                last = last + self.temps[k][h - 1][...].astype(jnp.float32)
                self.outs[m][row : row + rows, col : col + cols] = last
        if h < self.hops:
            self.hop(k, h).start()
        else:
            for g in range(self.hops):
                self.hop(k, g).wait_send()


LINK_RATE = 46e3
CORE_RATE = 380e3
LATENCY = 2.5


class Phase:
    def __init__(self, run, steps, marks, needs=(), makes=()):
        self.run, self.steps, self.marks = run, steps, marks
        self.needs, self.makes = set(needs), set(makes)


def plan_steps(jobs, phases):
    order = []
    for j, job in enumerate(jobs):
        order += sorted(
            (wave + h, wave, (j, k), h)
            for k, wave in enumerate(job.waves)
            for h in range(job.hops + 1)
        )
    times, first, after = [], [], {}
    clock = 0.0
    for phase in phases:
        first.append(len(times))
        for _ in range(phase.steps):
            times += [clock + mark for mark in phase.marks]
            clock += phase.marks[-1]
        for m in phase.makes:
            after[len(jobs) - 1, m] = len(times)
    total = len(times)
    limit = [total] * len(order)
    for phase, begin in zip(phases, first):
        last = -1
        for i, (_, _, n, h) in enumerate(order):
            j, k = n
            if j == 0 and h == jobs[j].hops and jobs[j].cuts[k][0] in phase.needs:
                last = i
        for i in range(last + 1):
            limit[i] = min(limit[i], begin)
    waiting, active, done = {}, {}, {}
    now = 0.0

    def advance(key, until):
        nonlocal now
        while key not in done and now < until:
            for axis, queue in waiting.items():
                if queue and axis not in active:
                    active[axis] = queue.pop(0)
            far = any(axis[0] == "d" and axis[1] > 2 for axis in active)
            rates, span = {}, until - now
            for axis, (_, left) in active.items():
                halved = far and axis[0] == "d" and axis[1] > 1
                rates[axis] = CORE_RATE if axis == CORE else LINK_RATE / (2 if halved else 1)
                span = min(span, left / rates[axis])
            now += span
            for axis in list(active):
                active[axis][1] -= span * rates[axis]
                if active[axis][1] <= 1e-3:
                    done[active.pop(axis)[0]] = now + LATENCY

    slots = [[] for _ in range(total)]
    tail = []
    at, late = 0, 0.0
    for i, (_, _, n, h) in enumerate(order):
        j, k = n
        job = jobs[j]
        ready = now
        if h:
            advance((n, h - 1), math.inf)
            ready = max(ready, done[n, h - 1])
        else:
            at = max(at, after.get((j, job.cuts[k][0]), 0))
        while at < min(limit[i], total) and times[at] + late < ready - 0.3:
            at += 1
        if at < total:
            slots[at].append((n, h))
            late += max(ready - times[at] - late, 0.0)
            ready = max(ready, times[at] + late)
        else:
            tail.append((n, h))
        advance(None, ready)
        if h < job.hops:
            waiting.setdefault(job.routes[k][h], []).append([(n, h), float(job.sizes(k)[h])])
    return slots, tail


class Names:
    def __init__(self, names, refs):
        for name, ref in zip(names, refs):
            setattr(self, name, ref)


def carrying_kernel(phases, jobs, plan, names, *refs):
    spans, start = [], 0
    for count in [len(group) for group in names]:
        spans.append(refs[start : start + count])
        start += count
    given, landed, worked = [], [], []
    for kind, parts in ((given, 1), (landed, 3), (worked, 5)):
        rest = list(spans[parts])
        for job in jobs:
            count = (len(job.given), len(job.out_shape), len(job.scratch))[parts // 2]
            kind.append([rest.pop(0) for _ in range(count)])
    r = Names(names[0] + names[2] + names[4], spans[0] + spans[2] + spans[4])
    now = pl.program_id(0)
    slots, tail = plan
    place = Place(jobs[0].nd, jobs[0].nf)
    r.gathered = landed[0]
    for job, ins, outs, scratch in zip(jobs, given, landed, worked):
        job.bind(place, ins + [getattr(r, name) for name in job.made], outs, scratch)

    def run(items, opening=False):
        if opening:
            for job in jobs:
                job.start()
            place.barrier()
        for (j, k), h in items:
            jobs[j].step(k, h)

    base, begin = 0, 0
    for phase in phases:
        ticks = len(phase.marks)

        def one(phase=phase, base=base, begin=begin, ticks=ticks):
            passed = [0]

            def tick():
                t = passed[0]
                passed[0] += 1
                for s in range(phase.steps):
                    items = slots[base + s * ticks + t]
                    opening = base + s * ticks + t == 0
                    if items or opening:
                        pl.when(now == begin + s)(functools.partial(run, items, opening))

            phase.run(r, now - begin, tick)
            assert passed[0] == ticks

        pl.when((now >= begin) & (now < begin + phase.steps))(one)
        base += ticks * phase.steps
        begin += phase.steps
    if tail:
        pl.when(now == begin - 1)(functools.partial(run, tail))


def carry(phases, ins, outs, scratch, jobs, ident):
    plan = plan_steps(jobs, phases)
    given = [array for job in jobs for array in job.given]
    landed = [shape for job in jobs for shape in job.out_shape]
    worked = [item for job in jobs for item in job.scratch]
    names = (
        list(ins),
        [None] * len(given),
        list(outs),
        [None] * len(landed),
        list(scratch),
        [None] * len(worked),
    )
    results = pl.pallas_call(
        functools.partial(carrying_kernel, phases, jobs, plan, names),
        grid=(sum(phase.steps for phase in phases),),
        in_specs=[spec for _, spec in ins.values()] + [ANYWHERE] * len(given),
        out_specs=[spec for _, spec in outs.values()]
        + [spec for job in jobs for spec in job.out_specs],
        out_shape=[shape for shape, _ in outs.values()] + landed,
        scratch_shapes=list(scratch.values()) + worked,
        compiler_params=pltpu.CompilerParams(
            collective_id=ident, has_side_effects=True, vmem_limit_bytes=VMEM_LIMIT
        ),
    )(*[array for array, _ in ins.values()], *given)
    r = Names(list(outs), results)
    r.landed, rest = [], list(results[len(outs) :])
    for job in jobs:
        r.landed.append([rest.pop(0) for _ in job.out_shape])
    return r


def dot_nn(a, b):
    return lax.dot_general(a, b, (((1,), (0,)), ((), ())), preferred_element_type=jnp.float32)


def dot_nt(a, b):
    return lax.dot_general(a, b, (((1,), (1,)), ((), ())), preferred_element_type=jnp.float32)


def dot_tn(a, b):
    return lax.dot_general(a, b, (((0,), (0,)), ((), ())), preferred_element_type=jnp.float32)


def low(value):
    return value.astype(jnp.bfloat16)


def times(value, matrix):
    parts = [dot_nn(value, matrix[f]) for f in range(matrix.shape[0])]
    return parts[0] if len(parts) == 1 else jnp.concatenate(parts, axis=1)


def times_back(value, matrix):
    cols = matrix.shape[2]
    total = None
    for f in range(matrix.shape[0]):
        term = dot_nt(value[:, f * cols : (f + 1) * cols], matrix[f])
        total = term if total is None else total + term
    return total


def fixed(shape):
    return pl.BlockSpec(shape, lambda i: (0,) * len(shape))


def resident(array):
    zeros = (0,) * array.ndim
    return (array, pl.BlockSpec(array.shape, lambda i: zeros, pipeline_mode=pl.Buffered(1)))


def during(begin, steps, block, axis=0):
    def index(i):
        at = jnp.minimum(jnp.maximum(i - begin, 0), steps - 1)
        return tuple(at if d == axis else 0 for d in range(len(block)))

    return pl.BlockSpec(block, index)


def struct(shape, dtype):
    return jax.ShapeDtypeStruct(shape, dtype)


def rows_at(step, size):
    return pl.ds(pl.multiple_of(step * size, size), size)


def fetch(pairs, sems):
    copies = [
        pltpu.make_async_copy(source, target, sems.at[n])
        for n, (source, target) in enumerate(pairs)
    ]
    for copy in copies:
        copy.start()
    for copy in copies:
        copy.wait()


ROW_PAIRS = 2


def softmax(scores, axis):
    top = jnp.max(scores, axis=axis, keepdims=True)
    weight = jnp.exp(scores - top)
    return weight * (1.0 / jnp.sum(weight, axis=axis, keepdims=True))


def gelu_pair(x):
    scaled = jnp.abs(x) * (1.0 / math.sqrt(2.0))
    bell = jnp.exp(-0.5 * x * x)
    t = 1.0 / (1.0 + 0.3275911 * scaled)
    poly = t * (
        0.254829592
        + t * (-0.284496736 + t * (1.421413741 + t * (-1.453152027 + t * 1.061405429)))
    )
    tail = 0.5 * poly * bell
    below = jnp.where(x < 0, tail, 1.0 - tail)
    return x * below, below + x * bell * (1.0 / math.sqrt(2.0 * math.pi))


def row_mean(value):
    return jnp.mean(value, axis=-1, keepdims=True)


def col_sum(value):
    return jnp.sum(value, axis=0, keepdims=True)


def own_image(r, p):
    return r.owner[p]


def flat(ref):
    return ref.reshape(-1, ref.shape[-1])


def merged(ref, blocks, rows):
    return ref.reshape(blocks, rows, ref.shape[-1])


def put_half(out, half, x, d):
    cols = out.shape[-1]
    nf = bits_of(lax.axis_size("fsdp"))
    whole = low(dot_tn(x, d))
    for f in range(1 << nf):
        at = tuple((f >> b) % 2 for b in range(nf - 1, -1, -1))
        part = whole[:, f * cols : (f + 1) * cols]
        out[at + (half,)] = part.reshape(out.shape[nf + 1 :])


def project_keys_phase(r, step, tick):
    tick()

    @pl.when(step == 0)
    def _():
        targets = (r.w_tk, r.w_tv, r.w_iq)
        fetch([(g.reshape(w.shape), w) for g, w in zip(r.gathered, targets)], r.sems)
        images, real = r.states.shape[:2]
        r.image[...] = jnp.zeros_like(r.image)
        for i in range(images):
            r.image[i, :real, :] = r.states[i]
            r.region_counts[i] = lax.fori_loop(
                0, real, lambda k, total, i=i: total + r.mask[i, k], 0
            )
        r.image_rows[...] = r.image[...]
        r.iq[...] = low(times(flat(r.image[...]), r.w_iq)).reshape(r.iq.shape)

    here = rows_at(step, r.text.shape[0] // r.owner.shape[0] * ROW_PAIRS)
    rows = r.text[here, :]
    r.tk[here, :] = low(times(rows, r.w_tk))
    r.tv[here, :] = low(times(rows, r.w_tv))
    tick()


def attend_image_phase(r, step, tick):
    tick()
    regions, length = r.iprob.shape[1:]
    heads = r.tk.shape[1] // HDIM
    columns = [slice(h * HDIM, (h + 1) * HDIM) for h in range(heads)]
    scale = 1.0 / math.sqrt(HDIM)
    for q in range(ROW_PAIRS):
        p = step * ROW_PAIRS + q
        mine = own_image(r, p)
        here, rows_i = rows_at(p, length), rows_at(p, regions)
        kept = lax.broadcasted_iota(jnp.int32, (regions, length), 1) < r.lens[p]
        scores = [scale * dot_nt(r.iq[mine, :, at], r.tk[here, at]) for at in columns]
        probs = [softmax(jnp.where(kept, one, masked_score), 1) for one in scores]
        for h in range(heads):
            r.iprob[p * heads + h] = probs[h]
        parts = [low(dot_nn(low(one), r.tv[here, at])) for one, at in zip(probs, columns)]
        r.ictx[rows_i, :] = jnp.concatenate(parts, axis=1)
        tick()


def attend_text_phase(r, step, tick):
    tick()

    @pl.when(step == 0)
    def _():
        targets = (r.w_tq, r.w_ik, r.w_iv)
        fetch([(g.reshape(w.shape), w) for g, w in zip(r.gathered[7:], targets)], r.sems)
        rows = flat(r.image[...])
        for w, out in ((r.w_ik, r.ik), (r.w_iv, r.iv)):
            out[...] = low(times(rows, w)).reshape(out.shape)

    regions, length = r.tprob.shape[1:]
    heads = r.tq.shape[1] // HDIM
    columns = [slice(h * HDIM, (h + 1) * HDIM) for h in range(heads)]
    scale = 1.0 / math.sqrt(HDIM)
    r.tq[...] = low(times(r.text[rows_at(step, r.tq.shape[0]), :], r.w_tq))
    tick()
    for q in range(ROW_PAIRS):
        mine = own_image(r, step * ROW_PAIRS + q)
        here = slice(q * length, (q + 1) * length)
        row = lax.broadcasted_iota(jnp.int32, (regions, length), 0)
        kept = row < r.region_counts[mine]
        scores = [scale * dot_nt(r.ik[mine, :, at], r.tq[here, at]) for at in columns]
        probs = [softmax(jnp.where(kept, one, masked_score), 0) for one in scores]
        for h in range(heads):
            r.tprob[q * heads + h] = probs[h]
        parts = [low(dot_tn(low(one), r.iv[mine, :, at])) for one, at in zip(probs, columns)]
        r.tctx[here, :] = jnp.concatenate(parts, axis=1)
        tick()


def stream_rows(r, step, tick, limits, x, ctx, cot, norms, weights, keeps, outs):
    w_out, w_inner, w_outer = weights
    mid_ref, act_ref, hid_ref, ffn_ref, branch_ref = keeps
    out, dz_out, dctx_out, ngrad = outs
    rows = x.shape[0]
    group, real = cot.shape[:2]
    slots = rows // group

    def normalize(z):
        offset = z - row_mean(z)
        inv = lax.rsqrt(row_mean(offset * offset) + norm_eps)
        return offset * inv, inv

    def normalize_back(dy, xhat, inv, gain):
        dx = dy * gain
        return inv * (dx - row_mean(dx) - xhat * row_mean(dx * xhat))

    @pl.when(step == 0)
    def _():
        ngrad[...] = jnp.zeros_like(ngrad)
        if real < slots:
            r.cot_wide[...] = jnp.zeros_like(r.cot_wide)

    row = lax.broadcasted_iota(jnp.int32, (rows, 1), 0)
    kept = row < 0
    for q in range(group):
        inside = (row >= q * slots) & (row < q * slots + limits(step * group + q))
        kept = kept | inside
        if real < slots:
            r.cot_wide[q * slots : q * slots + real, :] = cot[q].astype(jnp.float32)
    kept = kept.astype(jnp.float32)
    first_hat, first_inv = normalize(x[...].astype(jnp.float32) + times(ctx[...], w_out))
    mid = first_hat * norms[0] + norms[1]
    mid_low = low(mid)
    mid_ref[...] = mid_low
    tick()
    cols = w_inner.shape[2]
    for f in range(w_inner.shape[0]):
        at = slice(f * cols, (f + 1) * cols)
        act, grad = gelu_pair(dot_nn(mid_low, w_inner[f]))
        act_ref[:, at] = low(act)
        hid_ref[:, at] = low(grad)
        tick()
    second_hat, second_inv = normalize(mid + times(act_ref[...], w_outer))
    result = low((second_hat * norms[2] + norms[3]) * kept)
    for q in range(group):
        out[q] = result[q * slots : q * slots + real]
    if real < slots:
        dy = r.cot_wide[...] * kept
    else:
        dy = cot[...].reshape(rows, -1).astype(jnp.float32) * kept
    second_dz = normalize_back(dy, second_hat, second_inv, norms[2])
    ffn_low = low(second_dz)
    ffn_ref[...] = ffn_low
    sums = [col_sum(dy * second_hat), col_sum(dy)]
    tick()
    hid_ref[...] = low(times_back(ffn_low, w_outer) * hid_ref[...].astype(jnp.float32))
    tick()
    mid_grad = second_dz + times_back(hid_ref[...], w_inner)
    first_dz = normalize_back(mid_grad, first_hat, first_inv, norms[0])
    dz_out[...] = first_dz
    branch_low = low(first_dz)
    branch_ref[...] = branch_low
    tick()
    dctx_out[...] = low(times_back(branch_low, w_out))
    sums = [col_sum(mid_grad * first_hat), col_sum(mid_grad)] + sums
    for n in range(4):
        ngrad[n : n + 1, :] += sums[n]
    tick()


def store_grad(out, x, d):
    cols = out.shape[2]
    whole = low(dot_tn(x, d))
    for f in range(out.shape[0]):
        out[f] = whole[:, f * cols : (f + 1) * cols]


def add_to(ref, mine, value):
    value = low(value).astype(jnp.float32)
    for i in range(ref.shape[0]):
        ref[i] += jnp.where(mine == i, value, 0.0)


def image_phase(first_col, norm_wide, r, step, tick):
    tick()
    group, slots, wide = r.cot.shape[0], r.image.shape[1], r.image.shape[2]

    @pl.when(step == 0)
    def _():
        targets = (r.w_io, r.w_ii, r.w_iu)
        fetch(
            [(g.reshape(w.shape), w) for g, w in zip(r.gathered[4:], targets)]
            + [(r.gathered[3], r.norm_parts)],
            r.sems,
        )
        parts = r.norm_parts.shape[0:-2]
        nf = bits_of(lax.axis_size("fsdp"))
        for i in range(math.prod(parts)):
            at, rest = [], i
            for _ in parts:
                at.append(rest % 2)
                rest //= 2
            at = at[::-1]
            f = sum(bit << k for k, bit in enumerate(reversed(at[:nf])))
            d = sum(bit << k for k, bit in enumerate(reversed(at[nf:])))
            first = (d * (1 << nf) + f) * norm_wide
            r.norms[:, first : first + norm_wide] = r.norm_parts[tuple(at)]

    for q in range(group):
        r.visual[q * slots : (q + 1) * slots, :] = r.image[own_image(r, step * group + q)]
    here = rows_at(step, group * slots)
    norms = [r.norms[n : n + 1, first_col : first_col + wide] for n in range(4)]
    stream_rows(
        r,
        step,
        tick,
        lambda p: r.region_counts[own_image(r, p)],
        r.visual,
        r.ictx.at[here],
        r.cot,
        norms,
        (r.w_io, r.w_ii, r.w_iu),
        [ref.at[here] for ref in (r.mid, r.act, r.hid, r.ffn, r.branch)],
        (r.image_out, r.image_dz, r.dctx.at[here], r.image_ngrad),
    )


def image_grads_phase(r, step, tick):
    tick()
    here = rows_at(step, r.g_io.shape[1])
    store_grad(r.g_io, r.ictx[:, here], r.branch[...])
    store_grad(r.g_ii, r.mid[:, here], r.hid[...])
    store_grad(r.g_iu, r.act[:, here], r.ffn[...])
    tick()


def back_image_phase(r, step, tick):
    tick()
    regions, length = r.iprob.shape[1:]
    heads = r.tk.shape[1] // HDIM
    columns = [slice(h * HDIM, (h + 1) * HDIM) for h in range(heads)]
    scale = 1.0 / math.sqrt(HDIM)

    @pl.when(step == 0)
    def _():
        r.diq_sum[...] = jnp.zeros_like(r.diq_sum)

    for q in range(ROW_PAIRS):
        p = step * ROW_PAIRS + q
        mine = own_image(r, p)
        here, rows_i = rows_at(p, length), rows_at(p, regions)
        local = slice(q * length, (q + 1) * length)
        dprobs = [dot_nt(r.dctx[rows_i, at], r.tv[here, at]) for at in columns]
        dvalues = [
            low(dot_tn(low(r.iprob[p * heads + h]), r.dctx[rows_i, at]))
            for h, at in enumerate(columns)
        ]
        dscores = []
        for h in range(heads):
            probs = r.iprob[p * heads + h]
            inner = jnp.sum(probs * dprobs[h], axis=1, keepdims=True)
            dscores.append(low(probs * (dprobs[h] - inner)))
        parts = [scale * dot_nn(one, r.tk[here, at]) for one, at in zip(dscores, columns)]
        add_to(r.diq_sum, mine, jnp.concatenate(parts, axis=1))
        dkeys = [
            low(scale * dot_tn(one, r.iq[mine, :, at])) for one, at in zip(dscores, columns)
        ]
        for ref, out, values in ((r.tv, r.dtv, dvalues), (r.tk, r.dtk, dkeys)):
            values = jnp.concatenate(values, axis=1)
            ref[here, :] = values
            out[local, :] = values
        tick()


def key_grads_phase(r, step, tick):
    tick()
    diq = low(r.diq_sum[...])
    r.diq[...] = diq
    here = rows_at(step, r.g_iq.shape[1])
    store_grad(r.g_iq, flat(r.image[:, :, here]), flat(diq))
    here = rows_at(step, r.g_tk.shape[1])
    store_grad(r.g_tk, r.text[:, here], r.tk[...])
    store_grad(r.g_tv, r.text[:, here], r.tv[...])
    tick()


def text_phase(r, step, tick):
    tick()
    rows = r.x.shape[0]
    here = rows_at(step, rows)
    norms = [r.norms[n : n + 1, : r.x.shape[1]] for n in range(4)]
    stream_rows(
        r,
        step,
        tick,
        lambda p: r.lens[p],
        r.x,
        r.tctx.at[here],
        r.cot,
        norms,
        (r.w_to, r.w_ti, r.w_tu),
        [ref.at[here] for ref in (r.mid, r.act, r.hid, r.ffn, r.branch)],
        (r.text_out, r.text_dz, r.dctx, r.text_ngrad),
    )


def grad_phase(out, x, d, r, step, tick):
    tick()
    out = getattr(r, out)
    here = rows_at(step, out.shape[1])
    store_grad(out, getattr(r, x)[:, here], getattr(r, d)[...])
    tick()


def back_text_phase(r, step, tick):
    tick()
    regions, length = r.tprob.shape[1:]
    heads = r.tq.shape[1] // HDIM
    columns = [slice(h * HDIM, (h + 1) * HDIM) for h in range(heads)]
    scale = 1.0 / math.sqrt(HDIM)

    @pl.when(step == 0)
    def _():
        r.dik_sum[...] = jnp.zeros_like(r.dik_sum)
        r.div_sum[...] = jnp.zeros_like(r.div_sum)

    for q in range(ROW_PAIRS):
        p = step * ROW_PAIRS + q
        mine = own_image(r, p)
        here = rows_at(p, length)
        local = slice(q * length, (q + 1) * length)
        dprobs = [dot_nt(r.iv[mine, :, at], r.dtc[local, at]) for at in columns]
        parts = [
            dot_nn(low(r.tprob[q * heads + h]), r.dtc[local, at]) for h, at in enumerate(columns)
        ]
        add_to(r.div_sum, mine, jnp.concatenate(parts, axis=1))
        dscores = []
        for h in range(heads):
            probs = r.tprob[q * heads + h]
            inner = jnp.sum(probs * dprobs[h], axis=0, keepdims=True)
            dscores.append(low(probs * (dprobs[h] - inner)))
        parts = [scale * dot_nn(one, r.tq[local, at]) for one, at in zip(dscores, columns)]
        add_to(r.dik_sum, mine, jnp.concatenate(parts, axis=1))
        parts = [
            low(scale * dot_tn(one, r.ik[mine, :, at])) for one, at in zip(dscores, columns)
        ]
        r.dtq[here, :] = jnp.concatenate(parts, axis=1)
        tick()


def query_grads_phase(r, step, tick):
    tick()
    here = rows_at(step, r.text.shape[1] // 2)
    put_half(r.g_tq, step, r.text[:, here], r.dtq[...])
    dik, div = low(r.dik_sum[...]), low(r.div_sum[...])
    r.dik[...] = dik
    r.div[...] = div
    here = rows_at(step, r.image.shape[2] // 2)
    columns = flat(r.image[:, :, here])
    put_half(r.g_ik, step, columns, flat(dik))
    put_half(r.g_iv, step, columns, flat(div))
    tick()


def data_grads_phase(r, step, tick):
    images, real = r.image_grad.shape[:2]
    pairs = r.owner.shape[0]
    slots = r.image_dz.shape[0] // pairs
    tick()

    @pl.when(step == 0)
    def _():
        for i in range(images):
            total = jnp.zeros((slots, r.image_dz.shape[1]), jnp.float32)
            for p in range(pairs):
                rows = r.image_dz[p * slots : (p + 1) * slots, :]
                total += jnp.where(own_image(r, p) == i, rows, 0.0)
            for d, w in ((r.diq, r.w_iq), (r.dik, r.w_ik), (r.div, r.w_iv)):
                total = total + times_back(d[i], w)
            r.image_grad[i] = total[:real]

    total = r.text_dz[...]
    here = rows_at(step, total.shape[0])
    for d, w in ((r.dtq.at[here], r.w_tq), (r.dtk, r.w_tk), (r.dtv, r.w_tv)):
        total = total + times_back(d[...], w)
        tick()
    r.text_grad[...] = total


def pass_kernel(count, *refs):
    for source, target in zip(refs[:count], refs[count:]):
        target[...] = source[...]


def pass_on(arrays):
    return pl.pallas_call(
        functools.partial(pass_kernel, len(arrays)),
        out_shape=[struct(a.shape, a.dtype) for a in arrays],
        in_specs=[WHOLE] * len(arrays),
        out_specs=[WHOLE] * len(arrays),
        compiler_params=pltpu.CompilerParams(vmem_limit_bytes=VMEM_LIMIT),
    )(*arrays)


def whole_weight(shard, block):
    nd, nf = mesh_bits()
    rows, cols = shard.shape
    block = block.reshape(1 << nf, rows << nd, cols)
    if cols % 128:
        block = jnp.swapaxes(block, 0, 1).reshape(1, rows << nd, cols << nf)
    return block


def device_blocks(grad, shard):
    nd, nf = mesh_bits()
    rows, cols = shard.shape
    if cols % 128:
        grad = jnp.swapaxes(grad.reshape(rows << nd, 1 << nf, cols), 0, 1)
    return grad.reshape((2,) * (nd + nf) + (rows, cols))


def norm_blocks(rows):
    nd, nf = mesh_bits()
    wide = rows.shape[1] >> (nd + nf)
    split = rows.reshape(4, 1 << nd, 1 << nf, wide).transpose(2, 1, 0, 3)
    split = jnp.pad(split, ((0, 0), (0, 0), (0, 4), (0, 128 - wide)))
    return split.reshape((2,) * (nd + nf) + (8, 128))


def body(
    text_states,
    image_states,
    text_lengths,
    region_mask,
    group_ids,
    image_query,
    image_key,
    image_value,
    text_query,
    text_key,
    text_value,
    image_output,
    text_output,
    image_inner,
    image_outer,
    text_inner,
    text_outer,
    norm_params,
    cot_text,
    cot_image,
):
    nd, nf = mesh_bits()
    lead = (2,) * (nd + nf)
    bf, f32 = jnp.bfloat16, jnp.float32
    pairs, length, width_text = text_states.shape
    images, regions, width_image = image_states.shape
    padded = -(-regions // 16) * 16
    wide = image_query.shape[1] << nf
    heads = wide // HDIM
    rows_text, rows_image = pairs * length, pairs * padded
    norm_wide = norm_params.shape[1]
    device = lax.axis_index("dp") * lax.axis_size("fsdp") + lax.axis_index("fsdp")
    owner = group_ids - device * images
    text = text_states.reshape(rows_text, width_text)
    def full(shard):
        rows, cols = shard.shape
        return pltpu.VMEM((1 << nf, rows << nd, cols), bf)

    def vmem(rows, cols, dtype=bf):
        return pltpu.VMEM((rows, cols), dtype)

    n = ROW_PAIRS
    steps = pairs // n
    group = pairs // 2
    block_i = group * padded
    gather = Gather(
        [text_key, text_value, image_query, norm_params, image_output, image_inner, image_outer]
        + [text_query, image_key, image_value, text_output, text_inner, text_outer]
    )
    phases, begin = [], [0]

    def phase(run, count, marks, **kw):
        phases.append(Phase(run, count, marks, **kw))
        begin.append(begin[-1] + count)
        return begin[-2]

    phase(project_keys_phase, steps, (0.0, 1.4), needs=range(3))
    phase(attend_image_phase, steps, (0.0, 1.9, 3.8))
    stages = 1 << nf
    marks = [0.0, 1.2] + [1.2 + 1.2 * (k + 1) / stages for k in range(stages)]
    marks += [4.0, 5.3, 6.8, 7.6]
    at_image = phase(
        functools.partial(image_phase, width_text, norm_wide), 2, marks, needs=range(3, 7)
    )
    at_image_grads = phase(image_grads_phase, 2, (0.0, 4.2))
    at_back = phase(back_image_phase, steps, (0.0, 2.3, 4.6))
    at_grads = phase(key_grads_phase, 2, (0.0, 4.2))
    at_attend = phase(attend_text_phase, steps, (0.0, 0.8, 2.8, 4.8), needs=range(7, 10))
    third = width_text // 3

    def grad_out(weight_shard, inner, first, count, size):
        shape = (1 << nf, inner, weight_shard.shape[1])
        if weight_shard.shape[1] % 128:
            shape = (1, inner, weight_shard.shape[1] << nf)
        block = (shape[0], size, shape[2])
        return (struct(shape, bf), during(first, count, block, 1))

    by_pair = during(at_image, 2, (group, regions, width_image))
    probs = during(at_attend, steps, (n * heads, padded, length))
    pair_rows = during(at_attend, steps, (n * length, wide))
    back_rows = during(at_back, steps, (n * length, wide))
    image_shape = (images, padded, wide)
    a = carry(
        phases,
        dict(
            lens=(text_lengths, SCALARS),
            owner=(owner, SCALARS),
            mask=(region_mask, SCALARS),
            text=resident(text),
            states=resident(image_states),
            cot=(cot_image, by_pair),
        ),
        dict(
            ik=(struct(image_shape, bf), fixed(image_shape)),
            iv=(struct(image_shape, bf), fixed(image_shape)),
            tq=(struct((rows_text, wide), bf), pair_rows),
            tprob=(struct((pairs * heads, padded, length), f32), probs),
            tctx=(struct((rows_text, wide), bf), pair_rows),
            image_rows=(
                struct((images, padded, width_image), bf),
                fixed((images, padded, width_image)),
            ),
            norms=(struct((4, norm_wide << (nd + nf)), f32), fixed((4, norm_wide << (nd + nf)))),
            image_out=(struct(cot_image.shape, bf), by_pair),
            image_dz=(
                struct((rows_image, width_image), f32),
                during(at_image, 2, (block_i, width_image)),
            ),
            image_ngrad=(struct((4, width_image), f32), fixed((4, width_image))),
            dtk=(struct((rows_text, wide), bf), back_rows),
            dtv=(struct((rows_text, wide), bf), back_rows),
            diq=(struct(image_shape, bf), fixed(image_shape)),
            g_io=grad_out(image_output, wide, at_image_grads, 2, wide // 2),
            g_ii=grad_out(image_inner, width_image, at_image_grads, 2, width_image // 2),
            g_iu=grad_out(image_outer, width_image, at_image_grads, 2, width_image // 2),
            g_iq=grad_out(image_query, width_image, at_grads, 2, width_image // 2),
            g_tk=grad_out(text_key, width_text, at_grads, 2, width_text // 2),
            g_tv=grad_out(text_value, width_text, at_grads, 2, width_text // 2),
        ),
        dict(
            w_tq=full(text_query),
            w_tk=full(text_key),
            w_tv=full(text_value),
            w_iq=full(image_query),
            w_ik=full(image_key),
            w_iv=full(image_value),
            w_io=full(image_output),
            w_ii=full(image_inner),
            w_iu=full(image_outer),
            image=pltpu.VMEM((images, padded, width_image), bf),
            visual=vmem(block_i, width_image),
            region_counts=pltpu.SMEM((images,), jnp.int32),
            norm_parts=pltpu.VMEM(lead + norm_params.shape, f32),
            sems=pltpu.SemaphoreType.DMA((4,)),
            iq=pltpu.VMEM(image_shape, bf),
            tk=vmem(rows_text, wide),
            tv=vmem(rows_text, wide),
            iprob=pltpu.VMEM((pairs * heads, padded, length), f32),
            ictx=vmem(rows_image, wide),
            mid=vmem(rows_image, width_image),
            act=vmem(rows_image, width_image),
            hid=vmem(rows_image, width_image),
            ffn=vmem(rows_image, width_image),
            branch=vmem(rows_image, width_image),
            dctx=vmem(rows_image, wide),
            diq_sum=pltpu.VMEM(image_shape, f32),
            cot_wide=vmem(block_i, width_image, f32),
        ),
        [gather],
        0,
    )
    whole = [whole_weight(s, g) for s, g in zip(gather.given, a.landed[0]) if s is not norm_params]
    w_tk, w_tv, w_iq, _, _, _, w_tq, w_ik, w_iv, w_to, w_ti, w_tu = whole

    job = Reduce(
        [
            device_blocks(grad, shard)
            for grad, shard in (
                (a.g_io, image_output),
                (a.g_ii, image_inner),
                (a.g_iu, image_outer),
                (a.g_iq, image_query),
                (a.g_tk, text_key),
                (a.g_tv, text_value),
            )
        ]
    )
    phases, begin = [], [0]
    inner = w_ti.shape[0] * w_ti.shape[2]
    block_t = n * length
    stages = w_ti.shape[0]
    marks = [0.0, 1.8] + [1.8 + 4.8 * (k + 1) / stages for k in range(stages)]
    marks += [9.2, 11.2, 13.4, 14.2]
    at_text = phase(text_phase, steps, marks)
    at_tu = phase(functools.partial(grad_phase, "g_tu", "act", "ffn"), 6, (0.0, 1.4))
    at_ti = phase(functools.partial(grad_phase, "g_ti", "mid", "hid"), 6, (0.0, 1.4))
    at_to = phase(functools.partial(grad_phase, "g_to", "tctx", "branch"), 2, (0.0, 1.6))
    by_pair = during(at_text, steps, (n, length, width_text))

    def text_rows(cols):
        return during(at_text, steps, (block_t, cols))

    b = carry(
        phases,
        dict(
            lens=(text_lengths, SCALARS),
            x=(text, text_rows(width_text)),
            tctx=resident(a.tctx),
            cot=(cot_text, by_pair),
            norms=resident(a.norms),
            w_to=resident(w_to),
            w_ti=resident(w_ti),
            w_tu=resident(w_tu),
        ),
        dict(
            text_out=(struct(cot_text.shape, bf), by_pair),
            text_dz=(struct((rows_text, width_text), f32), text_rows(width_text)),
            dctx=(struct((rows_text, wide), bf), text_rows(wide)),
            text_ngrad=(struct((4, width_text), f32), fixed((4, width_text))),
            g_tu=grad_out(text_outer, inner, at_tu, 6, inner // 6),
            g_ti=grad_out(text_inner, width_text, at_ti, 6, width_text // 6),
            g_to=grad_out(text_output, wide, at_to, 2, wide // 2),
        ),
        dict(
            mid=vmem(rows_text, width_text),
            act=vmem(rows_text, inner),
            hid=vmem(rows_text, inner),
            ffn=vmem(rows_text, width_text),
            branch=vmem(rows_text, width_text),
        ),
        [job],
        1,
    )
    o_io, o_ii, o_iu, o_iq, o_tk, o_tv = b.landed[0]

    norm_rows = norm_blocks(jnp.concatenate([b.text_ngrad, a.image_ngrad], axis=1))
    job = Reduce(
        [
            device_blocks(b.g_tu, text_outer),
            device_blocks(b.g_ti, text_inner),
            device_blocks(b.g_to, text_output),
            norm_rows,
        ],
        dict(
            g_tq=struct(lead + text_query.shape, bf),
            g_ik=struct(lead + image_key.shape, bf),
            g_iv=struct(lead + image_value.shape, bf),
        ),
    )
    phases, begin = [], [0]
    at_back = phase(back_text_phase, steps, (0.0, 2.3, 4.6))
    phase(query_grads_phase, 2, (0.0, 3.2), makes=range(4, 7))
    at_data = phase(data_grads_phase, steps, (0.0, 1.0, 2.2, 3.6))
    probs = during(at_back, steps, (n * heads, padded, length))
    back_rows = during(at_back, steps, (n * length, wide))
    data_rows = during(at_data, steps, (block_t, wide))
    data_out = during(at_data, steps, (block_t, width_text))
    c = carry(
        phases,
        dict(
            owner=(owner, SCALARS),
            ik=resident(a.ik),
            iv=resident(a.iv),
            tq=(a.tq, back_rows),
            tprob=(a.tprob, probs),
            dtc=(b.dctx, back_rows),
            text=resident(text),
            image=resident(a.image_rows),
            text_dz=(b.text_dz, data_out),
            dtk=(a.dtk, data_rows),
            dtv=(a.dtv, data_rows),
            image_dz=resident(a.image_dz),
            diq=resident(a.diq),
            w_tq=resident(w_tq),
            w_tk=resident(w_tk),
            w_tv=resident(w_tv),
            w_iq=resident(w_iq),
            w_ik=resident(w_ik),
            w_iv=resident(w_iv),
        ),
        dict(
            text_grad=(struct((rows_text, width_text), f32), data_out),
            image_grad=(struct(image_states.shape, f32), fixed(image_states.shape)),
        ),
        dict(
            dtq=vmem(rows_text, wide),
            dik=pltpu.VMEM(image_shape, bf),
            div=pltpu.VMEM(image_shape, bf),
            dik_sum=pltpu.VMEM(image_shape, f32),
            div_sum=pltpu.VMEM(image_shape, f32),
            g_tq=pltpu.VMEM(lead + text_query.shape, bf),
            g_ik=pltpu.VMEM(lead + image_key.shape, bf),
            g_iv=pltpu.VMEM(lead + image_value.shape, bf),
        ),
        [job],
        2,
    )
    o_tu, o_ti, o_to, o_norm, o_tq, o_ik, o_iv = c.landed[0]
    owned = pass_on([o_iq, o_ik, o_iv, o_tq, o_tk, o_tv, o_io, o_to, o_ii, o_iu, o_ti, o_tu])
    return (
        b.text_out,
        a.image_out,
        c.text_grad.reshape(text_states.shape),
        c.image_grad,
        *owned,
        o_norm[:4, :norm_wide],
    )


def solution(mesh):
    placed = (
        P(("dp", "fsdp"), None, None),
        P(("dp", "fsdp"), None, None),
        P(("dp", "fsdp")),
        P(("dp", "fsdp"), None),
        P(("dp", "fsdp")),
        P("dp", "fsdp"),
        P("dp", "fsdp"),
        P("dp", "fsdp"),
        P("dp", "fsdp"),
        P("dp", "fsdp"),
        P("dp", "fsdp"),
        P("dp", "fsdp"),
        P("dp", "fsdp"),
        P("dp", "fsdp"),
        P("dp", "fsdp"),
        P("dp", "fsdp"),
        P("dp", "fsdp"),
        P(None, ("dp", "fsdp")),
        P(("dp", "fsdp"), None, None),
        P(("dp", "fsdp"), None, None),
    )
    return jax.shard_map(
        body,
        mesh=mesh,
        in_specs=placed,
        out_specs=(
            P(("dp", "fsdp"), None, None),
            P(("dp", "fsdp"), None, None),
            P(("dp", "fsdp"), None, None),
            P(("dp", "fsdp"), None, None),
            P("dp", "fsdp"),
            P("dp", "fsdp"),
            P("dp", "fsdp"),
            P("dp", "fsdp"),
            P("dp", "fsdp"),
            P("dp", "fsdp"),
            P("dp", "fsdp"),
            P("dp", "fsdp"),
            P("dp", "fsdp"),
            P("dp", "fsdp"),
            P("dp", "fsdp"),
            P("dp", "fsdp"),
            P(None, ("dp", "fsdp")),
        ),
        check_vma=False,
    )
```

```python
import functools
import math

import jax
import jax.numpy as jnp
from jax import lax
from jax.experimental import pallas as pl
from jax.experimental.pallas import tpu as pltpu
from jax.sharding import PartitionSpec as P

HDIM = 128

norm_eps = 1e-12
masked_score = -1e30

MESH_IDS = pl.DeviceIdType.MESH
VMEM_LIMIT = 63 * 1024 * 1024
WHOLE = pl.BlockSpec(memory_space=pltpu.VMEM)
SCALARS = pl.BlockSpec(memory_space=pltpu.SMEM)
ANYWHERE = pl.BlockSpec(memory_space=pl.ANY)
CORE = ("d", 0)


def bits_of(size):
    count = size.bit_length() - 1
    assert 1 << count == size
    return count


def mesh_bits():
    return bits_of(lax.axis_size("dp")), bits_of(lax.axis_size("fsdp"))


def hop_orders(nd, nf):
    high = [("d", b) for b in range(nd - 1, 2, -1)]
    low = [("d", 2)]
    near = [("d", 1)]
    wide = [("f", b) for b in range(nf)]
    return (low + near + high + wide, high + wide + low + near)


def cut_pieces(shapes):
    pieces, waves, large = [], [], 0
    for m, (rows, cols) in enumerate(shapes):
        count = 4 if rows * cols > 40000 else 2
        if rows % (16 * count) == 0:
            each = rows // count
            cuts = [(k * each, each, 0, cols) for k in range(count)]
        elif cols % (128 * count) == 0 and rows % 8 == 0:
            each = cols // count
            cuts = [(0, rows, k * each, each) for k in range(count)]
        else:
            cuts = [(0, rows, 0, cols)]
        for cut in cuts:
            pieces.append((m, *cut, large % 2))
            small = rows * cols < 2048
            waves.append(0 if small else large // 4)
            large += 0 if small else 1
    return pieces, waves


class Place:
    def __init__(self, nd, nf):
        self.d = lax.axis_index("dp")
        self.f = lax.axis_index("fsdp")
        self.axes = [("f", b) for b in range(nf - 1, -1, -1)] + [
            ("d", b) for b in range(nd - 1, -1, -1)
        ]

    def bit(self, axis):
        value = self.f if axis[0] == "f" else self.d
        return lax.rem(value // (1 << axis[1]), 2)

    def partner(self, axis):
        step = (1 << axis[1]) * (1 - 2 * self.bit(axis))
        if axis[0] == "f":
            return (self.d, self.f + step)
        return (self.d + step, self.f)

    def index(self, whole, flip=None):
        picked = []
        for axis in self.axes:
            if axis in whole:
                picked.append(slice(None))
            elif axis == flip:
                picked.append(1 - self.bit(axis))
            else:
                picked.append(self.bit(axis))
        return tuple(picked)

    def barrier(self):
        sem = pltpu.get_barrier_semaphore()
        for axis in self.axes:
            pl.semaphore_signal(
                sem, inc=1, device_id=self.partner(axis), device_id_type=MESH_IDS
            )
        pl.semaphore_wait(sem, len(self.axes))


class Gather:
    def __init__(self, arrays):
        self.arrays = arrays
        self.given = arrays
        self.made = []
        self.nd, self.nf = mesh_bits()
        orders = hop_orders(self.nd, self.nf)
        self.cuts, self.waves = cut_pieces([a.shape for a in arrays])
        self.routes = [tuple(orders[cut[-1]]) + (CORE,) for cut in self.cuts]
        self.hops = self.nd + self.nf
        lead = (2,) * self.hops
        self.out_shape = [jax.ShapeDtypeStruct(lead + a.shape, a.dtype) for a in arrays]
        self.out_specs = [ANYWHERE] * len(arrays)
        count = len(self.cuts)
        self.scratch = [
            pltpu.SemaphoreType.DMA((count,)),
            pltpu.SemaphoreType.DMA((count, self.hops)),
            pltpu.SemaphoreType.DMA((count, self.hops)),
        ]

    def sizes(self, k):
        m, row, rows, col, cols, _ = self.cuts[k]
        block = rows * cols * self.arrays[m].dtype.itemsize
        return [block << h for h in range(self.hops)]

    def window(self, k):
        m, row, rows, col, cols, _ = self.cuts[k]
        return (pl.ds(row, rows), pl.ds(col, cols))

    def bind(self, place, ins, outs, scratch):
        self.place, self.ins, self.outs = place, ins, outs
        self.local_sem, self.send_sem, self.recv_sem = scratch

    def local(self, k):
        m = self.cuts[k][0]
        return pltpu.make_async_copy(
            self.ins[m].at[self.window(k)],
            self.outs[m].at[self.place.index(()) + self.window(k)],
            self.local_sem.at[k],
        )

    def hop(self, k, h):
        m, route = self.cuts[k][0], self.routes[k]
        region = self.outs[m].at[self.place.index(route[:h]) + self.window(k)]
        return pltpu.make_async_remote_copy(
            src_ref=region,
            dst_ref=region,
            send_sem=self.send_sem.at[k, h],
            recv_sem=self.recv_sem.at[k, h],
            device_id=self.place.partner(route[h]),
            device_id_type=MESH_IDS,
        )

    def start(self):
        for k in range(len(self.cuts)):
            self.local(k).start()

    def step(self, k, h):
        if h == 0:
            self.local(k).wait()
        else:
            self.hop(k, h - 1).wait_recv()
        if h < self.hops:
            self.hop(k, h).start()
        else:
            for g in range(self.hops):
                self.hop(k, g).wait_send()


def add_blocks(acc, index, window, incoming):
    lead = incoming.shape[:-2]
    outer, inner = lead[:-2], lead[-2:]

    def one(i, carry):
        first = []
        for size in reversed(outer):
            first.append(lax.rem(i, size))
            i = i // size
        first = first[::-1]
        for j in range(math.prod(inner)):
            at, rest = [], j
            for size in reversed(inner):
                at.append(rest % size)
                rest //= size
            at = tuple(first + at[::-1])
            left = list(at)
            where = tuple(left.pop(0) if isinstance(p, slice) else p for p in index) + window
            acc[where] = acc[where] + incoming[at]
        return carry

    lax.fori_loop(0, math.prod(outer), one, 0)


class Reduce:
    def __init__(self, given, made=None):
        made = made or {}
        self.given = given
        self.made = list(made)
        arrays = list(given) + list(made.values())
        self.arrays = arrays
        self.nd, self.nf = mesh_bits()
        orders = hop_orders(self.nd, self.nf)
        self.hops = self.nd + self.nf
        self.cuts, self.waves = cut_pieces([a.shape[-2:] for a in arrays])
        self.routes = [(CORE,) + tuple(reversed(orders[cut[-1]])) for cut in self.cuts]
        self.scratch = []
        for m, row, rows, col, cols, _ in self.cuts:
            for h in range(-1 if m < len(self.given) else 0, self.hops):
                free = self.hops - 1 - max(h, 0)
                self.scratch.append(pltpu.VMEM((2,) * free + (rows, cols), arrays[m].dtype))
        count = len(self.cuts)
        self.scratch += [
            pltpu.SemaphoreType.DMA((count,)),
            pltpu.SemaphoreType.DMA((count, self.hops)),
            pltpu.SemaphoreType.DMA((count, self.hops)),
        ]
        shapes = [a.shape[-2:] for a in arrays]
        self.out_shape = [jax.ShapeDtypeStruct(s, jnp.float32) for s in shapes]
        self.out_specs = [pl.BlockSpec(s, lambda *_: (0, 0)) for s in shapes]

    def sizes(self, k):
        m, row, rows, col, cols, _ = self.cuts[k]
        block = rows * cols * self.arrays[m].dtype.itemsize
        return [block << (self.hops - 1 - h) for h in range(self.hops)]

    def window(self, k):
        m, row, rows, col, cols, _ = self.cuts[k]
        return (pl.ds(row, rows), pl.ds(col, cols))

    def bind(self, place, ins, outs, scratch):
        self.place, self.ins, self.outs = place, ins, outs
        self.local_sem, self.send_sem, self.recv_sem = scratch[-3:]
        rest = list(scratch[:-3])
        self.accs, self.temps = [], []
        for m, *_ in self.cuts:
            self.accs.append(rest.pop(0) if m < len(self.given) else None)
            self.temps.append([rest.pop(0) for _ in range(self.hops)])
        self.rest = [axis for axis in place.axes if axis != CORE]

    def local(self, k):
        source = self.ins[self.cuts[k][0]].at[self.place.index(self.rest) + self.window(k)]
        return pltpu.make_async_copy(source, self.accs[k], self.local_sem.at[k])

    def within(self, k, h, flip=None):
        full = self.place.index(self.routes[k][h + 1 :], flip)
        if self.accs[k] is None:
            m, row, rows, col, cols, _ = self.cuts[k]
            return self.ins[m], full, (slice(row, row + rows), slice(col, col + cols))
        return self.accs[k], tuple(p for p, a in zip(full, self.place.axes) if a != CORE), ()

    def hop(self, k, h):
        m, route = self.cuts[k][0], self.routes[k]
        if h == 0:
            region = self.ins[m].at[self.place.index(route[1:], CORE) + self.window(k)]
        else:
            acc, index, window = self.within(k, h, route[h])
            region = acc.at[index + window]
        return pltpu.make_async_remote_copy(
            src_ref=region,
            dst_ref=self.temps[k][h],
            send_sem=self.send_sem.at[k, h],
            recv_sem=self.recv_sem.at[k, h],
            device_id=self.place.partner(route[h]),
            device_id_type=MESH_IDS,
        )

    def start(self):
        pass

    def step(self, k, h):
        own = self.accs[k] is not None
        if h == 0 and own:
            self.local(k).start()
        if h > 0:
            self.hop(k, h - 1).wait_recv()
            if h == 1 and own:
                self.local(k).wait()
            acc, index, window = self.within(k, h - 1)
            if h < self.hops:
                add_blocks(acc, index, window, self.temps[k][h - 1])
            else:
                m, row, rows, col, cols, _ = self.cuts[k]
                last = acc[index + window].astype(jnp.float32)
                last = last + self.temps[k][h - 1][...].astype(jnp.float32)
                self.outs[m][row : row + rows, col : col + cols] = last
        if h < self.hops:
            self.hop(k, h).start()
        else:
            for g in range(self.hops):
                self.hop(k, g).wait_send()


LINK_RATE = 46e3
CORE_RATE = 380e3
LATENCY = 2.5


class Phase:
    def __init__(self, run, steps, marks, needs=(), makes=()):
        self.run, self.steps, self.marks = run, steps, marks
        self.needs, self.makes = set(needs), set(makes)


def plan_steps(jobs, phases):
    order = []
    for j, job in enumerate(jobs):
        order += sorted(
            (wave + h, wave, (j, k), h)
            for k, wave in enumerate(job.waves)
            for h in range(job.hops + 1)
        )
    times, first, after = [], [], {}
    clock = 0.0
    for phase in phases:
        first.append(len(times))
        for _ in range(phase.steps):
            times += [clock + mark for mark in phase.marks]
            clock += phase.marks[-1]
        for m in phase.makes:
            after[len(jobs) - 1, m] = len(times)
    total = len(times)
    limit = [total] * len(order)
    for phase, begin in zip(phases, first):
        last = -1
        for i, (_, _, n, h) in enumerate(order):
            j, k = n
            if j == 0 and h == jobs[j].hops and jobs[j].cuts[k][0] in phase.needs:
                last = i
        for i in range(last + 1):
            limit[i] = min(limit[i], begin)
    waiting, active, done = {}, {}, {}
    now = 0.0

    def advance(key, until):
        nonlocal now
        while key not in done and now < until:
            for axis, queue in waiting.items():
                if queue and axis not in active:
                    active[axis] = queue.pop(0)
            far = any(axis[0] == "d" and axis[1] > 2 for axis in active)
            rates, span = {}, until - now
            for axis, (_, left) in active.items():
                halved = far and axis[0] == "d" and axis[1] > 1
                rates[axis] = CORE_RATE if axis == CORE else LINK_RATE / (2 if halved else 1)
                span = min(span, left / rates[axis])
            now += span
            for axis in list(active):
                active[axis][1] -= span * rates[axis]
                if active[axis][1] <= 1e-3:
                    done[active.pop(axis)[0]] = now + LATENCY

    slots = [[] for _ in range(total)]
    tail = []
    at, late = 0, 0.0
    for i, (_, _, n, h) in enumerate(order):
        j, k = n
        job = jobs[j]
        ready = now
        if h:
            advance((n, h - 1), math.inf)
            ready = max(ready, done[n, h - 1])
        else:
            at = max(at, after.get((j, job.cuts[k][0]), 0))
        while at < min(limit[i], total) and times[at] + late < ready - 0.3:
            at += 1
        if at < total:
            slots[at].append((n, h))
            late += max(ready - times[at] - late, 0.0)
            ready = max(ready, times[at] + late)
        else:
            tail.append((n, h))
        advance(None, ready)
        if h < job.hops:
            waiting.setdefault(job.routes[k][h], []).append([(n, h), float(job.sizes(k)[h])])
    return slots, tail


class Names:
    def __init__(self, names, refs):
        for name, ref in zip(names, refs):
            setattr(self, name, ref)


def carrying_kernel(phases, jobs, plan, names, *refs):
    spans, start = [], 0
    for count in [len(group) for group in names]:
        spans.append(refs[start : start + count])
        start += count
    given, landed, worked = [], [], []
    for kind, parts in ((given, 1), (landed, 3), (worked, 5)):
        rest = list(spans[parts])
        for job in jobs:
            count = (len(job.given), len(job.out_shape), len(job.scratch))[parts // 2]
            kind.append([rest.pop(0) for _ in range(count)])
    r = Names(names[0] + names[2] + names[4], spans[0] + spans[2] + spans[4])
    now = pl.program_id(0)
    slots, tail = plan
    place = Place(jobs[0].nd, jobs[0].nf)
    r.gathered = landed[0]
    for job, ins, outs, scratch in zip(jobs, given, landed, worked):
        job.bind(place, ins + [getattr(r, name) for name in job.made], outs, scratch)

    def run(items, opening=False):
        if opening:
            for job in jobs:
                job.start()
            place.barrier()
        for (j, k), h in items:
            jobs[j].step(k, h)

    base, begin = 0, 0
    for phase in phases:
        ticks = len(phase.marks)

        def one(phase=phase, base=base, begin=begin, ticks=ticks):
            passed = [0]

            def tick():
                t = passed[0]
                passed[0] += 1
                for s in range(phase.steps):
                    items = slots[base + s * ticks + t]
                    opening = base + s * ticks + t == 0
                    if items or opening:
                        pl.when(now == begin + s)(functools.partial(run, items, opening))

            phase.run(r, now - begin, tick)
            assert passed[0] == ticks

        pl.when((now >= begin) & (now < begin + phase.steps))(one)
        base += ticks * phase.steps
        begin += phase.steps
    if tail:
        pl.when(now == begin - 1)(functools.partial(run, tail))


def carry(phases, ins, outs, scratch, jobs, ident):
    plan = plan_steps(jobs, phases)
    given = [array for job in jobs for array in job.given]
    landed = [shape for job in jobs for shape in job.out_shape]
    worked = [item for job in jobs for item in job.scratch]
    names = (
        list(ins),
        [None] * len(given),
        list(outs),
        [None] * len(landed),
        list(scratch),
        [None] * len(worked),
    )
    results = pl.pallas_call(
        functools.partial(carrying_kernel, phases, jobs, plan, names),
        grid=(sum(phase.steps for phase in phases),),
        in_specs=[spec for _, spec in ins.values()] + [ANYWHERE] * len(given),
        out_specs=[spec for _, spec in outs.values()]
        + [spec for job in jobs for spec in job.out_specs],
        out_shape=[shape for shape, _ in outs.values()] + landed,
        scratch_shapes=list(scratch.values()) + worked,
        compiler_params=pltpu.CompilerParams(
            collective_id=ident, has_side_effects=True, vmem_limit_bytes=VMEM_LIMIT
        ),
    )(*[array for array, _ in ins.values()], *given)
    r = Names(list(outs), results)
    r.landed, rest = [], list(results[len(outs) :])
    for job in jobs:
        r.landed.append([rest.pop(0) for _ in job.out_shape])
    return r


def dot_nn(a, b):
    return lax.dot_general(a, b, (((1,), (0,)), ((), ())), preferred_element_type=jnp.float32)


def dot_nt(a, b):
    return lax.dot_general(a, b, (((1,), (1,)), ((), ())), preferred_element_type=jnp.float32)


def dot_tn(a, b):
    return lax.dot_general(a, b, (((0,), (0,)), ((), ())), preferred_element_type=jnp.float32)


def low(value):
    return value.astype(jnp.bfloat16)


def times(value, matrix):
    parts = [dot_nn(value, matrix[f]) for f in range(matrix.shape[0])]
    return parts[0] if len(parts) == 1 else jnp.concatenate(parts, axis=1)


def times_back(value, matrix):
    cols = matrix.shape[2]
    total = None
    for f in range(matrix.shape[0]):
        term = dot_nt(value[:, f * cols : (f + 1) * cols], matrix[f])
        total = term if total is None else total + term
    return total


def fixed(shape):
    return pl.BlockSpec(shape, lambda i: (0,) * len(shape))


def resident(array):
    zeros = (0,) * array.ndim
    return (array, pl.BlockSpec(array.shape, lambda i: zeros, pipeline_mode=pl.Buffered(1)))


def during(begin, steps, block, axis=0):
    def index(i):
        at = jnp.minimum(jnp.maximum(i - begin, 0), steps - 1)
        return tuple(at if d == axis else 0 for d in range(len(block)))

    return pl.BlockSpec(block, index)


def struct(shape, dtype):
    return jax.ShapeDtypeStruct(shape, dtype)


def rows_at(step, size):
    return pl.ds(pl.multiple_of(step * size, size), size)


def fetch(pairs, sems):
    copies = [
        pltpu.make_async_copy(source, target, sems.at[n])
        for n, (source, target) in enumerate(pairs)
    ]
    for copy in copies:
        copy.start()
    for copy in copies:
        copy.wait()


ROW_PAIRS = 2


def softmax(scores, axis):
    top = jnp.max(scores, axis=axis, keepdims=True)
    weight = jnp.exp(scores - top)
    return weight * (1.0 / jnp.sum(weight, axis=axis, keepdims=True))


def gelu_pair(x):
    below = 0.5 + 0.5 * lax.erf(x * (1.0 / math.sqrt(2.0)))
    bell = jnp.exp(-0.5 * x * x) * (1.0 / math.sqrt(2.0 * math.pi))
    return x * below, below + x * bell


def row_mean(value):
    return jnp.mean(value, axis=-1, keepdims=True)


def col_sum(value):
    return jnp.sum(value, axis=0, keepdims=True)


def own_image(r, p):
    return r.owner[p]


def flat(ref):
    return ref.reshape(-1, ref.shape[-1])


def merged(ref, blocks, rows):
    return ref.reshape(blocks, rows, ref.shape[-1])


def put_half(out, half, x, d):
    cols = out.shape[-1]
    nf = bits_of(lax.axis_size("fsdp"))
    whole = low(dot_tn(x, d))
    for f in range(1 << nf):
        at = tuple((f >> b) % 2 for b in range(nf - 1, -1, -1))
        part = whole[:, f * cols : (f + 1) * cols]
        out[at + (half,)] = part.reshape(out.shape[nf + 1 :])


def project_keys_phase(r, step, tick):
    tick()

    @pl.when(step == 0)
    def _():
        targets = (r.w_tk, r.w_tv, r.w_iq)
        fetch([(g.reshape(w.shape), w) for g, w in zip(r.gathered, targets)], r.sems)
        images, real = r.states.shape[:2]
        r.image[...] = jnp.zeros_like(r.image)
        for i in range(images):
            r.image[i, :real, :] = r.states[i]
            r.region_counts[i] = lax.fori_loop(
                0, real, lambda k, total, i=i: total + r.mask[i, k], 0
            )
        r.image_rows[...] = r.image[...]
        r.iq[...] = low(times(flat(r.image[...]), r.w_iq)).reshape(r.iq.shape)

    here = rows_at(step, r.text.shape[0] // r.owner.shape[0] * ROW_PAIRS)
    rows = r.text[here, :]
    r.tk[here, :] = low(times(rows, r.w_tk))
    r.tv[here, :] = low(times(rows, r.w_tv))
    tick()


def attend_image_phase(r, step, tick):
    tick()
    regions, length = r.iprob.shape[1:]
    heads = r.tk.shape[1] // HDIM
    columns = [slice(h * HDIM, (h + 1) * HDIM) for h in range(heads)]
    scale = 1.0 / math.sqrt(HDIM)
    for q in range(ROW_PAIRS):
        p = step * ROW_PAIRS + q
        mine = own_image(r, p)
        here, rows_i = rows_at(p, length), rows_at(p, regions)
        kept = lax.broadcasted_iota(jnp.int32, (regions, length), 1) < r.lens[p]
        scores = [scale * dot_nt(r.iq[mine, :, at], r.tk[here, at]) for at in columns]
        probs = [softmax(jnp.where(kept, one, masked_score), 1) for one in scores]
        for h in range(heads):
            r.iprob[p * heads + h] = probs[h]
        parts = [low(dot_nn(low(one), r.tv[here, at])) for one, at in zip(probs, columns)]
        r.ictx[rows_i, :] = jnp.concatenate(parts, axis=1)
        tick()


def attend_text_phase(r, step, tick):
    tick()

    @pl.when(step == 0)
    def _():
        targets = (r.w_tq, r.w_ik, r.w_iv)
        fetch([(g.reshape(w.shape), w) for g, w in zip(r.gathered[7:], targets)], r.sems)
        rows = flat(r.image[...])
        for w, out in ((r.w_ik, r.ik), (r.w_iv, r.iv)):
            out[...] = low(times(rows, w)).reshape(out.shape)

    regions, length = r.tprob.shape[1:]
    heads = r.tq.shape[1] // HDIM
    columns = [slice(h * HDIM, (h + 1) * HDIM) for h in range(heads)]
    scale = 1.0 / math.sqrt(HDIM)
    r.tq[...] = low(times(r.text[rows_at(step, r.tq.shape[0]), :], r.w_tq))
    tick()
    for q in range(ROW_PAIRS):
        mine = own_image(r, step * ROW_PAIRS + q)
        here = slice(q * length, (q + 1) * length)
        row = lax.broadcasted_iota(jnp.int32, (regions, length), 0)
        kept = row < r.region_counts[mine]
        scores = [scale * dot_nt(r.ik[mine, :, at], r.tq[here, at]) for at in columns]
        probs = [softmax(jnp.where(kept, one, masked_score), 0) for one in scores]
        for h in range(heads):
            r.tprob[q * heads + h] = probs[h]
        parts = [low(dot_tn(low(one), r.iv[mine, :, at])) for one, at in zip(probs, columns)]
        r.tctx[here, :] = jnp.concatenate(parts, axis=1)
        tick()


def stream_rows(r, step, tick, limits, x, ctx, cot, norms, weights, keeps, outs):
    w_out, w_inner, w_outer = weights
    mid_ref, act_ref, hid_ref, ffn_ref, branch_ref = keeps
    out, dz_out, dctx_out, ngrad = outs
    rows = x.shape[0]
    group, real = cot.shape[:2]
    slots = rows // group

    def normalize(z):
        offset = z - row_mean(z)
        inv = lax.rsqrt(row_mean(offset * offset) + norm_eps)
        return offset * inv, inv

    def normalize_back(dy, xhat, inv, gain):
        dx = dy * gain
        return inv * (dx - row_mean(dx) - xhat * row_mean(dx * xhat))

    @pl.when(step == 0)
    def _():
        ngrad[...] = jnp.zeros_like(ngrad)
        if real < slots:
            r.cot_wide[...] = jnp.zeros_like(r.cot_wide)

    row = lax.broadcasted_iota(jnp.int32, (rows, 1), 0)
    kept = row < 0
    for q in range(group):
        inside = (row >= q * slots) & (row < q * slots + limits(step * group + q))
        kept = kept | inside
        if real < slots:
            r.cot_wide[q * slots : q * slots + real, :] = cot[q].astype(jnp.float32)
    kept = kept.astype(jnp.float32)
    first_hat, first_inv = normalize(x[...].astype(jnp.float32) + times(ctx[...], w_out))
    mid = first_hat * norms[0] + norms[1]
    mid_low = low(mid)
    mid_ref[...] = mid_low
    tick()
    cols = w_inner.shape[2]
    for f in range(w_inner.shape[0]):
        at = slice(f * cols, (f + 1) * cols)
        act, grad = gelu_pair(dot_nn(mid_low, w_inner[f]))
        act_ref[:, at] = low(act)
        hid_ref[:, at] = low(grad)
        tick()
    second_hat, second_inv = normalize(mid + times(act_ref[...], w_outer))
    result = low((second_hat * norms[2] + norms[3]) * kept)
    for q in range(group):
        out[q] = result[q * slots : q * slots + real]
    if real < slots:
        dy = r.cot_wide[...] * kept
    else:
        dy = cot[...].reshape(rows, -1).astype(jnp.float32) * kept
    second_dz = normalize_back(dy, second_hat, second_inv, norms[2])
    ffn_low = low(second_dz)
    ffn_ref[...] = ffn_low
    sums = [col_sum(dy * second_hat), col_sum(dy)]
    tick()
    hid_ref[...] = low(times_back(ffn_low, w_outer) * hid_ref[...].astype(jnp.float32))
    tick()
    mid_grad = second_dz + times_back(hid_ref[...], w_inner)
    first_dz = normalize_back(mid_grad, first_hat, first_inv, norms[0])
    dz_out[...] = first_dz
    branch_low = low(first_dz)
    branch_ref[...] = branch_low
    tick()
    dctx_out[...] = low(times_back(branch_low, w_out))
    sums = [col_sum(mid_grad * first_hat), col_sum(mid_grad)] + sums
    for n in range(4):
        ngrad[n : n + 1, :] += sums[n]
    tick()


def store_grad(out, x, d):
    cols = out.shape[2]
    whole = low(dot_tn(x, d))
    for f in range(out.shape[0]):
        out[f] = whole[:, f * cols : (f + 1) * cols]


def add_to(ref, mine, value):
    value = low(value).astype(jnp.float32)
    for i in range(ref.shape[0]):
        ref[i] += jnp.where(mine == i, value, 0.0)


def image_phase(first_col, norm_wide, r, step, tick):
    tick()
    group, slots, wide = r.cot.shape[0], r.image.shape[1], r.image.shape[2]

    @pl.when(step == 0)
    def _():
        targets = (r.w_io, r.w_ii, r.w_iu)
        fetch(
            [(g.reshape(w.shape), w) for g, w in zip(r.gathered[4:], targets)]
            + [(r.gathered[3], r.norm_parts)],
            r.sems,
        )
        parts = r.norm_parts.shape[0:-2]
        nf = bits_of(lax.axis_size("fsdp"))
        for i in range(math.prod(parts)):
            at, rest = [], i
            for _ in parts:
                at.append(rest % 2)
                rest //= 2
            at = at[::-1]
            f = sum(bit << k for k, bit in enumerate(reversed(at[:nf])))
            d = sum(bit << k for k, bit in enumerate(reversed(at[nf:])))
            first = (d * (1 << nf) + f) * norm_wide
            r.norms[:, first : first + norm_wide] = r.norm_parts[tuple(at)]

    for q in range(group):
        r.visual[q * slots : (q + 1) * slots, :] = r.image[own_image(r, step * group + q)]
    here = rows_at(step, group * slots)
    norms = [r.norms[n : n + 1, first_col : first_col + wide] for n in range(4)]
    stream_rows(
        r,
        step,
        tick,
        lambda p: r.region_counts[own_image(r, p)],
        r.visual,
        r.ictx.at[here],
        r.cot,
        norms,
        (r.w_io, r.w_ii, r.w_iu),
        [ref.at[here] for ref in (r.mid, r.act, r.hid, r.ffn, r.branch)],
        (r.image_out, r.image_dz, r.dctx.at[here], r.image_ngrad),
    )


def image_grads_phase(r, step, tick):
    tick()
    here = rows_at(step, r.g_io.shape[1])
    store_grad(r.g_io, r.ictx[:, here], r.branch[...])
    store_grad(r.g_ii, r.mid[:, here], r.hid[...])
    store_grad(r.g_iu, r.act[:, here], r.ffn[...])
    tick()


def back_image_phase(r, step, tick):
    tick()
    regions, length = r.iprob.shape[1:]
    heads = r.tk.shape[1] // HDIM
    columns = [slice(h * HDIM, (h + 1) * HDIM) for h in range(heads)]
    scale = 1.0 / math.sqrt(HDIM)

    @pl.when(step == 0)
    def _():
        r.diq_sum[...] = jnp.zeros_like(r.diq_sum)

    for q in range(ROW_PAIRS):
        p = step * ROW_PAIRS + q
        mine = own_image(r, p)
        here, rows_i = rows_at(p, length), rows_at(p, regions)
        local = slice(q * length, (q + 1) * length)
        dprobs = [dot_nt(r.dctx[rows_i, at], r.tv[here, at]) for at in columns]
        dvalues = [
            low(dot_tn(low(r.iprob[p * heads + h]), r.dctx[rows_i, at]))
            for h, at in enumerate(columns)
        ]
        dscores = []
        for h in range(heads):
            probs = r.iprob[p * heads + h]
            inner = jnp.sum(probs * dprobs[h], axis=1, keepdims=True)
            dscores.append(low(probs * (dprobs[h] - inner)))
        parts = [scale * dot_nn(one, r.tk[here, at]) for one, at in zip(dscores, columns)]
        add_to(r.diq_sum, mine, jnp.concatenate(parts, axis=1))
        dkeys = [
            low(scale * dot_tn(one, r.iq[mine, :, at])) for one, at in zip(dscores, columns)
        ]
        for ref, out, values in ((r.tv, r.dtv, dvalues), (r.tk, r.dtk, dkeys)):
            values = jnp.concatenate(values, axis=1)
            ref[here, :] = values
            out[local, :] = values
        tick()


def key_grads_phase(r, step, tick):
    tick()
    diq = low(r.diq_sum[...])
    r.diq[...] = diq
    here = rows_at(step, r.g_iq.shape[1])
    store_grad(r.g_iq, flat(r.image[:, :, here]), flat(diq))
    here = rows_at(step, r.g_tk.shape[1])
    store_grad(r.g_tk, r.text[:, here], r.tk[...])
    store_grad(r.g_tv, r.text[:, here], r.tv[...])
    tick()


def text_phase(r, step, tick):
    tick()
    rows = r.x.shape[0]
    here = rows_at(step, rows)
    norms = [r.norms[n : n + 1, : r.x.shape[1]] for n in range(4)]
    stream_rows(
        r,
        step,
        tick,
        lambda p: r.lens[p],
        r.x,
        r.tctx.at[here],
        r.cot,
        norms,
        (r.w_to, r.w_ti, r.w_tu),
        [ref.at[here] for ref in (r.mid, r.act, r.hid, r.ffn, r.branch)],
        (r.text_out, r.text_dz, r.dctx, r.text_ngrad),
    )


def grad_phase(out, x, d, r, step, tick):
    tick()
    out = getattr(r, out)
    here = rows_at(step, out.shape[1])
    store_grad(out, getattr(r, x)[:, here], getattr(r, d)[...])
    tick()


def back_text_phase(r, step, tick):
    tick()
    regions, length = r.tprob.shape[1:]
    heads = r.tq.shape[1] // HDIM
    columns = [slice(h * HDIM, (h + 1) * HDIM) for h in range(heads)]
    scale = 1.0 / math.sqrt(HDIM)

    @pl.when(step == 0)
    def _():
        r.dik_sum[...] = jnp.zeros_like(r.dik_sum)
        r.div_sum[...] = jnp.zeros_like(r.div_sum)

    for q in range(ROW_PAIRS):
        p = step * ROW_PAIRS + q
        mine = own_image(r, p)
        here = rows_at(p, length)
        local = slice(q * length, (q + 1) * length)
        dprobs = [dot_nt(r.iv[mine, :, at], r.dtc[local, at]) for at in columns]
        parts = [
            dot_nn(low(r.tprob[q * heads + h]), r.dtc[local, at]) for h, at in enumerate(columns)
        ]
        add_to(r.div_sum, mine, jnp.concatenate(parts, axis=1))
        dscores = []
        for h in range(heads):
            probs = r.tprob[q * heads + h]
            inner = jnp.sum(probs * dprobs[h], axis=0, keepdims=True)
            dscores.append(low(probs * (dprobs[h] - inner)))
        parts = [scale * dot_nn(one, r.tq[local, at]) for one, at in zip(dscores, columns)]
        add_to(r.dik_sum, mine, jnp.concatenate(parts, axis=1))
        parts = [
            low(scale * dot_tn(one, r.ik[mine, :, at])) for one, at in zip(dscores, columns)
        ]
        r.dtq[here, :] = jnp.concatenate(parts, axis=1)
        tick()


def query_grads_phase(r, step, tick):
    tick()
    here = rows_at(step, r.text.shape[1] // 2)
    put_half(r.g_tq, step, r.text[:, here], r.dtq[...])
    dik, div = low(r.dik_sum[...]), low(r.div_sum[...])
    r.dik[...] = dik
    r.div[...] = div
    here = rows_at(step, r.image.shape[2] // 2)
    columns = flat(r.image[:, :, here])
    put_half(r.g_ik, step, columns, flat(dik))
    put_half(r.g_iv, step, columns, flat(div))
    tick()


def data_grads_phase(r, step, tick):
    images, real = r.image_grad.shape[:2]
    pairs = r.owner.shape[0]
    slots = r.image_dz.shape[0] // pairs
    tick()

    @pl.when(step == 0)
    def _():
        for i in range(images):
            total = jnp.zeros((slots, r.image_dz.shape[1]), jnp.float32)
            for p in range(pairs):
                rows = r.image_dz[p * slots : (p + 1) * slots, :]
                total += jnp.where(own_image(r, p) == i, rows, 0.0)
            for d, w in ((r.diq, r.w_iq), (r.dik, r.w_ik), (r.div, r.w_iv)):
                total = total + times_back(d[i], w)
            r.image_grad[i] = total[:real]

    total = r.text_dz[...]
    here = rows_at(step, total.shape[0])
    for d, w in ((r.dtq.at[here], r.w_tq), (r.dtk, r.w_tk), (r.dtv, r.w_tv)):
        total = total + times_back(d[...], w)
        tick()
    r.text_grad[...] = total


def pass_kernel(count, *refs):
    for source, target in zip(refs[:count], refs[count:]):
        target[...] = source[...]


def pass_on(arrays):
    return pl.pallas_call(
        functools.partial(pass_kernel, len(arrays)),
        out_shape=[struct(a.shape, a.dtype) for a in arrays],
        in_specs=[WHOLE] * len(arrays),
        out_specs=[WHOLE] * len(arrays),
        compiler_params=pltpu.CompilerParams(vmem_limit_bytes=VMEM_LIMIT),
    )(*arrays)


def whole_weight(shard, block):
    nd, nf = mesh_bits()
    rows, cols = shard.shape
    block = block.reshape(1 << nf, rows << nd, cols)
    if cols % 128:
        block = jnp.swapaxes(block, 0, 1).reshape(1, rows << nd, cols << nf)
    return block


def device_blocks(grad, shard):
    nd, nf = mesh_bits()
    rows, cols = shard.shape
    if cols % 128:
        grad = jnp.swapaxes(grad.reshape(rows << nd, 1 << nf, cols), 0, 1)
    return grad.reshape((2,) * (nd + nf) + (rows, cols))


def norm_blocks(rows):
    nd, nf = mesh_bits()
    wide = rows.shape[1] >> (nd + nf)
    split = rows.reshape(4, 1 << nd, 1 << nf, wide).transpose(2, 1, 0, 3)
    split = jnp.pad(split, ((0, 0), (0, 0), (0, 4), (0, 128 - wide)))
    return split.reshape((2,) * (nd + nf) + (8, 128))


def body(
    text_states,
    image_states,
    text_lengths,
    region_mask,
    group_ids,
    image_query,
    image_key,
    image_value,
    text_query,
    text_key,
    text_value,
    image_output,
    text_output,
    image_inner,
    image_outer,
    text_inner,
    text_outer,
    norm_params,
    cot_text,
    cot_image,
):
    nd, nf = mesh_bits()
    lead = (2,) * (nd + nf)
    bf, f32 = jnp.bfloat16, jnp.float32
    pairs, length, width_text = text_states.shape
    images, regions, width_image = image_states.shape
    padded = -(-regions // 16) * 16
    wide = image_query.shape[1] << nf
    heads = wide // HDIM
    rows_text, rows_image = pairs * length, pairs * padded
    norm_wide = norm_params.shape[1]
    device = lax.axis_index("dp") * lax.axis_size("fsdp") + lax.axis_index("fsdp")
    owner = group_ids - device * images
    text = text_states.reshape(rows_text, width_text)
    def full(shard):
        rows, cols = shard.shape
        return pltpu.VMEM((1 << nf, rows << nd, cols), bf)

    def vmem(rows, cols, dtype=bf):
        return pltpu.VMEM((rows, cols), dtype)

    n = ROW_PAIRS
    steps = pairs // n
    group = pairs // 2
    block_i = group * padded
    gather = Gather(
        [text_key, text_value, image_query, norm_params, image_output, image_inner, image_outer]
        + [text_query, image_key, image_value, text_output, text_inner, text_outer]
    )
    phases, begin = [], [0]

    def phase(run, count, marks, **kw):
        phases.append(Phase(run, count, marks, **kw))
        begin.append(begin[-1] + count)
        return begin[-2]

    phase(project_keys_phase, steps, (0.0, 1.4), needs=range(3))
    phase(attend_image_phase, steps, (0.0, 1.9, 3.8))
    stages = 1 << nf
    marks = [0.0, 1.1] + [1.1 + 1.0 * (k + 1) / stages for k in range(stages)]
    marks += [3.3, 4.4, 5.7, 6.4]
    at_image = phase(
        functools.partial(image_phase, width_text, norm_wide), 2, marks, needs=range(3, 7)
    )
    at_image_grads = phase(image_grads_phase, 4, (0.0, 1.0))
    at_back = phase(back_image_phase, steps, (0.0, 2.3, 4.6))
    at_grads = phase(key_grads_phase, 2, (0.0, 4.2))
    at_attend = phase(attend_text_phase, steps, (0.0, 0.8, 2.8, 4.8), needs=range(7, 10))
    third = width_text // 3

    def grad_out(weight_shard, inner, first, count, size):
        shape = (1 << nf, inner, weight_shard.shape[1])
        if weight_shard.shape[1] % 128:
            shape = (1, inner, weight_shard.shape[1] << nf)
        block = (shape[0], size, shape[2])
        return (struct(shape, bf), during(first, count, block, 1))

    by_pair = during(at_image, 2, (group, regions, width_image))
    probs = during(at_attend, steps, (n * heads, padded, length))
    pair_rows = during(at_attend, steps, (n * length, wide))
    back_rows = during(at_back, steps, (n * length, wide))
    image_shape = (images, padded, wide)
    a = carry(
        phases,
        dict(
            lens=(text_lengths, SCALARS),
            owner=(owner, SCALARS),
            mask=(region_mask, SCALARS),
            text=resident(text),
            states=resident(image_states),
            cot=(cot_image, by_pair),
        ),
        dict(
            ik=(struct(image_shape, bf), fixed(image_shape)),
            iv=(struct(image_shape, bf), fixed(image_shape)),
            tq=(struct((rows_text, wide), bf), pair_rows),
            tprob=(struct((pairs * heads, padded, length), f32), probs),
            tctx=(struct((rows_text, wide), bf), pair_rows),
            image_rows=(
                struct((images, padded, width_image), bf),
                fixed((images, padded, width_image)),
            ),
            norms=(struct((4, norm_wide << (nd + nf)), f32), fixed((4, norm_wide << (nd + nf)))),
            image_out=(struct(cot_image.shape, bf), by_pair),
            image_dz=(
                struct((rows_image, width_image), f32),
                during(at_image, 2, (block_i, width_image)),
            ),
            image_ngrad=(struct((4, width_image), f32), fixed((4, width_image))),
            dtk=(struct((rows_text, wide), bf), back_rows),
            dtv=(struct((rows_text, wide), bf), back_rows),
            diq=(struct(image_shape, bf), fixed(image_shape)),
            g_io=grad_out(image_output, wide, at_image_grads, 4, wide // 4),
            g_ii=grad_out(image_inner, width_image, at_image_grads, 4, width_image // 4),
            g_iu=grad_out(image_outer, width_image, at_image_grads, 4, width_image // 4),
            g_iq=grad_out(image_query, width_image, at_grads, 2, width_image // 2),
            g_tk=grad_out(text_key, width_text, at_grads, 2, width_text // 2),
            g_tv=grad_out(text_value, width_text, at_grads, 2, width_text // 2),
        ),
        dict(
            w_tq=full(text_query),
            w_tk=full(text_key),
            w_tv=full(text_value),
            w_iq=full(image_query),
            w_ik=full(image_key),
            w_iv=full(image_value),
            w_io=full(image_output),
            w_ii=full(image_inner),
            w_iu=full(image_outer),
            image=pltpu.VMEM((images, padded, width_image), bf),
            visual=vmem(block_i, width_image),
            region_counts=pltpu.SMEM((images,), jnp.int32),
            norm_parts=pltpu.VMEM(lead + norm_params.shape, f32),
            sems=pltpu.SemaphoreType.DMA((4,)),
            iq=pltpu.VMEM(image_shape, bf),
            tk=vmem(rows_text, wide),
            tv=vmem(rows_text, wide),
            iprob=pltpu.VMEM((pairs * heads, padded, length), f32),
            ictx=vmem(rows_image, wide),
            mid=vmem(rows_image, width_image),
            act=vmem(rows_image, width_image),
            hid=vmem(rows_image, width_image),
            ffn=vmem(rows_image, width_image),
            branch=vmem(rows_image, width_image),
            dctx=vmem(rows_image, wide),
            diq_sum=pltpu.VMEM(image_shape, f32),
            cot_wide=vmem(block_i, width_image, f32),
        ),
        [gather],
        0,
    )
    whole = [whole_weight(s, g) for s, g in zip(gather.given, a.landed[0]) if s is not norm_params]
    w_tk, w_tv, w_iq, _, _, _, w_tq, w_ik, w_iv, w_to, w_ti, w_tu = whole

    job = Reduce(
        [
            device_blocks(grad, shard)
            for grad, shard in (
                (a.g_io, image_output),
                (a.g_ii, image_inner),
                (a.g_iu, image_outer),
                (a.g_iq, image_query),
                (a.g_tk, text_key),
                (a.g_tv, text_value),
            )
        ]
    )
    phases, begin = [], [0]
    inner = w_ti.shape[0] * w_ti.shape[2]
    block_t = n * length
    stages = w_ti.shape[0]
    marks = [0.0, 1.6] + [1.6 + 3.6 * (k + 1) / stages for k in range(stages)]
    marks += [7.8, 9.8, 11.8, 12.6]
    at_text = phase(text_phase, steps, marks)
    at_tu = phase(functools.partial(grad_phase, "g_tu", "act", "ffn"), 12, (0.0, 0.7))
    at_ti = phase(functools.partial(grad_phase, "g_ti", "mid", "hid"), 6, (0.0, 1.4))
    at_to = phase(functools.partial(grad_phase, "g_to", "tctx", "branch"), 4, (0.0, 0.8))
    by_pair = during(at_text, steps, (n, length, width_text))

    def text_rows(cols):
        return during(at_text, steps, (block_t, cols))

    b = carry(
        phases,
        dict(
            lens=(text_lengths, SCALARS),
            x=(text, text_rows(width_text)),
            tctx=resident(a.tctx),
            cot=(cot_text, by_pair),
            norms=resident(a.norms),
            w_to=resident(w_to),
            w_ti=resident(w_ti),
            w_tu=resident(w_tu),
        ),
        dict(
            text_out=(struct(cot_text.shape, bf), by_pair),
            text_dz=(struct((rows_text, width_text), f32), text_rows(width_text)),
            dctx=(struct((rows_text, wide), bf), text_rows(wide)),
            text_ngrad=(struct((4, width_text), f32), fixed((4, width_text))),
            g_tu=grad_out(text_outer, inner, at_tu, 12, inner // 12),
            g_ti=grad_out(text_inner, width_text, at_ti, 6, width_text // 6),
            g_to=grad_out(text_output, wide, at_to, 4, wide // 4),
        ),
        dict(
            mid=vmem(rows_text, width_text),
            act=vmem(rows_text, inner),
            hid=vmem(rows_text, inner),
            ffn=vmem(rows_text, width_text),
            branch=vmem(rows_text, width_text),
        ),
        [job],
        1,
    )
    o_io, o_ii, o_iu, o_iq, o_tk, o_tv = b.landed[0]

    norm_rows = norm_blocks(jnp.concatenate([b.text_ngrad, a.image_ngrad], axis=1))
    job = Reduce(
        [
            device_blocks(b.g_tu, text_outer),
            device_blocks(b.g_ti, text_inner),
            device_blocks(b.g_to, text_output),
            norm_rows,
        ],
        dict(
            g_tq=struct(lead + text_query.shape, bf),
            g_ik=struct(lead + image_key.shape, bf),
            g_iv=struct(lead + image_value.shape, bf),
        ),
    )
    phases, begin = [], [0]
    at_back = phase(back_text_phase, steps, (0.0, 2.3, 4.6))
    phase(query_grads_phase, 2, (0.0, 3.2), makes=range(4, 7))
    at_data = phase(data_grads_phase, steps, (0.0, 0.9, 1.8, 2.6))
    probs = during(at_back, steps, (n * heads, padded, length))
    back_rows = during(at_back, steps, (n * length, wide))
    data_rows = during(at_data, steps, (block_t, wide))
    data_out = during(at_data, steps, (block_t, width_text))
    c = carry(
        phases,
        dict(
            owner=(owner, SCALARS),
            ik=resident(a.ik),
            iv=resident(a.iv),
            tq=(a.tq, back_rows),
            tprob=(a.tprob, probs),
            dtc=(b.dctx, back_rows),
            text=resident(text),
            image=resident(a.image_rows),
            text_dz=(b.text_dz, data_out),
            dtk=(a.dtk, data_rows),
            dtv=(a.dtv, data_rows),
            image_dz=resident(a.image_dz),
            diq=resident(a.diq),
            w_tq=resident(w_tq),
            w_tk=resident(w_tk),
            w_tv=resident(w_tv),
            w_iq=resident(w_iq),
            w_ik=resident(w_ik),
            w_iv=resident(w_iv),
        ),
        dict(
            text_grad=(struct((rows_text, width_text), f32), data_out),
            image_grad=(struct(image_states.shape, f32), fixed(image_states.shape)),
        ),
        dict(
            dtq=vmem(rows_text, wide),
            dik=pltpu.VMEM(image_shape, bf),
            div=pltpu.VMEM(image_shape, bf),
            dik_sum=pltpu.VMEM(image_shape, f32),
            div_sum=pltpu.VMEM(image_shape, f32),
            g_tq=pltpu.VMEM(lead + text_query.shape, bf),
            g_ik=pltpu.VMEM(lead + image_key.shape, bf),
            g_iv=pltpu.VMEM(lead + image_value.shape, bf),
        ),
        [job],
        2,
    )
    o_tu, o_ti, o_to, o_norm, o_tq, o_ik, o_iv = c.landed[0]
    owned = pass_on([o_iq, o_ik, o_iv, o_tq, o_tk, o_tv, o_io, o_to, o_ii, o_iu, o_ti, o_tu])
    return (
        b.text_out,
        a.image_out,
        c.text_grad.reshape(text_states.shape),
        c.image_grad,
        *owned,
        o_norm[:4, :norm_wide],
    )


def solution(mesh):
    placed = (
        P(("dp", "fsdp"), None, None),
        P(("dp", "fsdp"), None, None),
        P(("dp", "fsdp")),
        P(("dp", "fsdp"), None),
        P(("dp", "fsdp")),
        P("dp", "fsdp"),
        P("dp", "fsdp"),
        P("dp", "fsdp"),
        P("dp", "fsdp"),
        P("dp", "fsdp"),
        P("dp", "fsdp"),
        P("dp", "fsdp"),
        P("dp", "fsdp"),
        P("dp", "fsdp"),
        P("dp", "fsdp"),
        P("dp", "fsdp"),
        P("dp", "fsdp"),
        P(None, ("dp", "fsdp")),
        P(("dp", "fsdp"), None, None),
        P(("dp", "fsdp"), None, None),
    )
    return jax.shard_map(
        body,
        mesh=mesh,
        in_specs=placed,
        out_specs=(
            P(("dp", "fsdp"), None, None),
            P(("dp", "fsdp"), None, None),
            P(("dp", "fsdp"), None, None),
            P(("dp", "fsdp"), None, None),
            P("dp", "fsdp"),
            P("dp", "fsdp"),
            P("dp", "fsdp"),
            P("dp", "fsdp"),
            P("dp", "fsdp"),
            P("dp", "fsdp"),
            P("dp", "fsdp"),
            P("dp", "fsdp"),
            P("dp", "fsdp"),
            P("dp", "fsdp"),
            P("dp", "fsdp"),
            P("dp", "fsdp"),
            P(None, ("dp", "fsdp")),
        ),
        check_vma=False,
    )
```

```python
import functools
import itertools
import math
import random

import jax
import jax.numpy as jnp
from jax import lax
from jax.experimental import pallas as pl
from jax.experimental.pallas import tpu as pltpu
from jax.sharding import PartitionSpec as P

HDIM = 128

norm_eps = 1e-12
masked_score = -1e30

MESH_IDS = pl.DeviceIdType.MESH
VMEM_LIMIT = 63 * 1024 * 1024
WHOLE = pl.BlockSpec(memory_space=pltpu.VMEM)
SCALARS = pl.BlockSpec(memory_space=pltpu.SMEM)
ANYWHERE = pl.BlockSpec(memory_space=pl.ANY)
CORE = ("d", 0)


def bits_of(size):
    count = size.bit_length() - 1
    assert 1 << count == size
    return count


def mesh_bits():
    return bits_of(lax.axis_size("dp")), bits_of(lax.axis_size("fsdp"))


def hop_orders(nd, nf):
    high = [("d", b) for b in range(nd - 1, 2, -1)]
    low = [("d", 2)]
    near = [("d", 1)]
    wide = [("f", b) for b in range(nf)]
    first = [(low, near, high, wide), (high, wide, low, near)]
    rest = [p for p in itertools.permutations((low, near, high, wide)) if p not in first]
    return [tuple(bit for group in order for bit in group) for order in first + rest]


def cut_pieces(shapes):
    pieces, ranks, large = [], [], 0
    for m, (rows, cols) in enumerate(shapes):
        count = 4 if rows * cols > 40000 else 2
        if rows % (16 * count) == 0:
            each = rows // count
            cuts = [(k * each, each, 0, cols) for k in range(count)]
        elif cols % (128 * count) == 0 and rows % 8 == 0:
            each = cols // count
            cuts = [(0, rows, k * each, each) for k in range(count)]
        else:
            cuts = [(0, rows, 0, cols)]
        for cut in cuts:
            pieces.append((m, *cut, large % 2))
            small = rows * cols < 2048
            ranks.append(0 if small else large)
            large += 0 if small else 1
    return pieces, ranks


class Place:
    def __init__(self, nd, nf):
        self.d = lax.axis_index("dp")
        self.f = lax.axis_index("fsdp")
        self.axes = [("f", b) for b in range(nf - 1, -1, -1)] + [
            ("d", b) for b in range(nd - 1, -1, -1)
        ]

    def bit(self, axis):
        value = self.f if axis[0] == "f" else self.d
        return lax.rem(value // (1 << axis[1]), 2)

    def partner(self, axis):
        step = (1 << axis[1]) * (1 - 2 * self.bit(axis))
        if axis[0] == "f":
            return (self.d, self.f + step)
        return (self.d + step, self.f)

    def index(self, whole, flip=None):
        picked = []
        for axis in self.axes:
            if axis in whole:
                picked.append(slice(None))
            elif axis == flip:
                picked.append(1 - self.bit(axis))
            else:
                picked.append(self.bit(axis))
        return tuple(picked)

    def barrier(self):
        sem = pltpu.get_barrier_semaphore()
        for axis in self.axes:
            pl.semaphore_signal(
                sem, inc=1, device_id=self.partner(axis), device_id_type=MESH_IDS
            )
        pl.semaphore_wait(sem, len(self.axes))


class Gather:
    def __init__(self, arrays):
        self.arrays = arrays
        self.given = arrays
        self.made = []
        self.adds = False
        self.nd, self.nf = mesh_bits()
        self.orders = [order + (CORE,) for order in hop_orders(self.nd, self.nf)]
        self.cuts, self.ranks = cut_pieces([a.shape for a in arrays])
        self.routes = [self.orders[cut[-1]] for cut in self.cuts]
        self.hops = self.nd + self.nf
        lead = (2,) * self.hops
        self.out_shape = [jax.ShapeDtypeStruct(lead + a.shape, a.dtype) for a in arrays]
        self.out_specs = [ANYWHERE] * len(arrays)
        count = len(self.cuts)
        self.scratch = [
            pltpu.SemaphoreType.DMA((count,)),
            pltpu.SemaphoreType.DMA((count, self.hops)),
            pltpu.SemaphoreType.DMA((count, self.hops)),
        ]

    def sizes(self, k):
        m, row, rows, col, cols, _ = self.cuts[k]
        block = rows * cols * self.arrays[m].dtype.itemsize
        return [block << h for h in range(self.hops)]

    def window(self, k):
        m, row, rows, col, cols, _ = self.cuts[k]
        return (pl.ds(row, rows), pl.ds(col, cols))

    def bind(self, place, ins, outs, scratch):
        self.place, self.ins, self.outs = place, ins, outs
        self.local_sem, self.send_sem, self.recv_sem = scratch

    def local(self, k):
        m = self.cuts[k][0]
        return pltpu.make_async_copy(
            self.ins[m].at[self.window(k)],
            self.outs[m].at[self.place.index(()) + self.window(k)],
            self.local_sem.at[k],
        )

    def hop(self, k, h):
        m, route = self.cuts[k][0], self.routes[k]
        region = self.outs[m].at[self.place.index(route[:h]) + self.window(k)]
        return pltpu.make_async_remote_copy(
            src_ref=region,
            dst_ref=region,
            send_sem=self.send_sem.at[k, h],
            recv_sem=self.recv_sem.at[k, h],
            device_id=self.place.partner(route[h]),
            device_id_type=MESH_IDS,
        )

    def start(self):
        for k in range(len(self.cuts)):
            self.local(k).start()

    def step(self, k, h):
        if h == 0:
            self.local(k).wait()
        else:
            self.hop(k, h - 1).wait_recv()
        if h < self.hops:
            self.hop(k, h).start()
        else:
            for g in range(self.hops):
                self.hop(k, g).wait_send()


def add_blocks(acc, index, window, incoming):
    lead = incoming.shape[:-2]
    outer, inner = lead[:-2], lead[-2:]

    def one(i, carry):
        first = []
        for size in reversed(outer):
            first.append(lax.rem(i, size))
            i = i // size
        first = first[::-1]
        for j in range(math.prod(inner)):
            at, rest = [], j
            for size in reversed(inner):
                at.append(rest % size)
                rest //= size
            at = tuple(first + at[::-1])
            left = list(at)
            where = tuple(left.pop(0) if isinstance(p, slice) else p for p in index) + window
            acc[where] = acc[where] + incoming[at]
        return carry

    lax.fori_loop(0, math.prod(outer), one, 0)


class Reduce:
    def __init__(self, given, made=None):
        made = made or {}
        self.given = given
        self.made = list(made)
        self.adds = True
        arrays = list(given) + list(made.values())
        self.arrays = arrays
        self.nd, self.nf = mesh_bits()
        self.orders = [(CORE,) + order[::-1] for order in hop_orders(self.nd, self.nf)]
        self.hops = self.nd + self.nf
        self.cuts, self.ranks = cut_pieces([a.shape[-2:] for a in arrays])
        self.routes = [self.orders[cut[-1]] for cut in self.cuts]
        self.scratch = []
        for m, row, rows, col, cols, _ in self.cuts:
            for h in range(-1 if m < len(self.given) else 0, self.hops):
                free = self.hops - 1 - max(h, 0)
                self.scratch.append(pltpu.VMEM((2,) * free + (rows, cols), arrays[m].dtype))
        count = len(self.cuts)
        self.scratch += [
            pltpu.SemaphoreType.DMA((count,)),
            pltpu.SemaphoreType.DMA((count, self.hops)),
            pltpu.SemaphoreType.DMA((count, self.hops)),
        ]
        shapes = [a.shape[-2:] for a in arrays]
        self.out_shape = [jax.ShapeDtypeStruct(s, jnp.float32) for s in shapes]
        self.out_specs = [pl.BlockSpec(s, lambda *_: (0, 0)) for s in shapes]

    def sizes(self, k):
        m, row, rows, col, cols, _ = self.cuts[k]
        block = rows * cols * self.arrays[m].dtype.itemsize
        return [block << (self.hops - 1 - h) for h in range(self.hops)]

    def window(self, k):
        m, row, rows, col, cols, _ = self.cuts[k]
        return (pl.ds(row, rows), pl.ds(col, cols))

    def bind(self, place, ins, outs, scratch):
        self.place, self.ins, self.outs = place, ins, outs
        self.local_sem, self.send_sem, self.recv_sem = scratch[-3:]
        rest = list(scratch[:-3])
        self.accs, self.temps = [], []
        for m, *_ in self.cuts:
            self.accs.append(rest.pop(0) if m < len(self.given) else None)
            self.temps.append([rest.pop(0) for _ in range(self.hops)])
        self.rest = [axis for axis in place.axes if axis != CORE]

    def local(self, k):
        source = self.ins[self.cuts[k][0]].at[self.place.index(self.rest) + self.window(k)]
        return pltpu.make_async_copy(source, self.accs[k], self.local_sem.at[k])

    def within(self, k, h, flip=None):
        full = self.place.index(self.routes[k][h + 1 :], flip)
        if self.accs[k] is None:
            m, row, rows, col, cols, _ = self.cuts[k]
            return self.ins[m], full, (slice(row, row + rows), slice(col, col + cols))
        return self.accs[k], tuple(p for p, a in zip(full, self.place.axes) if a != CORE), ()

    def hop(self, k, h):
        m, route = self.cuts[k][0], self.routes[k]
        if h == 0:
            region = self.ins[m].at[self.place.index(route[1:], CORE) + self.window(k)]
        else:
            acc, index, window = self.within(k, h, route[h])
            region = acc.at[index + window]
        return pltpu.make_async_remote_copy(
            src_ref=region,
            dst_ref=self.temps[k][h],
            send_sem=self.send_sem.at[k, h],
            recv_sem=self.recv_sem.at[k, h],
            device_id=self.place.partner(route[h]),
            device_id_type=MESH_IDS,
        )

    def start(self):
        pass

    def step(self, k, h):
        own = self.accs[k] is not None
        if h == 0 and own:
            self.local(k).start()
        if h > 0:
            self.hop(k, h - 1).wait_recv()
            if h == 1 and own:
                self.local(k).wait()
            acc, index, window = self.within(k, h - 1)
            if h < self.hops:
                add_blocks(acc, index, window, self.temps[k][h - 1])
            else:
                m, row, rows, col, cols, _ = self.cuts[k]
                last = acc[index + window].astype(jnp.float32)
                last = last + self.temps[k][h - 1][...].astype(jnp.float32)
                self.outs[m][row : row + rows, col : col + cols] = last
        if h < self.hops:
            self.hop(k, h).start()
        else:
            for g in range(self.hops):
                self.hop(k, g).wait_send()


LINK_RATE = 46e3
CORE_RATE = 380e3
LATENCY = 2.5
ENTRY = 3.0
ISSUE = 0.06
ADD_RATE = 1800e3
SEARCH = 1500


class Phase:
    def __init__(self, run, steps, marks, needs=(), makes=()):
        self.run, self.steps, self.marks = run, steps, marks
        self.needs, self.makes = set(needs), set(makes)


def place_steps(order, job, times, clock, limits, after, counted=True):
    total = len(times)
    limit = [total] * len(order)
    for needs, begin in limits:
        last = -1
        for i, (k, h) in enumerate(order):
            if h == job.hops and job.cuts[k][0] in needs:
                last = i
        for i in range(last + 1):
            limit[i] = min(limit[i], begin)
    waiting, active, done = {}, {}, {}
    now = 0.0

    def advance(key, until):
        nonlocal now
        while key not in done and now < until:
            for axis, queue in waiting.items():
                if queue and axis not in active:
                    active[axis] = queue.pop(0)
            far = any(axis[0] == "d" and axis[1] > 2 for axis in active)
            rates, span = {}, until - now
            for axis, (_, left) in active.items():
                halved = far and axis[0] == "d" and axis[1] > 1
                rates[axis] = CORE_RATE if axis == CORE else LINK_RATE / (2 if halved else 1)
                span = min(span, left / rates[axis])
            now += span
            for axis in list(active):
                active[axis][1] -= span * rates[axis]
                if active[axis][1] <= 1e-3:
                    done[active.pop(axis)[0]] = now + LATENCY

    slots = [[] for _ in range(total)]
    tail = []
    at, late, started = 0, ENTRY if counted else 0.0, 0.0
    for i, (k, h) in enumerate(order):
        ready = now
        if h:
            advance((k, h - 1), math.inf)
            ready = max(ready, done[k, h - 1])
        else:
            at = max(at, after.get(job.cuts[k][0], 0))
        while at < min(limit[i], total) and times[at] + late < ready - 0.3:
            at += 1
        spent = ISSUE + (job.sizes(k)[h - 1] / ADD_RATE if h and job.adds else 0.0)
        spent = spent if counted else 0.0
        if at < total:
            slots[at].append((k, h))
            ready = max(ready, times[at] + late) + spent
            late = ready - times[at]
        else:
            ready = max(ready, clock + late) + spent
            tail.append((k, h))
        started += ready
        advance(None, ready)
        if h < job.hops:
            waiting.setdefault(job.routes[k][h], []).append([(k, h), float(job.sizes(k)[h])])
    end = max(now, clock + late)
    return end + 0.2 * max(done.values()) + 0.1 * started / len(order), slots, tail


def plan_steps(job, phases, search):
    times, limits, after = [], [], {}
    clock = 0.0
    for phase in phases:
        limits.append((phase.needs, len(times)))
        for _ in range(phase.steps):
            times += [clock + mark for mark in phase.marks]
            clock += phase.marks[-1]
        for m in phase.makes:
            after[m] = len(times)
    known = (job, times, clock, limits, after)

    def waves(width, lag):
        order = []
        for k, rank in enumerate(job.ranks):
            wave = rank // width + (lag if job.cuts[k][0] in after else 0)
            order += [(wave + h, wave, k, h) for h in range(job.hops + 1)]
        return [(k, h) for _, _, k, h in sorted(order)]

    if not search:
        return place_steps(waves(4, 0), *known, False)[1:]
    lags = range(4) if after else (0,)
    starts = [waves(width, lag) for width in (3, 4, 5, 6) for lag in lags]
    best, order = min((place_steps(start, *known)[0], start) for start in starts)
    draw = random.Random(1)
    for _ in range(search):
        if draw.random() < 0.3:
            k = draw.randrange(len(job.cuts))
            kept = job.routes[k]
            job.routes[k] = draw.choice(job.orders)
            cost = place_steps(order, *known)[0]
            if cost < best:
                best = cost
            else:
                job.routes[k] = kept
            continue
        i = draw.randrange(len(order))
        k, h = order[i]
        low_end = order.index((k, h - 1)) + 1 if h else 0
        high_end = order.index((k, h + 1)) - 1 if h < job.hops else len(order) - 1
        j = draw.randint(max(low_end, i - 12), max(low_end, min(high_end, i + 12)))
        moved = list(order)
        moved.insert(j, moved.pop(i))
        cost = place_steps(moved, *known)[0]
        if cost < best:
            best, order = cost, moved
    return place_steps(order, *known)[1:]


class Names:
    def __init__(self, names, refs):
        for name, ref in zip(names, refs):
            setattr(self, name, ref)


def carrying_kernel(phases, job, plan, names, *refs):
    spans, start = [], 0
    for count in [len(group) for group in names]:
        spans.append(refs[start : start + count])
        start += count
    own_in, job_in, own_out, job_out, own_scratch, job_scratch = spans
    r = Names(names[0] + names[2] + names[4], own_in + own_out + own_scratch)
    now = pl.program_id(0)
    slots, tail = plan
    place = Place(job.nd, job.nf)
    r.gathered = job_out
    made = [getattr(r, name) for name in job.made]
    job.bind(place, list(job_in) + made, job_out, job_scratch)

    def run(items, opening=False):
        if opening:
            job.start()
            place.barrier()
        for k, h in items:
            job.step(k, h)

    base, begin = 0, 0
    for phase in phases:
        ticks = len(phase.marks)

        def one(phase=phase, base=base, begin=begin, ticks=ticks):
            passed = [0]

            def tick():
                t = passed[0]
                passed[0] += 1
                for s in range(phase.steps):
                    items = slots[base + s * ticks + t]
                    opening = base + s * ticks + t == 0
                    if items or opening:
                        pl.when(now == begin + s)(functools.partial(run, items, opening))

            phase.run(r, now - begin, tick)
            assert passed[0] == ticks

        pl.when((now >= begin) & (now < begin + phase.steps))(one)
        base += ticks * phase.steps
        begin += phase.steps
    if tail:
        pl.when(now == begin - 1)(functools.partial(run, tail))


def carry(phases, ins, outs, scratch, job, ident, search=0):
    plan = plan_steps(job, phases, search)
    given, landed, worked = list(job.given), list(job.out_shape), list(job.scratch)
    names = (
        list(ins),
        [None] * len(given),
        list(outs),
        [None] * len(landed),
        list(scratch),
        [None] * len(worked),
    )
    results = pl.pallas_call(
        functools.partial(carrying_kernel, phases, job, plan, names),
        grid=(sum(phase.steps for phase in phases),),
        in_specs=[spec for _, spec in ins.values()] + [ANYWHERE] * len(given),
        out_specs=[spec for _, spec in outs.values()] + list(job.out_specs),
        out_shape=[shape for shape, _ in outs.values()] + landed,
        scratch_shapes=list(scratch.values()) + worked,
        compiler_params=pltpu.CompilerParams(
            collective_id=ident, has_side_effects=True, vmem_limit_bytes=VMEM_LIMIT
        ),
    )(*[array for array, _ in ins.values()], *given)
    r = Names(list(outs), results)
    r.landed = results[len(outs) :]
    return r


def dot_nn(a, b):
    return lax.dot_general(a, b, (((1,), (0,)), ((), ())), preferred_element_type=jnp.float32)


def dot_nt(a, b):
    return lax.dot_general(a, b, (((1,), (1,)), ((), ())), preferred_element_type=jnp.float32)


def dot_tn(a, b):
    return lax.dot_general(a, b, (((0,), (0,)), ((), ())), preferred_element_type=jnp.float32)


def low(value):
    return value.astype(jnp.bfloat16)


def times(value, matrix):
    parts = [dot_nn(value, matrix[f]) for f in range(matrix.shape[0])]
    return parts[0] if len(parts) == 1 else jnp.concatenate(parts, axis=1)


def times_back(value, matrix):
    cols = matrix.shape[2]
    total = None
    for f in range(matrix.shape[0]):
        term = dot_nt(value[:, f * cols : (f + 1) * cols], matrix[f])
        total = term if total is None else total + term
    return total


def fixed(shape):
    return pl.BlockSpec(shape, lambda i: (0,) * len(shape))


def resident(array):
    zeros = (0,) * array.ndim
    return (array, pl.BlockSpec(array.shape, lambda i: zeros, pipeline_mode=pl.Buffered(1)))


def during(begin, steps, block, axis=0):
    def index(i):
        at = jnp.minimum(jnp.maximum(i - begin, 0), steps - 1)
        return tuple(at if d == axis else 0 for d in range(len(block)))

    return pl.BlockSpec(block, index)


def struct(shape, dtype):
    return jax.ShapeDtypeStruct(shape, dtype)


def rows_at(step, size):
    return pl.ds(pl.multiple_of(step * size, size), size)


def fetch(pairs, sems):
    copies = [
        pltpu.make_async_copy(source, target, sems.at[n])
        for n, (source, target) in enumerate(pairs)
    ]
    for copy in copies:
        copy.start()
    for copy in copies:
        copy.wait()


ROW_PAIRS = 2


def softmax(scores, axis):
    top = jnp.max(scores, axis=axis, keepdims=True)
    weight = jnp.exp(scores - top)
    return weight * (1.0 / jnp.sum(weight, axis=axis, keepdims=True))


def gelu_pair(x):
    below = 0.5 + 0.5 * lax.erf(x * (1.0 / math.sqrt(2.0)))
    bell = jnp.exp(-0.5 * x * x) * (1.0 / math.sqrt(2.0 * math.pi))
    return x * below, below + x * bell


def row_mean(value):
    return jnp.mean(value, axis=-1, keepdims=True)


def col_sum(value):
    return jnp.sum(value, axis=0, keepdims=True)


def own_image(r, p):
    return r.owner[p]


def flat(ref):
    return ref.reshape(-1, ref.shape[-1])


def merged(ref, blocks, rows):
    return ref.reshape(blocks, rows, ref.shape[-1])


def put_half(out, half, x, d):
    cols = out.shape[-1]
    nf = bits_of(lax.axis_size("fsdp"))
    whole = low(dot_tn(x, d))
    for f in range(1 << nf):
        at = tuple((f >> b) % 2 for b in range(nf - 1, -1, -1))
        part = whole[:, f * cols : (f + 1) * cols]
        out[at + (half,)] = part.reshape(out.shape[nf + 1 :])


def project_keys_phase(r, step, tick):
    tick()

    @pl.when(step == 0)
    def _():
        targets = (r.w_tk, r.w_tv, r.w_iq)
        fetch([(g.reshape(w.shape), w) for g, w in zip(r.gathered, targets)], r.sems)
        images, real = r.states.shape[:2]
        r.image[...] = jnp.zeros_like(r.image)
        for i in range(images):
            r.image[i, :real, :] = r.states[i]
            r.region_counts[i] = lax.fori_loop(
                0, real, lambda k, total, i=i: total + r.mask[i, k], 0
            )
        r.image_rows[...] = r.image[...]
        r.iq[...] = low(times(flat(r.image[...]), r.w_iq)).reshape(r.iq.shape)

    here = rows_at(step, r.text.shape[0] // r.owner.shape[0] * ROW_PAIRS)
    rows = r.text[here, :]
    r.tk[here, :] = low(times(rows, r.w_tk))
    r.tv[here, :] = low(times(rows, r.w_tv))
    tick()


def attend_image_phase(r, step, tick):
    tick()
    regions, length = r.iprob.shape[1:]
    heads = r.tk.shape[1] // HDIM
    columns = [slice(h * HDIM, (h + 1) * HDIM) for h in range(heads)]
    scale = 1.0 / math.sqrt(HDIM)
    for q in range(ROW_PAIRS):
        p = step * ROW_PAIRS + q
        mine = own_image(r, p)
        here, rows_i = rows_at(p, length), rows_at(p, regions)
        kept = lax.broadcasted_iota(jnp.int32, (regions, length), 1) < r.lens[p]
        scores = [scale * dot_nt(r.iq[mine, :, at], r.tk[here, at]) for at in columns]
        probs = [softmax(jnp.where(kept, one, masked_score), 1) for one in scores]
        for h in range(heads):
            r.iprob[p * heads + h] = probs[h]
        parts = [low(dot_nn(low(one), r.tv[here, at])) for one, at in zip(probs, columns)]
        r.ictx[rows_i, :] = jnp.concatenate(parts, axis=1)
        tick()


def attend_text_phase(r, step, tick):
    tick()

    @pl.when(step == 0)
    def _():
        targets = (r.w_tq, r.w_ik, r.w_iv)
        fetch([(g.reshape(w.shape), w) for g, w in zip(r.gathered[7:], targets)], r.sems)
        rows = flat(r.image[...])
        for w, out in ((r.w_ik, r.ik), (r.w_iv, r.iv)):
            out[...] = low(times(rows, w)).reshape(out.shape)

    regions, length = r.tprob.shape[1:]
    heads = r.tq.shape[1] // HDIM
    columns = [slice(h * HDIM, (h + 1) * HDIM) for h in range(heads)]
    scale = 1.0 / math.sqrt(HDIM)
    r.tq[...] = low(times(r.text[rows_at(step, r.tq.shape[0]), :], r.w_tq))
    tick()
    for q in range(ROW_PAIRS):
        mine = own_image(r, step * ROW_PAIRS + q)
        here = slice(q * length, (q + 1) * length)
        row = lax.broadcasted_iota(jnp.int32, (regions, length), 0)
        kept = row < r.region_counts[mine]
        scores = [scale * dot_nt(r.ik[mine, :, at], r.tq[here, at]) for at in columns]
        probs = [softmax(jnp.where(kept, one, masked_score), 0) for one in scores]
        for h in range(heads):
            r.tprob[q * heads + h] = probs[h]
        parts = [low(dot_tn(low(one), r.iv[mine, :, at])) for one, at in zip(probs, columns)]
        r.tctx[here, :] = jnp.concatenate(parts, axis=1)
        tick()


def stream_rows(r, step, tick, limits, x, ctx, cot, norms, weights, keeps, outs):
    w_out, w_inner, w_outer = weights
    mid_ref, act_ref, hid_ref, ffn_ref, branch_ref = keeps
    out, dz_out, dctx_out, ngrad = outs
    rows = x.shape[0]
    group, real = cot.shape[:2]
    slots = rows // group

    def normalize(z):
        offset = z - row_mean(z)
        inv = lax.rsqrt(row_mean(offset * offset) + norm_eps)
        return offset * inv, inv

    def normalize_back(dy, xhat, inv, gain):
        dx = dy * gain
        return inv * (dx - row_mean(dx) - xhat * row_mean(dx * xhat))

    @pl.when(step == 0)
    def _():
        ngrad[...] = jnp.zeros_like(ngrad)
        if real < slots:
            r.cot_wide[...] = jnp.zeros_like(r.cot_wide)

    row = lax.broadcasted_iota(jnp.int32, (rows, 1), 0)
    kept = row < 0
    for q in range(group):
        inside = (row >= q * slots) & (row < q * slots + limits(step * group + q))
        kept = kept | inside
        if real < slots:
            r.cot_wide[q * slots : q * slots + real, :] = cot[q].astype(jnp.float32)
    kept = kept.astype(jnp.float32)
    first_hat, first_inv = normalize(x[...].astype(jnp.float32) + times(ctx[...], w_out))
    mid = first_hat * norms[0] + norms[1]
    mid_low = low(mid)
    mid_ref[...] = mid_low
    tick()
    cols = w_inner.shape[2]
    for f in range(w_inner.shape[0]):
        at = slice(f * cols, (f + 1) * cols)
        act, grad = gelu_pair(dot_nn(mid_low, w_inner[f]))
        act_ref[:, at] = low(act)
        hid_ref[:, at] = low(grad)
        tick()
    second_hat, second_inv = normalize(mid + times(act_ref[...], w_outer))
    result = low((second_hat * norms[2] + norms[3]) * kept)
    for q in range(group):
        out[q] = result[q * slots : q * slots + real]
    if real < slots:
        dy = r.cot_wide[...] * kept
    else:
        dy = cot[...].reshape(rows, -1).astype(jnp.float32) * kept
    second_dz = normalize_back(dy, second_hat, second_inv, norms[2])
    ffn_low = low(second_dz)
    ffn_ref[...] = ffn_low
    sums = [col_sum(dy * second_hat), col_sum(dy)]
    tick()
    hid_ref[...] = low(times_back(ffn_low, w_outer) * hid_ref[...].astype(jnp.float32))
    tick()
    mid_grad = second_dz + times_back(hid_ref[...], w_inner)
    first_dz = normalize_back(mid_grad, first_hat, first_inv, norms[0])
    dz_out[...] = first_dz
    branch_low = low(first_dz)
    branch_ref[...] = branch_low
    tick()
    dctx_out[...] = low(times_back(branch_low, w_out))
    sums = [col_sum(mid_grad * first_hat), col_sum(mid_grad)] + sums
    for n in range(4):
        ngrad[n : n + 1, :] += sums[n]
    tick()


def store_grad(out, x, d):
    cols = out.shape[2]
    whole = low(dot_tn(x, d))
    for f in range(out.shape[0]):
        out[f] = whole[:, f * cols : (f + 1) * cols]


def add_to(ref, mine, value):
    value = low(value).astype(jnp.float32)
    for i in range(ref.shape[0]):
        ref[i] += jnp.where(mine == i, value, 0.0)


def image_phase(first_col, norm_wide, r, step, tick):
    tick()
    group, slots, wide = r.cot.shape[0], r.image.shape[1], r.image.shape[2]

    @pl.when(step == 0)
    def _():
        targets = (r.w_io, r.w_ii, r.w_iu)
        fetch(
            [(g.reshape(w.shape), w) for g, w in zip(r.gathered[4:], targets)]
            + [(r.gathered[3], r.norm_parts)],
            r.sems,
        )
        parts = r.norm_parts.shape[0:-2]
        nf = bits_of(lax.axis_size("fsdp"))
        for i in range(math.prod(parts)):
            at, rest = [], i
            for _ in parts:
                at.append(rest % 2)
                rest //= 2
            at = at[::-1]
            f = sum(bit << k for k, bit in enumerate(reversed(at[:nf])))
            d = sum(bit << k for k, bit in enumerate(reversed(at[nf:])))
            first = (d * (1 << nf) + f) * norm_wide
            r.norms[:, first : first + norm_wide] = r.norm_parts[tuple(at)]

    for q in range(group):
        r.visual[q * slots : (q + 1) * slots, :] = r.image[own_image(r, step * group + q)]
    here = rows_at(step, group * slots)
    norms = [r.norms[n : n + 1, first_col : first_col + wide] for n in range(4)]
    stream_rows(
        r,
        step,
        tick,
        lambda p: r.region_counts[own_image(r, p)],
        r.visual,
        r.ictx.at[here],
        r.cot,
        norms,
        (r.w_io, r.w_ii, r.w_iu),
        [ref.at[here] for ref in (r.mid, r.act, r.hid, r.ffn, r.branch)],
        (r.image_out, r.image_dz, r.dctx.at[here], r.image_ngrad),
    )


def image_grads_phase(r, step, tick):
    tick()
    here = rows_at(step, r.g_io.shape[1])
    store_grad(r.g_io, r.ictx[:, here], r.branch[...])
    store_grad(r.g_ii, r.mid[:, here], r.hid[...])
    store_grad(r.g_iu, r.act[:, here], r.ffn[...])
    tick()


def back_image_phase(r, step, tick):
    tick()
    regions, length = r.iprob.shape[1:]
    heads = r.tk.shape[1] // HDIM
    columns = [slice(h * HDIM, (h + 1) * HDIM) for h in range(heads)]
    scale = 1.0 / math.sqrt(HDIM)

    @pl.when(step == 0)
    def _():
        r.diq_sum[...] = jnp.zeros_like(r.diq_sum)

    for q in range(ROW_PAIRS):
        p = step * ROW_PAIRS + q
        mine = own_image(r, p)
        here, rows_i = rows_at(p, length), rows_at(p, regions)
        local = slice(q * length, (q + 1) * length)
        dprobs = [dot_nt(r.dctx[rows_i, at], r.tv[here, at]) for at in columns]
        dvalues = [
            low(dot_tn(low(r.iprob[p * heads + h]), r.dctx[rows_i, at]))
            for h, at in enumerate(columns)
        ]
        dscores = []
        for h in range(heads):
            probs = r.iprob[p * heads + h]
            inner = jnp.sum(probs * dprobs[h], axis=1, keepdims=True)
            dscores.append(low(probs * (dprobs[h] - inner)))
        parts = [scale * dot_nn(one, r.tk[here, at]) for one, at in zip(dscores, columns)]
        add_to(r.diq_sum, mine, jnp.concatenate(parts, axis=1))
        dkeys = [
            low(scale * dot_tn(one, r.iq[mine, :, at])) for one, at in zip(dscores, columns)
        ]
        for ref, out, values in ((r.tv, r.dtv, dvalues), (r.tk, r.dtk, dkeys)):
            values = jnp.concatenate(values, axis=1)
            ref[here, :] = values
            out[local, :] = values
        tick()


def key_grads_phase(r, step, tick):
    tick()
    diq = low(r.diq_sum[...])
    r.diq[...] = diq
    here = rows_at(step, r.g_iq.shape[1])
    store_grad(r.g_iq, flat(r.image[:, :, here]), flat(diq))
    here = rows_at(step, r.g_tk.shape[1])
    store_grad(r.g_tk, r.text[:, here], r.tk[...])
    store_grad(r.g_tv, r.text[:, here], r.tv[...])
    tick()


def text_phase(r, step, tick):
    tick()
    rows = r.x.shape[0]
    here = rows_at(step, rows)
    norms = [r.norms[n : n + 1, : r.x.shape[1]] for n in range(4)]
    stream_rows(
        r,
        step,
        tick,
        lambda p: r.lens[p],
        r.x,
        r.tctx.at[here],
        r.cot,
        norms,
        (r.w_to, r.w_ti, r.w_tu),
        [ref.at[here] for ref in (r.mid, r.act, r.hid, r.ffn, r.branch)],
        (r.text_out, r.text_dz, r.dctx, r.text_ngrad),
    )


def grad_phase(out, x, d, r, step, tick):
    tick()
    out = getattr(r, out)
    here = rows_at(step, out.shape[1])
    store_grad(out, getattr(r, x)[:, here], getattr(r, d)[...])
    tick()


def back_text_phase(r, step, tick):
    tick()
    regions, length = r.tprob.shape[1:]
    heads = r.tq.shape[1] // HDIM
    columns = [slice(h * HDIM, (h + 1) * HDIM) for h in range(heads)]
    scale = 1.0 / math.sqrt(HDIM)

    @pl.when(step == 0)
    def _():
        r.dik_sum[...] = jnp.zeros_like(r.dik_sum)
        r.div_sum[...] = jnp.zeros_like(r.div_sum)

    for q in range(ROW_PAIRS):
        p = step * ROW_PAIRS + q
        mine = own_image(r, p)
        here = rows_at(p, length)
        local = slice(q * length, (q + 1) * length)
        dprobs = [dot_nt(r.iv[mine, :, at], r.dtc[local, at]) for at in columns]
        parts = [
            dot_nn(low(r.tprob[q * heads + h]), r.dtc[local, at]) for h, at in enumerate(columns)
        ]
        add_to(r.div_sum, mine, jnp.concatenate(parts, axis=1))
        dscores = []
        for h in range(heads):
            probs = r.tprob[q * heads + h]
            inner = jnp.sum(probs * dprobs[h], axis=0, keepdims=True)
            dscores.append(low(probs * (dprobs[h] - inner)))
        parts = [scale * dot_nn(one, r.tq[local, at]) for one, at in zip(dscores, columns)]
        add_to(r.dik_sum, mine, jnp.concatenate(parts, axis=1))
        parts = [
            low(scale * dot_tn(one, r.ik[mine, :, at])) for one, at in zip(dscores, columns)
        ]
        r.dtq[here, :] = jnp.concatenate(parts, axis=1)
        tick()


def query_grads_phase(r, step, tick):
    tick()
    here = rows_at(step, r.text.shape[1] // 2)
    put_half(r.g_tq, step, r.text[:, here], r.dtq[...])
    dik, div = low(r.dik_sum[...]), low(r.div_sum[...])
    r.dik[...] = dik
    r.div[...] = div
    here = rows_at(step, r.image.shape[2] // 2)
    columns = flat(r.image[:, :, here])
    put_half(r.g_ik, step, columns, flat(dik))
    put_half(r.g_iv, step, columns, flat(div))
    tick()


def data_grads_phase(r, step, tick):
    images, real = r.image_grad.shape[:2]
    pairs = r.owner.shape[0]
    slots = r.image_dz.shape[0] // pairs
    tick()

    @pl.when(step == 0)
    def _():
        for i in range(images):
            total = jnp.zeros((slots, r.image_dz.shape[1]), jnp.float32)
            for p in range(pairs):
                rows = r.image_dz[p * slots : (p + 1) * slots, :]
                total += jnp.where(own_image(r, p) == i, rows, 0.0)
            for d, w in ((r.diq, r.w_iq), (r.dik, r.w_ik), (r.div, r.w_iv)):
                total = total + times_back(d[i], w)
            r.image_grad[i] = total[:real]

    total = r.text_dz[...]
    here = rows_at(step, total.shape[0])
    for d, w in ((r.dtq.at[here], r.w_tq), (r.dtk, r.w_tk), (r.dtv, r.w_tv)):
        total = total + times_back(d[...], w)
        tick()
    r.text_grad[...] = total


def pass_kernel(count, *refs):
    for source, target in zip(refs[:count], refs[count:]):
        target[...] = source[...]


def pass_on(arrays):
    return pl.pallas_call(
        functools.partial(pass_kernel, len(arrays)),
        out_shape=[struct(a.shape, a.dtype) for a in arrays],
        in_specs=[WHOLE] * len(arrays),
        out_specs=[WHOLE] * len(arrays),
        compiler_params=pltpu.CompilerParams(vmem_limit_bytes=VMEM_LIMIT),
    )(*arrays)


def whole_weight(shard, block):
    nd, nf = mesh_bits()
    rows, cols = shard.shape
    block = block.reshape(1 << nf, rows << nd, cols)
    if cols % 128:
        block = jnp.swapaxes(block, 0, 1).reshape(1, rows << nd, cols << nf)
    return block


def device_blocks(grad, shard):
    nd, nf = mesh_bits()
    rows, cols = shard.shape
    if cols % 128:
        grad = jnp.swapaxes(grad.reshape(rows << nd, 1 << nf, cols), 0, 1)
    return grad.reshape((2,) * (nd + nf) + (rows, cols))


def norm_blocks(rows):
    nd, nf = mesh_bits()
    wide = rows.shape[1] >> (nd + nf)
    split = rows.reshape(4, 1 << nd, 1 << nf, wide).transpose(2, 1, 0, 3)
    split = jnp.pad(split, ((0, 0), (0, 0), (0, 4), (0, 128 - wide)))
    return split.reshape((2,) * (nd + nf) + (8, 128))


def body(
    text_states,
    image_states,
    text_lengths,
    region_mask,
    group_ids,
    image_query,
    image_key,
    image_value,
    text_query,
    text_key,
    text_value,
    image_output,
    text_output,
    image_inner,
    image_outer,
    text_inner,
    text_outer,
    norm_params,
    cot_text,
    cot_image,
):
    nd, nf = mesh_bits()
    lead = (2,) * (nd + nf)
    bf, f32 = jnp.bfloat16, jnp.float32
    pairs, length, width_text = text_states.shape
    images, regions, width_image = image_states.shape
    padded = -(-regions // 16) * 16
    wide = image_query.shape[1] << nf
    heads = wide // HDIM
    rows_text, rows_image = pairs * length, pairs * padded
    norm_wide = norm_params.shape[1]
    device = lax.axis_index("dp") * lax.axis_size("fsdp") + lax.axis_index("fsdp")
    owner = group_ids - device * images
    text = text_states.reshape(rows_text, width_text)
    def full(shard):
        rows, cols = shard.shape
        return pltpu.VMEM((1 << nf, rows << nd, cols), bf)

    def vmem(rows, cols, dtype=bf):
        return pltpu.VMEM((rows, cols), dtype)

    n = ROW_PAIRS
    steps = pairs // n
    group = pairs // 2
    block_i = group * padded
    gather = Gather(
        [text_key, text_value, image_query, norm_params, image_output, image_inner, image_outer]
        + [text_query, image_key, image_value, text_output, text_inner, text_outer]
    )
    phases, begin = [], [0]

    def phase(run, count, marks, **kw):
        phases.append(Phase(run, count, marks, **kw))
        begin.append(begin[-1] + count)
        return begin[-2]

    phase(project_keys_phase, steps, (0.0, 1.7), needs=range(3))
    phase(attend_image_phase, steps, (0.0, 0.9, 1.8))
    stages = 1 << nf
    marks = [0.0, 1.1] + [1.1 + 1.0 * (k + 1) / stages for k in range(stages)]
    marks += [3.3, 4.4, 5.7, 6.4]
    at_image = phase(
        functools.partial(image_phase, width_text, norm_wide), 2, marks, needs=range(3, 7)
    )
    at_image_grads = phase(image_grads_phase, 4, (0.0, 1.0))
    at_back = phase(back_image_phase, steps, (0.0, 0.8, 1.7))
    at_grads = phase(key_grads_phase, 2, (0.0, 2.4))
    at_attend = phase(attend_text_phase, steps, (0.0, 0.8, 1.7, 2.6), needs=range(7, 10))
    third = width_text // 3

    def grad_out(weight_shard, inner, first, count, size):
        shape = (1 << nf, inner, weight_shard.shape[1])
        if weight_shard.shape[1] % 128:
            shape = (1, inner, weight_shard.shape[1] << nf)
        block = (shape[0], size, shape[2])
        return (struct(shape, bf), during(first, count, block, 1))

    by_pair = during(at_image, 2, (group, regions, width_image))
    probs = during(at_attend, steps, (n * heads, padded, length))
    pair_rows = during(at_attend, steps, (n * length, wide))
    back_rows = during(at_back, steps, (n * length, wide))
    image_shape = (images, padded, wide)
    a = carry(
        phases,
        dict(
            lens=(text_lengths, SCALARS),
            owner=(owner, SCALARS),
            mask=(region_mask, SCALARS),
            text=resident(text),
            states=resident(image_states),
            cot=(cot_image, by_pair),
        ),
        dict(
            ik=(struct(image_shape, bf), fixed(image_shape)),
            iv=(struct(image_shape, bf), fixed(image_shape)),
            tq=(struct((rows_text, wide), bf), pair_rows),
            tprob=(struct((pairs * heads, padded, length), f32), probs),
            tctx=(struct((rows_text, wide), bf), pair_rows),
            image_rows=(
                struct((images, padded, width_image), bf),
                fixed((images, padded, width_image)),
            ),
            norms=(struct((4, norm_wide << (nd + nf)), f32), fixed((4, norm_wide << (nd + nf)))),
            image_out=(struct(cot_image.shape, bf), by_pair),
            image_dz=(
                struct((rows_image, width_image), f32),
                during(at_image, 2, (block_i, width_image)),
            ),
            image_ngrad=(struct((4, width_image), f32), fixed((4, width_image))),
            dtk=(struct((rows_text, wide), bf), back_rows),
            dtv=(struct((rows_text, wide), bf), back_rows),
            diq=(struct(image_shape, bf), fixed(image_shape)),
            g_io=grad_out(image_output, wide, at_image_grads, 4, wide // 4),
            g_ii=grad_out(image_inner, width_image, at_image_grads, 4, width_image // 4),
            g_iu=grad_out(image_outer, width_image, at_image_grads, 4, width_image // 4),
            g_iq=grad_out(image_query, width_image, at_grads, 2, width_image // 2),
            g_tk=grad_out(text_key, width_text, at_grads, 2, width_text // 2),
            g_tv=grad_out(text_value, width_text, at_grads, 2, width_text // 2),
        ),
        dict(
            w_tq=full(text_query),
            w_tk=full(text_key),
            w_tv=full(text_value),
            w_iq=full(image_query),
            w_ik=full(image_key),
            w_iv=full(image_value),
            w_io=full(image_output),
            w_ii=full(image_inner),
            w_iu=full(image_outer),
            image=pltpu.VMEM((images, padded, width_image), bf),
            visual=vmem(block_i, width_image),
            region_counts=pltpu.SMEM((images,), jnp.int32),
            norm_parts=pltpu.VMEM(lead + norm_params.shape, f32),
            sems=pltpu.SemaphoreType.DMA((4,)),
            iq=pltpu.VMEM(image_shape, bf),
            tk=vmem(rows_text, wide),
            tv=vmem(rows_text, wide),
            iprob=pltpu.VMEM((pairs * heads, padded, length), f32),
            ictx=vmem(rows_image, wide),
            mid=vmem(rows_image, width_image),
            act=vmem(rows_image, width_image),
            hid=vmem(rows_image, width_image),
            ffn=vmem(rows_image, width_image),
            branch=vmem(rows_image, width_image),
            dctx=vmem(rows_image, wide),
            diq_sum=pltpu.VMEM(image_shape, f32),
            cot_wide=vmem(block_i, width_image, f32),
        ),
        gather,
        0,
        SEARCH,
    )
    whole = [whole_weight(s, g) for s, g in zip(gather.given, a.landed) if s is not norm_params]
    w_tk, w_tv, w_iq, _, _, _, w_tq, w_ik, w_iv, w_to, w_ti, w_tu = whole

    job = Reduce(
        [
            device_blocks(grad, shard)
            for grad, shard in (
                (a.g_io, image_output),
                (a.g_ii, image_inner),
                (a.g_iu, image_outer),
                (a.g_iq, image_query),
                (a.g_tk, text_key),
                (a.g_tv, text_value),
            )
        ]
    )
    phases, begin = [], [0]
    inner = w_ti.shape[0] * w_ti.shape[2]
    block_t = n * length
    stages = w_ti.shape[0]
    marks = [0.0, 1.6] + [1.6 + 3.6 * (k + 1) / stages for k in range(stages)]
    marks += [7.8, 9.8, 11.8, 12.6]
    at_text = phase(text_phase, steps, marks)
    at_tu = phase(functools.partial(grad_phase, "g_tu", "act", "ffn"), 12, (0.0, 0.7))
    at_ti = phase(functools.partial(grad_phase, "g_ti", "mid", "hid"), 6, (0.0, 1.4))
    at_to = phase(functools.partial(grad_phase, "g_to", "tctx", "branch"), 4, (0.0, 0.8))
    by_pair = during(at_text, steps, (n, length, width_text))

    def text_rows(cols):
        return during(at_text, steps, (block_t, cols))

    b = carry(
        phases,
        dict(
            lens=(text_lengths, SCALARS),
            x=(text, text_rows(width_text)),
            tctx=resident(a.tctx),
            cot=(cot_text, by_pair),
            norms=resident(a.norms),
            w_to=resident(w_to),
            w_ti=resident(w_ti),
            w_tu=resident(w_tu),
        ),
        dict(
            text_out=(struct(cot_text.shape, bf), by_pair),
            text_dz=(struct((rows_text, width_text), f32), text_rows(width_text)),
            dctx=(struct((rows_text, wide), bf), text_rows(wide)),
            text_ngrad=(struct((4, width_text), f32), fixed((4, width_text))),
            g_tu=grad_out(text_outer, inner, at_tu, 12, inner // 12),
            g_ti=grad_out(text_inner, width_text, at_ti, 6, width_text // 6),
            g_to=grad_out(text_output, wide, at_to, 4, wide // 4),
        ),
        dict(
            mid=vmem(rows_text, width_text),
            act=vmem(rows_text, inner),
            hid=vmem(rows_text, inner),
            ffn=vmem(rows_text, width_text),
            branch=vmem(rows_text, width_text),
        ),
        job,
        1,
    )
    o_io, o_ii, o_iu, o_iq, o_tk, o_tv = b.landed

    norm_rows = norm_blocks(jnp.concatenate([b.text_ngrad, a.image_ngrad], axis=1))
    job = Reduce(
        [
            device_blocks(b.g_tu, text_outer),
            device_blocks(b.g_ti, text_inner),
            device_blocks(b.g_to, text_output),
            norm_rows,
        ],
        dict(
            g_tq=struct(lead + text_query.shape, bf),
            g_ik=struct(lead + image_key.shape, bf),
            g_iv=struct(lead + image_value.shape, bf),
        ),
    )
    phases, begin = [], [0]
    at_back = phase(back_text_phase, steps, (0.0, 0.8, 1.7))
    phase(query_grads_phase, 2, (0.0, 2.0), makes=range(4, 7))
    at_data = phase(data_grads_phase, steps, (0.0, 0.9, 1.8, 2.6))
    probs = during(at_back, steps, (n * heads, padded, length))
    back_rows = during(at_back, steps, (n * length, wide))
    data_rows = during(at_data, steps, (block_t, wide))
    data_out = during(at_data, steps, (block_t, width_text))
    c = carry(
        phases,
        dict(
            owner=(owner, SCALARS),
            ik=resident(a.ik),
            iv=resident(a.iv),
            tq=(a.tq, back_rows),
            tprob=(a.tprob, probs),
            dtc=(b.dctx, back_rows),
            text=resident(text),
            image=resident(a.image_rows),
            text_dz=(b.text_dz, data_out),
            dtk=(a.dtk, data_rows),
            dtv=(a.dtv, data_rows),
            image_dz=resident(a.image_dz),
            diq=resident(a.diq),
            w_tq=resident(w_tq),
            w_tk=resident(w_tk),
            w_tv=resident(w_tv),
            w_iq=resident(w_iq),
            w_ik=resident(w_ik),
            w_iv=resident(w_iv),
        ),
        dict(
            text_grad=(struct((rows_text, width_text), f32), data_out),
            image_grad=(struct(image_states.shape, f32), fixed(image_states.shape)),
        ),
        dict(
            dtq=vmem(rows_text, wide),
            dik=pltpu.VMEM(image_shape, bf),
            div=pltpu.VMEM(image_shape, bf),
            dik_sum=pltpu.VMEM(image_shape, f32),
            div_sum=pltpu.VMEM(image_shape, f32),
            g_tq=pltpu.VMEM(lead + text_query.shape, bf),
            g_ik=pltpu.VMEM(lead + image_key.shape, bf),
            g_iv=pltpu.VMEM(lead + image_value.shape, bf),
        ),
        job,
        2,
        SEARCH,
    )
    o_tu, o_ti, o_to, o_norm, o_tq, o_ik, o_iv = c.landed
    owned = pass_on([o_iq, o_ik, o_iv, o_tq, o_tk, o_tv, o_io, o_to, o_ii, o_iu, o_ti, o_tu])
    return (
        b.text_out,
        a.image_out,
        c.text_grad.reshape(text_states.shape),
        c.image_grad,
        *owned,
        o_norm[:4, :norm_wide],
    )


def solution(mesh):
    placed = (
        P(("dp", "fsdp"), None, None),
        P(("dp", "fsdp"), None, None),
        P(("dp", "fsdp")),
        P(("dp", "fsdp"), None),
        P(("dp", "fsdp")),
        P("dp", "fsdp"),
        P("dp", "fsdp"),
        P("dp", "fsdp"),
        P("dp", "fsdp"),
        P("dp", "fsdp"),
        P("dp", "fsdp"),
        P("dp", "fsdp"),
        P("dp", "fsdp"),
        P("dp", "fsdp"),
        P("dp", "fsdp"),
        P("dp", "fsdp"),
        P("dp", "fsdp"),
        P(None, ("dp", "fsdp")),
        P(("dp", "fsdp"), None, None),
        P(("dp", "fsdp"), None, None),
    )
    return jax.shard_map(
        body,
        mesh=mesh,
        in_specs=placed,
        out_specs=(
            P(("dp", "fsdp"), None, None),
            P(("dp", "fsdp"), None, None),
            P(("dp", "fsdp"), None, None),
            P(("dp", "fsdp"), None, None),
            P("dp", "fsdp"),
            P("dp", "fsdp"),
            P("dp", "fsdp"),
            P("dp", "fsdp"),
            P("dp", "fsdp"),
            P("dp", "fsdp"),
            P("dp", "fsdp"),
            P("dp", "fsdp"),
            P("dp", "fsdp"),
            P("dp", "fsdp"),
            P("dp", "fsdp"),
            P("dp", "fsdp"),
            P(None, ("dp", "fsdp")),
        ),
        check_vma=False,
    )
```

```python
import functools
import itertools
import math
import random

import jax
import jax.numpy as jnp
from jax import lax
from jax.experimental import pallas as pl
from jax.experimental.pallas import tpu as pltpu
from jax.sharding import PartitionSpec as P

HDIM = 128

norm_eps = 1e-12
masked_score = -1e30

MESH_IDS = pl.DeviceIdType.MESH
VMEM_LIMIT = 63 * 1024 * 1024
WHOLE = pl.BlockSpec(memory_space=pltpu.VMEM)
SCALARS = pl.BlockSpec(memory_space=pltpu.SMEM)
ANYWHERE = pl.BlockSpec(memory_space=pl.ANY)
CORE = ("d", 0)


def bits_of(size):
    count = size.bit_length() - 1
    assert 1 << count == size
    return count


def mesh_bits():
    return bits_of(lax.axis_size("dp")), bits_of(lax.axis_size("fsdp"))


def hop_orders(nd, nf):
    high = [("d", b) for b in range(nd - 1, 2, -1)]
    low = [("d", 2)]
    near = [("d", 1)]
    wide = [("f", b) for b in range(nf)]
    first = [(low, near, high, wide), (high, wide, low, near)]
    rest = [p for p in itertools.permutations((low, near, high, wide)) if p not in first]
    return [tuple(bit for group in order for bit in group) for order in first + rest]


def cut_pieces(shapes):
    pieces, ranks, large = [], [], 0
    for m, (rows, cols) in enumerate(shapes):
        count = 4 if rows * cols > 40000 else 2
        if rows % (16 * count) == 0:
            each = rows // count
            cuts = [(k * each, each, 0, cols) for k in range(count)]
        elif cols % (128 * count) == 0 and rows % 8 == 0:
            each = cols // count
            cuts = [(0, rows, k * each, each) for k in range(count)]
        else:
            cuts = [(0, rows, 0, cols)]
        for cut in cuts:
            pieces.append((m, *cut, large % 2))
            small = rows * cols < 2048
            ranks.append(0 if small else large)
            large += 0 if small else 1
    return pieces, ranks


class Place:
    def __init__(self, nd, nf):
        self.d = lax.axis_index("dp")
        self.f = lax.axis_index("fsdp")
        self.axes = [("f", b) for b in range(nf - 1, -1, -1)] + [
            ("d", b) for b in range(nd - 1, -1, -1)
        ]

    def bit(self, axis):
        value = self.f if axis[0] == "f" else self.d
        return lax.rem(value // (1 << axis[1]), 2)

    def partner(self, axis):
        step = (1 << axis[1]) * (1 - 2 * self.bit(axis))
        if axis[0] == "f":
            return (self.d, self.f + step)
        return (self.d + step, self.f)

    def index(self, whole, flip=None):
        picked = []
        for axis in self.axes:
            if axis in whole:
                picked.append(slice(None))
            elif axis == flip:
                picked.append(1 - self.bit(axis))
            else:
                picked.append(self.bit(axis))
        return tuple(picked)

    def barrier(self):
        sem = pltpu.get_barrier_semaphore()
        for axis in self.axes:
            pl.semaphore_signal(
                sem, inc=1, device_id=self.partner(axis), device_id_type=MESH_IDS
            )
        pl.semaphore_wait(sem, len(self.axes))


class Gather:
    def __init__(self, arrays):
        self.arrays = arrays
        self.given = arrays
        self.made = []
        self.adds = False
        self.nd, self.nf = mesh_bits()
        self.orders = [order + (CORE,) for order in hop_orders(self.nd, self.nf)]
        self.cuts, self.ranks = cut_pieces([a.shape for a in arrays])
        self.routes = [self.orders[cut[-1]] for cut in self.cuts]
        self.hops = self.nd + self.nf
        lead = (2,) * self.hops
        self.out_shape = [jax.ShapeDtypeStruct(lead + a.shape, a.dtype) for a in arrays]
        self.out_specs = [ANYWHERE] * len(arrays)
        count = len(self.cuts)
        self.scratch = [
            pltpu.SemaphoreType.DMA((count,)),
            pltpu.SemaphoreType.DMA((count, self.hops)),
            pltpu.SemaphoreType.DMA((count, self.hops)),
        ]

    def sizes(self, k):
        m, row, rows, col, cols, _ = self.cuts[k]
        block = rows * cols * self.arrays[m].dtype.itemsize
        return [block << h for h in range(self.hops)]

    def window(self, k):
        m, row, rows, col, cols, _ = self.cuts[k]
        return (pl.ds(row, rows), pl.ds(col, cols))

    def bind(self, place, ins, outs, scratch):
        self.place, self.ins, self.outs = place, ins, outs
        self.local_sem, self.send_sem, self.recv_sem = scratch

    def local(self, k):
        m = self.cuts[k][0]
        return pltpu.make_async_copy(
            self.ins[m].at[self.window(k)],
            self.outs[m].at[self.place.index(()) + self.window(k)],
            self.local_sem.at[k],
        )

    def hop(self, k, h):
        m, route = self.cuts[k][0], self.routes[k]
        region = self.outs[m].at[self.place.index(route[:h]) + self.window(k)]
        return pltpu.make_async_remote_copy(
            src_ref=region,
            dst_ref=region,
            send_sem=self.send_sem.at[k, h],
            recv_sem=self.recv_sem.at[k, h],
            device_id=self.place.partner(route[h]),
            device_id_type=MESH_IDS,
        )

    def start(self):
        for k in range(len(self.cuts)):
            self.local(k).start()

    def step(self, k, h):
        if h == 0:
            self.local(k).wait()
        else:
            self.hop(k, h - 1).wait_recv()
        if h < self.hops:
            self.hop(k, h).start()
        else:
            for g in range(self.hops):
                self.hop(k, g).wait_send()


def add_blocks(acc, index, window, incoming):
    lead = incoming.shape[:-2]
    outer, inner = lead[:-2], lead[-2:]

    def one(i, carry):
        first = []
        for size in reversed(outer):
            first.append(lax.rem(i, size))
            i = i // size
        first = first[::-1]
        for j in range(math.prod(inner)):
            at, rest = [], j
            for size in reversed(inner):
                at.append(rest % size)
                rest //= size
            at = tuple(first + at[::-1])
            left = list(at)
            where = tuple(left.pop(0) if isinstance(p, slice) else p for p in index) + window
            acc[where] = acc[where] + incoming[at]
        return carry

    lax.fori_loop(0, math.prod(outer), one, 0)


class Reduce:
    def __init__(self, given, made=None):
        made = made or {}
        self.given = given
        self.made = list(made)
        self.adds = True
        arrays = list(given) + list(made.values())
        self.arrays = arrays
        self.nd, self.nf = mesh_bits()
        self.orders = [(CORE,) + order[::-1] for order in hop_orders(self.nd, self.nf)]
        self.hops = self.nd + self.nf
        self.cuts, self.ranks = cut_pieces([a.shape[-2:] for a in arrays])
        self.routes = [self.orders[cut[-1]] for cut in self.cuts]
        self.scratch = []
        for m, row, rows, col, cols, _ in self.cuts:
            for h in range(-1 if m < len(self.given) else 0, self.hops):
                free = self.hops - 1 - max(h, 0)
                self.scratch.append(pltpu.VMEM((2,) * free + (rows, cols), arrays[m].dtype))
        count = len(self.cuts)
        self.scratch += [
            pltpu.SemaphoreType.DMA((count,)),
            pltpu.SemaphoreType.DMA((count, self.hops)),
            pltpu.SemaphoreType.DMA((count, self.hops)),
        ]
        shapes = [a.shape[-2:] for a in arrays]
        self.out_shape = [jax.ShapeDtypeStruct(s, jnp.float32) for s in shapes]
        self.out_specs = [pl.BlockSpec(s, lambda *_: (0, 0)) for s in shapes]

    def sizes(self, k):
        m, row, rows, col, cols, _ = self.cuts[k]
        block = rows * cols * self.arrays[m].dtype.itemsize
        return [block << (self.hops - 1 - h) for h in range(self.hops)]

    def window(self, k):
        m, row, rows, col, cols, _ = self.cuts[k]
        return (pl.ds(row, rows), pl.ds(col, cols))

    def bind(self, place, ins, outs, scratch):
        self.place, self.ins, self.outs = place, ins, outs
        self.local_sem, self.send_sem, self.recv_sem = scratch[-3:]
        rest = list(scratch[:-3])
        self.accs, self.temps = [], []
        for m, *_ in self.cuts:
            self.accs.append(rest.pop(0) if m < len(self.given) else None)
            self.temps.append([rest.pop(0) for _ in range(self.hops)])
        self.rest = [axis for axis in place.axes if axis != CORE]

    def local(self, k):
        source = self.ins[self.cuts[k][0]].at[self.place.index(self.rest) + self.window(k)]
        return pltpu.make_async_copy(source, self.accs[k], self.local_sem.at[k])

    def within(self, k, h, flip=None):
        full = self.place.index(self.routes[k][h + 1 :], flip)
        if self.accs[k] is None:
            m, row, rows, col, cols, _ = self.cuts[k]
            return self.ins[m], full, (slice(row, row + rows), slice(col, col + cols))
        return self.accs[k], tuple(p for p, a in zip(full, self.place.axes) if a != CORE), ()

    def hop(self, k, h):
        m, route = self.cuts[k][0], self.routes[k]
        if h == 0:
            region = self.ins[m].at[self.place.index(route[1:], CORE) + self.window(k)]
        else:
            acc, index, window = self.within(k, h, route[h])
            region = acc.at[index + window]
        return pltpu.make_async_remote_copy(
            src_ref=region,
            dst_ref=self.temps[k][h],
            send_sem=self.send_sem.at[k, h],
            recv_sem=self.recv_sem.at[k, h],
            device_id=self.place.partner(route[h]),
            device_id_type=MESH_IDS,
        )

    def start(self):
        pass

    def step(self, k, h):
        own = self.accs[k] is not None
        if h == 0 and own:
            self.local(k).start()
        if h > 0:
            self.hop(k, h - 1).wait_recv()
            if h == 1 and own:
                self.local(k).wait()
            acc, index, window = self.within(k, h - 1)
            if h < self.hops:
                add_blocks(acc, index, window, self.temps[k][h - 1])
            else:
                m, row, rows, col, cols, _ = self.cuts[k]
                last = acc[index + window].astype(jnp.float32)
                last = last + self.temps[k][h - 1][...].astype(jnp.float32)
                self.outs[m][row : row + rows, col : col + cols] = last
        if h < self.hops:
            self.hop(k, h).start()
        else:
            for g in range(self.hops):
                self.hop(k, g).wait_send()


LINK_RATE = 46e3
CORE_RATE = 380e3
LATENCY = 3.2
ENTRY = 3.0
ISSUE = 0.06
ADD_RATE = 1800e3
SEARCH = 1500


class Phase:
    def __init__(self, run, steps, marks, needs=(), makes=()):
        self.run, self.steps, self.marks = run, steps, marks
        self.needs, self.makes = set(needs), set(makes)


def place_steps(order, job, times, clock, limits, after, counted=True):
    total = len(times)
    limit = [total] * len(order)
    for needs, begin in limits:
        last = -1
        for i, (k, h) in enumerate(order):
            if h == job.hops and job.cuts[k][0] in needs:
                last = i
        for i in range(last + 1):
            limit[i] = min(limit[i], begin)
    waiting, active, done = {}, {}, {}
    now = 0.0

    def advance(key, until):
        nonlocal now
        while key not in done and now < until:
            for axis, queue in waiting.items():
                if queue and axis not in active:
                    active[axis] = queue.pop(0)
            far = any(axis[0] == "d" and axis[1] > 2 for axis in active)
            rates, span = {}, until - now
            for axis, (_, left) in active.items():
                halved = far and axis[0] == "d" and axis[1] > 1
                rates[axis] = CORE_RATE if axis == CORE else LINK_RATE / (2 if halved else 1)
                span = min(span, left / rates[axis])
            now += span
            for axis in list(active):
                active[axis][1] -= span * rates[axis]
                if active[axis][1] <= 1e-3:
                    done[active.pop(axis)[0]] = now + LATENCY

    slots = [[] for _ in range(total)]
    tail = []
    at, late, started = 0, ENTRY if counted else 0.0, 0.0
    for i, (k, h) in enumerate(order):
        ready = now
        if h:
            advance((k, h - 1), math.inf)
            ready = max(ready, done[k, h - 1])
        else:
            at = max(at, after.get(job.cuts[k][0], 0))
        while at < min(limit[i], total) and times[at] + late < ready - 0.3:
            at += 1
        spent = ISSUE + (job.sizes(k)[h - 1] / ADD_RATE if h and job.adds else 0.0)
        spent = spent if counted else 0.0
        if at < total:
            slots[at].append((k, h))
            ready = max(ready, times[at] + late) + spent
            late = ready - times[at]
        else:
            ready = max(ready, clock + late) + spent
            tail.append((k, h))
        started += ready
        advance(None, ready)
        if h < job.hops:
            waiting.setdefault(job.routes[k][h], []).append([(k, h), float(job.sizes(k)[h])])
    end = max(now, clock + late)
    return end + 0.2 * max(done.values()) + 0.1 * started / len(order), slots, tail


def plan_steps(job, phases, search):
    times, limits, after = [], [], {}
    clock = 0.0
    for phase in phases:
        limits.append((phase.needs, len(times)))
        for _ in range(phase.steps):
            times += [clock + mark for mark in phase.marks]
            clock += phase.marks[-1]
        for m in phase.makes:
            after[m] = len(times)
    known = (job, times, clock, limits, after)

    def waves(width, lag):
        order = []
        for k, rank in enumerate(job.ranks):
            wave = rank // width + (lag if job.cuts[k][0] in after else 0)
            order += [(wave + h, wave, k, h) for h in range(job.hops + 1)]
        return [(k, h) for _, _, k, h in sorted(order)]

    if not search:
        return place_steps(waves(4, 0), *known, False)[1:]
    lags = range(4) if after else (0,)
    starts = [waves(width, lag) for width in (3, 4, 5, 6) for lag in lags]
    best, order = min((place_steps(start, *known)[0], start) for start in starts)
    draw = random.Random(1)
    for _ in range(search):
        if draw.random() < 0.3:
            k = draw.randrange(len(job.cuts))
            kept = job.routes[k]
            job.routes[k] = draw.choice(job.orders)
            cost = place_steps(order, *known)[0]
            if cost < best:
                best = cost
            else:
                job.routes[k] = kept
            continue
        i = draw.randrange(len(order))
        k, h = order[i]
        low_end = order.index((k, h - 1)) + 1 if h else 0
        high_end = order.index((k, h + 1)) - 1 if h < job.hops else len(order) - 1
        j = draw.randint(max(low_end, i - 12), max(low_end, min(high_end, i + 12)))
        moved = list(order)
        moved.insert(j, moved.pop(i))
        cost = place_steps(moved, *known)[0]
        if cost < best:
            best, order = cost, moved
    return place_steps(order, *known)[1:]


class Names:
    def __init__(self, names, refs):
        for name, ref in zip(names, refs):
            setattr(self, name, ref)


def carrying_kernel(phases, job, plan, names, *refs):
    spans, start = [], 0
    for count in [len(group) for group in names]:
        spans.append(refs[start : start + count])
        start += count
    own_in, job_in, own_out, job_out, own_scratch, job_scratch = spans
    r = Names(names[0] + names[2] + names[4], own_in + own_out + own_scratch)
    now = pl.program_id(0)
    slots, tail = plan
    place = Place(job.nd, job.nf)
    r.gathered = job_out
    made = [getattr(r, name) for name in job.made]
    job.bind(place, list(job_in) + made, job_out, job_scratch)

    def run(items, opening=False):
        if opening:
            job.start()
            place.barrier()
        for k, h in items:
            job.step(k, h)

    base, begin = 0, 0
    for phase in phases:
        ticks = len(phase.marks)

        def one(phase=phase, base=base, begin=begin, ticks=ticks):
            passed = [0]

            def tick():
                t = passed[0]
                passed[0] += 1
                for s in range(phase.steps):
                    items = slots[base + s * ticks + t]
                    opening = base + s * ticks + t == 0
                    if items or opening:
                        pl.when(now == begin + s)(functools.partial(run, items, opening))

            phase.run(r, now - begin, tick)
            assert passed[0] == ticks

        pl.when((now >= begin) & (now < begin + phase.steps))(one)
        base += ticks * phase.steps
        begin += phase.steps
    if tail:
        pl.when(now == begin - 1)(functools.partial(run, tail))


def carry(phases, ins, outs, scratch, job, ident, search=0):
    plan = plan_steps(job, phases, search)
    given, landed, worked = list(job.given), list(job.out_shape), list(job.scratch)
    names = (
        list(ins),
        [None] * len(given),
        list(outs),
        [None] * len(landed),
        list(scratch),
        [None] * len(worked),
    )
    results = pl.pallas_call(
        functools.partial(carrying_kernel, phases, job, plan, names),
        grid=(sum(phase.steps for phase in phases),),
        in_specs=[spec for _, spec in ins.values()] + [ANYWHERE] * len(given),
        out_specs=[spec for _, spec in outs.values()] + list(job.out_specs),
        out_shape=[shape for shape, _ in outs.values()] + landed,
        scratch_shapes=list(scratch.values()) + worked,
        compiler_params=pltpu.CompilerParams(
            collective_id=ident, has_side_effects=True, vmem_limit_bytes=VMEM_LIMIT
        ),
    )(*[array for array, _ in ins.values()], *given)
    r = Names(list(outs), results)
    r.landed = results[len(outs) :]
    return r


def dot_nn(a, b):
    return lax.dot_general(a, b, (((1,), (0,)), ((), ())), preferred_element_type=jnp.float32)


def dot_nt(a, b):
    return lax.dot_general(a, b, (((1,), (1,)), ((), ())), preferred_element_type=jnp.float32)


def dot_tn(a, b):
    return lax.dot_general(a, b, (((0,), (0,)), ((), ())), preferred_element_type=jnp.float32)


def low(value):
    return value.astype(jnp.bfloat16)


def times(value, matrix):
    parts = [dot_nn(value, matrix[f]) for f in range(matrix.shape[0])]
    return parts[0] if len(parts) == 1 else jnp.concatenate(parts, axis=1)


def times_back(value, matrix):
    cols = matrix.shape[2]
    total = None
    for f in range(matrix.shape[0]):
        term = dot_nt(value[:, f * cols : (f + 1) * cols], matrix[f])
        total = term if total is None else total + term
    return total


def fixed(shape):
    return pl.BlockSpec(shape, lambda i: (0,) * len(shape))


def resident(array):
    zeros = (0,) * array.ndim
    return (array, pl.BlockSpec(array.shape, lambda i: zeros, pipeline_mode=pl.Buffered(1)))


def during(begin, steps, block, axis=0):
    def index(i):
        at = jnp.minimum(jnp.maximum(i - begin, 0), steps - 1)
        return tuple(at if d == axis else 0 for d in range(len(block)))

    return pl.BlockSpec(block, index)


def struct(shape, dtype):
    return jax.ShapeDtypeStruct(shape, dtype)


def rows_at(step, size):
    return pl.ds(pl.multiple_of(step * size, size), size)


def fetch(pairs, sems):
    copies = [
        pltpu.make_async_copy(source, target, sems.at[n])
        for n, (source, target) in enumerate(pairs)
    ]
    for copy in copies:
        copy.start()
    for copy in copies:
        copy.wait()


def coming(r, names):
    return [
        pltpu.make_async_copy(getattr(r, "far_" + name), getattr(r, name), r.sems.at[n])
        for n, name in names
    ]


def start_all(copies):
    for copy in copies:
        copy.start()


def wait_all(copies):
    for copy in copies:
        copy.wait()


def at_first(step, act, copies):
    pl.when(step == 0)(functools.partial(act, copies))


TEXT_FAR = ((0, "w_ti"), (1, "w_tu"))
LAST_FAR = tuple(
    enumerate(("text", "image_dz", "w_iq", "w_ik", "w_iv", "w_tq", "w_tk", "w_tv"))
)


ROW_PAIRS = 2


def softmax(scores, axis):
    top = jnp.max(scores, axis=axis, keepdims=True)
    weight = jnp.exp(scores - top)
    return weight * (1.0 / jnp.sum(weight, axis=axis, keepdims=True))


def gelu_pair(x):
    below = 0.5 + 0.5 * lax.erf(x * (1.0 / math.sqrt(2.0)))
    bell = jnp.exp(-0.5 * x * x) * (1.0 / math.sqrt(2.0 * math.pi))
    return x * below, below + x * bell


def row_mean(value):
    return jnp.mean(value, axis=-1, keepdims=True)


def col_sum(value):
    return jnp.sum(value, axis=0, keepdims=True)


def own_image(r, p):
    return r.owner[p]


def flat(ref):
    return ref.reshape(-1, ref.shape[-1])


def merged(ref, blocks, rows):
    return ref.reshape(blocks, rows, ref.shape[-1])


def put_half(out, half, x, d):
    cols = out.shape[-1]
    nf = bits_of(lax.axis_size("fsdp"))
    whole = low(dot_tn(x, d))
    for f in range(1 << nf):
        at = tuple((f >> b) % 2 for b in range(nf - 1, -1, -1))
        part = whole[:, f * cols : (f + 1) * cols]
        out[at + (half,)] = part.reshape(out.shape[nf + 1 :])


def project_keys_phase(r, step, tick):
    tick()

    @pl.when(step == 0)
    def _():
        targets = (r.w_tk, r.w_tv, r.w_iq)
        fetch([(g.reshape(w.shape), w) for g, w in zip(r.gathered, targets)], r.sems)
        images, real = r.states.shape[:2]
        r.image[...] = jnp.zeros_like(r.image)
        for i in range(images):
            r.image[i, :real, :] = r.states[i]
            r.region_counts[i] = lax.fori_loop(
                0, real, lambda k, total, i=i: total + r.mask[i, k], 0
            )
        r.image_rows[...] = r.image[...]
        r.iq[...] = low(times(flat(r.image[...]), r.w_iq)).reshape(r.iq.shape)

    here = rows_at(step, r.text.shape[0] // r.owner.shape[0] * ROW_PAIRS)
    rows = r.text[here, :]
    r.tk[here, :] = low(times(rows, r.w_tk))
    r.tv[here, :] = low(times(rows, r.w_tv))
    tick()


def attend_image_phase(r, step, tick):
    tick()
    regions, length = r.iprob.shape[1:]
    heads = r.tk.shape[1] // HDIM
    columns = [slice(h * HDIM, (h + 1) * HDIM) for h in range(heads)]
    scale = 1.0 / math.sqrt(HDIM)
    for q in range(ROW_PAIRS):
        p = step * ROW_PAIRS + q
        mine = own_image(r, p)
        here, rows_i = rows_at(p, length), rows_at(p, regions)
        kept = lax.broadcasted_iota(jnp.int32, (regions, length), 1) < r.lens[p]
        scores = [scale * dot_nt(r.iq[mine, :, at], r.tk[here, at]) for at in columns]
        probs = [softmax(jnp.where(kept, one, masked_score), 1) for one in scores]
        for h in range(heads):
            r.iprob[p * heads + h] = probs[h]
        parts = [low(dot_nn(low(one), r.tv[here, at])) for one, at in zip(probs, columns)]
        r.ictx[rows_i, :] = jnp.concatenate(parts, axis=1)
        tick()


def attend_text_phase(r, step, tick):
    tick()

    @pl.when(step == 0)
    def _():
        targets = (r.w_tq, r.w_ik, r.w_iv)
        fetch([(g.reshape(w.shape), w) for g, w in zip(r.gathered[7:], targets)], r.sems)
        rows = flat(r.image[...])
        for w, out in ((r.w_ik, r.ik), (r.w_iv, r.iv)):
            out[...] = low(times(rows, w)).reshape(out.shape)

    regions, length = r.tprob.shape[1:]
    heads = r.tq.shape[1] // HDIM
    columns = [slice(h * HDIM, (h + 1) * HDIM) for h in range(heads)]
    scale = 1.0 / math.sqrt(HDIM)
    r.tq[...] = low(times(r.text[rows_at(step, r.tq.shape[0]), :], r.w_tq))
    tick()
    for q in range(ROW_PAIRS):
        mine = own_image(r, step * ROW_PAIRS + q)
        here = slice(q * length, (q + 1) * length)
        row = lax.broadcasted_iota(jnp.int32, (regions, length), 0)
        kept = row < r.region_counts[mine]
        scores = [scale * dot_nt(r.ik[mine, :, at], r.tq[here, at]) for at in columns]
        probs = [softmax(jnp.where(kept, one, masked_score), 0) for one in scores]
        for h in range(heads):
            r.tprob[q * heads + h] = probs[h]
        parts = [low(dot_tn(low(one), r.iv[mine, :, at])) for one, at in zip(probs, columns)]
        r.tctx[here, :] = jnp.concatenate(parts, axis=1)
        tick()


def stream_rows(r, step, tick, limits, x, ctx, cot, norms, weights, keeps, outs, waits=()):
    w_out, w_inner, w_outer = weights
    mid_ref, act_ref, hid_ref, ffn_ref, branch_ref = keeps
    out, dz_out, dctx_out, ngrad = outs
    rows = x.shape[0]
    group, real = cot.shape[:2]
    slots = rows // group

    def normalize(z):
        offset = z - row_mean(z)
        inv = lax.rsqrt(row_mean(offset * offset) + norm_eps)
        return offset * inv, inv

    def normalize_back(dy, xhat, inv, gain):
        dx = dy * gain
        return inv * (dx - row_mean(dx) - xhat * row_mean(dx * xhat))

    @pl.when(step == 0)
    def _():
        ngrad[...] = jnp.zeros_like(ngrad)
        if real < slots:
            r.cot_wide[...] = jnp.zeros_like(r.cot_wide)

    row = lax.broadcasted_iota(jnp.int32, (rows, 1), 0)
    kept = row < 0
    for q in range(group):
        inside = (row >= q * slots) & (row < q * slots + limits(step * group + q))
        kept = kept | inside
        if real < slots:
            r.cot_wide[q * slots : q * slots + real, :] = cot[q].astype(jnp.float32)
    kept = kept.astype(jnp.float32)
    first_hat, first_inv = normalize(x[...].astype(jnp.float32) + times(ctx[...], w_out))
    mid = first_hat * norms[0] + norms[1]
    mid_low = low(mid)
    mid_ref[...] = mid_low
    tick()
    cols = w_inner.shape[2]
    if waits:
        at_first(step, wait_all, waits[:1])
    for f in range(w_inner.shape[0]):
        at = slice(f * cols, (f + 1) * cols)
        act, grad = gelu_pair(dot_nn(mid_low, w_inner[f]))
        act_ref[:, at] = low(act)
        hid_ref[:, at] = low(grad)
        tick()
    if waits:
        at_first(step, wait_all, waits[1:])
    second_hat, second_inv = normalize(mid + times(act_ref[...], w_outer))
    result = low((second_hat * norms[2] + norms[3]) * kept)
    for q in range(group):
        out[q] = result[q * slots : q * slots + real]
    if real < slots:
        dy = r.cot_wide[...] * kept
    else:
        dy = cot[...].reshape(rows, -1).astype(jnp.float32) * kept
    second_dz = normalize_back(dy, second_hat, second_inv, norms[2])
    ffn_low = low(second_dz)
    ffn_ref[...] = ffn_low
    sums = [col_sum(dy * second_hat), col_sum(dy)]
    tick()
    hid_ref[...] = low(times_back(ffn_low, w_outer) * hid_ref[...].astype(jnp.float32))
    tick()
    mid_grad = second_dz + times_back(hid_ref[...], w_inner)
    first_dz = normalize_back(mid_grad, first_hat, first_inv, norms[0])
    dz_out[...] = first_dz
    branch_low = low(first_dz)
    branch_ref[...] = branch_low
    tick()
    dctx_out[...] = low(times_back(branch_low, w_out))
    sums = [col_sum(mid_grad * first_hat), col_sum(mid_grad)] + sums
    for n in range(4):
        ngrad[n : n + 1, :] += sums[n]
    tick()


def store_grad(out, x, d):
    cols = out.shape[2]
    whole = low(dot_tn(x, d))
    for f in range(out.shape[0]):
        out[f] = whole[:, f * cols : (f + 1) * cols]


def add_to(ref, mine, value):
    value = low(value).astype(jnp.float32)
    for i in range(ref.shape[0]):
        ref[i] += jnp.where(mine == i, value, 0.0)


def image_phase(first_col, norm_wide, r, step, tick):
    tick()
    group, slots, wide = r.cot.shape[0], r.image.shape[1], r.image.shape[2]

    @pl.when(step == 0)
    def _():
        targets = (r.w_io, r.w_ii, r.w_iu)
        fetch(
            [(g.reshape(w.shape), w) for g, w in zip(r.gathered[4:], targets)]
            + [(r.gathered[3], r.norm_parts)],
            r.sems,
        )
        parts = r.norm_parts.shape[0:-2]
        nf = bits_of(lax.axis_size("fsdp"))
        for i in range(math.prod(parts)):
            at, rest = [], i
            for _ in parts:
                at.append(rest % 2)
                rest //= 2
            at = at[::-1]
            f = sum(bit << k for k, bit in enumerate(reversed(at[:nf])))
            d = sum(bit << k for k, bit in enumerate(reversed(at[nf:])))
            first = (d * (1 << nf) + f) * norm_wide
            r.norms[:, first : first + norm_wide] = r.norm_parts[tuple(at)]

    for q in range(group):
        r.visual[q * slots : (q + 1) * slots, :] = r.image[own_image(r, step * group + q)]
    here = rows_at(step, group * slots)
    norms = [r.norms[n : n + 1, first_col : first_col + wide] for n in range(4)]
    stream_rows(
        r,
        step,
        tick,
        lambda p: r.region_counts[own_image(r, p)],
        r.visual,
        r.ictx.at[here],
        r.cot,
        norms,
        (r.w_io, r.w_ii, r.w_iu),
        [ref.at[here] for ref in (r.mid, r.act, r.hid, r.ffn, r.branch)],
        (r.image_out, r.image_dz, r.dctx.at[here], r.image_ngrad),
    )


def image_grads_phase(r, step, tick):
    tick()
    here = rows_at(step, r.g_io.shape[1])
    store_grad(r.g_io, r.ictx[:, here], r.branch[...])
    store_grad(r.g_ii, r.mid[:, here], r.hid[...])
    store_grad(r.g_iu, r.act[:, here], r.ffn[...])
    tick()


def back_image_phase(r, step, tick):
    tick()
    regions, length = r.iprob.shape[1:]
    heads = r.tk.shape[1] // HDIM
    columns = [slice(h * HDIM, (h + 1) * HDIM) for h in range(heads)]
    scale = 1.0 / math.sqrt(HDIM)

    @pl.when(step == 0)
    def _():
        r.diq_sum[...] = jnp.zeros_like(r.diq_sum)

    for q in range(ROW_PAIRS):
        p = step * ROW_PAIRS + q
        mine = own_image(r, p)
        here, rows_i = rows_at(p, length), rows_at(p, regions)
        local = slice(q * length, (q + 1) * length)
        dprobs = [dot_nt(r.dctx[rows_i, at], r.tv[here, at]) for at in columns]
        dvalues = [
            low(dot_tn(low(r.iprob[p * heads + h]), r.dctx[rows_i, at]))
            for h, at in enumerate(columns)
        ]
        dscores = []
        for h in range(heads):
            probs = r.iprob[p * heads + h]
            inner = jnp.sum(probs * dprobs[h], axis=1, keepdims=True)
            dscores.append(low(probs * (dprobs[h] - inner)))
        parts = [scale * dot_nn(one, r.tk[here, at]) for one, at in zip(dscores, columns)]
        add_to(r.diq_sum, mine, jnp.concatenate(parts, axis=1))
        dkeys = [
            low(scale * dot_tn(one, r.iq[mine, :, at])) for one, at in zip(dscores, columns)
        ]
        for ref, out, values in ((r.tv, r.dtv, dvalues), (r.tk, r.dtk, dkeys)):
            values = jnp.concatenate(values, axis=1)
            ref[here, :] = values
            out[local, :] = values
        tick()


def key_grads_phase(r, step, tick):
    tick()
    diq = low(r.diq_sum[...])
    r.diq[...] = diq
    here = rows_at(step, r.g_iq.shape[1])
    store_grad(r.g_iq, flat(r.image[:, :, here]), flat(diq))
    here = rows_at(step, r.g_tk.shape[1])
    store_grad(r.g_tk, r.text[:, here], r.tk[...])
    store_grad(r.g_tv, r.text[:, here], r.tv[...])
    tick()


def text_phase(r, step, tick):
    tick()
    copies = coming(r, TEXT_FAR)
    at_first(step, start_all, copies)
    rows = r.x.shape[0]
    here = rows_at(step, rows)
    norms = [r.norms[n : n + 1, : r.x.shape[1]] for n in range(4)]
    stream_rows(
        r,
        step,
        tick,
        lambda p: r.lens[p],
        r.x,
        r.tctx.at[here],
        r.cot,
        norms,
        (r.w_to, r.w_ti, r.w_tu),
        [ref.at[here] for ref in (r.mid, r.act, r.hid, r.ffn, r.branch)],
        (r.text_out, r.text_dz, r.dctx, r.text_ngrad),
        copies,
    )


def grad_phase(out, x, d, r, step, tick):
    tick()
    out = getattr(r, out)
    here = rows_at(step, out.shape[1])
    store_grad(out, getattr(r, x)[:, here], getattr(r, d)[...])
    tick()


def back_text_phase(r, step, tick):
    tick()
    at_first(step, start_all, coming(r, LAST_FAR))
    regions, length = r.tprob.shape[1:]
    heads = r.tq.shape[1] // HDIM
    columns = [slice(h * HDIM, (h + 1) * HDIM) for h in range(heads)]
    scale = 1.0 / math.sqrt(HDIM)

    @pl.when(step == 0)
    def _():
        r.dik_sum[...] = jnp.zeros_like(r.dik_sum)
        r.div_sum[...] = jnp.zeros_like(r.div_sum)

    for q in range(ROW_PAIRS):
        p = step * ROW_PAIRS + q
        mine = own_image(r, p)
        here = rows_at(p, length)
        local = slice(q * length, (q + 1) * length)
        dprobs = [dot_nt(r.iv[mine, :, at], r.dtc[local, at]) for at in columns]
        parts = [
            dot_nn(low(r.tprob[q * heads + h]), r.dtc[local, at]) for h, at in enumerate(columns)
        ]
        add_to(r.div_sum, mine, jnp.concatenate(parts, axis=1))
        dscores = []
        for h in range(heads):
            probs = r.tprob[q * heads + h]
            inner = jnp.sum(probs * dprobs[h], axis=0, keepdims=True)
            dscores.append(low(probs * (dprobs[h] - inner)))
        parts = [scale * dot_nn(one, r.tq[local, at]) for one, at in zip(dscores, columns)]
        add_to(r.dik_sum, mine, jnp.concatenate(parts, axis=1))
        parts = [
            low(scale * dot_tn(one, r.ik[mine, :, at])) for one, at in zip(dscores, columns)
        ]
        r.dtq[here, :] = jnp.concatenate(parts, axis=1)
        tick()


def query_grads_phase(r, step, tick):
    tick()
    at_first(step, wait_all, coming(r, LAST_FAR[:1]))
    here = rows_at(step, r.text.shape[1] // 2)
    put_half(r.g_tq, step, r.text[:, here], r.dtq[...])
    dik, div = low(r.dik_sum[...]), low(r.div_sum[...])
    r.dik[...] = dik
    r.div[...] = div
    here = rows_at(step, r.image.shape[2] // 2)
    columns = flat(r.image[:, :, here])
    put_half(r.g_ik, step, columns, flat(dik))
    put_half(r.g_iv, step, columns, flat(div))
    tick()


def data_grads_phase(r, step, tick):
    images, real = r.image_grad.shape[:2]
    pairs = r.owner.shape[0]
    slots = r.image_dz.shape[0] // pairs
    tick()
    at_first(step, wait_all, coming(r, LAST_FAR[1:]))

    @pl.when(step == 0)
    def _():
        for i in range(images):
            total = jnp.zeros((slots, r.image_dz.shape[1]), jnp.float32)
            for p in range(pairs):
                rows = r.image_dz[p * slots : (p + 1) * slots, :]
                total += jnp.where(own_image(r, p) == i, rows, 0.0)
            for d, w in ((r.diq, r.w_iq), (r.dik, r.w_ik), (r.div, r.w_iv)):
                total = total + times_back(d[i], w)
            r.image_grad[i] = total[:real]

    total = r.text_dz[...]
    here = rows_at(step, total.shape[0])
    for d, w in ((r.dtq.at[here], r.w_tq), (r.dtk, r.w_tk), (r.dtv, r.w_tv)):
        total = total + times_back(d[...], w)
        tick()
    r.text_grad[...] = total


def pass_kernel(count, *refs):
    for source, target in zip(refs[:count], refs[count:]):
        target[...] = source[...]


def pass_on(arrays):
    return pl.pallas_call(
        functools.partial(pass_kernel, len(arrays)),
        out_shape=[struct(a.shape, a.dtype) for a in arrays],
        in_specs=[WHOLE] * len(arrays),
        out_specs=[WHOLE] * len(arrays),
        compiler_params=pltpu.CompilerParams(vmem_limit_bytes=VMEM_LIMIT),
    )(*arrays)


def whole_weight(shard, block):
    nd, nf = mesh_bits()
    rows, cols = shard.shape
    block = block.reshape(1 << nf, rows << nd, cols)
    if cols % 128:
        block = jnp.swapaxes(block, 0, 1).reshape(1, rows << nd, cols << nf)
    return block


def device_blocks(grad, shard):
    nd, nf = mesh_bits()
    rows, cols = shard.shape
    if cols % 128:
        grad = jnp.swapaxes(grad.reshape(rows << nd, 1 << nf, cols), 0, 1)
    return grad.reshape((2,) * (nd + nf) + (rows, cols))


def norm_blocks(rows):
    nd, nf = mesh_bits()
    wide = rows.shape[1] >> (nd + nf)
    split = rows.reshape(4, 1 << nd, 1 << nf, wide).transpose(2, 1, 0, 3)
    split = jnp.pad(split, ((0, 0), (0, 0), (0, 4), (0, 128 - wide)))
    return split.reshape((2,) * (nd + nf) + (8, 128))


def body(
    text_states,
    image_states,
    text_lengths,
    region_mask,
    group_ids,
    image_query,
    image_key,
    image_value,
    text_query,
    text_key,
    text_value,
    image_output,
    text_output,
    image_inner,
    image_outer,
    text_inner,
    text_outer,
    norm_params,
    cot_text,
    cot_image,
):
    nd, nf = mesh_bits()
    lead = (2,) * (nd + nf)
    bf, f32 = jnp.bfloat16, jnp.float32
    pairs, length, width_text = text_states.shape
    images, regions, width_image = image_states.shape
    padded = -(-regions // 16) * 16
    wide = image_query.shape[1] << nf
    heads = wide // HDIM
    rows_text, rows_image = pairs * length, pairs * padded
    norm_wide = norm_params.shape[1]
    device = lax.axis_index("dp") * lax.axis_size("fsdp") + lax.axis_index("fsdp")
    owner = group_ids - device * images
    text = text_states.reshape(rows_text, width_text)
    def full(shard):
        rows, cols = shard.shape
        return pltpu.VMEM((1 << nf, rows << nd, cols), bf)

    def vmem(rows, cols, dtype=bf):
        return pltpu.VMEM((rows, cols), dtype)

    n = ROW_PAIRS
    steps = pairs // n
    group = pairs // 2
    block_i = group * padded
    gather = Gather(
        [text_key, text_value, image_query, norm_params, image_output, image_inner, image_outer]
        + [text_query, image_key, image_value, text_output, text_inner, text_outer]
    )
    phases, begin = [], [0]

    def phase(run, count, marks, **kw):
        phases.append(Phase(run, count, marks, **kw))
        begin.append(begin[-1] + count)
        return begin[-2]

    phase(project_keys_phase, steps, (0.0, 1.7), needs=range(3))
    phase(attend_image_phase, steps, (0.0, 0.9, 1.8))
    stages = 1 << nf
    marks = [0.0, 1.1] + [1.1 + 1.0 * (k + 1) / stages for k in range(stages)]
    marks += [3.3, 4.4, 5.7, 6.4]
    at_image = phase(
        functools.partial(image_phase, width_text, norm_wide), 2, marks, needs=range(3, 7)
    )
    at_image_grads = phase(image_grads_phase, 4, (0.0, 1.0))
    at_back = phase(back_image_phase, steps, (0.0, 0.8, 1.7))
    at_grads = phase(key_grads_phase, 2, (0.0, 2.4))
    at_attend = phase(attend_text_phase, steps, (0.0, 0.8, 1.7, 2.6), needs=range(7, 10))
    third = width_text // 3

    def grad_out(weight_shard, inner, first, count, size):
        shape = (1 << nf, inner, weight_shard.shape[1])
        if weight_shard.shape[1] % 128:
            shape = (1, inner, weight_shard.shape[1] << nf)
        block = (shape[0], size, shape[2])
        return (struct(shape, bf), during(first, count, block, 1))

    by_pair = during(at_image, 2, (group, regions, width_image))
    probs = during(at_attend, steps, (n * heads, padded, length))
    pair_rows = during(at_attend, steps, (n * length, wide))
    back_rows = during(at_back, steps, (n * length, wide))
    image_shape = (images, padded, wide)
    a = carry(
        phases,
        dict(
            lens=(text_lengths, SCALARS),
            owner=(owner, SCALARS),
            mask=(region_mask, SCALARS),
            text=resident(text),
            states=resident(image_states),
            cot=(cot_image, by_pair),
        ),
        dict(
            ik=(struct(image_shape, bf), fixed(image_shape)),
            iv=(struct(image_shape, bf), fixed(image_shape)),
            tq=(struct((rows_text, wide), bf), pair_rows),
            tprob=(struct((pairs * heads, padded, length), f32), probs),
            tctx=(struct((rows_text, wide), bf), pair_rows),
            image_rows=(
                struct((images, padded, width_image), bf),
                fixed((images, padded, width_image)),
            ),
            norms=(struct((4, norm_wide << (nd + nf)), f32), fixed((4, norm_wide << (nd + nf)))),
            image_out=(struct(cot_image.shape, bf), by_pair),
            image_dz=(
                struct((rows_image, width_image), f32),
                during(at_image, 2, (block_i, width_image)),
            ),
            image_ngrad=(struct((4, width_image), f32), fixed((4, width_image))),
            dtk=(struct((rows_text, wide), bf), back_rows),
            dtv=(struct((rows_text, wide), bf), back_rows),
            diq=(struct(image_shape, bf), fixed(image_shape)),
            g_io=grad_out(image_output, wide, at_image_grads, 4, wide // 4),
            g_ii=grad_out(image_inner, width_image, at_image_grads, 4, width_image // 4),
            g_iu=grad_out(image_outer, width_image, at_image_grads, 4, width_image // 4),
            g_iq=grad_out(image_query, width_image, at_grads, 2, width_image // 2),
            g_tk=grad_out(text_key, width_text, at_grads, 2, width_text // 2),
            g_tv=grad_out(text_value, width_text, at_grads, 2, width_text // 2),
        ),
        dict(
            w_tq=full(text_query),
            w_tk=full(text_key),
            w_tv=full(text_value),
            w_iq=full(image_query),
            w_ik=full(image_key),
            w_iv=full(image_value),
            w_io=full(image_output),
            w_ii=full(image_inner),
            w_iu=full(image_outer),
            image=pltpu.VMEM((images, padded, width_image), bf),
            visual=vmem(block_i, width_image),
            region_counts=pltpu.SMEM((images,), jnp.int32),
            norm_parts=pltpu.VMEM(lead + norm_params.shape, f32),
            sems=pltpu.SemaphoreType.DMA((4,)),
            iq=pltpu.VMEM(image_shape, bf),
            tk=vmem(rows_text, wide),
            tv=vmem(rows_text, wide),
            iprob=pltpu.VMEM((pairs * heads, padded, length), f32),
            ictx=vmem(rows_image, wide),
            mid=vmem(rows_image, width_image),
            act=vmem(rows_image, width_image),
            hid=vmem(rows_image, width_image),
            ffn=vmem(rows_image, width_image),
            branch=vmem(rows_image, width_image),
            dctx=vmem(rows_image, wide),
            diq_sum=pltpu.VMEM(image_shape, f32),
            cot_wide=vmem(block_i, width_image, f32),
        ),
        gather,
        0,
        SEARCH,
    )
    whole = [whole_weight(s, g) for s, g in zip(gather.given, a.landed) if s is not norm_params]
    w_tk, w_tv, w_iq, _, _, _, w_tq, w_ik, w_iv, w_to, w_ti, w_tu = whole

    job = Reduce(
        [
            device_blocks(grad, shard)
            for grad, shard in (
                (a.g_io, image_output),
                (a.g_ii, image_inner),
                (a.g_iu, image_outer),
                (a.g_iq, image_query),
                (a.g_tk, text_key),
                (a.g_tv, text_value),
            )
        ]
    )
    phases, begin = [], [0]
    inner = w_ti.shape[0] * w_ti.shape[2]
    block_t = n * length
    stages = w_ti.shape[0]
    marks = [0.0, 1.6] + [1.6 + 3.6 * (k + 1) / stages for k in range(stages)]
    marks += [7.8, 9.8, 11.8, 12.6]
    at_text = phase(text_phase, steps, marks)
    at_tu = phase(functools.partial(grad_phase, "g_tu", "act", "ffn"), 12, (0.0, 0.7))
    at_ti = phase(functools.partial(grad_phase, "g_ti", "mid", "hid"), 6, (0.0, 1.4))
    at_to = phase(functools.partial(grad_phase, "g_to", "tctx", "branch"), 4, (0.0, 0.8))
    by_pair = during(at_text, steps, (n, length, width_text))

    def text_rows(cols):
        return during(at_text, steps, (block_t, cols))

    b = carry(
        phases,
        dict(
            lens=(text_lengths, SCALARS),
            x=(text, text_rows(width_text)),
            tctx=resident(a.tctx),
            cot=(cot_text, by_pair),
            norms=resident(a.norms),
            w_to=resident(w_to),
            far_w_ti=(w_ti, ANYWHERE),
            far_w_tu=(w_tu, ANYWHERE),
        ),
        dict(
            text_out=(struct(cot_text.shape, bf), by_pair),
            text_dz=(struct((rows_text, width_text), f32), text_rows(width_text)),
            dctx=(struct((rows_text, wide), bf), text_rows(wide)),
            text_ngrad=(struct((4, width_text), f32), fixed((4, width_text))),
            g_tu=grad_out(text_outer, inner, at_tu, 12, inner // 12),
            g_ti=grad_out(text_inner, width_text, at_ti, 6, width_text // 6),
            g_to=grad_out(text_output, wide, at_to, 4, wide // 4),
        ),
        dict(
            w_ti=pltpu.VMEM(w_ti.shape, bf),
            w_tu=pltpu.VMEM(w_tu.shape, bf),
            sems=pltpu.SemaphoreType.DMA((len(TEXT_FAR),)),
            mid=vmem(rows_text, width_text),
            act=vmem(rows_text, inner),
            hid=vmem(rows_text, inner),
            ffn=vmem(rows_text, width_text),
            branch=vmem(rows_text, width_text),
        ),
        job,
        1,
    )
    o_io, o_ii, o_iu, o_iq, o_tk, o_tv = b.landed

    norm_rows = norm_blocks(jnp.concatenate([b.text_ngrad, a.image_ngrad], axis=1))
    job = Reduce(
        [
            device_blocks(b.g_tu, text_outer),
            device_blocks(b.g_ti, text_inner),
            device_blocks(b.g_to, text_output),
            norm_rows,
        ],
        dict(
            g_tq=struct(lead + text_query.shape, bf),
            g_ik=struct(lead + image_key.shape, bf),
            g_iv=struct(lead + image_value.shape, bf),
        ),
    )
    phases, begin = [], [0]
    at_back = phase(back_text_phase, steps, (0.0, 0.8, 1.7))
    phase(query_grads_phase, 2, (0.0, 2.0), makes=range(4, 7))
    at_data = phase(data_grads_phase, steps, (0.0, 0.9, 1.8, 2.6))
    probs = during(at_back, steps, (n * heads, padded, length))
    back_rows = during(at_back, steps, (n * length, wide))
    data_rows = during(at_data, steps, (block_t, wide))
    data_out = during(at_data, steps, (block_t, width_text))
    c = carry(
        phases,
        dict(
            owner=(owner, SCALARS),
            ik=resident(a.ik),
            iv=resident(a.iv),
            tq=(a.tq, back_rows),
            tprob=(a.tprob, probs),
            dtc=(b.dctx, back_rows),
            far_text=(text, ANYWHERE),
            image=resident(a.image_rows),
            text_dz=(b.text_dz, data_out),
            dtk=(a.dtk, data_rows),
            dtv=(a.dtv, data_rows),
            far_image_dz=(a.image_dz, ANYWHERE),
            diq=resident(a.diq),
            far_w_tq=(w_tq, ANYWHERE),
            far_w_tk=(w_tk, ANYWHERE),
            far_w_tv=(w_tv, ANYWHERE),
            far_w_iq=(w_iq, ANYWHERE),
            far_w_ik=(w_ik, ANYWHERE),
            far_w_iv=(w_iv, ANYWHERE),
        ),
        dict(
            text_grad=(struct((rows_text, width_text), f32), data_out),
            image_grad=(struct(image_states.shape, f32), fixed(image_states.shape)),
        ),
        dict(
            text=vmem(rows_text, width_text),
            image_dz=vmem(rows_image, width_image, f32),
            w_tq=pltpu.VMEM(w_tq.shape, bf),
            w_tk=pltpu.VMEM(w_tk.shape, bf),
            w_tv=pltpu.VMEM(w_tv.shape, bf),
            w_iq=pltpu.VMEM(w_iq.shape, bf),
            w_ik=pltpu.VMEM(w_ik.shape, bf),
            w_iv=pltpu.VMEM(w_iv.shape, bf),
            sems=pltpu.SemaphoreType.DMA((len(LAST_FAR),)),
            dtq=vmem(rows_text, wide),
            dik=pltpu.VMEM(image_shape, bf),
            div=pltpu.VMEM(image_shape, bf),
            dik_sum=pltpu.VMEM(image_shape, f32),
            div_sum=pltpu.VMEM(image_shape, f32),
            g_tq=pltpu.VMEM(lead + text_query.shape, bf),
            g_ik=pltpu.VMEM(lead + image_key.shape, bf),
            g_iv=pltpu.VMEM(lead + image_value.shape, bf),
        ),
        job,
        2,
        SEARCH,
    )
    o_tu, o_ti, o_to, o_norm, o_tq, o_ik, o_iv = c.landed
    owned = pass_on([o_iq, o_ik, o_iv, o_tq, o_tk, o_tv, o_io, o_to, o_ii, o_iu, o_ti, o_tu])
    return (
        b.text_out,
        a.image_out,
        c.text_grad.reshape(text_states.shape),
        c.image_grad,
        *owned,
        o_norm[:4, :norm_wide],
    )


def solution(mesh):
    placed = (
        P(("dp", "fsdp"), None, None),
        P(("dp", "fsdp"), None, None),
        P(("dp", "fsdp")),
        P(("dp", "fsdp"), None),
        P(("dp", "fsdp")),
        P("dp", "fsdp"),
        P("dp", "fsdp"),
        P("dp", "fsdp"),
        P("dp", "fsdp"),
        P("dp", "fsdp"),
        P("dp", "fsdp"),
        P("dp", "fsdp"),
        P("dp", "fsdp"),
        P("dp", "fsdp"),
        P("dp", "fsdp"),
        P("dp", "fsdp"),
        P("dp", "fsdp"),
        P(None, ("dp", "fsdp")),
        P(("dp", "fsdp"), None, None),
        P(("dp", "fsdp"), None, None),
    )
    return jax.shard_map(
        body,
        mesh=mesh,
        in_specs=placed,
        out_specs=(
            P(("dp", "fsdp"), None, None),
            P(("dp", "fsdp"), None, None),
            P(("dp", "fsdp"), None, None),
            P(("dp", "fsdp"), None, None),
            P("dp", "fsdp"),
            P("dp", "fsdp"),
            P("dp", "fsdp"),
            P("dp", "fsdp"),
            P("dp", "fsdp"),
            P("dp", "fsdp"),
            P("dp", "fsdp"),
            P("dp", "fsdp"),
            P("dp", "fsdp"),
            P("dp", "fsdp"),
            P("dp", "fsdp"),
            P("dp", "fsdp"),
            P(None, ("dp", "fsdp")),
        ),
        check_vma=False,
    )
```

```python
import functools
import itertools
import math
import random

import jax
import jax.numpy as jnp
from jax import lax
from jax.experimental import pallas as pl
from jax.experimental.pallas import tpu as pltpu
from jax.sharding import PartitionSpec as P

HDIM = 128

norm_eps = 1e-12
masked_score = -1e30

MESH_IDS = pl.DeviceIdType.MESH
VMEM_LIMIT = 63 * 1024 * 1024
WHOLE = pl.BlockSpec(memory_space=pltpu.VMEM)
SCALARS = pl.BlockSpec(memory_space=pltpu.SMEM)
ANYWHERE = pl.BlockSpec(memory_space=pl.ANY)
CORE = ("d", 0)


def bits_of(size):
    count = size.bit_length() - 1
    assert 1 << count == size
    return count


def mesh_bits():
    return bits_of(lax.axis_size("dp")), bits_of(lax.axis_size("fsdp"))


def hop_orders(nd, nf):
    high = [("d", b) for b in range(nd - 1, 2, -1)]
    low = [("d", 2)]
    near = [("d", 1)]
    wide = [("f", b) for b in range(nf)]
    first = [(low, near, high, wide), (high, wide, low, near)]
    rest = [p for p in itertools.permutations((low, near, high, wide)) if p not in first]
    return [tuple(bit for group in order for bit in group) for order in first + rest]


def cut_pieces(shapes):
    pieces, ranks, large = [], [], 0
    for m, (rows, cols) in enumerate(shapes):
        count = 4 if rows * cols > 40000 else 2
        if rows % (16 * count) == 0:
            each = rows // count
            cuts = [(k * each, each, 0, cols) for k in range(count)]
        elif cols % (128 * count) == 0 and rows % 8 == 0:
            each = cols // count
            cuts = [(0, rows, k * each, each) for k in range(count)]
        else:
            cuts = [(0, rows, 0, cols)]
        for cut in cuts:
            pieces.append((m, *cut, large % 2))
            small = rows * cols < 2048
            ranks.append(0 if small else large)
            large += 0 if small else 1
    return pieces, ranks


class Place:
    def __init__(self, nd, nf):
        self.d = lax.axis_index("dp")
        self.f = lax.axis_index("fsdp")
        self.axes = [("f", b) for b in range(nf - 1, -1, -1)] + [
            ("d", b) for b in range(nd - 1, -1, -1)
        ]

    def bit(self, axis):
        value = self.f if axis[0] == "f" else self.d
        return lax.rem(value // (1 << axis[1]), 2)

    def partner(self, axis):
        step = (1 << axis[1]) * (1 - 2 * self.bit(axis))
        if axis[0] == "f":
            return (self.d, self.f + step)
        return (self.d + step, self.f)

    def index(self, whole, flip=None):
        picked = []
        for axis in self.axes:
            if axis in whole:
                picked.append(slice(None))
            elif axis == flip:
                picked.append(1 - self.bit(axis))
            else:
                picked.append(self.bit(axis))
        return tuple(picked)

    def barrier(self):
        sem = pltpu.get_barrier_semaphore()
        for axis in self.axes:
            pl.semaphore_signal(
                sem, inc=1, device_id=self.partner(axis), device_id_type=MESH_IDS
            )
        pl.semaphore_wait(sem, len(self.axes))


class Gather:
    def __init__(self, arrays):
        self.arrays = arrays
        self.given = arrays
        self.made = []
        self.adds = False
        self.nd, self.nf = mesh_bits()
        self.orders = [order + (CORE,) for order in hop_orders(self.nd, self.nf)]
        self.cuts, self.ranks = cut_pieces([a.shape for a in arrays])
        self.routes = [self.orders[cut[-1]] for cut in self.cuts]
        self.hops = self.nd + self.nf
        lead = (2,) * self.hops
        self.out_shape = [jax.ShapeDtypeStruct(lead + a.shape, a.dtype) for a in arrays]
        self.out_specs = [ANYWHERE] * len(arrays)
        count = len(self.cuts)
        self.scratch = [
            pltpu.SemaphoreType.DMA((count,)),
            pltpu.SemaphoreType.DMA((count, self.hops)),
            pltpu.SemaphoreType.DMA((count, self.hops)),
        ]

    def sizes(self, k):
        m, row, rows, col, cols, _ = self.cuts[k]
        block = rows * cols * self.arrays[m].dtype.itemsize
        return [block << h for h in range(self.hops)]

    def window(self, k):
        m, row, rows, col, cols, _ = self.cuts[k]
        return (pl.ds(row, rows), pl.ds(col, cols))

    def bind(self, place, ins, outs, scratch):
        self.place, self.ins, self.outs = place, ins, outs
        self.local_sem, self.send_sem, self.recv_sem = scratch

    def local(self, k):
        m = self.cuts[k][0]
        return pltpu.make_async_copy(
            self.ins[m].at[self.window(k)],
            self.outs[m].at[self.place.index(()) + self.window(k)],
            self.local_sem.at[k],
        )

    def hop(self, k, h):
        m, route = self.cuts[k][0], self.routes[k]
        region = self.outs[m].at[self.place.index(route[:h]) + self.window(k)]
        return pltpu.make_async_remote_copy(
            src_ref=region,
            dst_ref=region,
            send_sem=self.send_sem.at[k, h],
            recv_sem=self.recv_sem.at[k, h],
            device_id=self.place.partner(route[h]),
            device_id_type=MESH_IDS,
        )

    def start(self):
        for k in range(len(self.cuts)):
            self.local(k).start()

    def step(self, k, h):
        if h == 0:
            self.local(k).wait()
        else:
            self.hop(k, h - 1).wait_recv()
        if h < self.hops:
            self.hop(k, h).start()
        else:
            for g in range(self.hops):
                self.hop(k, g).wait_send()


def add_blocks(acc, index, window, incoming):
    lead = incoming.shape[:-2]
    outer, inner = lead[:-2], lead[-2:]

    def one(i, carry):
        first = []
        for size in reversed(outer):
            first.append(lax.rem(i, size))
            i = i // size
        first = first[::-1]
        for j in range(math.prod(inner)):
            at, rest = [], j
            for size in reversed(inner):
                at.append(rest % size)
                rest //= size
            at = tuple(first + at[::-1])
            left = list(at)
            where = tuple(left.pop(0) if isinstance(p, slice) else p for p in index) + window
            acc[where] = acc[where] + incoming[at]
        return carry

    lax.fori_loop(0, math.prod(outer), one, 0)


class Reduce:
    def __init__(self, given, made=None):
        made = made or {}
        self.given = given
        self.made = list(made)
        self.adds = True
        arrays = list(given) + list(made.values())
        self.arrays = arrays
        self.nd, self.nf = mesh_bits()
        self.orders = [(CORE,) + order[::-1] for order in hop_orders(self.nd, self.nf)]
        self.hops = self.nd + self.nf
        self.cuts, self.ranks = cut_pieces([a.shape[-2:] for a in arrays])
        self.routes = [self.orders[cut[-1]] for cut in self.cuts]
        self.scratch = []
        for m, row, rows, col, cols, _ in self.cuts:
            for h in range(-1 if m < len(self.given) else 0, self.hops):
                free = self.hops - 1 - max(h, 0)
                self.scratch.append(pltpu.VMEM((2,) * free + (rows, cols), arrays[m].dtype))
        count = len(self.cuts)
        self.scratch += [
            pltpu.SemaphoreType.DMA((count,)),
            pltpu.SemaphoreType.DMA((count, self.hops)),
            pltpu.SemaphoreType.DMA((count, self.hops)),
        ]
        shapes = [a.shape[-2:] for a in arrays]
        self.out_shape = [jax.ShapeDtypeStruct(s, jnp.float32) for s in shapes]
        self.out_specs = [pl.BlockSpec(s, lambda *_: (0, 0)) for s in shapes]

    def sizes(self, k):
        m, row, rows, col, cols, _ = self.cuts[k]
        block = rows * cols * self.arrays[m].dtype.itemsize
        return [block << (self.hops - 1 - h) for h in range(self.hops)]

    def window(self, k):
        m, row, rows, col, cols, _ = self.cuts[k]
        return (pl.ds(row, rows), pl.ds(col, cols))

    def bind(self, place, ins, outs, scratch):
        self.place, self.ins, self.outs = place, ins, outs
        self.local_sem, self.send_sem, self.recv_sem = scratch[-3:]
        rest = list(scratch[:-3])
        self.accs, self.temps = [], []
        for m, *_ in self.cuts:
            self.accs.append(rest.pop(0) if m < len(self.given) else None)
            self.temps.append([rest.pop(0) for _ in range(self.hops)])
        self.rest = [axis for axis in place.axes if axis != CORE]

    def local(self, k):
        source = self.ins[self.cuts[k][0]].at[self.place.index(self.rest) + self.window(k)]
        return pltpu.make_async_copy(source, self.accs[k], self.local_sem.at[k])

    def within(self, k, h, flip=None):
        full = self.place.index(self.routes[k][h + 1 :], flip)
        if self.accs[k] is None:
            m, row, rows, col, cols, _ = self.cuts[k]
            return self.ins[m], full, (slice(row, row + rows), slice(col, col + cols))
        return self.accs[k], tuple(p for p, a in zip(full, self.place.axes) if a != CORE), ()

    def hop(self, k, h):
        m, route = self.cuts[k][0], self.routes[k]
        if h == 0:
            region = self.ins[m].at[self.place.index(route[1:], CORE) + self.window(k)]
        else:
            acc, index, window = self.within(k, h, route[h])
            region = acc.at[index + window]
        return pltpu.make_async_remote_copy(
            src_ref=region,
            dst_ref=self.temps[k][h],
            send_sem=self.send_sem.at[k, h],
            recv_sem=self.recv_sem.at[k, h],
            device_id=self.place.partner(route[h]),
            device_id_type=MESH_IDS,
        )

    def start(self):
        pass

    def step(self, k, h):
        own = self.accs[k] is not None
        if h == 0 and own:
            self.local(k).start()
        if h > 0:
            self.hop(k, h - 1).wait_recv()
            if h == 1 and own:
                self.local(k).wait()
            acc, index, window = self.within(k, h - 1)
            if h < self.hops:
                add_blocks(acc, index, window, self.temps[k][h - 1])
            else:
                m, row, rows, col, cols, _ = self.cuts[k]
                last = acc[index + window].astype(jnp.float32)
                last = last + self.temps[k][h - 1][...].astype(jnp.float32)
                self.outs[m][row : row + rows, col : col + cols] = last
        if h < self.hops:
            self.hop(k, h).start()
        else:
            for g in range(self.hops):
                self.hop(k, g).wait_send()


LINK_RATE = 46e3
CORE_RATE = 380e3
LATENCY = 3.2
ENTRY = 3.0
ISSUE = 0.06
ADD_RATE = 1800e3
SEARCH = 1500


class Phase:
    def __init__(self, run, steps, marks, needs=(), makes=()):
        self.run, self.steps, self.marks = run, steps, marks
        self.needs, self.makes = set(needs), set(makes)


def place_steps(order, job, times, clock, limits, after, counted=True):
    total = len(times)
    limit = [total] * len(order)
    for needs, begin in limits:
        last = -1
        for i, (k, h) in enumerate(order):
            if h == job.hops and job.cuts[k][0] in needs:
                last = i
        for i in range(last + 1):
            limit[i] = min(limit[i], begin)
    waiting, active, done = {}, {}, {}
    now = 0.0

    def advance(key, until):
        nonlocal now
        while key not in done and now < until:
            for axis, queue in waiting.items():
                if queue and axis not in active:
                    active[axis] = queue.pop(0)
            far = any(axis[0] == "d" and axis[1] > 2 for axis in active)
            rates, span = {}, until - now
            for axis, (_, left) in active.items():
                halved = far and axis[0] == "d" and axis[1] > 1
                rates[axis] = CORE_RATE if axis == CORE else LINK_RATE / (2 if halved else 1)
                span = min(span, left / rates[axis])
            now += span
            for axis in list(active):
                active[axis][1] -= span * rates[axis]
                if active[axis][1] <= 1e-3:
                    done[active.pop(axis)[0]] = now + LATENCY

    slots = [[] for _ in range(total)]
    tail = []
    at, late, started = 0, ENTRY if counted else 0.0, 0.0
    for i, (k, h) in enumerate(order):
        ready = now
        if h:
            advance((k, h - 1), math.inf)
            ready = max(ready, done[k, h - 1])
        else:
            at = max(at, after.get(job.cuts[k][0], 0))
        while at < min(limit[i], total) and times[at] + late < ready - 0.3:
            at += 1
        spent = ISSUE + (job.sizes(k)[h - 1] / ADD_RATE if h and job.adds else 0.0)
        spent = spent if counted else 0.0
        if at < total:
            slots[at].append((k, h))
            ready = max(ready, times[at] + late) + spent
            late = ready - times[at]
        else:
            ready = max(ready, clock + late) + spent
            tail.append((k, h))
        started += ready
        advance(None, ready)
        if h < job.hops:
            waiting.setdefault(job.routes[k][h], []).append([(k, h), float(job.sizes(k)[h])])
    end = max(now, clock + late)
    return end + 0.2 * max(done.values()) + 0.1 * started / len(order), slots, tail


def plan_steps(job, phases, search):
    times, limits, after = [], [], {}
    clock = 0.0
    for phase in phases:
        limits.append((phase.needs, len(times)))
        for _ in range(phase.steps):
            times += [clock + mark for mark in phase.marks]
            clock += phase.marks[-1]
        for m in phase.makes:
            after[m] = len(times)
    known = (job, times, clock, limits, after)

    def waves(width, lag):
        order = []
        for k, rank in enumerate(job.ranks):
            wave = rank // width + (lag if job.cuts[k][0] in after else 0)
            order += [(wave + h, wave, k, h) for h in range(job.hops + 1)]
        return [(k, h) for _, _, k, h in sorted(order)]

    if not search:
        return place_steps(waves(4, 0), *known, False)[1:]
    lags = range(4) if after else (0,)
    starts = [waves(width, lag) for width in (3, 4, 5, 6) for lag in lags]
    best, order = min((place_steps(start, *known)[0], start) for start in starts)
    draw = random.Random(1 if job.adds else 7)
    for _ in range(search):
        if draw.random() < 0.3:
            k = draw.randrange(len(job.cuts))
            kept = job.routes[k]
            job.routes[k] = draw.choice(job.orders)
            cost = place_steps(order, *known)[0]
            if cost < best:
                best = cost
            else:
                job.routes[k] = kept
            continue
        i = draw.randrange(len(order))
        k, h = order[i]
        low_end = order.index((k, h - 1)) + 1 if h else 0
        high_end = order.index((k, h + 1)) - 1 if h < job.hops else len(order) - 1
        j = draw.randint(max(low_end, i - 12), max(low_end, min(high_end, i + 12)))
        moved = list(order)
        moved.insert(j, moved.pop(i))
        cost = place_steps(moved, *known)[0]
        if cost < best:
            best, order = cost, moved
    return place_steps(order, *known)[1:]


class Names:
    def __init__(self, names, refs):
        for name, ref in zip(names, refs):
            setattr(self, name, ref)


def carrying_kernel(phases, job, plan, names, *refs):
    spans, start = [], 0
    for count in [len(group) for group in names]:
        spans.append(refs[start : start + count])
        start += count
    own_in, job_in, own_out, job_out, own_scratch, job_scratch = spans
    r = Names(names[0] + names[2] + names[4], own_in + own_out + own_scratch)
    now = pl.program_id(0)
    slots, tail = plan
    place = Place(job.nd, job.nf)
    r.gathered = job_out
    made = [getattr(r, name) for name in job.made]
    job.bind(place, list(job_in) + made, job_out, job_scratch)

    def run(items, opening=False):
        if opening:
            job.start()
            place.barrier()
        for k, h in items:
            job.step(k, h)

    base, begin = 0, 0
    for phase in phases:
        ticks = len(phase.marks)

        def one(phase=phase, base=base, begin=begin, ticks=ticks):
            passed = [0]

            def tick():
                t = passed[0]
                passed[0] += 1
                for s in range(phase.steps):
                    items = slots[base + s * ticks + t]
                    opening = base + s * ticks + t == 0
                    if items or opening:
                        pl.when(now == begin + s)(functools.partial(run, items, opening))

            phase.run(r, now - begin, tick)
            assert passed[0] == ticks

        pl.when((now >= begin) & (now < begin + phase.steps))(one)
        base += ticks * phase.steps
        begin += phase.steps
    if tail:
        pl.when(now == begin - 1)(functools.partial(run, tail))


def carry(phases, ins, outs, scratch, job, ident, search=0):
    plan = plan_steps(job, phases, search)
    given, landed, worked = list(job.given), list(job.out_shape), list(job.scratch)
    names = (
        list(ins),
        [None] * len(given),
        list(outs),
        [None] * len(landed),
        list(scratch),
        [None] * len(worked),
    )
    results = pl.pallas_call(
        functools.partial(carrying_kernel, phases, job, plan, names),
        grid=(sum(phase.steps for phase in phases),),
        in_specs=[spec for _, spec in ins.values()] + [ANYWHERE] * len(given),
        out_specs=[spec for _, spec in outs.values()] + list(job.out_specs),
        out_shape=[shape for shape, _ in outs.values()] + landed,
        scratch_shapes=list(scratch.values()) + worked,
        compiler_params=pltpu.CompilerParams(
            collective_id=ident, has_side_effects=True, vmem_limit_bytes=VMEM_LIMIT
        ),
    )(*[array for array, _ in ins.values()], *given)
    r = Names(list(outs), results)
    r.landed = results[len(outs) :]
    return r


def dot_nn(a, b):
    return lax.dot_general(a, b, (((1,), (0,)), ((), ())), preferred_element_type=jnp.float32)


def dot_nt(a, b):
    return lax.dot_general(a, b, (((1,), (1,)), ((), ())), preferred_element_type=jnp.float32)


def dot_tn(a, b):
    return lax.dot_general(a, b, (((0,), (0,)), ((), ())), preferred_element_type=jnp.float32)


def low(value):
    return value.astype(jnp.bfloat16)


def times(value, matrix):
    parts = [dot_nn(value, matrix[f]) for f in range(matrix.shape[0])]
    return parts[0] if len(parts) == 1 else jnp.concatenate(parts, axis=1)


def times_back(value, matrix):
    cols = matrix.shape[2]
    total = None
    for f in range(matrix.shape[0]):
        term = dot_nt(value[:, f * cols : (f + 1) * cols], matrix[f])
        total = term if total is None else total + term
    return total


def fixed(shape):
    return pl.BlockSpec(shape, lambda i: (0,) * len(shape))


def resident(array):
    zeros = (0,) * array.ndim
    return (array, pl.BlockSpec(array.shape, lambda i: zeros, pipeline_mode=pl.Buffered(1)))


def during(begin, steps, block, axis=0):
    def index(i):
        at = jnp.minimum(jnp.maximum(i - begin, 0), steps - 1)
        return tuple(at if d == axis else 0 for d in range(len(block)))

    return pl.BlockSpec(block, index)


def struct(shape, dtype):
    return jax.ShapeDtypeStruct(shape, dtype)


def rows_at(step, size):
    return pl.ds(pl.multiple_of(step * size, size), size)


def fetch(pairs, sems):
    copies = [
        pltpu.make_async_copy(source, target, sems.at[n])
        for n, (source, target) in enumerate(pairs)
    ]
    for copy in copies:
        copy.start()
    for copy in copies:
        copy.wait()


def coming(r, names):
    return [
        pltpu.make_async_copy(getattr(r, "far_" + name), getattr(r, name), r.sems.at[n])
        for n, name in names
    ]


def start_all(copies):
    for copy in copies:
        copy.start()


def wait_all(copies):
    for copy in copies:
        copy.wait()


def at_first(step, act, copies):
    pl.when(step == 0)(functools.partial(act, copies))


TEXT_FAR = ((0, "w_ti"), (1, "w_tu"))
LAST_FAR = tuple(
    enumerate(("text", "image_dz", "w_iq", "w_ik", "w_iv", "w_tq", "w_tk", "w_tv"))
)


ROW_PAIRS = 2


def softmax(scores, axis):
    top = jnp.max(scores, axis=axis, keepdims=True)
    weight = jnp.exp(scores - top)
    return weight * (1.0 / jnp.sum(weight, axis=axis, keepdims=True))


def gelu_pair(x):
    below = 0.5 + 0.5 * lax.erf(x * (1.0 / math.sqrt(2.0)))
    bell = jnp.exp(-0.5 * x * x) * (1.0 / math.sqrt(2.0 * math.pi))
    return x * below, below + x * bell


def row_mean(value):
    return jnp.mean(value, axis=-1, keepdims=True)


def col_sum(value):
    return jnp.sum(value, axis=0, keepdims=True)


def own_image(r, p):
    return r.owner[p]


def flat(ref):
    return ref.reshape(-1, ref.shape[-1])


def merged(ref, blocks, rows):
    return ref.reshape(blocks, rows, ref.shape[-1])


def put_half(out, half, x, d):
    cols = out.shape[-1]
    nf = bits_of(lax.axis_size("fsdp"))
    whole = low(dot_tn(x, d))
    for f in range(1 << nf):
        at = tuple((f >> b) % 2 for b in range(nf - 1, -1, -1))
        part = whole[:, f * cols : (f + 1) * cols]
        out[at + (half,)] = part.reshape(out.shape[nf + 1 :])


def project_keys_phase(r, step, tick):
    tick()

    @pl.when(step == 0)
    def _():
        targets = (r.w_tk, r.w_tv, r.w_iq)
        fetch([(g.reshape(w.shape), w) for g, w in zip(r.gathered, targets)], r.sems)
        images, real = r.states.shape[:2]
        r.image[...] = jnp.zeros_like(r.image)
        for i in range(images):
            r.image[i, :real, :] = r.states[i]
            r.region_counts[i] = lax.fori_loop(
                0, real, lambda k, total, i=i: total + r.mask[i, k], 0
            )
        r.image_rows[...] = r.image[...]
        r.iq[...] = low(times(flat(r.image[...]), r.w_iq)).reshape(r.iq.shape)

    here = rows_at(step, r.text.shape[0] // r.owner.shape[0] * ROW_PAIRS)
    rows = r.text[here, :]
    r.tk[here, :] = low(times(rows, r.w_tk))
    r.tv[here, :] = low(times(rows, r.w_tv))
    tick()


def attend_image_phase(r, step, tick):
    tick()
    regions, length = r.iprob.shape[1:]
    heads = r.tk.shape[1] // HDIM
    columns = [slice(h * HDIM, (h + 1) * HDIM) for h in range(heads)]
    scale = 1.0 / math.sqrt(HDIM)
    for q in range(ROW_PAIRS):
        p = step * ROW_PAIRS + q
        mine = own_image(r, p)
        here, rows_i = rows_at(p, length), rows_at(p, regions)
        kept = lax.broadcasted_iota(jnp.int32, (regions, length), 1) < r.lens[p]
        scores = [scale * dot_nt(r.iq[mine, :, at], r.tk[here, at]) for at in columns]
        probs = [softmax(jnp.where(kept, one, masked_score), 1) for one in scores]
        for h in range(heads):
            r.iprob[p * heads + h] = probs[h]
        parts = [low(dot_nn(low(one), r.tv[here, at])) for one, at in zip(probs, columns)]
        r.ictx[rows_i, :] = jnp.concatenate(parts, axis=1)
        tick()


def attend_text_phase(r, step, tick):
    tick()

    @pl.when(step == 0)
    def _():
        targets = (r.w_tq, r.w_ik, r.w_iv)
        fetch([(g.reshape(w.shape), w) for g, w in zip(r.gathered[7:], targets)], r.sems)
        rows = flat(r.image[...])
        for w, out in ((r.w_ik, r.ik), (r.w_iv, r.iv)):
            out[...] = low(times(rows, w)).reshape(out.shape)

    regions, length = r.tprob.shape[1:]
    heads = r.tq.shape[1] // HDIM
    columns = [slice(h * HDIM, (h + 1) * HDIM) for h in range(heads)]
    scale = 1.0 / math.sqrt(HDIM)
    r.tq[...] = low(times(r.text[rows_at(step, r.tq.shape[0]), :], r.w_tq))
    tick()
    for q in range(ROW_PAIRS):
        mine = own_image(r, step * ROW_PAIRS + q)
        here = slice(q * length, (q + 1) * length)
        row = lax.broadcasted_iota(jnp.int32, (regions, length), 0)
        kept = row < r.region_counts[mine]
        scores = [scale * dot_nt(r.ik[mine, :, at], r.tq[here, at]) for at in columns]
        probs = [softmax(jnp.where(kept, one, masked_score), 0) for one in scores]
        for h in range(heads):
            r.tprob[q * heads + h] = probs[h]
        parts = [low(dot_tn(low(one), r.iv[mine, :, at])) for one, at in zip(probs, columns)]
        r.tctx[here, :] = jnp.concatenate(parts, axis=1)
        tick()


def stream_rows(r, step, tick, limits, x, ctx, cot, norms, weights, keeps, outs, waits=()):
    w_out, w_inner, w_outer = weights
    mid_ref, act_ref, hid_ref, ffn_ref, branch_ref = keeps
    out, dz_out, dctx_out, ngrad = outs
    rows = x.shape[0]
    group, real = cot.shape[:2]
    slots = rows // group

    def normalize(z):
        offset = z - row_mean(z)
        inv = lax.rsqrt(row_mean(offset * offset) + norm_eps)
        return offset * inv, inv

    def normalize_back(dy, xhat, inv, gain):
        dx = dy * gain
        return inv * (dx - row_mean(dx) - xhat * row_mean(dx * xhat))

    @pl.when(step == 0)
    def _():
        ngrad[...] = jnp.zeros_like(ngrad)
        if real < slots:
            r.cot_wide[...] = jnp.zeros_like(r.cot_wide)

    row = lax.broadcasted_iota(jnp.int32, (rows, 1), 0)
    kept = row < 0
    for q in range(group):
        inside = (row >= q * slots) & (row < q * slots + limits(step * group + q))
        kept = kept | inside
        if real < slots:
            r.cot_wide[q * slots : q * slots + real, :] = cot[q].astype(jnp.float32)
    kept = kept.astype(jnp.float32)
    first_hat, first_inv = normalize(x[...].astype(jnp.float32) + times(ctx[...], w_out))
    mid = first_hat * norms[0] + norms[1]
    mid_low = low(mid)
    mid_ref[...] = mid_low
    tick()
    cols = w_inner.shape[2]
    if waits:
        at_first(step, wait_all, waits[:1])
    for f in range(w_inner.shape[0]):
        at = slice(f * cols, (f + 1) * cols)
        act, grad = gelu_pair(dot_nn(mid_low, w_inner[f]))
        act_ref[:, at] = low(act)
        hid_ref[:, at] = low(grad)
        tick()
    if waits:
        at_first(step, wait_all, waits[1:])
    second_hat, second_inv = normalize(mid + times(act_ref[...], w_outer))
    result = low((second_hat * norms[2] + norms[3]) * kept)
    for q in range(group):
        out[q] = result[q * slots : q * slots + real]
    if real < slots:
        dy = r.cot_wide[...] * kept
    else:
        dy = cot[...].reshape(rows, -1).astype(jnp.float32) * kept
    second_dz = normalize_back(dy, second_hat, second_inv, norms[2])
    ffn_low = low(second_dz)
    ffn_ref[...] = ffn_low
    sums = [col_sum(dy * second_hat), col_sum(dy)]
    tick()
    hid_ref[...] = low(times_back(ffn_low, w_outer) * hid_ref[...].astype(jnp.float32))
    tick()
    mid_grad = second_dz + times_back(hid_ref[...], w_inner)
    first_dz = normalize_back(mid_grad, first_hat, first_inv, norms[0])
    dz_out[...] = first_dz
    branch_low = low(first_dz)
    branch_ref[...] = branch_low
    tick()
    dctx_out[...] = low(times_back(branch_low, w_out))
    sums = [col_sum(mid_grad * first_hat), col_sum(mid_grad)] + sums
    for n in range(4):
        ngrad[n : n + 1, :] += sums[n]
    tick()


def store_grad(out, x, d):
    cols = out.shape[2]
    whole = low(dot_tn(x, d))
    for f in range(out.shape[0]):
        out[f] = whole[:, f * cols : (f + 1) * cols]


def add_to(ref, mine, value):
    value = low(value).astype(jnp.float32)
    for i in range(ref.shape[0]):
        ref[i] += jnp.where(mine == i, value, 0.0)


def image_phase(first_col, norm_wide, r, step, tick):
    tick()
    group, slots, wide = r.cot.shape[0], r.image.shape[1], r.image.shape[2]

    @pl.when(step == 0)
    def _():
        targets = (r.w_io, r.w_ii, r.w_iu)
        fetch(
            [(g.reshape(w.shape), w) for g, w in zip(r.gathered[4:], targets)]
            + [(r.gathered[3], r.norm_parts)],
            r.sems,
        )
        parts = r.norm_parts.shape[0:-2]
        nf = bits_of(lax.axis_size("fsdp"))
        for i in range(math.prod(parts)):
            at, rest = [], i
            for _ in parts:
                at.append(rest % 2)
                rest //= 2
            at = at[::-1]
            f = sum(bit << k for k, bit in enumerate(reversed(at[:nf])))
            d = sum(bit << k for k, bit in enumerate(reversed(at[nf:])))
            first = (d * (1 << nf) + f) * norm_wide
            r.norms[:, first : first + norm_wide] = r.norm_parts[tuple(at)]

    for q in range(group):
        r.visual[q * slots : (q + 1) * slots, :] = r.image[own_image(r, step * group + q)]
    here = rows_at(step, group * slots)
    norms = [r.norms[n : n + 1, first_col : first_col + wide] for n in range(4)]
    stream_rows(
        r,
        step,
        tick,
        lambda p: r.region_counts[own_image(r, p)],
        r.visual,
        r.ictx.at[here],
        r.cot,
        norms,
        (r.w_io, r.w_ii, r.w_iu),
        [ref.at[here] for ref in (r.mid, r.act, r.hid, r.ffn, r.branch)],
        (r.image_out, r.image_dz, r.dctx.at[here], r.image_ngrad),
    )


def image_grads_phase(r, step, tick):
    tick()
    here = rows_at(step, r.g_io.shape[1])
    store_grad(r.g_io, r.ictx[:, here], r.branch[...])
    store_grad(r.g_ii, r.mid[:, here], r.hid[...])
    store_grad(r.g_iu, r.act[:, here], r.ffn[...])
    tick()


def back_image_phase(r, step, tick):
    tick()
    regions, length = r.iprob.shape[1:]
    heads = r.tk.shape[1] // HDIM
    columns = [slice(h * HDIM, (h + 1) * HDIM) for h in range(heads)]
    scale = 1.0 / math.sqrt(HDIM)

    @pl.when(step == 0)
    def _():
        r.diq_sum[...] = jnp.zeros_like(r.diq_sum)

    for q in range(ROW_PAIRS):
        p = step * ROW_PAIRS + q
        mine = own_image(r, p)
        here, rows_i = rows_at(p, length), rows_at(p, regions)
        local = slice(q * length, (q + 1) * length)
        dprobs = [dot_nt(r.dctx[rows_i, at], r.tv[here, at]) for at in columns]
        dvalues = [
            low(dot_tn(low(r.iprob[p * heads + h]), r.dctx[rows_i, at]))
            for h, at in enumerate(columns)
        ]
        dscores = []
        for h in range(heads):
            probs = r.iprob[p * heads + h]
            inner = jnp.sum(probs * dprobs[h], axis=1, keepdims=True)
            dscores.append(low(probs * (dprobs[h] - inner)))
        parts = [scale * dot_nn(one, r.tk[here, at]) for one, at in zip(dscores, columns)]
        add_to(r.diq_sum, mine, jnp.concatenate(parts, axis=1))
        dkeys = [
            low(scale * dot_tn(one, r.iq[mine, :, at])) for one, at in zip(dscores, columns)
        ]
        for ref, out, values in ((r.tv, r.dtv, dvalues), (r.tk, r.dtk, dkeys)):
            values = jnp.concatenate(values, axis=1)
            ref[here, :] = values
            out[local, :] = values
        tick()


def key_grads_phase(r, step, tick):
    tick()
    diq = low(r.diq_sum[...])
    r.diq[...] = diq
    here = rows_at(step, r.g_iq.shape[1])
    store_grad(r.g_iq, flat(r.image[:, :, here]), flat(diq))
    here = rows_at(step, r.g_tk.shape[1])
    store_grad(r.g_tk, r.text[:, here], r.tk[...])
    store_grad(r.g_tv, r.text[:, here], r.tv[...])
    tick()


def text_phase(r, step, tick):
    tick()
    copies = coming(r, TEXT_FAR)
    at_first(step, start_all, copies)
    rows = r.x.shape[0]
    here = rows_at(step, rows)
    norms = [r.norms[n : n + 1, : r.x.shape[1]] for n in range(4)]
    stream_rows(
        r,
        step,
        tick,
        lambda p: r.lens[p],
        r.x,
        r.tctx.at[here],
        r.cot,
        norms,
        (r.w_to, r.w_ti, r.w_tu),
        [ref.at[here] for ref in (r.mid, r.act, r.hid, r.ffn, r.branch)],
        (r.text_out, r.text_dz, r.dctx, r.text_ngrad),
        copies,
    )


def grad_phase(out, x, d, r, step, tick):
    tick()
    out = getattr(r, out)
    here = rows_at(step, out.shape[1])
    store_grad(out, getattr(r, x)[:, here], getattr(r, d)[...])
    tick()


def back_text_phase(r, step, tick):
    tick()
    at_first(step, start_all, coming(r, LAST_FAR))
    regions, length = r.tprob.shape[1:]
    heads = r.tq.shape[1] // HDIM
    columns = [slice(h * HDIM, (h + 1) * HDIM) for h in range(heads)]
    scale = 1.0 / math.sqrt(HDIM)

    @pl.when(step == 0)
    def _():
        r.dik_sum[...] = jnp.zeros_like(r.dik_sum)
        r.div_sum[...] = jnp.zeros_like(r.div_sum)

    for q in range(ROW_PAIRS):
        p = step * ROW_PAIRS + q
        mine = own_image(r, p)
        here = rows_at(p, length)
        local = slice(q * length, (q + 1) * length)
        dprobs = [dot_nt(r.iv[mine, :, at], r.dtc[local, at]) for at in columns]
        parts = [
            dot_nn(low(r.tprob[q * heads + h]), r.dtc[local, at]) for h, at in enumerate(columns)
        ]
        add_to(r.div_sum, mine, jnp.concatenate(parts, axis=1))
        dscores = []
        for h in range(heads):
            probs = r.tprob[q * heads + h]
            inner = jnp.sum(probs * dprobs[h], axis=0, keepdims=True)
            dscores.append(low(probs * (dprobs[h] - inner)))
        parts = [scale * dot_nn(one, r.tq[local, at]) for one, at in zip(dscores, columns)]
        add_to(r.dik_sum, mine, jnp.concatenate(parts, axis=1))
        parts = [
            low(scale * dot_tn(one, r.ik[mine, :, at])) for one, at in zip(dscores, columns)
        ]
        r.dtq[here, :] = jnp.concatenate(parts, axis=1)
        tick()


def query_grads_phase(r, step, tick):
    tick()
    at_first(step, wait_all, coming(r, LAST_FAR[:1]))
    here = rows_at(step, r.text.shape[1] // 2)
    put_half(r.g_tq, step, r.text[:, here], r.dtq[...])
    dik, div = low(r.dik_sum[...]), low(r.div_sum[...])
    r.dik[...] = dik
    r.div[...] = div
    here = rows_at(step, r.image.shape[2] // 2)
    columns = flat(r.image[:, :, here])
    put_half(r.g_ik, step, columns, flat(dik))
    put_half(r.g_iv, step, columns, flat(div))
    tick()


def data_grads_phase(r, step, tick):
    images, real = r.image_grad.shape[:2]
    pairs = r.owner.shape[0]
    slots = r.image_dz.shape[0] // pairs
    tick()
    at_first(step, wait_all, coming(r, LAST_FAR[1:]))

    @pl.when(step == 0)
    def _():
        for i in range(images):
            total = jnp.zeros((slots, r.image_dz.shape[1]), jnp.float32)
            for p in range(pairs):
                rows = r.image_dz[p * slots : (p + 1) * slots, :]
                total += jnp.where(own_image(r, p) == i, rows, 0.0)
            for d, w in ((r.diq, r.w_iq), (r.dik, r.w_ik), (r.div, r.w_iv)):
                total = total + times_back(d[i], w)
            r.image_grad[i] = total[:real]

    total = r.text_dz[...]
    here = rows_at(step, total.shape[0])
    for d, w in ((r.dtq.at[here], r.w_tq), (r.dtk, r.w_tk), (r.dtv, r.w_tv)):
        total = total + times_back(d[...], w)
        tick()
    r.text_grad[...] = total


def pass_kernel(count, *refs):
    for source, target in zip(refs[:count], refs[count:]):
        target[...] = source[...]


def pass_on(arrays):
    return pl.pallas_call(
        functools.partial(pass_kernel, len(arrays)),
        out_shape=[struct(a.shape, a.dtype) for a in arrays],
        in_specs=[WHOLE] * len(arrays),
        out_specs=[WHOLE] * len(arrays),
        compiler_params=pltpu.CompilerParams(vmem_limit_bytes=VMEM_LIMIT),
    )(*arrays)


def whole_weight(shard, block):
    nd, nf = mesh_bits()
    rows, cols = shard.shape
    block = block.reshape(1 << nf, rows << nd, cols)
    if cols % 128:
        block = jnp.swapaxes(block, 0, 1).reshape(1, rows << nd, cols << nf)
    return block


def device_blocks(grad, shard):
    nd, nf = mesh_bits()
    rows, cols = shard.shape
    if cols % 128:
        grad = jnp.swapaxes(grad.reshape(rows << nd, 1 << nf, cols), 0, 1)
    return grad.reshape((2,) * (nd + nf) + (rows, cols))


def norm_blocks(rows):
    nd, nf = mesh_bits()
    wide = rows.shape[1] >> (nd + nf)
    split = rows.reshape(4, 1 << nd, 1 << nf, wide).transpose(2, 1, 0, 3)
    split = jnp.pad(split, ((0, 0), (0, 0), (0, 4), (0, 128 - wide)))
    return split.reshape((2,) * (nd + nf) + (8, 128))


def body(
    text_states,
    image_states,
    text_lengths,
    region_mask,
    group_ids,
    image_query,
    image_key,
    image_value,
    text_query,
    text_key,
    text_value,
    image_output,
    text_output,
    image_inner,
    image_outer,
    text_inner,
    text_outer,
    norm_params,
    cot_text,
    cot_image,
):
    nd, nf = mesh_bits()
    lead = (2,) * (nd + nf)
    bf, f32 = jnp.bfloat16, jnp.float32
    pairs, length, width_text = text_states.shape
    images, regions, width_image = image_states.shape
    padded = -(-regions // 16) * 16
    wide = image_query.shape[1] << nf
    heads = wide // HDIM
    rows_text, rows_image = pairs * length, pairs * padded
    norm_wide = norm_params.shape[1]
    device = lax.axis_index("dp") * lax.axis_size("fsdp") + lax.axis_index("fsdp")
    owner = group_ids - device * images
    text = text_states.reshape(rows_text, width_text)
    def full(shard):
        rows, cols = shard.shape
        return pltpu.VMEM((1 << nf, rows << nd, cols), bf)

    def vmem(rows, cols, dtype=bf):
        return pltpu.VMEM((rows, cols), dtype)

    n = ROW_PAIRS
    steps = pairs // n
    group = pairs // 2
    block_i = group * padded
    gather = Gather(
        [text_key, text_value, image_query, norm_params, image_output, image_inner, image_outer]
        + [text_query, image_key, image_value, text_output, text_inner, text_outer]
    )
    phases, begin = [], [0]

    def phase(run, count, marks, **kw):
        phases.append(Phase(run, count, marks, **kw))
        begin.append(begin[-1] + count)
        return begin[-2]

    phase(project_keys_phase, steps, (0.0, 1.7), needs=range(3))
    phase(attend_image_phase, steps, (0.0, 0.9, 1.8))
    stages = 1 << nf
    marks = [0.0, 1.1] + [1.1 + 1.0 * (k + 1) / stages for k in range(stages)]
    marks += [3.3, 4.4, 5.7, 6.4]
    at_image = phase(
        functools.partial(image_phase, width_text, norm_wide), 2, marks, needs=range(3, 7)
    )
    at_image_grads = phase(image_grads_phase, 4, (0.0, 1.0))
    at_back = phase(back_image_phase, steps, (0.0, 0.8, 1.7))
    at_grads = phase(key_grads_phase, 2, (0.0, 2.4))
    at_attend = phase(attend_text_phase, steps, (0.0, 0.8, 1.7, 2.6), needs=range(7, 10))
    third = width_text // 3

    def grad_out(weight_shard, inner, first, count, size):
        shape = (1 << nf, inner, weight_shard.shape[1])
        if weight_shard.shape[1] % 128:
            shape = (1, inner, weight_shard.shape[1] << nf)
        block = (shape[0], size, shape[2])
        return (struct(shape, bf), during(first, count, block, 1))

    by_pair = during(at_image, 2, (group, regions, width_image))
    probs = during(at_attend, steps, (n * heads, padded, length))
    pair_rows = during(at_attend, steps, (n * length, wide))
    back_rows = during(at_back, steps, (n * length, wide))
    image_shape = (images, padded, wide)
    a = carry(
        phases,
        dict(
            lens=(text_lengths, SCALARS),
            owner=(owner, SCALARS),
            mask=(region_mask, SCALARS),
            text=resident(text),
            states=resident(image_states),
            cot=(cot_image, by_pair),
        ),
        dict(
            ik=(struct(image_shape, bf), fixed(image_shape)),
            iv=(struct(image_shape, bf), fixed(image_shape)),
            tq=(struct((rows_text, wide), bf), pair_rows),
            tprob=(struct((pairs * heads, padded, length), f32), probs),
            tctx=(struct((rows_text, wide), bf), pair_rows),
            image_rows=(
                struct((images, padded, width_image), bf),
                fixed((images, padded, width_image)),
            ),
            norms=(struct((4, norm_wide << (nd + nf)), f32), fixed((4, norm_wide << (nd + nf)))),
            image_out=(struct(cot_image.shape, bf), by_pair),
            image_dz=(
                struct((rows_image, width_image), f32),
                during(at_image, 2, (block_i, width_image)),
            ),
            image_ngrad=(struct((4, width_image), f32), fixed((4, width_image))),
            dtk=(struct((rows_text, wide), bf), back_rows),
            dtv=(struct((rows_text, wide), bf), back_rows),
            diq=(struct(image_shape, bf), fixed(image_shape)),
            g_io=grad_out(image_output, wide, at_image_grads, 4, wide // 4),
            g_ii=grad_out(image_inner, width_image, at_image_grads, 4, width_image // 4),
            g_iu=grad_out(image_outer, width_image, at_image_grads, 4, width_image // 4),
            g_iq=grad_out(image_query, width_image, at_grads, 2, width_image // 2),
            g_tk=grad_out(text_key, width_text, at_grads, 2, width_text // 2),
            g_tv=grad_out(text_value, width_text, at_grads, 2, width_text // 2),
        ),
        dict(
            w_tq=full(text_query),
            w_tk=full(text_key),
            w_tv=full(text_value),
            w_iq=full(image_query),
            w_ik=full(image_key),
            w_iv=full(image_value),
            w_io=full(image_output),
            w_ii=full(image_inner),
            w_iu=full(image_outer),
            image=pltpu.VMEM((images, padded, width_image), bf),
            visual=vmem(block_i, width_image),
            region_counts=pltpu.SMEM((images,), jnp.int32),
            norm_parts=pltpu.VMEM(lead + norm_params.shape, f32),
            sems=pltpu.SemaphoreType.DMA((4,)),
            iq=pltpu.VMEM(image_shape, bf),
            tk=vmem(rows_text, wide),
            tv=vmem(rows_text, wide),
            iprob=pltpu.VMEM((pairs * heads, padded, length), f32),
            ictx=vmem(rows_image, wide),
            mid=vmem(rows_image, width_image),
            act=vmem(rows_image, width_image),
            hid=vmem(rows_image, width_image),
            ffn=vmem(rows_image, width_image),
            branch=vmem(rows_image, width_image),
            dctx=vmem(rows_image, wide),
            diq_sum=pltpu.VMEM(image_shape, f32),
            cot_wide=vmem(block_i, width_image, f32),
        ),
        gather,
        0,
        SEARCH,
    )
    whole = [whole_weight(s, g) for s, g in zip(gather.given, a.landed) if s is not norm_params]
    w_tk, w_tv, w_iq, _, _, _, w_tq, w_ik, w_iv, w_to, w_ti, w_tu = whole

    job = Reduce(
        [
            device_blocks(grad, shard)
            for grad, shard in (
                (a.g_io, image_output),
                (a.g_ii, image_inner),
                (a.g_iu, image_outer),
                (a.g_iq, image_query),
                (a.g_tk, text_key),
                (a.g_tv, text_value),
            )
        ]
    )
    phases, begin = [], [0]
    inner = w_ti.shape[0] * w_ti.shape[2]
    block_t = n * length
    stages = w_ti.shape[0]
    marks = [0.0, 1.6] + [1.6 + 3.6 * (k + 1) / stages for k in range(stages)]
    marks += [7.8, 9.8, 11.8, 12.6]
    at_text = phase(text_phase, steps, marks)
    at_tu = phase(functools.partial(grad_phase, "g_tu", "act", "ffn"), 12, (0.0, 0.7))
    at_ti = phase(functools.partial(grad_phase, "g_ti", "mid", "hid"), 6, (0.0, 1.4))
    at_to = phase(functools.partial(grad_phase, "g_to", "tctx", "branch"), 4, (0.0, 0.8))
    by_pair = during(at_text, steps, (n, length, width_text))

    def text_rows(cols):
        return during(at_text, steps, (block_t, cols))

    b = carry(
        phases,
        dict(
            lens=(text_lengths, SCALARS),
            x=(text, text_rows(width_text)),
            tctx=resident(a.tctx),
            cot=(cot_text, by_pair),
            norms=resident(a.norms),
            w_to=resident(w_to),
            far_w_ti=(w_ti, ANYWHERE),
            far_w_tu=(w_tu, ANYWHERE),
        ),
        dict(
            text_out=(struct(cot_text.shape, bf), by_pair),
            text_dz=(struct((rows_text, width_text), f32), text_rows(width_text)),
            dctx=(struct((rows_text, wide), bf), text_rows(wide)),
            text_ngrad=(struct((4, width_text), f32), fixed((4, width_text))),
            g_tu=grad_out(text_outer, inner, at_tu, 12, inner // 12),
            g_ti=grad_out(text_inner, width_text, at_ti, 6, width_text // 6),
            g_to=grad_out(text_output, wide, at_to, 4, wide // 4),
        ),
        dict(
            w_ti=pltpu.VMEM(w_ti.shape, bf),
            w_tu=pltpu.VMEM(w_tu.shape, bf),
            sems=pltpu.SemaphoreType.DMA((len(TEXT_FAR),)),
            mid=vmem(rows_text, width_text),
            act=vmem(rows_text, inner),
            hid=vmem(rows_text, inner),
            ffn=vmem(rows_text, width_text),
            branch=vmem(rows_text, width_text),
        ),
        job,
        1,
    )
    o_io, o_ii, o_iu, o_iq, o_tk, o_tv = b.landed

    norm_rows = norm_blocks(jnp.concatenate([b.text_ngrad, a.image_ngrad], axis=1))
    job = Reduce(
        [
            device_blocks(b.g_tu, text_outer),
            device_blocks(b.g_ti, text_inner),
            device_blocks(b.g_to, text_output),
            norm_rows,
        ],
        dict(
            g_tq=struct(lead + text_query.shape, bf),
            g_ik=struct(lead + image_key.shape, bf),
            g_iv=struct(lead + image_value.shape, bf),
        ),
    )
    phases, begin = [], [0]
    at_back = phase(back_text_phase, steps, (0.0, 0.8, 1.7))
    phase(query_grads_phase, 2, (0.0, 2.0), makes=range(4, 7))
    at_data = phase(data_grads_phase, steps, (0.0, 0.9, 1.8, 2.6))
    probs = during(at_back, steps, (n * heads, padded, length))
    back_rows = during(at_back, steps, (n * length, wide))
    data_rows = during(at_data, steps, (block_t, wide))
    data_out = during(at_data, steps, (block_t, width_text))
    c = carry(
        phases,
        dict(
            owner=(owner, SCALARS),
            ik=resident(a.ik),
            iv=resident(a.iv),
            tq=(a.tq, back_rows),
            tprob=(a.tprob, probs),
            dtc=(b.dctx, back_rows),
            far_text=(text, ANYWHERE),
            image=resident(a.image_rows),
            text_dz=(b.text_dz, data_out),
            dtk=(a.dtk, data_rows),
            dtv=(a.dtv, data_rows),
            far_image_dz=(a.image_dz, ANYWHERE),
            diq=resident(a.diq),
            far_w_tq=(w_tq, ANYWHERE),
            far_w_tk=(w_tk, ANYWHERE),
            far_w_tv=(w_tv, ANYWHERE),
            far_w_iq=(w_iq, ANYWHERE),
            far_w_ik=(w_ik, ANYWHERE),
            far_w_iv=(w_iv, ANYWHERE),
        ),
        dict(
            text_grad=(struct((rows_text, width_text), f32), data_out),
            image_grad=(struct(image_states.shape, f32), fixed(image_states.shape)),
        ),
        dict(
            text=vmem(rows_text, width_text),
            image_dz=vmem(rows_image, width_image, f32),
            w_tq=pltpu.VMEM(w_tq.shape, bf),
            w_tk=pltpu.VMEM(w_tk.shape, bf),
            w_tv=pltpu.VMEM(w_tv.shape, bf),
            w_iq=pltpu.VMEM(w_iq.shape, bf),
            w_ik=pltpu.VMEM(w_ik.shape, bf),
            w_iv=pltpu.VMEM(w_iv.shape, bf),
            sems=pltpu.SemaphoreType.DMA((len(LAST_FAR),)),
            dtq=vmem(rows_text, wide),
            dik=pltpu.VMEM(image_shape, bf),
            div=pltpu.VMEM(image_shape, bf),
            dik_sum=pltpu.VMEM(image_shape, f32),
            div_sum=pltpu.VMEM(image_shape, f32),
            g_tq=pltpu.VMEM(lead + text_query.shape, bf),
            g_ik=pltpu.VMEM(lead + image_key.shape, bf),
            g_iv=pltpu.VMEM(lead + image_value.shape, bf),
        ),
        job,
        2,
        SEARCH,
    )
    o_tu, o_ti, o_to, o_norm, o_tq, o_ik, o_iv = c.landed
    owned = pass_on([o_iq, o_ik, o_iv, o_tq, o_tk, o_tv, o_io, o_to, o_ii, o_iu, o_ti, o_tu])
    return (
        b.text_out,
        a.image_out,
        c.text_grad.reshape(text_states.shape),
        c.image_grad,
        *owned,
        o_norm[:4, :norm_wide],
    )


def solution(mesh):
    placed = (
        P(("dp", "fsdp"), None, None),
        P(("dp", "fsdp"), None, None),
        P(("dp", "fsdp")),
        P(("dp", "fsdp"), None),
        P(("dp", "fsdp")),
        P("dp", "fsdp"),
        P("dp", "fsdp"),
        P("dp", "fsdp"),
        P("dp", "fsdp"),
        P("dp", "fsdp"),
        P("dp", "fsdp"),
        P("dp", "fsdp"),
        P("dp", "fsdp"),
        P("dp", "fsdp"),
        P("dp", "fsdp"),
        P("dp", "fsdp"),
        P("dp", "fsdp"),
        P(None, ("dp", "fsdp")),
        P(("dp", "fsdp"), None, None),
        P(("dp", "fsdp"), None, None),
    )
    return jax.shard_map(
        body,
        mesh=mesh,
        in_specs=placed,
        out_specs=(
            P(("dp", "fsdp"), None, None),
            P(("dp", "fsdp"), None, None),
            P(("dp", "fsdp"), None, None),
            P(("dp", "fsdp"), None, None),
            P("dp", "fsdp"),
            P("dp", "fsdp"),
            P("dp", "fsdp"),
            P("dp", "fsdp"),
            P("dp", "fsdp"),
            P("dp", "fsdp"),
            P("dp", "fsdp"),
            P("dp", "fsdp"),
            P("dp", "fsdp"),
            P("dp", "fsdp"),
            P("dp", "fsdp"),
            P("dp", "fsdp"),
            P(None, ("dp", "fsdp")),
        ),
        check_vma=False,
    )
```
